32 devices in a mesh: dp: 8 (over z, y), head: 4 (over x, core).
Axes of the slice: x: 2, y: 2, z: 4, core: 2. Of those that a mesh axis runs over, the one named last changes fastest.
Arguments:
- q_latent: bfloat16 [768, 65536], P('dp', 'head'), may hold values from -64 to 64
- q_rope: bfloat16 [768, 8192], P('dp', 'head'), may hold values from -6 to 6
- cache_latent: bfloat16 [32, 512, 512], P('dp'), may hold values from -6 to 6
- cache_rope: bfloat16 [32, 64, 512], P('dp'), may hold values from -6 to 6
- lengths: int32 [32], P('dp'), may hold values from 128 to 512
- loads: int32 [8], replicated, may hold values from 1 to 4
- owner_rank: int32 [64], P('dp'), may hold values from 0 to 7, as said below
- owner_pick: int32 [64], P('dp'), may hold values from 0 to 839
- w_uv: bfloat16 [128, 512, 128], P('head'), may hold values from -0.25 to 0.25
- w_out: bfloat16 [16384, 7168], P('head', 'dp'), may hold values from -0.046875 to 0.046875
Outputs:
- layer_out: bfloat16 [768, 7168], P('head', 'dp')
The draws below stay inside these ranges and needn't reach their ends.
Inputs may be any that keep to these rules, and one draw needn't show every extreme that they name: `owner_rank`: the 8 bundles of one dp rank name distinct owner ranks, and in every draw some rank is named by every dp rank.
All inputs are finite; a program needn't handle non-finite values.
Results may differ from the reference program's by a relative error of at most 0.0064.
Values may be sent and summed in bfloat16 or wider, within the bound.
No kernel may reach another device: no remote copies, remote signals or barrier semaphores. Data moves between devices by JAX's collectives and lax.ppermute only.
A program may use at most 128 MiB of HBM per device.

```python
import math
import jax
import jax.numpy as jnp
from jax import lax

D = 7168
H = 128
LAT = 512
ROPE = 64
VD = 128
ROLL = 12
LMAX = 512
PR_DEV = 4
BUND_DEV = 8
PROMPTS = 32
BUNDLES = 64
ROWS = 768
N_DP = 8


def draw_owner_rank(key, part):
    base_key = jax.random.fold_in(key, 7)
    jitter_key, level_key, hot_key, order_key = jax.random.split(base_key, 4)
    jitter = jax.random.randint(jitter_key, (N_DP, N_DP), 0, 2 ** 12)
    levels = jax.random.permutation(level_key, N_DP)
    hot_rank = jax.random.randint(hot_key, (), 0, N_DP)
    columns = jnp.arange(N_DP)
    scores = jitter + levels[None, :] * (2 ** 12 // N_DP) + jnp.where(columns == hot_rank, 2 ** 14, 0)[None, :]
    scores = scores * 256 + columns[None, :]
    chosen = lax.top_k(scores, BUND_DEV)[1]
    row_keys = jax.random.split(order_key, N_DP)
    shuffled = jax.vmap(jax.random.permutation)(row_keys, chosen)
    return shuffled.reshape(N_DP * BUND_DEV).astype(jnp.int32)


def draw_q_latent(key, part):
    base_key = jax.random.fold_in(key, 21)
    entry_key = jax.random.fold_in(base_key, 0)
    row_count = N_DP * BUND_DEV * ROLL
    entries = jnp.clip(jax.random.normal(entry_key, (row_count, H, LAT), jnp.float32), -6.0, 6.0)
    return entries.reshape(row_count, H * LAT).astype(jnp.bfloat16)


def draw_cache_latent(key, part):
    base_key = jax.random.fold_in(key, 33)
    entry_key = jax.random.fold_in(base_key, 0)
    prompt_count = N_DP * PR_DEV
    entries = jnp.clip(jax.random.normal(entry_key, (prompt_count, LMAX, LAT), jnp.float32), -6.0, 6.0)
    return entries.astype(jnp.bfloat16)


def touch_ends(values, stream_key, least, largest):
    dims = values.shape
    index_at = [jax.random.randint(jax.random.fold_in(stream_key, axis), (), 0, dims[axis]) for axis in range(len(dims))]
    values = values.at[tuple(index_at)].set(least)
    longest = dims.index(max(dims))
    index_at[longest] = (index_at[longest] + 1) % dims[longest]
    return values.at[tuple(index_at)].set(largest)


def steps_of(stream_key, dims, cuts, low, high):
    level = 1.0
    for position, blocks in cuts:
        heights = jax.random.uniform(jax.random.fold_in(jax.random.fold_in(stream_key, 6), position), (blocks,), jnp.float32, low / len(cuts), high / len(cuts))
        level = level * jnp.repeat(jnp.exp(heights), dims[position] // blocks).reshape((-1,) + (1,) * (len(dims) - 1 - position))
    return level


def scatter_about(stream_key, shape, spread, reach, pieces=(), dtype=jnp.bfloat16):
    loudness = steps_of(stream_key, shape, pieces, -0.22, 0.18) if pieces else 1.0
    drawn = jax.random.normal(stream_key, shape, jnp.float32) * spread * loudness
    return jnp.minimum(jnp.maximum(drawn, -reach), reach).astype(dtype)


def setup_inputs(seed: int = 0) -> dict:
    streams_of = jax.random.split(jax.random.key(seed), 11)
    return {
        "q_latent": draw_q_latent(jax.random.fold_in(streams_of[10], 71), 0),
        "q_rope": scatter_about(streams_of[1], (ROWS, H * ROPE), 1.0, 6.0, ((0, 8), (1, 4))),
        "cache_latent": draw_cache_latent(jax.random.fold_in(streams_of[10], 71), 0),
        "cache_rope": scatter_about(streams_of[3], (PROMPTS, ROPE, LMAX), 1.0, 6.0, ((0, 8),)),
        "lengths": touch_ends(jax.random.randint(streams_of[4], (PROMPTS,), LMAX // 4, LMAX + 1), jax.random.fold_in(streams_of[4], 1), LMAX // 4, LMAX).astype(jnp.int32),
        "loads": touch_ends(jax.random.randint(streams_of[5], (N_DP,), 1, PR_DEV + 1), jax.random.fold_in(streams_of[5], 1), 1, PR_DEV).astype(jnp.int32),
        "owner_rank": draw_owner_rank(jax.random.fold_in(streams_of[10], 71), 0),
        "owner_pick": touch_ends(jax.random.randint(streams_of[7], (BUNDLES,), 0, 840), jax.random.fold_in(streams_of[7], 1), 0, 839).astype(jnp.int32),
        "w_uv": scatter_about(streams_of[8], (H, LAT, VD), LAT ** -0.5, 0.25, ((0, 4),)),
        "w_out": scatter_about(streams_of[9], (H * VD, D), (H * VD) ** -0.5, 0.046875, ((0, 4), (1, 8))),
    }


def reference(q_latent, q_rope, cache_latent, cache_rope, lengths, loads, owner_rank, owner_pick, w_uv, w_out):
    row_count = q_latent.shape[0]
    bundles = row_count // ROLL
    slot_pick = owner_pick % loads[owner_rank]
    prompt_id = (owner_rank * PR_DEV + slot_pick).astype(jnp.int32)
    score_scale = 1.0 / math.sqrt(VD + ROPE)
    lat_bundles = q_latent.reshape(bundles, ROLL * H, LAT)
    rope_bundles = q_rope.reshape(bundles, ROLL * H, ROPE)
    positions = jnp.arange(LMAX)

    def attend_one(item_args):
        queries, rope_queries, prompt_index = item_args
        key_rows = cache_latent[prompt_index]
        rope_keys = cache_rope[prompt_index]
        length = lengths[prompt_index]
        scores = lax.dot_general(queries, key_rows, (((1,), (1,)), ((), ())), preferred_element_type=jnp.float32)
        scores = scores + jnp.dot(rope_queries, rope_keys, preferred_element_type=jnp.float32)
        scores = scores * score_scale
        live_mask = positions[None, :] < length
        scores = jnp.where(live_mask, scores, -1e+30)
        row_max = lax.optimization_barrier(jnp.max(scores, axis=1, keepdims=True))
        weights = jnp.where(live_mask, jnp.exp(scores - row_max), 0.0)
        row_total = lax.optimization_barrier(jnp.sum(weights, axis=1, keepdims=True))
        weights_bf = (weights / row_total).astype(jnp.bfloat16)
        mixed_lat = jnp.dot(weights_bf, key_rows, preferred_element_type=jnp.float32).astype(jnp.bfloat16)
        grouped = mixed_lat.reshape(ROLL, H, LAT).astype(jnp.float32)
        values = jnp.einsum('rhl,hlv->rhv', grouped, w_uv.astype(jnp.float32)).astype(jnp.bfloat16)
        return values.reshape(ROLL, H * VD)
    values = lax.map(attend_one, (lat_bundles, rope_bundles, prompt_id))
    layer_out = jnp.dot(values.reshape(row_count, H * VD), w_out, preferred_element_type=jnp.float32)
    return layer_out.astype(jnp.bfloat16)
```

```python
import functools
import math

import jax
import jax.numpy as jnp
from jax import lax
from jax.experimental import pallas as pl
from jax.experimental.pallas import tpu as pltpu
from jax.sharding import PartitionSpec as P

ROPE = 64
VD = 128


def ring_order(size):
    fast = 1 << (max(size.bit_length() - 1, 0) // 2)
    slow = size // fast
    if fast == 1 or slow % 2:
        return list(range(size))
    cells = [(z, 0) for z in range(slow)]
    for step, z in enumerate(range(slow - 1, -1, -1)):
        ys = range(1, fast) if step % 2 == 0 else range(fast - 1, 0, -1)
        cells += [(z, y) for y in ys]
    return [z * fast + y for z, y in cells]


def slot_for(info, loads, width, bundles, requester, owner):
    pick = jnp.int32(0)
    for j in range(bundles):
        hit = info[requester * width + j] == owner
        pick = jnp.where(hit, info[requester * width + bundles + j], pick)
    return lax.rem(pick, loads[owner])


def pack_kernel(info, loads, place, lat_ref, rope_ref, out_ref):
    rows = lat_ref.shape[1]
    out_ref[0, :rows, :] = lat_ref[0]
    out_ref[0, rows:, :] = rope_ref[0]


def pack(info, loads, place, cache_latent, cache_rope, ranks, heads, width, bundles):
    rows = cache_latent.shape[1] // heads
    dims = cache_rope.shape[1] // heads
    wide = cache_latent.shape[2]

    def source(i, info, loads, place):
        return slot_for(info, loads, width, bundles, i, place[0]), place[1], 0

    return pl.pallas_call(
        pack_kernel,
        out_shape=jax.ShapeDtypeStruct((ranks, rows + dims, wide), cache_latent.dtype),
        grid_spec=pltpu.PrefetchScalarGridSpec(
            num_scalar_prefetch=3,
            grid=(ranks,),
            in_specs=[pl.BlockSpec((1, rows, wide), source), pl.BlockSpec((1, dims, wide), source)],
            out_specs=pl.BlockSpec((1, rows + dims, wide), lambda i, *_: (i, 0, 0)),
        ),
        name="pack",
    )(info, loads, place, cache_latent, cache_rope)


def attend_kernel(
    heads, width, bundles, scale, block, info, loads, place, q_ref, qr_ref, *refs
):
    parts = refs[:heads]
    w_ref, out_ref, lat, rope, mixed = refs[heads:]
    b = pl.program_id(0)
    rows = lat.shape[0] // heads
    dims = rope.shape[0] // heads
    for m in range(heads):
        at = jnp.bitwise_xor(place[1], m)
        lat[pl.ds(pl.multiple_of(at * rows, rows), rows), :] = parts[m][0, :rows, :]
        rope[pl.ds(pl.multiple_of(at * dims, dims), dims), :] = parts[m][0, rows:, :]
    base = place[0] * width
    owner = info[base + b]
    slot = lax.rem(info[base + bundles + b], loads[owner])
    length = info[owner * width + 2 * bundles + slot]
    total_rows = q_ref.shape[1]
    live = lax.broadcasted_iota(jnp.int32, (block, lat.shape[0]), 1) < length
    for i in range(total_rows // block):
        at = slice(i * block, (i + 1) * block)
        s = lax.dot_general(
            q_ref[0, at, :], lat[...], (((1,), (1,)), ((), ())), preferred_element_type=jnp.float32
        )
        s = s + jnp.dot(qr_ref[0, at, :], rope[...], preferred_element_type=jnp.float32)
        s = jnp.where(live, s * scale, -1e30)
        w = jnp.exp(s - jnp.max(s, axis=1, keepdims=True))
        total = jnp.sum(w, axis=1, keepdims=True)
        o = jnp.dot(w.astype(jnp.bfloat16), lat[...], preferred_element_type=jnp.float32)
        o = o / total
        for c in range(mixed.shape[0]):
            piece = o[:, c * 128 : (c + 1) * 128]
            mixed[c, pl.ds(b * total_rows + i * block, block), :] = piece

    @pl.when(b == pl.num_programs(0) - 1)
    def _():
        local_heads, _, value_width = w_ref.shape
        n = mixed.shape[1] // local_heads
        for h in range(local_heads):
            x = jnp.concatenate(
                [mixed[c, pl.ds(h, n, stride=local_heads), :] for c in range(mixed.shape[0])], axis=1
            ).astype(jnp.bfloat16)
            v = jnp.dot(x, w_ref[h], preferred_element_type=jnp.float32)
            out_ref[:, h * value_width : (h + 1) * value_width] = v.astype(jnp.bfloat16)


def attend(info, loads, place, q, qr, parts, w_uv, width, bundles):
    heads = len(parts)
    _, q_rows, wide = q.shape
    _, part_rows, _ = parts[0].shape
    local_heads, _, value_width = w_uv.shape
    dims = qr.shape[2] // heads
    rows = part_rows - dims
    row_count = bundles * q_rows // local_heads

    def theirs(b, info, loads, place):
        return info[place[0] * width + b], 0, 0

    block = math.gcd(q_rows, 128)
    return pl.pallas_call(
        functools.partial(
            attend_kernel, heads, width, bundles, 1.0 / math.sqrt(VD + ROPE), block
        ),
        out_shape=jax.ShapeDtypeStruct((row_count, local_heads * value_width), jnp.bfloat16),
        grid_spec=pltpu.PrefetchScalarGridSpec(
            num_scalar_prefetch=3,
            grid=(bundles,),
            in_specs=[
                pl.BlockSpec((1, q_rows, wide), lambda b, *_: (b, 0, 0)),
                pl.BlockSpec((1, q_rows, qr.shape[2]), lambda b, *_: (b, 0, 0)),
            ]
            + [pl.BlockSpec((1, part_rows, wide), theirs)] * heads
            + [pl.BlockSpec(w_uv.shape, lambda b, *_: (0, 0, 0))],
            out_specs=pl.BlockSpec((row_count, local_heads * value_width), lambda b, *_: (0, 0)),
            scratch_shapes=[
                pltpu.VMEM((rows * heads, wide), jnp.bfloat16),
                pltpu.VMEM((dims * heads, wide), jnp.bfloat16),
                pltpu.VMEM((wide // 128, bundles * q_rows, 128), jnp.float32),
            ],
        ),
        name="attend",
    )(info, loads, place, q, qr, *parts, w_uv)


def local(
    q_latent, q_rope, cache_latent, cache_rope, lengths, loads, owner_rank, owner_pick, w_uv, w_out
):
    ranks = lax.axis_size("dp")
    heads = lax.axis_size("head")
    me = lax.axis_index("dp")
    head = lax.axis_index("head")
    bundles = owner_rank.shape[0]
    roll_count = q_latent.shape[0] // bundles
    local_heads = w_uv.shape[0]
    place = jnp.stack([me, head]).astype(jnp.int32)

    facts = jnp.concatenate([owner_rank, owner_pick, lengths])
    width = 32
    facts = jnp.pad(facts, (0, width - facts.shape[0]))
    info = lax.all_to_all(
        jnp.broadcast_to(facts[None], (ranks, width)), "dp", split_axis=0, concat_axis=0, tiled=True
    ).reshape(-1)
    q = q_latent.reshape(bundles, roll_count * local_heads, -1)
    qr = q_rope.reshape(bundles, roll_count * local_heads, -1)

    packed = pack(info, loads, place, cache_latent, cache_rope, ranks, heads, width, bundles)
    mine = lax.all_to_all(packed, "dp", split_axis=0, concat_axis=0, tiled=True)
    parts = [mine]
    bit = heads // 2
    found = {0: mine}
    while bit:
        pairs = [(i, i ^ bit) for i in range(heads)]
        for m in list(found):
            found[m ^ bit] = lax.ppermute(found[m], "head", pairs)
        bit //= 2
    parts = [found[m] for m in range(heads)]
    values = attend(info, loads, place, q, qr, parts, w_uv, width, bundles)

    order = ring_order(ranks)
    ahead = [(order[i], order[(i + 1) % ranks]) for i in range(ranks)]
    behind = [(b, a) for a, b in ahead]
    half = values.shape[1] // 2

    def project(x):
        return jnp.dot(x, w_out, preferred_element_type=jnp.float32).astype(jnp.bfloat16)

    partial = {0: project(values)}
    fore = back = values
    for step in range(1, (ranks + 1) // 2):
        fore = lax.ppermute(fore, "dp", ahead)
        back = lax.ppermute(back, "dp", behind)
        both = project(jnp.concatenate([fore, back], axis=0))
        partial[-step] = both[: values.shape[0]]
        partial[step] = both[values.shape[0] :]
    if ranks % 2 == 0:
        left = lax.ppermute(fore[:, :half], "dp", ahead)
        right = lax.ppermute(back[:, half:], "dp", behind)
        partial[ranks // 2] = project(jnp.concatenate([left, right], axis=1))
    stacked = jnp.stack([partial[k if 2 * k <= ranks else k - ranks] for k in range(ranks)])
    position = [0] * ranks
    for i, r in enumerate(order):
        position[r] = i
    position = jnp.asarray(position, jnp.int32)
    by_rank = stacked[(position - position[me]) % ranks]
    shares = by_rank.reshape(heads, -1, w_out.shape[1])
    got = lax.all_to_all(shares, "head", split_axis=0, concat_axis=0, tiled=True)
    return jnp.sum(got.astype(jnp.float32), axis=0).astype(jnp.bfloat16)


def solution(mesh):
    in_specs = (
        P("dp", "head"),
        P("dp", "head"),
        P("dp", None, None),
        P("dp", None, None),
        P("dp"),
        P(),
        P("dp"),
        P("dp"),
        P("head", None, None),
        P("head", "dp"),
    )
    out_specs = P("head", "dp")
    return jax.shard_map(local, mesh=mesh, in_specs=in_specs, out_specs=out_specs, check_vma=False)
```

```python
import functools
import math

import jax
import jax.numpy as jnp
from jax import lax
from jax.experimental import pallas as pl
from jax.experimental.pallas import tpu as pltpu
from jax.sharding import PartitionSpec as P

ROPE = 64
VD = 128


def ring_order(size):
    fast = 1 << (max(size.bit_length() - 1, 0) // 2)
    slow = size // fast
    if fast == 1 or slow % 2:
        return list(range(size))
    cells = [(z, 0) for z in range(slow)]
    for step, z in enumerate(range(slow - 1, -1, -1)):
        ys = range(1, fast) if step % 2 == 0 else range(fast - 1, 0, -1)
        cells += [(z, y) for y in ys]
    return [z * fast + y for z, y in cells]


def ring_fits(ranks, heads):
    if ranks % 2 or ranks < 4 or ranks % heads or heads & (heads - 1):
        return False
    order, per_head = ring_order(ranks), ranks // heads
    return all(
        order[p - k] // per_head != order[(p + k) % ranks] // per_head
        for p in range(ranks)
        for k in range(1, ranks // 2)
    )


def slot_for(info, loads, width, bundles, requester, owner):
    pick = jnp.int32(0)
    for j in range(bundles):
        hit = info[requester * width + j] == owner
        pick = jnp.where(hit, info[requester * width + bundles + j], pick)
    return lax.rem(pick, loads[owner])


def pack_kernel(info, loads, place, lat_ref, rope_ref, out_ref):
    rows = lat_ref.shape[1]
    out_ref[0, :rows, :] = lat_ref[0]
    out_ref[0, rows:, :] = rope_ref[0]


def pack(info, loads, place, cache_latent, cache_rope, ranks, heads, width, bundles):
    rows = cache_latent.shape[1] // heads
    dims = cache_rope.shape[1] // heads
    wide = cache_latent.shape[2]

    def source(i, info, loads, place):
        return slot_for(info, loads, width, bundles, i, place[0]), place[1], 0

    return pl.pallas_call(
        pack_kernel,
        out_shape=jax.ShapeDtypeStruct((ranks, rows + dims, wide), cache_latent.dtype),
        grid_spec=pltpu.PrefetchScalarGridSpec(
            num_scalar_prefetch=3,
            grid=(ranks,),
            in_specs=[pl.BlockSpec((1, rows, wide), source), pl.BlockSpec((1, dims, wide), source)],
            out_specs=pl.BlockSpec((1, rows + dims, wide), lambda i, *_: (i, 0, 0)),
        ),
        name="pack",
    )(info, loads, place, cache_latent, cache_rope)


def attend_kernel(
    heads, width, bundles, scale, block, info, loads, place, q_ref, qr_ref, *refs
):
    parts = refs[:heads]
    w_ref, out_ref, lat, rope, mixed = refs[heads:]
    b = pl.program_id(0)
    rows = lat.shape[0] // heads
    dims = rope.shape[0] // heads
    for m in range(heads):
        at = jnp.bitwise_xor(place[1], m)
        lat[pl.ds(pl.multiple_of(at * rows, rows), rows), :] = parts[m][0, :rows, :]
        rope[pl.ds(pl.multiple_of(at * dims, dims), dims), :] = parts[m][0, rows:, :]
    base = place[0] * width
    owner = info[base + b]
    slot = lax.rem(info[base + bundles + b], loads[owner])
    length = info[owner * width + 2 * bundles + slot]
    total_rows = q_ref.shape[1]
    live = lax.broadcasted_iota(jnp.int32, (block, lat.shape[0]), 1) < length
    for i in range(total_rows // block):
        at = slice(i * block, (i + 1) * block)
        s = lax.dot_general(
            q_ref[0, at, :], lat[...], (((1,), (1,)), ((), ())), preferred_element_type=jnp.float32
        )
        s = s + jnp.dot(qr_ref[0, at, :], rope[...], preferred_element_type=jnp.float32)
        s = jnp.where(live, s * scale, -1e30)
        w = jnp.exp(s - jnp.max(s, axis=1, keepdims=True))
        w = w * (1.0 / jnp.sum(w, axis=1, keepdims=True))
        o = jnp.dot(w.astype(jnp.bfloat16), lat[...], preferred_element_type=jnp.float32)
        for c in range(mixed.shape[0]):
            piece = o[:, c * 128 : (c + 1) * 128]
            mixed[c, pl.ds(b * total_rows + i * block, block), :] = piece

    @pl.when(b == pl.num_programs(0) - 1)
    def _():
        local_heads, _, value_width = w_ref.shape
        n = mixed.shape[1] // local_heads
        for h in range(local_heads):
            x = jnp.concatenate(
                [mixed[c, pl.ds(h, n, stride=local_heads), :] for c in range(mixed.shape[0])], axis=1
            ).astype(jnp.bfloat16)
            v = jnp.dot(x, w_ref[h], preferred_element_type=jnp.float32)
            out_ref[:, h * value_width : (h + 1) * value_width] = v.astype(jnp.bfloat16)


def attend(info, loads, place, q, qr, parts, w_uv, width, bundles):
    heads = len(parts)
    _, q_rows, wide = q.shape
    _, part_rows, _ = parts[0].shape
    local_heads, _, value_width = w_uv.shape
    dims = qr.shape[2] // heads
    rows = part_rows - dims
    row_count = bundles * q_rows // local_heads

    def theirs(b, info, loads, place):
        return info[place[0] * width + b], 0, 0

    block = math.gcd(q_rows, 128)
    return pl.pallas_call(
        functools.partial(
            attend_kernel, heads, width, bundles, 1.0 / math.sqrt(VD + ROPE), block
        ),
        out_shape=jax.ShapeDtypeStruct((row_count, local_heads * value_width), jnp.bfloat16),
        grid_spec=pltpu.PrefetchScalarGridSpec(
            num_scalar_prefetch=3,
            grid=(bundles,),
            in_specs=[
                pl.BlockSpec((1, q_rows, wide), lambda b, *_: (b, 0, 0)),
                pl.BlockSpec((1, q_rows, qr.shape[2]), lambda b, *_: (b, 0, 0)),
            ]
            + [pl.BlockSpec((1, part_rows, wide), theirs)] * heads
            + [pl.BlockSpec(w_uv.shape, lambda b, *_: (0, 0, 0))],
            out_specs=pl.BlockSpec((row_count, local_heads * value_width), lambda b, *_: (0, 0)),
            scratch_shapes=[
                pltpu.VMEM((rows * heads, wide), jnp.bfloat16),
                pltpu.VMEM((dims * heads, wide), jnp.bfloat16),
                pltpu.VMEM((wide // 128, bundles * q_rows, 128), jnp.float32),
            ],
        ),
        name="attend",
    )(info, loads, place, q, qr, *parts, w_uv)


def local_general(
    q_latent, q_rope, cache_latent, cache_rope, lengths, loads, owner_rank, owner_pick, w_uv, w_out
):
    ranks = lax.axis_size("dp")
    heads = lax.axis_size("head")
    me = lax.axis_index("dp")
    head = lax.axis_index("head")
    bundles = owner_rank.shape[0]
    roll_count = q_latent.shape[0] // bundles
    local_heads = w_uv.shape[0]
    place = jnp.stack([me, head]).astype(jnp.int32)

    facts = jnp.concatenate([owner_rank, owner_pick, lengths])
    width = 32
    facts = jnp.pad(facts, (0, width - facts.shape[0]))
    info = lax.all_to_all(
        jnp.broadcast_to(facts[None], (ranks, width)), "dp", split_axis=0, concat_axis=0, tiled=True
    ).reshape(-1)
    q = q_latent.reshape(bundles, roll_count * local_heads, -1)
    qr = q_rope.reshape(bundles, roll_count * local_heads, -1)

    packed = pack(info, loads, place, cache_latent, cache_rope, ranks, heads, width, bundles)
    mine = lax.all_to_all(packed, "dp", split_axis=0, concat_axis=0, tiled=True)
    parts = [mine]
    bit = heads // 2
    found = {0: mine}
    while bit:
        pairs = [(i, i ^ bit) for i in range(heads)]
        for m in list(found):
            found[m ^ bit] = lax.ppermute(found[m], "head", pairs)
        bit //= 2
    parts = [found[m] for m in range(heads)]
    values = attend(info, loads, place, q, qr, parts, w_uv, width, bundles)

    order = ring_order(ranks)
    ahead = [(order[i], order[(i + 1) % ranks]) for i in range(ranks)]
    behind = [(b, a) for a, b in ahead]
    half = values.shape[1] // 2

    def project(x):
        return jnp.dot(x, w_out, preferred_element_type=jnp.float32).astype(jnp.bfloat16)

    partial = {0: project(values)}
    fore = back = values
    for step in range(1, (ranks + 1) // 2):
        fore = lax.ppermute(fore, "dp", ahead)
        back = lax.ppermute(back, "dp", behind)
        both = project(jnp.concatenate([fore, back], axis=0))
        partial[-step] = both[: values.shape[0]]
        partial[step] = both[values.shape[0] :]
    if ranks % 2 == 0:
        left = lax.ppermute(fore[:, :half], "dp", ahead)
        right = lax.ppermute(back[:, half:], "dp", behind)
        partial[ranks // 2] = project(jnp.concatenate([left, right], axis=1))
    stacked = jnp.stack([partial[k if 2 * k <= ranks else k - ranks] for k in range(ranks)])
    position = [0] * ranks
    for i, r in enumerate(order):
        position[r] = i
    position = jnp.asarray(position, jnp.int32)
    by_rank = stacked[(position - position[me]) % ranks]
    shares = by_rank.reshape(heads, -1, w_out.shape[1])
    got = lax.all_to_all(shares, "head", split_axis=0, concat_axis=0, tiled=True)
    return jnp.sum(got.astype(jnp.float32), axis=0).astype(jnp.bfloat16)


def slots_kernel(plan, own, heads, scale, block, table, info, place, q_ref, qr_ref, *refs):
    count = len(plan)
    refs = list(refs)
    if own:
        full_lat, full_rope = refs.pop(0), refs.pop(0)
    shipped = count - own
    parts = [refs[j * heads : (j + 1) * heads] for j in range(shipped)]
    w_hbm, out_ref, lat, rope, mixed, w_ref, sem = refs[shipped * heads :]
    i = pl.program_id(0)
    rows = lat.shape[0] // heads
    dims = rope.shape[0] // heads
    w_copy = pltpu.make_async_copy(w_hbm, w_ref, sem)

    @pl.when(i == 0)
    def _():
        w_copy.start()

    for j in range(count):

        @pl.when(i == j)
        def _():
            if own and j == 0:
                lat[...] = full_lat[0]
                rope[...] = full_rope[0]
                return
            for m in range(heads):
                part = parts[j - own][m]
                at = jnp.bitwise_xor(place[1], m)
                lat[pl.ds(pl.multiple_of(at * rows, rows), rows), :] = part[0, :rows, :]
                rope[pl.ds(pl.multiple_of(at * dims, dims), dims), :] = part[0, rows:, :]

    length = info[plan[0]]
    for j in range(1, count):
        length = jnp.where(i == j, info[plan[j]], length)
    total_rows = q_ref.shape[1]
    live = lax.broadcasted_iota(jnp.int32, (block, lat.shape[0]), 1) < length
    for r in range(total_rows // block):
        at = slice(r * block, (r + 1) * block)
        s = lax.dot_general(
            q_ref[0, at, :], lat[...], (((1,), (1,)), ((), ())), preferred_element_type=jnp.float32
        )
        s = s + jnp.dot(qr_ref[0, at, :], rope[...], preferred_element_type=jnp.float32)
        s = jnp.where(live, s * scale, -1e30)
        w = jnp.exp(s - jnp.max(s, axis=1, keepdims=True))
        w = w * (1.0 / jnp.sum(w, axis=1, keepdims=True))
        o = jnp.dot(w.astype(jnp.bfloat16), lat[...], preferred_element_type=jnp.float32)
        for c in range(mixed.shape[0]):
            mixed[c, pl.ds(i * total_rows + r * block, block), :] = o[:, c * 128 : (c + 1) * 128]

    @pl.when(i == count - 1)
    def _():
        w_copy.wait()
        local_heads, _, value_width = w_ref.shape
        n = mixed.shape[1] // local_heads
        for h in range(local_heads):
            x = jnp.concatenate(
                [mixed[c, pl.ds(h, n, stride=local_heads), :] for c in range(mixed.shape[0])], axis=1
            ).astype(jnp.bfloat16)
            v = jnp.dot(x, w_ref[h], preferred_element_type=jnp.float32)
            out_ref[:, h * value_width : (h + 1) * value_width] = v.astype(jnp.bfloat16)


def attend_slots(plan, table, info, place, q, qr, full, parts, w_uv, heads):
    own = 1 if full is not None else 0
    count = len(plan)
    _, q_rows, wide = q.shape
    local_heads, _, value_width = w_uv.shape
    row_count = count * q_rows // local_heads
    part_rows = parts[0][0][0].shape[1]
    dims = qr.shape[2] // heads
    rows = part_rows - dims
    block = math.gcd(q_rows, 128)

    def bundle(i, table, info, place):
        at = table[0, plan[0]]
        for j in range(1, count):
            at = jnp.where(i == j, table[0, plan[j]], at)
        return at, 0, 0

    in_specs = [
        pl.BlockSpec((1, q_rows, wide), bundle),
        pl.BlockSpec((1, q_rows, qr.shape[2]), bundle),
    ]
    args = [q, qr]
    if own:
        here = lambda i, table, info, place: (table[1, plan[0]], 0, 0)
        in_specs += [
            pl.BlockSpec((1, rows * heads, wide), here),
            pl.BlockSpec((1, dims * heads, wide), here),
        ]
        args += list(full)
    for slot in parts:
        for array, index in slot:
            in_specs.append(
                pl.BlockSpec((1, part_rows, wide), lambda i, *_, index=index: (index, 0, 0))
            )
            args.append(array)
    in_specs.append(pl.BlockSpec(memory_space=pl.ANY))
    args.append(w_uv)
    return pl.pallas_call(
        functools.partial(
            slots_kernel, plan, own, heads, 1.0 / math.sqrt(VD + ROPE), block
        ),
        out_shape=jax.ShapeDtypeStruct((row_count, local_heads * value_width), jnp.bfloat16),
        grid_spec=pltpu.PrefetchScalarGridSpec(
            num_scalar_prefetch=3,
            grid=(count,),
            in_specs=in_specs,
            out_specs=pl.BlockSpec((row_count, local_heads * value_width), lambda i, *_: (0, 0)),
            scratch_shapes=[
                pltpu.VMEM((rows * heads, wide), jnp.bfloat16),
                pltpu.VMEM((dims * heads, wide), jnp.bfloat16),
                pltpu.VMEM((wide // 128, count * q_rows, 128), jnp.float32),
                pltpu.VMEM(w_uv.shape, w_uv.dtype),
                pltpu.SemaphoreType.DMA,
            ],
        ),
        name="attend_slots",
    )(table, info, place, *args)


def local_ring(
    q_latent, q_rope, cache_latent, cache_rope, lengths, loads, owner_rank, owner_pick, w_uv, w_out
):
    ranks = lax.axis_size("dp")
    heads = lax.axis_size("head")
    me = lax.axis_index("dp")
    head = lax.axis_index("head")
    bundles = owner_rank.shape[0]
    local_heads = w_uv.shape[0]
    roll_count = q_latent.shape[0] // bundles
    columns = w_out.shape[1]
    place = jnp.stack([me, head]).astype(jnp.int32)
    per_head = ranks // heads

    order = ring_order(ranks)
    where = [order.index(r) for r in range(ranks)]
    ahead = [(order[i], order[(i + 1) % ranks]) for i in range(ranks)]
    behind = [(b, a) for a, b in ahead]
    last = ranks // 2
    offsets = [0]
    for k in range(1, last):
        offsets += [-k, k]
    offsets.append(last)
    seen = jnp.asarray(
        [[order[(where[r] + o) % ranks] for o in offsets] for r in range(ranks)], jnp.int32
    )

    rows = cache_latent.shape[1] // heads
    dims = cache_rope.shape[1] // heads
    payload = jnp.concatenate(
        [
            lax.dynamic_slice_in_dim(cache_latent, head * rows, rows, 1),
            lax.dynamic_slice_in_dim(cache_rope, head * dims, dims, 1),
        ],
        axis=1,
    )
    slots = payload.shape[0]

    facts = jnp.concatenate([owner_rank, lengths])
    width = 32
    facts = jnp.pad(facts, (0, width - facts.shape[0]))

    owners = seen[me]
    match = owners[:, None] == owner_rank[None, :]
    bundle_of = jnp.sum(jnp.where(match, jnp.arange(bundles)[None, :], 0), axis=1)
    pick_of = jnp.sum(jnp.where(match, owner_pick[None, :], 0), axis=1)
    load_of = jnp.sum(
        jnp.where(owners[:, None] == jnp.arange(ranks)[None, :], loads[None, :], 0), axis=1
    )
    slot_of = pick_of % load_of
    table = jnp.stack([bundle_of, slot_of]).astype(jnp.int32)

    fore = back = payload
    first = (lax.ppermute(payload, "dp", ahead), lax.ppermute(payload, "dp", behind))
    info = lax.all_to_all(
        jnp.broadcast_to(facts[None], (ranks, width)), "dp", split_axis=0, concat_axis=0, tiled=True
    )
    q = q_latent.reshape(bundles, roll_count * local_heads, -1)
    qr = q_rope.reshape(bundles, roll_count * local_heads, -1)

    def share(chosen):
        found = {0: chosen}
        bit = heads // 2
        while bit:
            pairs = [(i, i ^ bit) for i in range(heads)]
            for m in list(found):
                found[m ^ bit] = lax.ppermute(found[m], "head", pairs)
            bit //= 2
        return [found[m] for m in range(heads)]

    groups = {}
    for k in range(1, last):
        if k == 1:
            fore, back = first
            fore, back, q, qr, info = lax.optimization_barrier((fore, back, q, qr, info))
        else:
            fore = lax.ppermute(fore, "dp", ahead)
            back = lax.ppermute(back, "dp", behind)
        chosen = jnp.stack([fore[slot_of[2 * k - 1]], back[slot_of[2 * k]]])
        parts = share(chosen)
        groups[2 * k - 1] = [(p, 0) for p in parts]
        groups[2 * k] = [(p, 1) for p in parts]
    cut = slots // 2
    left = lax.ppermute(fore[:cut], "dp", ahead)
    right = lax.ppermute(back[cut:], "dp", behind)
    wanted = slot_of[2 * last - 1]
    chosen = jnp.where(
        wanted < cut, left[jnp.minimum(wanted, cut - 1)], right[jnp.maximum(wanted - cut, 0)]
    )[None]
    groups[2 * last - 1] = [(p, 0) for p in share(chosen)]

    lengths_of = jnp.sum(
        jnp.where(
            (owners[:, None] == jnp.arange(ranks)[None, :])[:, :, None]
            & (slot_of[:, None] == jnp.arange(slots)[None, :])[:, None, :],
            info[None, :, bundles : bundles + slots],
            0,
        ),
        axis=(1, 2),
    ).astype(jnp.int32)

    split = ranks // 2
    plan_a, plan_b = list(range(split)), list(range(split, ranks))
    values_a = attend_slots(
        plan_a, table, lengths_of, place, q, qr, (cache_latent, cache_rope),
        [groups[c] for c in plan_a[1:]], w_uv, heads,
    )
    values_b = attend_slots(
        plan_b, table, lengths_of, place, q, qr, None, [groups[c] for c in plan_b], w_uv, heads
    )
    chunk = values_a.shape[0]
    half = values_a.shape[1] // 2

    def project(x):
        return jnp.dot(x, w_out, preferred_element_type=jnp.float32)

    def ring(values):
        result = {0: project(values)}
        fore = back = values
        for k in range(1, last):
            fore = lax.ppermute(fore, "dp", ahead)
            back = lax.ppermute(back, "dp", behind)
            both = project(jnp.concatenate([fore, back], axis=0))
            result[2 * k - 1], result[2 * k] = both[:chunk], both[chunk:]
        left = lax.ppermute(fore[:, :half], "dp", ahead)
        right = lax.ppermute(back[:, half:], "dp", behind)
        result[2 * last - 1] = project(jnp.concatenate([left, right], axis=1))
        return result

    part_a = ring(values_a)
    part_b = ring(values_b)

    def target(p, column):
        return order[(where[p] + offsets[column]) % ranks] // per_head

    targets = jnp.asarray(
        [[target(p, c) for c in range(ranks)] for p in range(ranks)], jnp.int32
    )[me]
    mine_at = (head * per_head + jnp.arange(per_head))[:, None] == owners[None, :]
    total = jnp.zeros((per_head, 2 * chunk, columns), jnp.float32)
    steps = [[0]] + [[2 * k - 1, 2 * k] for k in range(1, last)] + [[2 * last - 1]]
    for step in steps:
        known = [jnp.concatenate([part_a[c], part_b[c]], axis=0) for c in step]
        sendable = [x.astype(jnp.bfloat16) for x in known]
        received = known[0]
        if len(step) > 1:
            received = jnp.where(targets[step[0]] == head, known[0], known[1])
        for m in range(1, heads):
            pairs = []
            for p in range(ranks):
                for t in sorted({target(p, c) for c in step}):
                    pairs.append((p * heads + (t ^ m), p * heads + t))
            out = sendable[0]
            if len(step) > 1:
                out = jnp.where(
                    targets[step[0]] == jnp.bitwise_xor(head, m), sendable[0], sendable[1]
                )
            got = lax.ppermute(out, ("dp", "head"), pairs)
            received = received + got.astype(jnp.float32)
        hit = mine_at[:, step[0]]
        if len(step) > 1:
            hit = hit | mine_at[:, step[1]]
        total = total + jnp.where(hit[:, None, None], received[None], 0.0)

    ranks_here = head * per_head + jnp.arange(per_head)
    bundle_owner = lax.dynamic_slice_in_dim(info, head * per_head, per_head, 0)[:, :bundles]
    order_here = lax.dynamic_slice_in_dim(seen, head * per_head, per_head, 0)
    row = jnp.arange(2 * chunk)
    to_owner = bundle_owner[:, row // roll_count]
    from_owner = order_here[:, row // roll_count]
    pick = (to_owner[:, :, None] == from_owner[:, None, :]) & (
        (row % roll_count)[:, None] == (row % roll_count)[None, :]
    )[None]
    out = lax.dot_general(
        pick.astype(jnp.bfloat16),
        total.astype(jnp.bfloat16),
        (((2,), (1,)), ((0,), (0,))),
        preferred_element_type=jnp.float32,
    )
    return out.astype(jnp.bfloat16).reshape(per_head * 2 * chunk, columns)


def local(*args):
    ranks, heads = lax.axis_size("dp"), lax.axis_size("head")
    bundles = args[6].shape[0]
    if ranks == bundles and ring_fits(ranks, heads):
        return local_ring(*args)
    return local_general(*args)


def solution(mesh):
    in_specs = (
        P("dp", "head"),
        P("dp", "head"),
        P("dp", None, None),
        P("dp", None, None),
        P("dp"),
        P(),
        P("dp"),
        P("dp"),
        P("head", None, None),
        P("head", "dp"),
    )
    out_specs = P("head", "dp")
    return jax.shard_map(local, mesh=mesh, in_specs=in_specs, out_specs=out_specs, check_vma=False)
```

```python
import functools
import math

import jax
import jax.numpy as jnp
from jax import lax
from jax.experimental import pallas as pl
from jax.experimental.pallas import tpu as pltpu
from jax.sharding import PartitionSpec as P


ROPE = 64
VD = 128


def ring_order(size):
    fast = 1 << (max(size.bit_length() - 1, 0) // 2)
    slow = size // fast
    if fast == 1 or slow % 2:
        return list(range(size))
    cells = [(z, 0) for z in range(slow)]
    for step, z in enumerate(range(slow - 1, -1, -1)):
        ys = range(1, fast) if step % 2 == 0 else range(fast - 1, 0, -1)
        cells += [(z, y) for y in ys]
    return [z * fast + y for z, y in cells]


def ring_fits(ranks, heads):
    if ranks % 2 or ranks < 4 or ranks % heads or heads & (heads - 1):
        return False
    order, per_head = ring_order(ranks), ranks // heads
    return all(
        order[p - k] // per_head != order[(p + k) % ranks] // per_head
        for p in range(ranks)
        for k in range(1, ranks // 2)
    )


def slot_for(info, loads, width, bundles, requester, owner):
    pick = jnp.int32(0)
    for j in range(bundles):
        hit = info[requester * width + j] == owner
        pick = jnp.where(hit, info[requester * width + bundles + j], pick)
    return lax.rem(pick, loads[owner])


def pack_kernel(info, loads, place, lat_ref, rope_ref, out_ref):
    rows = lat_ref.shape[1]
    out_ref[0, :rows, :] = lat_ref[0]
    out_ref[0, rows:, :] = rope_ref[0]


def pack(info, loads, place, cache_latent, cache_rope, ranks, heads, width, bundles):
    rows = cache_latent.shape[1] // heads
    dims = cache_rope.shape[1] // heads
    wide = cache_latent.shape[2]

    def source(i, info, loads, place):
        return slot_for(info, loads, width, bundles, i, place[0]), place[1], 0

    return pl.pallas_call(
        pack_kernel,
        out_shape=jax.ShapeDtypeStruct((ranks, rows + dims, wide), cache_latent.dtype),
        grid_spec=pltpu.PrefetchScalarGridSpec(
            num_scalar_prefetch=3,
            grid=(ranks,),
            in_specs=[pl.BlockSpec((1, rows, wide), source), pl.BlockSpec((1, dims, wide), source)],
            out_specs=pl.BlockSpec((1, rows + dims, wide), lambda i, *_: (i, 0, 0)),
        ),
        name="pack",
    )(info, loads, place, cache_latent, cache_rope)


def attend_kernel(
    heads, width, bundles, scale, block, info, loads, place, q_ref, qr_ref, *refs
):
    parts = refs[:heads]
    w_ref, out_ref, lat, rope, mixed = refs[heads:]
    b = pl.program_id(0)
    rows = lat.shape[0] // heads
    dims = rope.shape[0] // heads
    for m in range(heads):
        at = jnp.bitwise_xor(place[1], m)
        lat[pl.ds(pl.multiple_of(at * rows, rows), rows), :] = parts[m][0, :rows, :]
        rope[pl.ds(pl.multiple_of(at * dims, dims), dims), :] = parts[m][0, rows:, :]
    base = place[0] * width
    owner = info[base + b]
    slot = lax.rem(info[base + bundles + b], loads[owner])
    length = info[owner * width + 2 * bundles + slot]
    total_rows = q_ref.shape[1]
    live = lax.broadcasted_iota(jnp.int32, (block, lat.shape[0]), 1) < length
    for i in range(total_rows // block):
        at = slice(i * block, (i + 1) * block)
        s = lax.dot_general(
            q_ref[0, at, :], lat[...], (((1,), (1,)), ((), ())), preferred_element_type=jnp.float32
        )
        s = s + jnp.dot(qr_ref[0, at, :], rope[...], preferred_element_type=jnp.float32)
        s = jnp.where(live, s * scale, -1e30)
        w = jnp.exp(s - jnp.max(s, axis=1, keepdims=True))
        w = w * (1.0 / jnp.sum(w, axis=1, keepdims=True))
        o = jnp.dot(w.astype(jnp.bfloat16), lat[...], preferred_element_type=jnp.float32)
        for c in range(mixed.shape[0]):
            piece = o[:, c * 128 : (c + 1) * 128]
            mixed[c, pl.ds(b * total_rows + i * block, block), :] = piece

    @pl.when(b == pl.num_programs(0) - 1)
    def _():
        local_heads, _, value_width = w_ref.shape
        n = mixed.shape[1] // local_heads
        for h in range(local_heads):
            x = jnp.concatenate(
                [mixed[c, pl.ds(h, n, stride=local_heads), :] for c in range(mixed.shape[0])], axis=1
            ).astype(jnp.bfloat16)
            v = jnp.dot(x, w_ref[h], preferred_element_type=jnp.float32)
            out_ref[:, h * value_width : (h + 1) * value_width] = v.astype(jnp.bfloat16)


def attend(info, loads, place, q, qr, parts, w_uv, width, bundles):
    heads = len(parts)
    _, q_rows, wide = q.shape
    _, part_rows, _ = parts[0].shape
    local_heads, _, value_width = w_uv.shape
    dims = qr.shape[2] // heads
    rows = part_rows - dims
    row_count = bundles * q_rows // local_heads

    def theirs(b, info, loads, place):
        return info[place[0] * width + b], 0, 0

    block = math.gcd(q_rows, 128)
    return pl.pallas_call(
        functools.partial(
            attend_kernel, heads, width, bundles, 1.0 / math.sqrt(VD + ROPE), block
        ),
        out_shape=jax.ShapeDtypeStruct((row_count, local_heads * value_width), jnp.bfloat16),
        grid_spec=pltpu.PrefetchScalarGridSpec(
            num_scalar_prefetch=3,
            grid=(bundles,),
            in_specs=[
                pl.BlockSpec((1, q_rows, wide), lambda b, *_: (b, 0, 0)),
                pl.BlockSpec((1, q_rows, qr.shape[2]), lambda b, *_: (b, 0, 0)),
            ]
            + [pl.BlockSpec((1, part_rows, wide), theirs)] * heads
            + [pl.BlockSpec(w_uv.shape, lambda b, *_: (0, 0, 0))],
            out_specs=pl.BlockSpec((row_count, local_heads * value_width), lambda b, *_: (0, 0)),
            scratch_shapes=[
                pltpu.VMEM((rows * heads, wide), jnp.bfloat16),
                pltpu.VMEM((dims * heads, wide), jnp.bfloat16),
                pltpu.VMEM((wide // 128, bundles * q_rows, 128), jnp.float32),
            ],
        ),
        name="attend",
    )(info, loads, place, q, qr, *parts, w_uv)


def local_general(
    q_latent, q_rope, cache_latent, cache_rope, lengths, loads, owner_rank, owner_pick, w_uv, w_out
):
    ranks = lax.axis_size("dp")
    heads = lax.axis_size("head")
    me = lax.axis_index("dp")
    head = lax.axis_index("head")
    bundles = owner_rank.shape[0]
    roll_count = q_latent.shape[0] // bundles
    local_heads = w_uv.shape[0]
    place = jnp.stack([me, head]).astype(jnp.int32)

    facts = jnp.concatenate([owner_rank, owner_pick, lengths])
    width = 32
    facts = jnp.pad(facts, (0, width - facts.shape[0]))
    info = lax.all_to_all(
        jnp.broadcast_to(facts[None], (ranks, width)), "dp", split_axis=0, concat_axis=0, tiled=True
    ).reshape(-1)
    q = q_latent.reshape(bundles, roll_count * local_heads, -1)
    qr = q_rope.reshape(bundles, roll_count * local_heads, -1)

    packed = pack(info, loads, place, cache_latent, cache_rope, ranks, heads, width, bundles)
    mine = lax.all_to_all(packed, "dp", split_axis=0, concat_axis=0, tiled=True)
    parts = [mine]
    bit = heads // 2
    found = {0: mine}
    while bit:
        pairs = [(i, i ^ bit) for i in range(heads)]
        for m in list(found):
            found[m ^ bit] = lax.ppermute(found[m], "head", pairs)
        bit //= 2
    parts = [found[m] for m in range(heads)]
    values = attend(info, loads, place, q, qr, parts, w_uv, width, bundles)

    order = ring_order(ranks)
    ahead = [(order[i], order[(i + 1) % ranks]) for i in range(ranks)]
    behind = [(b, a) for a, b in ahead]
    half = values.shape[1] // 2

    def project(x):
        return jnp.dot(x, w_out, preferred_element_type=jnp.float32).astype(jnp.bfloat16)

    partial = {0: project(values)}
    fore = back = values
    for step in range(1, (ranks + 1) // 2):
        fore = lax.ppermute(fore, "dp", ahead)
        back = lax.ppermute(back, "dp", behind)
        both = project(jnp.concatenate([fore, back], axis=0))
        partial[-step] = both[: values.shape[0]]
        partial[step] = both[values.shape[0] :]
    if ranks % 2 == 0:
        left = lax.ppermute(fore[:, :half], "dp", ahead)
        right = lax.ppermute(back[:, half:], "dp", behind)
        partial[ranks // 2] = project(jnp.concatenate([left, right], axis=1))
    stacked = jnp.stack([partial[k if 2 * k <= ranks else k - ranks] for k in range(ranks)])
    position = [0] * ranks
    for i, r in enumerate(order):
        position[r] = i
    position = jnp.asarray(position, jnp.int32)
    by_rank = stacked[(position - position[me]) % ranks]
    shares = by_rank.reshape(heads, -1, w_out.shape[1])
    got = lax.all_to_all(shares, "head", split_axis=0, concat_axis=0, tiled=True)
    return jnp.sum(got.astype(jnp.float32), axis=0).astype(jnp.bfloat16)


def in_hbm(x):
    return pltpu.with_memory_space_constraint(x, pltpu.MemorySpace.HBM)


def slots_kernel(plan, own, heads, carried, final, scale, block, table, lengths, place, *refs):
    count = len(plan)
    refs = list(refs)
    q_ref, qr_ref = refs.pop(0), refs.pop(0)
    if own:
        full_lat, full_rope = refs.pop(0), refs.pop(0)
    shipped = count - own
    parts = [[refs.pop(0) for _ in range(heads)] for _ in range(shipped)]
    i = pl.program_id(0)
    total_rows = q_ref.shape[1]
    before = sum(carried) * total_rows
    if final:
        earlier = [refs.pop(0) for _ in carried]
        w_hbm, out_ref, lat, rope, mixed, w_ref, sems = refs
        copies, at = [pltpu.make_async_copy(w_hbm, w_ref, sems.at[0])], 0
        for k, n in enumerate(carried):
            span = n * total_rows
            copies.append(
                pltpu.make_async_copy(earlier[k], mixed.at[:, pl.ds(at, span), :], sems.at[k + 1])
            )
            at += span

        @pl.when(i == 0)
        def _():
            for copy in copies:
                copy.start()
    else:
        mixed, lat, rope = refs
    rows = lat.shape[0] // heads
    dims = rope.shape[0] // heads

    for j in range(count):

        @pl.when(i == j)
        def _():
            if own and j == 0:
                lat[...] = full_lat[0]
                rope[...] = full_rope[0]
                return
            for m in range(heads):
                part = parts[j - own][m]
                to = jnp.bitwise_xor(place[1], m)
                lat[pl.ds(pl.multiple_of(to * rows, rows), rows), :] = part[0, :rows, :]
                rope[pl.ds(pl.multiple_of(to * dims, dims), dims), :] = part[0, rows:, :]

    length = lengths[plan[0]]
    for j in range(1, count):
        length = jnp.where(i == j, lengths[plan[j]], length)
    live = lax.broadcasted_iota(jnp.int32, (block, lat.shape[0]), 1) < length
    for r in range(total_rows // block):
        at = slice(r * block, (r + 1) * block)
        s = lax.dot_general(
            q_ref[0, at, :], lat[...], (((1,), (1,)), ((), ())), preferred_element_type=jnp.float32
        )
        s = s + jnp.dot(qr_ref[0, at, :], rope[...], preferred_element_type=jnp.float32)
        s = jnp.where(live, s * scale, -1e30)
        w = jnp.exp(s - jnp.max(s, axis=1, keepdims=True))
        w = w * (1.0 / jnp.sum(w, axis=1, keepdims=True))
        o = jnp.dot(w.astype(jnp.bfloat16), lat[...], preferred_element_type=jnp.float32)
        for c in range(mixed.shape[0]):
            mixed[c, pl.ds(before + i * total_rows + r * block, block), :] = o[
                :, c * 128 : (c + 1) * 128
            ]

    if final:

        @pl.when(i == count - 1)
        def _():
            for copy in copies:
                copy.wait()
            local_heads, _, value_width = w_ref.shape
            n = mixed.shape[1] // local_heads
            for h in range(local_heads):
                x = jnp.concatenate(
                    [mixed[c, pl.ds(h, n, stride=local_heads), :] for c in range(mixed.shape[0])],
                    axis=1,
                ).astype(jnp.bfloat16)
                v = jnp.dot(x, w_ref[h], preferred_element_type=jnp.float32)
                out_ref[:, h * value_width : (h + 1) * value_width] = v.astype(jnp.bfloat16)


def attend_slots(plan, table, lengths, place, q, qr, full, parts, heads, earlier=(), w_uv=None):
    own = 1 if full is not None else 0
    final = w_uv is not None
    count = len(plan)
    _, q_rows, wide = q.shape
    part_rows = parts[0][0][0].shape[1]
    dims = qr.shape[2] // heads
    rows = part_rows - dims
    block = math.gcd(q_rows, 128)
    carried = [e.shape[1] // q_rows for e in earlier]

    def bundle(i, table, lengths, place):
        at = table[0, plan[0]]
        for j in range(1, count):
            at = jnp.where(i == j, table[0, plan[j]], at)
        return at, 0, 0

    in_specs = [
        pl.BlockSpec((1, q_rows, wide), bundle),
        pl.BlockSpec((1, q_rows, qr.shape[2]), bundle),
    ]
    args = [in_hbm(q), in_hbm(qr)]
    if own:
        here = lambda i, table, lengths, place: (table[1, plan[0]], 0, 0)
        in_specs += [
            pl.BlockSpec((1, rows * heads, wide), here),
            pl.BlockSpec((1, dims * heads, wide), here),
        ]
        args += [in_hbm(x) for x in full]
    for slot in parts:
        for array, index in slot:
            in_specs.append(
                pl.BlockSpec((1, part_rows, wide), lambda i, *_, index=index: (index, 0, 0))
            )
            args.append(in_hbm(array))
    scratch = [
        pltpu.VMEM((rows * heads, wide), jnp.bfloat16),
        pltpu.VMEM((dims * heads, wide), jnp.bfloat16),
    ]
    if final:
        in_specs += [pl.BlockSpec(memory_space=pltpu.MemorySpace.HBM)] * (len(earlier) + 1)
        args += [in_hbm(x) for x in (*earlier, w_uv)]
        local_heads, _, value_width = w_uv.shape
        done = sum(carried) + count
        out_shape = (done * q_rows // local_heads, local_heads * value_width)
        out = jax.ShapeDtypeStruct(out_shape, jnp.bfloat16)
        out_spec = pl.BlockSpec(out_shape, lambda i, *_: (0, 0))
        scratch += [
            pltpu.VMEM((wide // 128, done * q_rows, 128), jnp.float32),
            pltpu.VMEM(w_uv.shape, w_uv.dtype),
            pltpu.SemaphoreType.DMA((1 + len(earlier),)),
        ]
    else:
        out_shape = (wide // 128, count * q_rows, 128)
        out = jax.ShapeDtypeStruct(out_shape, jnp.float32)
        out_spec = pl.BlockSpec(out_shape, lambda i, *_: (0, 0, 0))
    return pl.pallas_call(
        functools.partial(
            slots_kernel, plan, own, heads, carried, final, 1.0 / math.sqrt(VD + ROPE), block
        ),
        out_shape=out,
        grid_spec=pltpu.PrefetchScalarGridSpec(
            num_scalar_prefetch=3,
            grid=(count,),
            in_specs=in_specs,
            out_specs=out_spec,
            scratch_shapes=scratch,
        ),
        compiler_params=pltpu.CompilerParams(vmem_limit_bytes=26 * 2**20),
        name="attend_slots",
    )(table, lengths, place, *args)


def local_ring(
    q_latent, q_rope, cache_latent, cache_rope, lengths, loads, owner_rank, owner_pick, w_uv, w_out
):
    ranks = lax.axis_size("dp")
    heads = lax.axis_size("head")
    me = lax.axis_index("dp")
    head = lax.axis_index("head")
    bundles = owner_rank.shape[0]
    local_heads = w_uv.shape[0]
    roll_count = q_latent.shape[0] // bundles
    columns = w_out.shape[1]
    place = jnp.stack([me, head]).astype(jnp.int32)
    per_head = ranks // heads

    order = ring_order(ranks)
    where = [order.index(r) for r in range(ranks)]
    ahead = [(order[i], order[(i + 1) % ranks]) for i in range(ranks)]
    behind = [(b, a) for a, b in ahead]
    last = ranks // 2
    offsets = [0]
    for k in range(1, last):
        offsets += [-k, k]
    offsets.append(last)
    seen = jnp.asarray(
        [[order[(where[r] + o) % ranks] for o in offsets] for r in range(ranks)], jnp.int32
    )

    rows = cache_latent.shape[1] // heads
    dims = cache_rope.shape[1] // heads
    payload = jnp.concatenate(
        [
            lax.dynamic_slice_in_dim(cache_latent, head * rows, rows, 1),
            lax.dynamic_slice_in_dim(cache_rope, head * dims, dims, 1),
        ],
        axis=1,
    )
    slots = payload.shape[0]

    owners = seen[me]
    match = owners[:, None] == owner_rank[None, :]
    bundle_of = jnp.sum(jnp.where(match, jnp.arange(bundles)[None, :], 0), axis=1)
    pick_of = jnp.sum(jnp.where(match, owner_pick[None, :], 0), axis=1)
    load_of = jnp.sum(
        jnp.where(owners[:, None] == jnp.arange(ranks)[None, :], loads[None, :], 0), axis=1
    )
    slot_of = pick_of % load_of
    table = jnp.stack([bundle_of, slot_of]).astype(jnp.int32)

    facts = jnp.concatenate([owner_rank, lengths])
    width = 32
    facts = jnp.pad(facts, (0, width - facts.shape[0]))

    def move(x, pairs, axis="dp"):
        return lax.ppermute(x, axis, pairs)

    fore, back = move(payload, ahead), move(payload, behind)
    info = lax.all_to_all(
        jnp.broadcast_to(facts[None], (ranks, width)), "dp", split_axis=0, concat_axis=0, tiled=True
    )
    q = q_latent.reshape(bundles, roll_count * local_heads, -1)
    qr = q_rope.reshape(bundles, roll_count * local_heads, -1)

    def share(chosen):
        found = {0: chosen}
        bit = heads // 2
        while bit:
            pairs = [(i, i ^ bit) for i in range(heads)]
            for m in list(found):
                found[m ^ bit] = move(found[m], pairs, "head")
            bit //= 2
        return [found[m] for m in range(heads)]

    groups = {}
    for k in range(1, last):
        if k > 1:
            fore = move(fore, ahead)
            back = move(back, behind)
        if k == 2:
            fore, q, qr = lax.optimization_barrier((fore, q, qr))
        chosen = jnp.stack([fore[slot_of[2 * k - 1]], back[slot_of[2 * k]]])
        parts = share(chosen)
        groups[2 * k - 1] = [(p, 0) for p in parts]
        groups[2 * k] = [(p, 1) for p in parts]
    cut = slots // 2
    left = move(fore[:cut], ahead)
    right = move(back[cut:], behind)
    wanted = slot_of[2 * last - 1]
    chosen = jnp.where(
        wanted < cut, left[jnp.minimum(wanted, cut - 1)], right[jnp.maximum(wanted - cut, 0)]
    )[None]
    groups[2 * last - 1] = [(p, 0) for p in share(chosen)]

    lengths_of = jnp.sum(
        jnp.where(
            (owners[:, None] == jnp.arange(ranks)[None, :])[:, :, None]
            & (slot_of[:, None] == jnp.arange(slots)[None, :])[:, None, :],
            info[None, :, bundles : bundles + slots],
            0,
        ),
        axis=(1, 2),
    ).astype(jnp.int32)

    def attend(plan, full=None, earlier=(), w_uv=None):
        return attend_slots(
            plan, table, lengths_of, place, q, qr, full,
            [groups[c] for c in plan[(full is not None) :]], heads, earlier, w_uv,
        )

    earlier = [attend([0, 1, 2], (cache_latent, cache_rope))]
    for k in range(2, last):
        earlier.append(attend([2 * k - 1, 2 * k]))
    values = attend([2 * last - 1], None, earlier, w_uv)
    block_rows = values.shape[0]
    half = values.shape[1] // 2

    def target(p, column):
        return order[(where[p] + offsets[column]) % ranks] // per_head

    targets = jnp.asarray(
        [[target(p, c) for c in range(ranks)] for p in range(ranks)], jnp.int32
    )[me]
    mine_at = (head * per_head + jnp.arange(per_head))[:, None] == owners[None, :]

    def project(x):
        return jnp.dot(x, w_out, preferred_element_type=jnp.float32)

    def settle(total, known, columns_here):
        sendable = [x.astype(jnp.bfloat16) for x in known]
        received = known[0]
        if len(known) > 1:
            received = jnp.where(targets[columns_here[0]] == head, known[0], known[1])
        for m in range(1, heads):
            pairs = []
            for p in range(ranks):
                for t in sorted({target(p, c) for c in columns_here}):
                    pairs.append((p * heads + (t ^ m), p * heads + t))
            out = sendable[0]
            if len(known) > 1:
                out = jnp.where(
                    targets[columns_here[0]] == jnp.bitwise_xor(head, m), sendable[0], sendable[1]
                )
            got = move(out, pairs, ("dp", "head"))
            received = received + got.astype(jnp.float32)
        hit = mine_at[:, columns_here[0]]
        for c in columns_here[1:]:
            hit = hit | mine_at[:, c]
        update = jnp.where(hit[:, None, None], received[None], 0.0)
        return update if total is None else total + update

    total = settle(None, [project(values)], [0])
    fore = back = values
    for k in range(1, last):
        fore = move(fore, ahead)
        back = move(back, behind)
        both = project(jnp.concatenate([fore, back], axis=0))
        total = settle(total, [both[:block_rows], both[block_rows:]], [2 * k - 1, 2 * k])
    left = move(fore[:, :half], ahead)
    right = move(back[:, half:], behind)
    ends = project(jnp.concatenate([left, right], axis=1))
    total = settle(total, [ends], [2 * last - 1])

    bundle_owner = lax.dynamic_slice_in_dim(info, head * per_head, per_head, 0)[:, :bundles]
    order_here = lax.dynamic_slice_in_dim(seen, head * per_head, per_head, 0)
    row = jnp.arange(block_rows)
    to_owner = bundle_owner[:, row // roll_count]
    from_owner = order_here[:, row // roll_count]
    pick = (to_owner[:, :, None] == from_owner[:, None, :]) & (
        (row % roll_count)[:, None] == (row % roll_count)[None, :]
    )[None]
    out = lax.dot_general(
        pick.astype(jnp.bfloat16),
        total.astype(jnp.bfloat16),
        (((2,), (1,)), ((0,), (0,))),
        preferred_element_type=jnp.float32,
    )
    return out.astype(jnp.bfloat16).reshape(per_head * block_rows, columns)


def local(*args):
    ranks, heads = lax.axis_size("dp"), lax.axis_size("head")
    bundles = args[6].shape[0]
    if ranks == bundles and ring_fits(ranks, heads):
        return local_ring(*args)
    return local_general(*args)


def solution(mesh):
    in_specs = (
        P("dp", "head"),
        P("dp", "head"),
        P("dp", None, None),
        P("dp", None, None),
        P("dp"),
        P(),
        P("dp"),
        P("dp"),
        P("head", None, None),
        P("head", "dp"),
    )
    out_specs = P("head", "dp")
    return jax.shard_map(local, mesh=mesh, in_specs=in_specs, out_specs=out_specs, check_vma=False)
```

```python
import functools
import math

import jax
import jax.numpy as jnp
from jax import lax
from jax.experimental import pallas as pl
from jax.experimental.pallas import tpu as pltpu
from jax.sharding import PartitionSpec as P


ROPE = 64
VD = 128


def ring_order(size):
    fast = 1 << (max(size.bit_length() - 1, 0) // 2)
    slow = size // fast
    if fast == 1 or slow % 2:
        return list(range(size))
    cells = [(z, 0) for z in range(slow)]
    for step, z in enumerate(range(slow - 1, -1, -1)):
        ys = range(1, fast) if step % 2 == 0 else range(fast - 1, 0, -1)
        cells += [(z, y) for y in ys]
    return [z * fast + y for z, y in cells]


def ring_fits(ranks, heads):
    if ranks % 2 or ranks < 4 or ranks % heads or heads & (heads - 1):
        return False
    order, per_head = ring_order(ranks), ranks // heads
    return all(
        order[p - k] // per_head != order[(p + k) % ranks] // per_head
        for p in range(ranks)
        for k in range(1, ranks // 2)
    )


def slot_for(info, loads, width, bundles, requester, owner):
    pick = jnp.int32(0)
    for j in range(bundles):
        hit = info[requester * width + j] == owner
        pick = jnp.where(hit, info[requester * width + bundles + j], pick)
    return lax.rem(pick, loads[owner])


def pack_kernel(info, loads, place, lat_ref, rope_ref, out_ref):
    rows = lat_ref.shape[1]
    out_ref[0, :rows, :] = lat_ref[0]
    out_ref[0, rows:, :] = rope_ref[0]


def pack(info, loads, place, cache_latent, cache_rope, ranks, heads, width, bundles):
    rows = cache_latent.shape[1] // heads
    dims = cache_rope.shape[1] // heads
    wide = cache_latent.shape[2]

    def source(i, info, loads, place):
        return slot_for(info, loads, width, bundles, i, place[0]), place[1], 0

    return pl.pallas_call(
        pack_kernel,
        out_shape=jax.ShapeDtypeStruct((ranks, rows + dims, wide), cache_latent.dtype),
        grid_spec=pltpu.PrefetchScalarGridSpec(
            num_scalar_prefetch=3,
            grid=(ranks,),
            in_specs=[pl.BlockSpec((1, rows, wide), source), pl.BlockSpec((1, dims, wide), source)],
            out_specs=pl.BlockSpec((1, rows + dims, wide), lambda i, *_: (i, 0, 0)),
        ),
        name="pack",
    )(info, loads, place, cache_latent, cache_rope)


def attend_kernel(
    heads, width, bundles, scale, block, info, loads, place, q_ref, qr_ref, *refs
):
    parts = refs[:heads]
    w_ref, out_ref, lat, rope, mixed = refs[heads:]
    b = pl.program_id(0)
    rows = lat.shape[0] // heads
    dims = rope.shape[0] // heads
    for m in range(heads):
        at = jnp.bitwise_xor(place[1], m)
        lat[pl.ds(pl.multiple_of(at * rows, rows), rows), :] = parts[m][0, :rows, :]
        rope[pl.ds(pl.multiple_of(at * dims, dims), dims), :] = parts[m][0, rows:, :]
    base = place[0] * width
    owner = info[base + b]
    slot = lax.rem(info[base + bundles + b], loads[owner])
    length = info[owner * width + 2 * bundles + slot]
    total_rows = q_ref.shape[1]
    live = lax.broadcasted_iota(jnp.int32, (block, lat.shape[0]), 1) < length
    for i in range(total_rows // block):
        at = slice(i * block, (i + 1) * block)
        s = lax.dot_general(
            q_ref[0, at, :], lat[...], (((1,), (1,)), ((), ())), preferred_element_type=jnp.float32
        )
        s = s + jnp.dot(qr_ref[0, at, :], rope[...], preferred_element_type=jnp.float32)
        s = jnp.where(live, s * scale, -1e30)
        w = jnp.exp(s - jnp.max(s, axis=1, keepdims=True))
        w = w * (1.0 / jnp.sum(w, axis=1, keepdims=True))
        o = jnp.dot(w.astype(jnp.bfloat16), lat[...], preferred_element_type=jnp.float32)
        for c in range(mixed.shape[0]):
            piece = o[:, c * 128 : (c + 1) * 128]
            mixed[c, pl.ds(b * total_rows + i * block, block), :] = piece

    @pl.when(b == pl.num_programs(0) - 1)
    def _():
        local_heads, _, value_width = w_ref.shape
        n = mixed.shape[1] // local_heads
        for h in range(local_heads):
            x = jnp.concatenate(
                [mixed[c, pl.ds(h, n, stride=local_heads), :] for c in range(mixed.shape[0])], axis=1
            ).astype(jnp.bfloat16)
            v = jnp.dot(x, w_ref[h], preferred_element_type=jnp.float32)
            out_ref[:, h * value_width : (h + 1) * value_width] = v.astype(jnp.bfloat16)


def attend(info, loads, place, q, qr, parts, w_uv, width, bundles):
    heads = len(parts)
    _, q_rows, wide = q.shape
    _, part_rows, _ = parts[0].shape
    local_heads, _, value_width = w_uv.shape
    dims = qr.shape[2] // heads
    rows = part_rows - dims
    row_count = bundles * q_rows // local_heads

    def theirs(b, info, loads, place):
        return info[place[0] * width + b], 0, 0

    block = math.gcd(q_rows, 128)
    return pl.pallas_call(
        functools.partial(
            attend_kernel, heads, width, bundles, 1.0 / math.sqrt(VD + ROPE), block
        ),
        out_shape=jax.ShapeDtypeStruct((row_count, local_heads * value_width), jnp.bfloat16),
        grid_spec=pltpu.PrefetchScalarGridSpec(
            num_scalar_prefetch=3,
            grid=(bundles,),
            in_specs=[
                pl.BlockSpec((1, q_rows, wide), lambda b, *_: (b, 0, 0)),
                pl.BlockSpec((1, q_rows, qr.shape[2]), lambda b, *_: (b, 0, 0)),
            ]
            + [pl.BlockSpec((1, part_rows, wide), theirs)] * heads
            + [pl.BlockSpec(w_uv.shape, lambda b, *_: (0, 0, 0))],
            out_specs=pl.BlockSpec((row_count, local_heads * value_width), lambda b, *_: (0, 0)),
            scratch_shapes=[
                pltpu.VMEM((rows * heads, wide), jnp.bfloat16),
                pltpu.VMEM((dims * heads, wide), jnp.bfloat16),
                pltpu.VMEM((wide // 128, bundles * q_rows, 128), jnp.float32),
            ],
        ),
        name="attend",
    )(info, loads, place, q, qr, *parts, w_uv)


def local_general(
    q_latent, q_rope, cache_latent, cache_rope, lengths, loads, owner_rank, owner_pick, w_uv, w_out
):
    ranks = lax.axis_size("dp")
    heads = lax.axis_size("head")
    me = lax.axis_index("dp")
    head = lax.axis_index("head")
    bundles = owner_rank.shape[0]
    roll_count = q_latent.shape[0] // bundles
    local_heads = w_uv.shape[0]
    place = jnp.stack([me, head]).astype(jnp.int32)

    facts = jnp.concatenate([owner_rank, owner_pick, lengths])
    width = 32
    facts = jnp.pad(facts, (0, width - facts.shape[0]))
    info = lax.all_to_all(
        jnp.broadcast_to(facts[None], (ranks, width)), "dp", split_axis=0, concat_axis=0, tiled=True
    ).reshape(-1)
    q = q_latent.reshape(bundles, roll_count * local_heads, -1)
    qr = q_rope.reshape(bundles, roll_count * local_heads, -1)

    packed = pack(info, loads, place, cache_latent, cache_rope, ranks, heads, width, bundles)
    mine = lax.all_to_all(packed, "dp", split_axis=0, concat_axis=0, tiled=True)
    parts = [mine]
    bit = heads // 2
    found = {0: mine}
    while bit:
        pairs = [(i, i ^ bit) for i in range(heads)]
        for m in list(found):
            found[m ^ bit] = lax.ppermute(found[m], "head", pairs)
        bit //= 2
    parts = [found[m] for m in range(heads)]
    values = attend(info, loads, place, q, qr, parts, w_uv, width, bundles)

    order = ring_order(ranks)
    ahead = [(order[i], order[(i + 1) % ranks]) for i in range(ranks)]
    behind = [(b, a) for a, b in ahead]
    half = values.shape[1] // 2

    def project(x):
        return jnp.dot(x, w_out, preferred_element_type=jnp.float32).astype(jnp.bfloat16)

    partial = {0: project(values)}
    fore = back = values
    for step in range(1, (ranks + 1) // 2):
        fore = lax.ppermute(fore, "dp", ahead)
        back = lax.ppermute(back, "dp", behind)
        both = project(jnp.concatenate([fore, back], axis=0))
        partial[-step] = both[: values.shape[0]]
        partial[step] = both[values.shape[0] :]
    if ranks % 2 == 0:
        left = lax.ppermute(fore[:, :half], "dp", ahead)
        right = lax.ppermute(back[:, half:], "dp", behind)
        partial[ranks // 2] = project(jnp.concatenate([left, right], axis=1))
    stacked = jnp.stack([partial[k if 2 * k <= ranks else k - ranks] for k in range(ranks)])
    position = [0] * ranks
    for i, r in enumerate(order):
        position[r] = i
    position = jnp.asarray(position, jnp.int32)
    by_rank = stacked[(position - position[me]) % ranks]
    shares = by_rank.reshape(heads, -1, w_out.shape[1])
    got = lax.all_to_all(shares, "head", split_axis=0, concat_axis=0, tiled=True)
    return jnp.sum(got.astype(jnp.float32), axis=0).astype(jnp.bfloat16)


def ring_tables(ranks):
    order = ring_order(ranks)
    where = [order.index(r) for r in range(ranks)]
    offsets = [0]
    for k in range(1, ranks // 2):
        offsets += [-k, k]
    offsets.append(ranks // 2)
    seen = [[order[(where[r] + o) % ranks] for o in offsets] for r in range(ranks)]
    return order, where, offsets, seen


BUNDLE, SLOT, TARGET, OWNER, PLACE, PLAN_ROWS = 0, 1, 2, 3, 4, 8


def plan_kernel(per_head, seen, owner_rank, owner_pick, loads, table):
    ranks = seen.shape[1]
    me, head = lax.axis_index("dp"), lax.axis_index("head")
    table[PLACE, 0] = me
    table[PLACE, 1] = head
    for c in range(ranks):
        owner = seen[me, c]
        bundle, pick = jnp.int32(0), jnp.int32(0)
        for b in range(owner_rank.shape[0]):
            hit = owner_rank[b] == owner
            bundle = jnp.where(hit, b, bundle)
            pick = jnp.where(hit, owner_pick[b], pick)
        table[BUNDLE, c] = bundle
        table[SLOT, c] = lax.rem(pick, loads[owner])
        table[TARGET, c] = lax.div(owner, per_head)
        table[OWNER, c] = owner


def plan_of(seen, owner_rank, owner_pick, loads, per_head):
    smem = pl.BlockSpec(memory_space=pltpu.MemorySpace.SMEM)
    return pl.pallas_call(
        functools.partial(plan_kernel, per_head),
        out_shape=jax.ShapeDtypeStruct((PLAN_ROWS, seen.shape[1]), jnp.int32),
        in_specs=[smem] * 4,
        out_specs=smem,
        name="plan",
    )(seen, owner_rank, owner_pick, loads)


def payload_kernel(lat, rope, out, sems):
    head = lax.axis_index("head")
    dims = rope.shape[1] * (out.shape[1]) // (rope.shape[1] + lat.shape[1])
    rows = out.shape[1] - dims
    copies = [
        pltpu.make_async_copy(
            lat.at[:, pl.ds(pl.multiple_of(head * rows, rows), rows), :],
            out.at[:, pl.ds(0, rows), :],
            sems.at[0],
        ),
        pltpu.make_async_copy(
            rope.at[:, pl.ds(pl.multiple_of(head * dims, dims), dims), :],
            out.at[:, pl.ds(rows, dims), :],
            sems.at[1],
        ),
    ]
    for copy in copies:
        copy.start()
    for copy in copies:
        copy.wait()


def payload_of(cache_latent, cache_rope, heads):
    slots, positions, wide = cache_latent.shape
    rows = (positions + cache_rope.shape[1]) // heads
    return pl.pallas_call(
        payload_kernel,
        out_shape=jax.ShapeDtypeStruct((slots, rows, wide), cache_latent.dtype),
        in_specs=[pl.BlockSpec(memory_space=pl.ANY)] * 2,
        out_specs=pl.BlockSpec(memory_space=pl.ANY),
        scratch_shapes=[pltpu.SemaphoreType.DMA((2,))],
        name="payload",
    )(cache_latent, cache_rope)


def choose_kernel(cut, column, table, a_ref, b_ref, out_ref):
    if cut is None:
        out_ref[0] = a_ref[0]
        out_ref[1] = b_ref[0]
    else:
        first = table[SLOT, column] < cut

        @pl.when(first)
        def _():
            out_ref[0] = a_ref[0]

        @pl.when(jnp.logical_not(first))
        def _():
            out_ref[0] = b_ref[0]


def choose(table, a, b, columns, cut=None):
    _, rows, wide = a.shape
    if cut is None:
        index_a = lambda i, table: (table[SLOT, columns[0]], 0, 0)
        index_b = lambda i, table: (table[SLOT, columns[1]], 0, 0)
    else:
        index_a = lambda i, table: (jnp.minimum(table[SLOT, columns[0]], cut - 1), 0, 0)
        index_b = lambda i, table: (jnp.maximum(table[SLOT, columns[0]] - cut, 0), 0, 0)
    return pl.pallas_call(
        functools.partial(choose_kernel, cut, columns[0]),
        out_shape=jax.ShapeDtypeStruct((len(columns), rows, wide), a.dtype),
        grid_spec=pltpu.PrefetchScalarGridSpec(
            num_scalar_prefetch=1,
            grid=(1,),
            in_specs=[pl.BlockSpec((1, rows, wide), index_a), pl.BlockSpec((1, rows, wide), index_b)],
            out_specs=pl.BlockSpec((len(columns), rows, wide), lambda i, *_: (0, 0, 0)),
        ),
        compiler_params=pltpu.CompilerParams(vmem_limit_bytes=4 * 2**20),
        name="choose",
    )(table, a, b)


def slots_kernel(plan, own, heads, bundles, carried, final, scale, block, table, info, *refs):
    count = len(plan)
    refs = list(refs)
    q_ref, qr_ref = refs.pop(0), refs.pop(0)
    if own:
        full_lat, full_rope = refs.pop(0), refs.pop(0)
    shipped = count - own
    parts = [[refs.pop(0) for _ in range(heads)] for _ in range(shipped)]
    earlier = [refs.pop(0) for _ in carried]
    w_hbm, out_ref, lat, rope, mixed, w_ref, sem = refs[:7]
    i = pl.program_id(0)
    total_rows = q_ref.shape[1]
    w_copy = pltpu.make_async_copy(w_hbm, w_ref, sem)

    @pl.when(i == 0)
    def _():
        w_copy.start()

    rows = lat.shape[0] // heads
    dims = rope.shape[0] // heads

    for j in range(count):

        @pl.when(i == j)
        def _():
            if own and j == 0:
                lat[...] = full_lat[0]
                rope[...] = full_rope[0]
                return
            for m in range(heads):
                part = parts[j - own][m]
                to = jnp.bitwise_xor(table[PLACE, 1], m)
                lat[pl.ds(pl.multiple_of(to * rows, rows), rows), :] = part[0, :rows, :]
                rope[pl.ds(pl.multiple_of(to * dims, dims), dims), :] = part[0, rows:, :]

    column = jnp.int32(plan[0]) + i
    length = info[table[OWNER, column], 0, bundles + table[SLOT, column]]
    live = lax.broadcasted_iota(jnp.int32, (block, lat.shape[0]), 1) < length
    for r in range(total_rows // block):
        at = slice(r * block, (r + 1) * block)
        s = lax.dot_general(
            q_ref[0, at, :], lat[...], (((1,), (1,)), ((), ())), preferred_element_type=jnp.float32
        )
        s = s + jnp.dot(qr_ref[0, at, :], rope[...], preferred_element_type=jnp.float32)
        s = jnp.where(live, s * scale, -1e30)
        w = jnp.exp(s - jnp.max(s, axis=1, keepdims=True))
        w = w * (1.0 / jnp.sum(w, axis=1, keepdims=True))
        o = jnp.dot(w.astype(jnp.bfloat16), lat[...], preferred_element_type=jnp.float32)
        for c in range(mixed.shape[0]):
            mixed[c, pl.ds(i * total_rows + r * block, block), :] = o[:, c * 128 : (c + 1) * 128]

    @pl.when(i == count - 1)
    def _():
        w_copy.wait()
        local_heads, _, value_width = w_ref.shape
        n = mixed.shape[1] // local_heads
        into, at = out_ref, 0
        if final:
            into = refs[7]
            for piece in earlier:
                into[pl.ds(at, piece.shape[0]), :] = piece[...]
                at += piece.shape[0]
        for h in range(local_heads):
            x = jnp.concatenate(
                [mixed[c, pl.ds(h, n, stride=local_heads), :] for c in range(mixed.shape[0])], axis=1
            ).astype(jnp.bfloat16)
            v = jnp.dot(x, w_ref[h], preferred_element_type=jnp.float32)
            into[pl.ds(at, n), h * value_width : (h + 1) * value_width] = v
        if final:
            out_ref[...] = into[...].astype(out_ref.dtype)


def in_hbm(x):
    return pltpu.with_memory_space_constraint(x, pltpu.MemorySpace.HBM)


def attend_slots(plan, table, info, q, qr, full, parts, heads, bundles, w_uv, earlier=None):
    own = 1 if full is not None else 0
    final = earlier is not None
    earlier = list(earlier or ())
    count = len(plan)
    _, q_rows, wide = q.shape
    part_rows = parts[0][0][0].shape[1]
    dims = qr.shape[2] // heads
    rows = part_rows - dims
    block = math.gcd(q_rows, 128)
    local_heads, _, value_width = w_uv.shape
    carried = [e.shape[0] for e in earlier]

    def bundle(i, table, info):
        return table[BUNDLE, plan[0] + i], 0, 0

    in_specs = [
        pl.BlockSpec((1, q_rows, wide), bundle),
        pl.BlockSpec((1, q_rows, qr.shape[2]), bundle),
    ]
    args = [in_hbm(q), in_hbm(qr)]
    if own:
        here = lambda i, table, info: (table[SLOT, plan[0]], 0, 0)
        in_specs += [
            pl.BlockSpec((1, rows * heads, wide), here),
            pl.BlockSpec((1, dims * heads, wide), here),
        ]
        args += [in_hbm(x) for x in full]
    for slot in parts:
        for array, index in slot:
            in_specs.append(
                pl.BlockSpec((1, part_rows, wide), lambda i, *_, index=index: (index, 0, 0))
            )
            args.append(array)
    for piece in earlier:
        in_specs.append(pl.BlockSpec(piece.shape, lambda i, *_: (0, 0)))
        args.append(piece)
    in_specs.append(pl.BlockSpec(memory_space=pl.ANY))
    args.append(in_hbm(w_uv))
    done = sum(carried) + count * q_rows // local_heads
    out_shape = (done, local_heads * value_width)
    scratch = [
        pltpu.VMEM((rows * heads, wide), jnp.bfloat16),
        pltpu.VMEM((dims * heads, wide), jnp.bfloat16),
        pltpu.VMEM((wide // 128, count * q_rows, 128), jnp.float32),
        pltpu.VMEM(w_uv.shape, w_uv.dtype),
        pltpu.SemaphoreType.DMA,
    ]
    if final:
        scratch.append(pltpu.VMEM(out_shape, jnp.float32))
    return pl.pallas_call(
        functools.partial(
            slots_kernel, plan, own, heads, bundles, carried, final,
            1.0 / math.sqrt(VD + ROPE), block,
        ),
        out_shape=jax.ShapeDtypeStruct(out_shape, jnp.bfloat16 if final else jnp.float32),
        grid_spec=pltpu.PrefetchScalarGridSpec(
            num_scalar_prefetch=2,
            grid=(count,),
            in_specs=in_specs,
            out_specs=pl.BlockSpec(out_shape, lambda i, *_: (0, 0)),
            scratch_shapes=scratch,
        ),
        compiler_params=pltpu.CompilerParams(vmem_limit_bytes=24 * 2**20),
        name="attend_slots",
    )(table, info, *args)


def add_in(table, per_head, columns, own, got, before, after):
    part = own[...]
    for g in got:
        part = part + g[...].astype(jnp.float32)
    for y in range(per_head):
        rank = table[PLACE, 1] * per_head + y
        hit = table[OWNER, columns[0]] == rank
        for c in columns[1:]:
            hit = hit | (table[OWNER, c] == rank)
        now = jnp.where(hit, part, 0.0)
        after[y] = now if before is None else before[y] + now


def settle_kernel(heads, per_head, columns, prev_columns, has_total, table, both, *refs):
    refs = list(refs)
    if prev_columns:
        prev_own, prev_got = refs.pop(0), [refs.pop(0) for _ in range(heads - 1)]
        before = refs.pop(0) if has_total else None
    block = both.shape[0] // len(columns)
    sends = len(refs) - 1 - bool(prev_columns)
    own = refs[sends]
    head = table[PLACE, 1]
    if len(columns) == 1:
        own[...] = both[...]
        refs[0][...] = both[...].astype(jnp.bfloat16)
    else:
        for m in range(heads):
            first = table[TARGET, columns[0]] == jnp.bitwise_xor(head, m)
            piece = jnp.where(first, both[:block], both[block:])
            if m == 0:
                own[...] = piece
            else:
                refs[m - 1][...] = piece.astype(jnp.bfloat16)
    if prev_columns:
        add_in(table, per_head, prev_columns, prev_own, prev_got, before, refs[sends + 1])


def settle_step(table, heads, per_head, columns, both, previous):
    n = both.shape[0] // len(columns)
    wide = both.shape[1]
    vmem = pl.BlockSpec(memory_space=pltpu.MemorySpace.VMEM)
    args, prev_columns, has_total = [both], None, False
    if previous is not None:
        prev_columns, prev_own, prev_got, total = previous
        has_total = total is not None
        args += [prev_own, *prev_got] + ([total] if has_total else [])
    sends = 1 if len(columns) == 1 else heads - 1
    out = [jax.ShapeDtypeStruct((n, wide), jnp.bfloat16)] * sends
    out.append(jax.ShapeDtypeStruct((n, wide), jnp.float32))
    if previous is not None:
        out.append(jax.ShapeDtypeStruct((per_head, n, wide), jnp.float32))
    outs = pl.pallas_call(
        functools.partial(settle_kernel, heads, per_head, columns, prev_columns, has_total),
        out_shape=out,
        in_specs=[pl.BlockSpec(memory_space=pltpu.MemorySpace.SMEM)] + [vmem] * len(args),
        out_specs=[vmem] * len(out),
        compiler_params=pltpu.CompilerParams(vmem_limit_bytes=4 * 2**20),
        name="settle",
    )(table, *args)
    to_send = list(outs[:sends]) * (1 if sends > 1 else heads - 1)
    return to_send, outs[sends], outs[sends + 1] if previous is not None else None


def finish_kernel(heads, per_head, columns, roll, table, info, seen, own, *refs):
    got, before, out, total = refs[: heads - 1], refs[heads - 1], refs[heads], refs[heads + 1]
    add_in(table, per_head, columns, own, got, before, total)
    n = total.shape[1]
    slots = n // roll
    to = lax.broadcasted_iota(jnp.int32, (n, n), 0)
    source = lax.broadcasted_iota(jnp.int32, (n, n), 1)
    for y in range(per_head):
        rank = table[PLACE, 1] * per_head + y
        wanted = to
        for b in range(slots):
            place = jnp.int32(0)
            for c in range(slots):
                place = jnp.where(seen[rank, c] == info[rank, 0, b], c, place)
            inside = (to >= b * roll) & (to < (b + 1) * roll)
            wanted = jnp.where(inside, to + (place - b) * roll, wanted)
        pick = jnp.where(wanted == source, 1.0, 0.0).astype(jnp.bfloat16)
        moved = jnp.dot(pick, total[y].astype(jnp.bfloat16), preferred_element_type=jnp.float32)
        out[pl.ds(y * n, n), :] = moved.astype(out.dtype)


def finish(table, info, seen, heads, per_head, columns, roll, own, got, total):
    n, wide = own.shape
    vmem = pl.BlockSpec(memory_space=pltpu.MemorySpace.VMEM)
    smem = pl.BlockSpec(memory_space=pltpu.MemorySpace.SMEM)
    return pl.pallas_call(
        functools.partial(finish_kernel, heads, per_head, columns, roll),
        out_shape=jax.ShapeDtypeStruct((per_head * n, wide), jnp.bfloat16),
        in_specs=[smem] * 3 + [vmem] * (heads + 1),
        out_specs=vmem,
        scratch_shapes=[pltpu.VMEM((per_head, n, wide), jnp.float32)],
        compiler_params=pltpu.CompilerParams(vmem_limit_bytes=6 * 2**20),
        name="finish",
    )(table, info, seen, own, *got, total)


def local_ring(
    q_latent, q_rope, cache_latent, cache_rope, lengths, loads, owner_rank, owner_pick, w_uv, w_out
):
    ranks = lax.axis_size("dp")
    heads = lax.axis_size("head")
    bundles = owner_rank.shape[0]
    local_heads = w_uv.shape[0]
    roll_count = q_latent.shape[0] // bundles
    per_head = ranks // heads
    last = ranks // 2
    order, where, offsets, seen = ring_tables(ranks)
    seen = jnp.asarray(seen, jnp.int32)
    ahead = [(order[i], order[(i + 1) % ranks]) for i in range(ranks)]
    behind = [(b, a) for a, b in ahead]

    def move(x, pairs, axis="dp"):
        return lax.ppermute(x, axis, pairs)

    payload = payload_of(cache_latent, cache_rope, heads)
    slots = payload.shape[0]
    fore, back = move(payload, ahead), move(payload, behind)
    facts = jnp.concatenate([owner_rank, lengths])
    width = 32
    facts = jnp.pad(facts, (0, width - facts.shape[0]))
    info = lax.all_to_all(
        jnp.broadcast_to(facts[None], (ranks, width)), "dp", split_axis=0, concat_axis=0, tiled=True
    )
    info = jnp.maximum(info, 0)[:, None]
    table = plan_of(seen, owner_rank, owner_pick, loads, per_head)
    q = q_latent.reshape(bundles, roll_count * local_heads, -1)
    qr = q_rope.reshape(bundles, roll_count * local_heads, -1)

    def share(chosen):
        found = {0: chosen}
        bit = heads // 2
        while bit:
            pairs = [(i, i ^ bit) for i in range(heads)]
            for m in list(found):
                found[m ^ bit] = move(found[m], pairs, "head")
            bit //= 2
        return [found[m] for m in range(heads)]

    groups = {}
    for k in range(1, last):
        if k > 1:
            fore = move(fore, ahead)
            back = move(back, behind)
        chosen = choose(table, fore, back, [2 * k - 1, 2 * k])
        parts = share(chosen)
        groups[2 * k - 1] = [(p, 0) for p in parts]
        groups[2 * k] = [(p, 1) for p in parts]
    cut = slots // 2
    left = move(fore[:cut], ahead)
    right = move(back[cut:], behind)
    chosen = choose(table, left, right, [2 * last - 1], cut)
    parts = share(chosen)
    groups[2 * last - 1] = [(p, 0) for p in parts]

    def attend(plan, full=None, earlier=None):
        return attend_slots(
            plan, table, info, q, qr, full, [groups[c] for c in plan[(full is not None) :]],
            heads, bundles, w_uv, earlier,
        )

    earlier = [attend([0, 1, 2], (cache_latent, cache_rope))]
    for k in range(2, last):
        earlier.append(attend([2 * k - 1, 2 * k]))
    values = attend([2 * last - 1], None, earlier)
    half = values.shape[1] // 2

    def project(x):
        return jnp.dot(x, w_out, preferred_element_type=jnp.float32)

    def target(p, column):
        return order[(where[p] + offsets[column]) % ranks] // per_head

    def settle(columns, both, previous):
        to_send, own, total = settle_step(table, heads, per_head, columns, both, previous)
        got = []
        for m in range(1, heads):
            pairs = []
            for p in range(ranks):
                for t in sorted({target(p, c) for c in columns}):
                    pairs.append((p * heads + (t ^ m), p * heads + t))
            got.append(move(to_send[m - 1], pairs, ("dp", "head")))
        return columns, own, got, total

    state = settle([0], project(values), None)
    fore = back = values
    for k in range(1, last):
        fore = move(fore, ahead)
        back = move(back, behind)
        both = project(jnp.concatenate([fore, back], axis=0))
        state = settle([2 * k - 1, 2 * k], both, state)
    left = move(fore[:, :half], ahead)
    right = move(back[:, half:], behind)
    ends = project(jnp.concatenate([left, right], axis=1))
    columns, own, got, total = settle([2 * last - 1], ends, state)
    return finish(table, info, seen, heads, per_head, columns, roll_count, own, got, total)


def local(*args):
    ranks, heads = lax.axis_size("dp"), lax.axis_size("head")
    bundles = args[6].shape[0]
    if ranks == bundles and ring_fits(ranks, heads):
        return local_ring(*args)
    return local_general(*args)


def solution(mesh):
    in_specs = (
        P("dp", "head"),
        P("dp", "head"),
        P("dp", None, None),
        P("dp", None, None),
        P("dp"),
        P(),
        P("dp"),
        P("dp"),
        P("head", None, None),
        P("head", "dp"),
    )
    out_specs = P("head", "dp")
    return jax.shard_map(local, mesh=mesh, in_specs=in_specs, out_specs=out_specs, check_vma=False)
```

```python
import functools
import math

import jax
import jax.numpy as jnp
from jax import lax
from jax.experimental import pallas as pl
from jax.experimental.pallas import tpu as pltpu
from jax.sharding import PartitionSpec as P


ROPE = 64
VD = 128


def ring_order(size):
    fast = 1 << (max(size.bit_length() - 1, 0) // 2)
    slow = size // fast
    if fast == 1 or slow % 2:
        return list(range(size))
    cells = [(z, 0) for z in range(slow)]
    for step, z in enumerate(range(slow - 1, -1, -1)):
        ys = range(1, fast) if step % 2 == 0 else range(fast - 1, 0, -1)
        cells += [(z, y) for y in ys]
    return [z * fast + y for z, y in cells]


def ring_fits(ranks, heads):
    if ranks % 2 or ranks < 4 or ranks % heads or heads & (heads - 1):
        return False
    order, per_head = ring_order(ranks), ranks // heads
    return all(
        order[p - k] // per_head != order[(p + k) % ranks] // per_head
        for p in range(ranks)
        for k in range(1, ranks // 2)
    )


def slot_for(info, loads, width, bundles, requester, owner):
    pick = jnp.int32(0)
    for j in range(bundles):
        hit = info[requester * width + j] == owner
        pick = jnp.where(hit, info[requester * width + bundles + j], pick)
    return lax.rem(pick, loads[owner])


def pack_kernel(info, loads, place, lat_ref, rope_ref, out_ref):
    rows = lat_ref.shape[1]
    out_ref[0, :rows, :] = lat_ref[0]
    out_ref[0, rows:, :] = rope_ref[0]


def pack(info, loads, place, cache_latent, cache_rope, ranks, heads, width, bundles):
    rows = cache_latent.shape[1] // heads
    dims = cache_rope.shape[1] // heads
    wide = cache_latent.shape[2]

    def source(i, info, loads, place):
        return slot_for(info, loads, width, bundles, i, place[0]), place[1], 0

    return pl.pallas_call(
        pack_kernel,
        out_shape=jax.ShapeDtypeStruct((ranks, rows + dims, wide), cache_latent.dtype),
        grid_spec=pltpu.PrefetchScalarGridSpec(
            num_scalar_prefetch=3,
            grid=(ranks,),
            in_specs=[pl.BlockSpec((1, rows, wide), source), pl.BlockSpec((1, dims, wide), source)],
            out_specs=pl.BlockSpec((1, rows + dims, wide), lambda i, *_: (i, 0, 0)),
        ),
        name="pack",
    )(info, loads, place, cache_latent, cache_rope)


def attend_kernel(
    heads, width, bundles, scale, block, info, loads, place, q_ref, qr_ref, *refs
):
    parts = refs[:heads]
    w_ref, out_ref, lat, rope, mixed = refs[heads:]
    b = pl.program_id(0)
    rows = lat.shape[0] // heads
    dims = rope.shape[0] // heads
    for m in range(heads):
        at = jnp.bitwise_xor(place[1], m)
        lat[pl.ds(pl.multiple_of(at * rows, rows), rows), :] = parts[m][0, :rows, :]
        rope[pl.ds(pl.multiple_of(at * dims, dims), dims), :] = parts[m][0, rows:, :]
    base = place[0] * width
    owner = info[base + b]
    slot = lax.rem(info[base + bundles + b], loads[owner])
    length = info[owner * width + 2 * bundles + slot]
    total_rows = q_ref.shape[1]
    live = lax.broadcasted_iota(jnp.int32, (block, lat.shape[0]), 1) < length
    for i in range(total_rows // block):
        at = slice(i * block, (i + 1) * block)
        s = lax.dot_general(
            q_ref[0, at, :], lat[...], (((1,), (1,)), ((), ())), preferred_element_type=jnp.float32
        )
        s = s + jnp.dot(qr_ref[0, at, :], rope[...], preferred_element_type=jnp.float32)
        s = jnp.where(live, s * scale, -1e30)
        w = jnp.exp(s - jnp.max(s, axis=1, keepdims=True))
        w = w * (1.0 / jnp.sum(w, axis=1, keepdims=True))
        o = jnp.dot(w.astype(jnp.bfloat16), lat[...], preferred_element_type=jnp.float32)
        for c in range(mixed.shape[0]):
            piece = o[:, c * 128 : (c + 1) * 128]
            mixed[c, pl.ds(b * total_rows + i * block, block), :] = piece

    @pl.when(b == pl.num_programs(0) - 1)
    def _():
        local_heads, _, value_width = w_ref.shape
        n = mixed.shape[1] // local_heads
        for h in range(local_heads):
            x = jnp.concatenate(
                [mixed[c, pl.ds(h, n, stride=local_heads), :] for c in range(mixed.shape[0])], axis=1
            ).astype(jnp.bfloat16)
            v = jnp.dot(x, w_ref[h], preferred_element_type=jnp.float32)
            out_ref[:, h * value_width : (h + 1) * value_width] = v.astype(jnp.bfloat16)


def attend(info, loads, place, q, qr, parts, w_uv, width, bundles):
    heads = len(parts)
    _, q_rows, wide = q.shape
    _, part_rows, _ = parts[0].shape
    local_heads, _, value_width = w_uv.shape
    dims = qr.shape[2] // heads
    rows = part_rows - dims
    row_count = bundles * q_rows // local_heads

    def theirs(b, info, loads, place):
        return info[place[0] * width + b], 0, 0

    block = math.gcd(q_rows, 128)
    return pl.pallas_call(
        functools.partial(
            attend_kernel, heads, width, bundles, 1.0 / math.sqrt(VD + ROPE), block
        ),
        out_shape=jax.ShapeDtypeStruct((row_count, local_heads * value_width), jnp.bfloat16),
        grid_spec=pltpu.PrefetchScalarGridSpec(
            num_scalar_prefetch=3,
            grid=(bundles,),
            in_specs=[
                pl.BlockSpec((1, q_rows, wide), lambda b, *_: (b, 0, 0)),
                pl.BlockSpec((1, q_rows, qr.shape[2]), lambda b, *_: (b, 0, 0)),
            ]
            + [pl.BlockSpec((1, part_rows, wide), theirs)] * heads
            + [pl.BlockSpec(w_uv.shape, lambda b, *_: (0, 0, 0))],
            out_specs=pl.BlockSpec((row_count, local_heads * value_width), lambda b, *_: (0, 0)),
            scratch_shapes=[
                pltpu.VMEM((rows * heads, wide), jnp.bfloat16),
                pltpu.VMEM((dims * heads, wide), jnp.bfloat16),
                pltpu.VMEM((wide // 128, bundles * q_rows, 128), jnp.float32),
            ],
        ),
        name="attend",
    )(info, loads, place, q, qr, *parts, w_uv)


def local_general(
    q_latent, q_rope, cache_latent, cache_rope, lengths, loads, owner_rank, owner_pick, w_uv, w_out
):
    ranks = lax.axis_size("dp")
    heads = lax.axis_size("head")
    me = lax.axis_index("dp")
    head = lax.axis_index("head")
    bundles = owner_rank.shape[0]
    roll_count = q_latent.shape[0] // bundles
    local_heads = w_uv.shape[0]
    place = jnp.stack([me, head]).astype(jnp.int32)

    facts = jnp.concatenate([owner_rank, owner_pick, lengths])
    width = 32
    facts = jnp.pad(facts, (0, width - facts.shape[0]))
    info = lax.all_to_all(
        jnp.broadcast_to(facts[None], (ranks, width)), "dp", split_axis=0, concat_axis=0, tiled=True
    ).reshape(-1)
    q = q_latent.reshape(bundles, roll_count * local_heads, -1)
    qr = q_rope.reshape(bundles, roll_count * local_heads, -1)

    packed = pack(info, loads, place, cache_latent, cache_rope, ranks, heads, width, bundles)
    mine = lax.all_to_all(packed, "dp", split_axis=0, concat_axis=0, tiled=True)
    parts = [mine]
    bit = heads // 2
    found = {0: mine}
    while bit:
        pairs = [(i, i ^ bit) for i in range(heads)]
        for m in list(found):
            found[m ^ bit] = lax.ppermute(found[m], "head", pairs)
        bit //= 2
    parts = [found[m] for m in range(heads)]
    values = attend(info, loads, place, q, qr, parts, w_uv, width, bundles)

    order = ring_order(ranks)
    ahead = [(order[i], order[(i + 1) % ranks]) for i in range(ranks)]
    behind = [(b, a) for a, b in ahead]
    half = values.shape[1] // 2

    def project(x):
        return jnp.dot(x, w_out, preferred_element_type=jnp.float32).astype(jnp.bfloat16)

    partial = {0: project(values)}
    fore = back = values
    for step in range(1, (ranks + 1) // 2):
        fore = lax.ppermute(fore, "dp", ahead)
        back = lax.ppermute(back, "dp", behind)
        both = project(jnp.concatenate([fore, back], axis=0))
        partial[-step] = both[: values.shape[0]]
        partial[step] = both[values.shape[0] :]
    if ranks % 2 == 0:
        left = lax.ppermute(fore[:, :half], "dp", ahead)
        right = lax.ppermute(back[:, half:], "dp", behind)
        partial[ranks // 2] = project(jnp.concatenate([left, right], axis=1))
    stacked = jnp.stack([partial[k if 2 * k <= ranks else k - ranks] for k in range(ranks)])
    position = [0] * ranks
    for i, r in enumerate(order):
        position[r] = i
    position = jnp.asarray(position, jnp.int32)
    by_rank = stacked[(position - position[me]) % ranks]
    shares = by_rank.reshape(heads, -1, w_out.shape[1])
    got = lax.all_to_all(shares, "head", split_axis=0, concat_axis=0, tiled=True)
    return jnp.sum(got.astype(jnp.float32), axis=0).astype(jnp.bfloat16)


def in_hbm(x):
    return pltpu.with_memory_space_constraint(x, pltpu.MemorySpace.HBM)


def ring_tables(ranks):
    order = ring_order(ranks)
    where = [order.index(r) for r in range(ranks)]
    offsets = [0]
    for k in range(1, ranks // 2):
        offsets += [-k, k]
    offsets.append(ranks // 2)
    seen = [[order[(where[r] + o) % ranks] for o in offsets] for r in range(ranks)]
    return order, where, offsets, seen


BUNDLE, SLOT, TARGET, OWNER, PLACE, PLAN_ROWS = 0, 1, 2, 3, 4, 8


def plan_kernel(per_head, seen, owner_rank, owner_pick, loads, table):
    ranks = seen.shape[1]
    me, head = lax.axis_index("dp"), lax.axis_index("head")
    table[PLACE, 0] = me
    table[PLACE, 1] = head
    for c in range(ranks):
        owner = seen[me, c]
        bundle, pick = jnp.int32(0), jnp.int32(0)
        for b in range(owner_rank.shape[0]):
            hit = owner_rank[b] == owner
            bundle = jnp.where(hit, b, bundle)
            pick = jnp.where(hit, owner_pick[b], pick)
        table[BUNDLE, c] = bundle
        table[SLOT, c] = lax.rem(pick, loads[owner])
        table[TARGET, c] = lax.div(owner, per_head)
        table[OWNER, c] = owner


def plan_of(seen, owner_rank, owner_pick, loads, per_head):
    smem = pl.BlockSpec(memory_space=pltpu.MemorySpace.SMEM)
    return pl.pallas_call(
        functools.partial(plan_kernel, per_head),
        out_shape=jax.ShapeDtypeStruct((PLAN_ROWS, seen.shape[1]), jnp.int32),
        in_specs=[smem] * 4,
        out_specs=smem,
        name="plan",
    )(seen, owner_rank, owner_pick, loads)


def payload_kernel(lat, rope, out, sems):
    head = lax.axis_index("head")
    dims = rope.shape[1] * (out.shape[1]) // (rope.shape[1] + lat.shape[1])
    rows = out.shape[1] - dims
    copies = [
        pltpu.make_async_copy(
            lat.at[:, pl.ds(pl.multiple_of(head * rows, rows), rows), :],
            out.at[:, pl.ds(0, rows), :],
            sems.at[0],
        ),
        pltpu.make_async_copy(
            rope.at[:, pl.ds(pl.multiple_of(head * dims, dims), dims), :],
            out.at[:, pl.ds(rows, dims), :],
            sems.at[1],
        ),
    ]
    for copy in copies:
        copy.start()
    for copy in copies:
        copy.wait()


def payload_of(cache_latent, cache_rope, heads):
    slots, positions, wide = cache_latent.shape
    rows = (positions + cache_rope.shape[1]) // heads
    return pl.pallas_call(
        payload_kernel,
        out_shape=jax.ShapeDtypeStruct((slots, rows, wide), cache_latent.dtype),
        in_specs=[pl.BlockSpec(memory_space=pl.ANY)] * 2,
        out_specs=pl.BlockSpec(memory_space=pltpu.MemorySpace.VMEM),
        scratch_shapes=[pltpu.SemaphoreType.DMA((2,))],
        compiler_params=pltpu.CompilerParams(vmem_limit_bytes=4 * 2**20),
        name="payload",
    )(in_hbm(cache_latent), in_hbm(cache_rope))


def choose_kernel(cut, column, table, a_ref, b_ref, out_ref):
    if cut is None:
        out_ref[0] = a_ref[0]
        out_ref[1] = b_ref[0]
    else:
        first = table[SLOT, column] < cut

        @pl.when(first)
        def _():
            out_ref[0] = a_ref[0]

        @pl.when(jnp.logical_not(first))
        def _():
            out_ref[0] = b_ref[0]


def choose(table, a, b, columns, cut=None):
    _, rows, wide = a.shape
    if cut is None:
        index_a = lambda i, table: (table[SLOT, columns[0]], 0, 0)
        index_b = lambda i, table: (table[SLOT, columns[1]], 0, 0)
    else:
        index_a = lambda i, table: (jnp.minimum(table[SLOT, columns[0]], cut - 1), 0, 0)
        index_b = lambda i, table: (jnp.maximum(table[SLOT, columns[0]] - cut, 0), 0, 0)
    return pl.pallas_call(
        functools.partial(choose_kernel, cut, columns[0]),
        out_shape=jax.ShapeDtypeStruct((len(columns), rows, wide), a.dtype),
        grid_spec=pltpu.PrefetchScalarGridSpec(
            num_scalar_prefetch=1,
            grid=(1,),
            in_specs=[pl.BlockSpec((1, rows, wide), index_a), pl.BlockSpec((1, rows, wide), index_b)],
            out_specs=pl.BlockSpec((len(columns), rows, wide), lambda i, *_: (0, 0, 0)),
        ),
        compiler_params=pltpu.CompilerParams(vmem_limit_bytes=4 * 2**20),
        name="choose",
    )(table, a, b)


def slots_kernel(plan, own, heads, bundles, carried, final, scale, block, table, info, *refs):
    count = len(plan)
    refs = list(refs)
    q_ref, qr_ref = refs.pop(0), refs.pop(0)
    if own:
        full_lat, full_rope = refs.pop(0), refs.pop(0)
    shipped = count - own
    parts = [[refs.pop(0) for _ in range(heads)] for _ in range(shipped)]
    earlier = [refs.pop(0) for _ in carried]
    w_hbm, out_ref, lat, rope, mixed, w_ref, sem = refs[:7]
    i = pl.program_id(0)
    total_rows = q_ref.shape[1]
    w_copy = pltpu.make_async_copy(w_hbm, w_ref, sem)

    @pl.when(i == 0)
    def _():
        w_copy.start()

    rows = lat.shape[0] // heads
    dims = rope.shape[0] // heads

    for j in range(count):

        @pl.when(i == j)
        def _():
            if own and j == 0:
                lat[...] = full_lat[0]
                rope[...] = full_rope[0]
                return
            for m in range(heads):
                part = parts[j - own][m]
                to = jnp.bitwise_xor(table[PLACE, 1], m)
                lat[pl.ds(pl.multiple_of(to * rows, rows), rows), :] = part[0, :rows, :]
                rope[pl.ds(pl.multiple_of(to * dims, dims), dims), :] = part[0, rows:, :]

    column = jnp.int32(plan[0]) + i
    length = info[table[OWNER, column], 0, bundles + table[SLOT, column]]
    live = lax.broadcasted_iota(jnp.int32, (block, lat.shape[0]), 1) < length
    for r in range(total_rows // block):
        at = slice(r * block, (r + 1) * block)
        s = lax.dot_general(
            q_ref[0, at, :], lat[...], (((1,), (1,)), ((), ())), preferred_element_type=jnp.float32
        )
        s = s + jnp.dot(qr_ref[0, at, :], rope[...], preferred_element_type=jnp.float32)
        s = jnp.where(live, s * scale, -1e30)
        w = jnp.exp(s - jnp.max(s, axis=1, keepdims=True))
        w = w * (1.0 / jnp.sum(w, axis=1, keepdims=True))
        o = jnp.dot(w.astype(jnp.bfloat16), lat[...], preferred_element_type=jnp.float32)
        for c in range(mixed.shape[0]):
            mixed[c, pl.ds(i * total_rows + r * block, block), :] = o[:, c * 128 : (c + 1) * 128]

    @pl.when(i == count - 1)
    def _():
        w_copy.wait()
        local_heads, _, value_width = w_ref.shape
        n = mixed.shape[1] // local_heads
        into, at = out_ref, 0
        if final:
            into = refs[7]
            for piece in earlier:
                into[pl.ds(at, piece.shape[0]), :] = piece[...]
                at += piece.shape[0]
        for h in range(local_heads):
            x = jnp.concatenate(
                [mixed[c, pl.ds(h, n, stride=local_heads), :] for c in range(mixed.shape[0])], axis=1
            ).astype(jnp.bfloat16)
            v = jnp.dot(x, w_ref[h], preferred_element_type=jnp.float32)
            into[pl.ds(at, n), h * value_width : (h + 1) * value_width] = v
        if final:
            out_ref[...] = into[...].astype(out_ref.dtype)


def attend_slots(plan, table, info, q, qr, full, parts, heads, bundles, w_uv, earlier=None):
    own = 1 if full is not None else 0
    final = earlier is not None
    earlier = list(earlier or ())
    count = len(plan)
    _, q_rows, wide = q.shape
    part_rows = parts[0][0][0].shape[1]
    dims = qr.shape[2] // heads
    rows = part_rows - dims
    block = math.gcd(q_rows, 128)
    local_heads, _, value_width = w_uv.shape
    carried = [e.shape[0] for e in earlier]

    def bundle(i, table, info):
        return table[BUNDLE, plan[0] + i], 0, 0

    in_specs = [
        pl.BlockSpec((1, q_rows, wide), bundle),
        pl.BlockSpec((1, q_rows, qr.shape[2]), bundle),
    ]
    args = [in_hbm(q), in_hbm(qr)]
    if own:
        here = lambda i, table, info: (table[SLOT, plan[0]], 0, 0)
        in_specs += [
            pl.BlockSpec((1, rows * heads, wide), here),
            pl.BlockSpec((1, dims * heads, wide), here),
        ]
        args += [in_hbm(x) for x in full]
    for slot in parts:
        for array, index in slot:
            in_specs.append(
                pl.BlockSpec((1, part_rows, wide), lambda i, *_, index=index: (index, 0, 0))
            )
            args.append(array)
    for piece in earlier:
        in_specs.append(pl.BlockSpec(piece.shape, lambda i, *_: (0, 0)))
        args.append(piece)
    in_specs.append(pl.BlockSpec(memory_space=pl.ANY))
    args.append(in_hbm(w_uv))
    done = sum(carried) + count * q_rows // local_heads
    out_shape = (done, local_heads * value_width)
    scratch = [
        pltpu.VMEM((rows * heads, wide), jnp.bfloat16),
        pltpu.VMEM((dims * heads, wide), jnp.bfloat16),
        pltpu.VMEM((wide // 128, count * q_rows, 128), jnp.float32),
        pltpu.VMEM(w_uv.shape, w_uv.dtype),
        pltpu.SemaphoreType.DMA,
    ]
    if final:
        scratch.append(pltpu.VMEM(out_shape, jnp.float32))
    return pl.pallas_call(
        functools.partial(
            slots_kernel, plan, own, heads, bundles, carried, final,
            1.0 / math.sqrt(VD + ROPE), block,
        ),
        out_shape=jax.ShapeDtypeStruct(out_shape, jnp.bfloat16 if final else jnp.float32),
        grid_spec=pltpu.PrefetchScalarGridSpec(
            num_scalar_prefetch=2,
            grid=(count,),
            in_specs=in_specs,
            out_specs=pl.BlockSpec(out_shape, lambda i, *_: (0, 0)),
            scratch_shapes=scratch,
        ),
        compiler_params=pltpu.CompilerParams(vmem_limit_bytes=24 * 2**20),
        name="attend_slots",
    )(table, info, *args)


def add_in(table, per_head, columns, own, got, before, after):
    part = own[...]
    for g in got:
        part = part + g[...].astype(jnp.float32)
    for y in range(per_head):
        rank = table[PLACE, 1] * per_head + y
        hit = table[OWNER, columns[0]] == rank
        for c in columns[1:]:
            hit = hit | (table[OWNER, c] == rank)
        now = jnp.where(hit, part, 0.0)
        after[y] = now if before is None else before[y] + now


def settle_kernel(heads, per_head, columns, prev_columns, has_total, table, both, *refs):
    refs = list(refs)
    if prev_columns:
        prev_own, prev_got = refs.pop(0), [refs.pop(0) for _ in range(heads - 1)]
        before = refs.pop(0) if has_total else None
    block = both.shape[0] // len(columns)
    sends = len(refs) - 1 - bool(prev_columns)
    own = refs[sends]
    head = table[PLACE, 1]
    if len(columns) == 1:
        own[...] = both[...]
        refs[0][...] = both[...].astype(jnp.bfloat16)
    else:
        for m in range(heads):
            first = table[TARGET, columns[0]] == jnp.bitwise_xor(head, m)
            piece = jnp.where(first, both[:block], both[block:])
            if m == 0:
                own[...] = piece
            else:
                refs[m - 1][...] = piece.astype(jnp.bfloat16)
    if prev_columns:
        add_in(table, per_head, prev_columns, prev_own, prev_got, before, refs[sends + 1])


def settle_step(table, heads, per_head, columns, both, previous):
    n = both.shape[0] // len(columns)
    wide = both.shape[1]
    vmem = pl.BlockSpec(memory_space=pltpu.MemorySpace.VMEM)
    args, prev_columns, has_total = [both], None, False
    if previous is not None:
        prev_columns, prev_own, prev_got, total = previous
        has_total = total is not None
        args += [prev_own, *prev_got] + ([total] if has_total else [])
    sends = 1 if len(columns) == 1 else heads - 1
    out = [jax.ShapeDtypeStruct((n, wide), jnp.bfloat16)] * sends
    out.append(jax.ShapeDtypeStruct((n, wide), jnp.float32))
    if previous is not None:
        out.append(jax.ShapeDtypeStruct((per_head, n, wide), jnp.float32))
    outs = pl.pallas_call(
        functools.partial(settle_kernel, heads, per_head, columns, prev_columns, has_total),
        out_shape=out,
        in_specs=[pl.BlockSpec(memory_space=pltpu.MemorySpace.SMEM)] + [vmem] * len(args),
        out_specs=[vmem] * len(out),
        compiler_params=pltpu.CompilerParams(vmem_limit_bytes=4 * 2**20),
        name="settle",
    )(table, *args)
    to_send = list(outs[:sends]) * (1 if sends > 1 else heads - 1)
    return to_send, outs[sends], outs[sends + 1] if previous is not None else None


def finish_kernel(heads, per_head, steps, roll, table, info, seen, before, *refs):
    out, total = refs[heads * len(steps) :]
    for i, columns in enumerate(steps):
        own, *got = refs[heads * i : heads * (i + 1)]
        add_in(table, per_head, columns, own, got, total if i else before, total)
    n = total.shape[1]
    slots = n // roll
    to = lax.broadcasted_iota(jnp.int32, (n, n), 0)
    source = lax.broadcasted_iota(jnp.int32, (n, n), 1)
    for y in range(per_head):
        rank = table[PLACE, 1] * per_head + y
        wanted = to
        for b in range(slots):
            place = jnp.int32(0)
            for c in range(slots):
                place = jnp.where(seen[rank, c] == info[rank, 0, b], c, place)
            inside = (to >= b * roll) & (to < (b + 1) * roll)
            wanted = jnp.where(inside, to + (place - b) * roll, wanted)
        pick = jnp.where(wanted == source, 1.0, 0.0).astype(jnp.bfloat16)
        moved = jnp.dot(pick, total[y].astype(jnp.bfloat16), preferred_element_type=jnp.float32)
        out[pl.ds(y * n, n), :] = moved.astype(out.dtype)


def finish(table, info, seen, heads, per_head, roll, total, states):
    _, n, wide = total.shape
    steps = [state[0] for state in states]
    args = [x for _, own, got in states for x in (own, *got)]
    vmem = pl.BlockSpec(memory_space=pltpu.MemorySpace.VMEM)
    smem = pl.BlockSpec(memory_space=pltpu.MemorySpace.SMEM)
    return pl.pallas_call(
        functools.partial(finish_kernel, heads, per_head, steps, roll),
        out_shape=jax.ShapeDtypeStruct((per_head * n, wide), jnp.bfloat16),
        in_specs=[smem] * 3 + [vmem] * (1 + len(args)),
        out_specs=vmem,
        scratch_shapes=[pltpu.VMEM((per_head, n, wide), jnp.float32)],
        compiler_params=pltpu.CompilerParams(vmem_limit_bytes=6 * 2**20),
        name="finish",
    )(table, info, seen, total, *args)


def local_ring(
    q_latent, q_rope, cache_latent, cache_rope, lengths, loads, owner_rank, owner_pick, w_uv, w_out
):
    ranks = lax.axis_size("dp")
    heads = lax.axis_size("head")
    bundles = owner_rank.shape[0]
    local_heads = w_uv.shape[0]
    roll_count = q_latent.shape[0] // bundles
    per_head = ranks // heads
    last = ranks // 2
    order, where, offsets, seen = ring_tables(ranks)
    seen = jnp.asarray(seen, jnp.int32)
    ahead = [(order[i], order[(i + 1) % ranks]) for i in range(ranks)]
    behind = [(b, a) for a, b in ahead]

    def move(x, pairs, axis="dp"):
        return lax.ppermute(x, axis, pairs)

    payload = payload_of(cache_latent, cache_rope, heads)
    slots = payload.shape[0]
    fore, back = move(payload, ahead), move(payload, behind)
    facts = jnp.concatenate([owner_rank, lengths])
    width = 32
    facts = jnp.pad(facts, (0, width - facts.shape[0]))
    info = lax.all_to_all(
        jnp.broadcast_to(facts[None], (ranks, width)), "dp", split_axis=0, concat_axis=0, tiled=True
    )
    info = jnp.maximum(info, 0)[:, None]
    table = plan_of(seen, owner_rank, owner_pick, loads, per_head)
    q = q_latent.reshape(bundles, roll_count * local_heads, -1)
    qr = q_rope.reshape(bundles, roll_count * local_heads, -1)

    def share(chosen):
        found = {0: chosen}
        bit = heads // 2
        while bit:
            pairs = [(i, i ^ bit) for i in range(heads)]
            for m in list(found):
                found[m ^ bit] = move(found[m], pairs, "head")
            bit //= 2
        return [found[m] for m in range(heads)]

    groups = {}
    for k in range(1, last):
        if k > 1:
            fore = move(fore, ahead)
            back = move(back, behind)
        chosen = choose(table, fore, back, [2 * k - 1, 2 * k])
        parts = share(chosen)
        groups[2 * k - 1] = [(p, 0) for p in parts]
        groups[2 * k] = [(p, 1) for p in parts]
    cut = slots // 2
    left = move(fore[:cut], ahead)
    right = move(back[cut:], behind)
    chosen = choose(table, left, right, [2 * last - 1], cut)
    parts = share(chosen)
    groups[2 * last - 1] = [(p, 0) for p in parts]

    def attend(plan, full=None, earlier=None):
        return attend_slots(
            plan, table, info, q, qr, full, [groups[c] for c in plan[(full is not None) :]],
            heads, bundles, w_uv, earlier,
        )

    earlier = [attend([0, 1, 2], (cache_latent, cache_rope))]
    for k in range(2, last):
        earlier.append(attend([2 * k - 1, 2 * k]))
    values = attend([2 * last - 1], None, earlier)
    half = values.shape[1] // 2

    def project(x):
        return jnp.dot(x, w_out, preferred_element_type=jnp.float32)

    def target(p, column):
        return order[(where[p] + offsets[column]) % ranks] // per_head

    def settle(columns, both, previous):
        to_send, own, total = settle_step(table, heads, per_head, columns, both, previous)
        got = []
        for m in range(1, heads):
            pairs = []
            for p in range(ranks):
                for t in sorted({target(p, c) for c in columns}):
                    pairs.append((p * heads + (t ^ m), p * heads + t))
            got.append(move(to_send[m - 1], pairs, ("dp", "head")))
        return columns, own, got, total

    state = settle([0], project(values), None)
    fore = back = values
    for k in range(1, last):
        fore = move(fore, ahead)
        back = move(back, behind)
        both = project(jnp.concatenate([fore, back], axis=0))
        state = settle([2 * k - 1, 2 * k], both, state)
    left = move(fore[:, :half], ahead)
    right = move(back[:, half:], behind)
    ends = project(jnp.concatenate([left, right], axis=1))
    *before, total = state
    *final, _ = settle([2 * last - 1], ends, None)
    return finish(table, info, seen, heads, per_head, roll_count, total, [before, final])


def local(*args):
    ranks, heads = lax.axis_size("dp"), lax.axis_size("head")
    bundles = args[6].shape[0]
    if ranks == bundles and ring_fits(ranks, heads):
        return local_ring(*args)
    return local_general(*args)


def solution(mesh):
    in_specs = (
        P("dp", "head"),
        P("dp", "head"),
        P("dp", None, None),
        P("dp", None, None),
        P("dp"),
        P(),
        P("dp"),
        P("dp"),
        P("head", None, None),
        P("head", "dp"),
    )
    out_specs = P("head", "dp")
    return jax.shard_map(local, mesh=mesh, in_specs=in_specs, out_specs=out_specs, check_vma=False)
```

```python
import functools
import math

import jax
import jax.numpy as jnp
from jax import lax
from jax.experimental import pallas as pl
from jax.experimental.pallas import tpu as pltpu
from jax.sharding import PartitionSpec as P


ROPE = 64
VD = 128


def ring_order(size):
    fast = 1 << (max(size.bit_length() - 1, 0) // 2)
    slow = size // fast
    if fast == 1 or slow % 2:
        return list(range(size))
    cells = [(z, 0) for z in range(slow)]
    for step, z in enumerate(range(slow - 1, -1, -1)):
        ys = range(1, fast) if step % 2 == 0 else range(fast - 1, 0, -1)
        cells += [(z, y) for y in ys]
    return [z * fast + y for z, y in cells]


def ring_fits(ranks, heads):
    if ranks % 2 or ranks < 4 or ranks % heads or heads & (heads - 1):
        return False
    order, per_head = ring_order(ranks), ranks // heads
    return all(
        order[p - k] // per_head != order[(p + k) % ranks] // per_head
        for p in range(ranks)
        for k in range(1, ranks // 2)
    )


def slot_for(info, loads, width, bundles, requester, owner):
    pick = jnp.int32(0)
    for j in range(bundles):
        hit = info[requester * width + j] == owner
        pick = jnp.where(hit, info[requester * width + bundles + j], pick)
    return lax.rem(pick, loads[owner])


def pack_kernel(info, loads, place, lat_ref, rope_ref, out_ref):
    rows = lat_ref.shape[1]
    out_ref[0, :rows, :] = lat_ref[0]
    out_ref[0, rows:, :] = rope_ref[0]


def pack(info, loads, place, cache_latent, cache_rope, ranks, heads, width, bundles):
    rows = cache_latent.shape[1] // heads
    dims = cache_rope.shape[1] // heads
    wide = cache_latent.shape[2]

    def source(i, info, loads, place):
        return slot_for(info, loads, width, bundles, i, place[0]), place[1], 0

    return pl.pallas_call(
        pack_kernel,
        out_shape=jax.ShapeDtypeStruct((ranks, rows + dims, wide), cache_latent.dtype),
        grid_spec=pltpu.PrefetchScalarGridSpec(
            num_scalar_prefetch=3,
            grid=(ranks,),
            in_specs=[pl.BlockSpec((1, rows, wide), source), pl.BlockSpec((1, dims, wide), source)],
            out_specs=pl.BlockSpec((1, rows + dims, wide), lambda i, *_: (i, 0, 0)),
        ),
        name="pack",
    )(info, loads, place, cache_latent, cache_rope)


def attend_kernel(
    heads, width, bundles, scale, block, info, loads, place, q_ref, qr_ref, *refs
):
    parts = refs[:heads]
    w_ref, out_ref, lat, rope, mixed = refs[heads:]
    b = pl.program_id(0)
    rows = lat.shape[0] // heads
    dims = rope.shape[0] // heads
    for m in range(heads):
        at = jnp.bitwise_xor(place[1], m)
        lat[pl.ds(pl.multiple_of(at * rows, rows), rows), :] = parts[m][0, :rows, :]
        rope[pl.ds(pl.multiple_of(at * dims, dims), dims), :] = parts[m][0, rows:, :]
    base = place[0] * width
    owner = info[base + b]
    slot = lax.rem(info[base + bundles + b], loads[owner])
    length = info[owner * width + 2 * bundles + slot]
    total_rows = q_ref.shape[1]
    live = lax.broadcasted_iota(jnp.int32, (block, lat.shape[0]), 1) < length
    for i in range(total_rows // block):
        at = slice(i * block, (i + 1) * block)
        s = lax.dot_general(
            q_ref[0, at, :], lat[...], (((1,), (1,)), ((), ())), preferred_element_type=jnp.float32
        )
        s = s + jnp.dot(qr_ref[0, at, :], rope[...], preferred_element_type=jnp.float32)
        s = jnp.where(live, s * scale, -1e30)
        w = jnp.exp(s - jnp.max(s, axis=1, keepdims=True))
        w = w * (1.0 / jnp.sum(w, axis=1, keepdims=True))
        o = jnp.dot(w.astype(jnp.bfloat16), lat[...], preferred_element_type=jnp.float32)
        for c in range(mixed.shape[0]):
            piece = o[:, c * 128 : (c + 1) * 128]
            mixed[c, pl.ds(b * total_rows + i * block, block), :] = piece

    @pl.when(b == pl.num_programs(0) - 1)
    def _():
        local_heads, _, value_width = w_ref.shape
        n = mixed.shape[1] // local_heads
        for h in range(local_heads):
            x = jnp.concatenate(
                [mixed[c, pl.ds(h, n, stride=local_heads), :] for c in range(mixed.shape[0])], axis=1
            ).astype(jnp.bfloat16)
            v = jnp.dot(x, w_ref[h], preferred_element_type=jnp.float32)
            out_ref[:, h * value_width : (h + 1) * value_width] = v.astype(jnp.bfloat16)


def attend(info, loads, place, q, qr, parts, w_uv, width, bundles):
    heads = len(parts)
    _, q_rows, wide = q.shape
    _, part_rows, _ = parts[0].shape
    local_heads, _, value_width = w_uv.shape
    dims = qr.shape[2] // heads
    rows = part_rows - dims
    row_count = bundles * q_rows // local_heads

    def theirs(b, info, loads, place):
        return info[place[0] * width + b], 0, 0

    block = math.gcd(q_rows, 128)
    return pl.pallas_call(
        functools.partial(
            attend_kernel, heads, width, bundles, 1.0 / math.sqrt(VD + ROPE), block
        ),
        out_shape=jax.ShapeDtypeStruct((row_count, local_heads * value_width), jnp.bfloat16),
        grid_spec=pltpu.PrefetchScalarGridSpec(
            num_scalar_prefetch=3,
            grid=(bundles,),
            in_specs=[
                pl.BlockSpec((1, q_rows, wide), lambda b, *_: (b, 0, 0)),
                pl.BlockSpec((1, q_rows, qr.shape[2]), lambda b, *_: (b, 0, 0)),
            ]
            + [pl.BlockSpec((1, part_rows, wide), theirs)] * heads
            + [pl.BlockSpec(w_uv.shape, lambda b, *_: (0, 0, 0))],
            out_specs=pl.BlockSpec((row_count, local_heads * value_width), lambda b, *_: (0, 0)),
            scratch_shapes=[
                pltpu.VMEM((rows * heads, wide), jnp.bfloat16),
                pltpu.VMEM((dims * heads, wide), jnp.bfloat16),
                pltpu.VMEM((wide // 128, bundles * q_rows, 128), jnp.float32),
            ],
        ),
        name="attend",
    )(info, loads, place, q, qr, *parts, w_uv)


def local_general(
    q_latent, q_rope, cache_latent, cache_rope, lengths, loads, owner_rank, owner_pick, w_uv, w_out
):
    ranks = lax.axis_size("dp")
    heads = lax.axis_size("head")
    me = lax.axis_index("dp")
    head = lax.axis_index("head")
    bundles = owner_rank.shape[0]
    roll_count = q_latent.shape[0] // bundles
    local_heads = w_uv.shape[0]
    place = jnp.stack([me, head]).astype(jnp.int32)

    facts = jnp.concatenate([owner_rank, owner_pick, lengths])
    width = 32
    facts = jnp.pad(facts, (0, width - facts.shape[0]))
    info = lax.all_to_all(
        jnp.broadcast_to(facts[None], (ranks, width)), "dp", split_axis=0, concat_axis=0, tiled=True
    ).reshape(-1)
    q = q_latent.reshape(bundles, roll_count * local_heads, -1)
    qr = q_rope.reshape(bundles, roll_count * local_heads, -1)

    packed = pack(info, loads, place, cache_latent, cache_rope, ranks, heads, width, bundles)
    mine = lax.all_to_all(packed, "dp", split_axis=0, concat_axis=0, tiled=True)
    parts = [mine]
    bit = heads // 2
    found = {0: mine}
    while bit:
        pairs = [(i, i ^ bit) for i in range(heads)]
        for m in list(found):
            found[m ^ bit] = lax.ppermute(found[m], "head", pairs)
        bit //= 2
    parts = [found[m] for m in range(heads)]
    values = attend(info, loads, place, q, qr, parts, w_uv, width, bundles)

    order = ring_order(ranks)
    ahead = [(order[i], order[(i + 1) % ranks]) for i in range(ranks)]
    behind = [(b, a) for a, b in ahead]
    half = values.shape[1] // 2

    def project(x):
        return jnp.dot(x, w_out, preferred_element_type=jnp.float32).astype(jnp.bfloat16)

    partial = {0: project(values)}
    fore = back = values
    for step in range(1, (ranks + 1) // 2):
        fore = lax.ppermute(fore, "dp", ahead)
        back = lax.ppermute(back, "dp", behind)
        both = project(jnp.concatenate([fore, back], axis=0))
        partial[-step] = both[: values.shape[0]]
        partial[step] = both[values.shape[0] :]
    if ranks % 2 == 0:
        left = lax.ppermute(fore[:, :half], "dp", ahead)
        right = lax.ppermute(back[:, half:], "dp", behind)
        partial[ranks // 2] = project(jnp.concatenate([left, right], axis=1))
    stacked = jnp.stack([partial[k if 2 * k <= ranks else k - ranks] for k in range(ranks)])
    position = [0] * ranks
    for i, r in enumerate(order):
        position[r] = i
    position = jnp.asarray(position, jnp.int32)
    by_rank = stacked[(position - position[me]) % ranks]
    shares = by_rank.reshape(heads, -1, w_out.shape[1])
    got = lax.all_to_all(shares, "head", split_axis=0, concat_axis=0, tiled=True)
    return jnp.sum(got.astype(jnp.float32), axis=0).astype(jnp.bfloat16)


def in_hbm(x):
    return pltpu.with_memory_space_constraint(x, pltpu.MemorySpace.HBM)


def ring_tables(ranks):
    order = ring_order(ranks)
    where = [order.index(r) for r in range(ranks)]
    offsets = [0]
    for k in range(1, ranks // 2):
        offsets += [-k, k]
    offsets.append(ranks // 2)
    seen = [[order[(where[r] + o) % ranks] for o in offsets] for r in range(ranks)]
    return order, where, offsets, seen


BUNDLE, SLOT, TARGET, OWNER, PLACE, PLAN_ROWS = 0, 1, 2, 3, 4, 8


def chunk_plans(ranks):
    middle = ranks // 2
    return {
        "p": [list(range(middle - 1)), [middle - 1]],
        "s": [list(range(middle, ranks - 1)), [ranks - 1]],
    }


def plan_kernel(per_head, seen, owner_rank, owner_pick, loads, table):
    ranks = seen.shape[1]
    me, head = lax.axis_index("dp"), lax.axis_index("head")
    table[PLACE, 0] = me
    table[PLACE, 1] = head
    for c in range(ranks):
        owner = seen[me, c]
        bundle, pick = jnp.int32(0), jnp.int32(0)
        for b in range(owner_rank.shape[0]):
            hit = owner_rank[b] == owner
            bundle = jnp.where(hit, b, bundle)
            pick = jnp.where(hit, owner_pick[b], pick)
        table[BUNDLE, c] = bundle
        table[SLOT, c] = lax.rem(pick, loads[owner])
        table[TARGET, c] = lax.div(owner, per_head)
        table[OWNER, c] = owner


def plan_of(seen, owner_rank, owner_pick, loads, per_head):
    smem = pl.BlockSpec(memory_space=pltpu.MemorySpace.SMEM)
    return pl.pallas_call(
        functools.partial(plan_kernel, per_head),
        out_shape=jax.ShapeDtypeStruct((PLAN_ROWS, seen.shape[1]), jnp.int32),
        in_specs=[smem] * 4,
        out_specs=smem,
        name="plan",
    )(seen, owner_rank, owner_pick, loads)


def payload_kernel(lat, rope, out, sems):
    head = lax.axis_index("head")
    dims = rope.shape[1] * (out.shape[1]) // (rope.shape[1] + lat.shape[1])
    rows = out.shape[1] - dims
    copies = [
        pltpu.make_async_copy(
            lat.at[:, pl.ds(pl.multiple_of(head * rows, rows), rows), :],
            out.at[:, pl.ds(0, rows), :],
            sems.at[0],
        ),
        pltpu.make_async_copy(
            rope.at[:, pl.ds(pl.multiple_of(head * dims, dims), dims), :],
            out.at[:, pl.ds(rows, dims), :],
            sems.at[1],
        ),
    ]
    for copy in copies:
        copy.start()
    for copy in copies:
        copy.wait()


def payload_of(cache_latent, cache_rope, heads):
    slots, positions, wide = cache_latent.shape
    rows = (positions + cache_rope.shape[1]) // heads
    return pl.pallas_call(
        payload_kernel,
        out_shape=jax.ShapeDtypeStruct((slots, rows, wide), cache_latent.dtype),
        in_specs=[pl.BlockSpec(memory_space=pl.ANY)] * 2,
        out_specs=pl.BlockSpec(memory_space=pltpu.MemorySpace.VMEM),
        scratch_shapes=[pltpu.SemaphoreType.DMA((2,))],
        compiler_params=pltpu.CompilerParams(vmem_limit_bytes=4 * 2**20),
        name="payload",
    )(in_hbm(cache_latent), in_hbm(cache_rope))


def choose_kernel(cut, column, table, a_ref, b_ref, out_ref):
    if cut is None:
        out_ref[0] = a_ref[0]
        out_ref[1] = b_ref[0]
    else:
        first = table[SLOT, column] < cut

        @pl.when(first)
        def _():
            out_ref[0] = a_ref[0]

        @pl.when(jnp.logical_not(first))
        def _():
            out_ref[0] = b_ref[0]


def choose(table, a, b, columns, cut=None):
    _, rows, wide = a.shape
    if cut is None:
        index_a = lambda i, table: (table[SLOT, columns[0]], 0, 0)
        index_b = lambda i, table: (table[SLOT, columns[1]], 0, 0)
    else:
        index_a = lambda i, table: (jnp.minimum(table[SLOT, columns[0]], cut - 1), 0, 0)
        index_b = lambda i, table: (jnp.maximum(table[SLOT, columns[0]] - cut, 0), 0, 0)
    return pl.pallas_call(
        functools.partial(choose_kernel, cut, columns[0]),
        out_shape=jax.ShapeDtypeStruct((len(columns), rows, wide), a.dtype),
        grid_spec=pltpu.PrefetchScalarGridSpec(
            num_scalar_prefetch=1,
            grid=(1,),
            in_specs=[pl.BlockSpec((1, rows, wide), index_a), pl.BlockSpec((1, rows, wide), index_b)],
            out_specs=pl.BlockSpec((len(columns), rows, wide), lambda i, *_: (0, 0, 0)),
        ),
        compiler_params=pltpu.CompilerParams(vmem_limit_bytes=4 * 2**20),
        name="choose",
    )(table, a, b)


def slots_kernel(plan, own, heads, bundles, carried, final, scale, block, table, info, *refs):
    count = len(plan)
    refs = list(refs)
    q_ref, qr_ref = refs.pop(0), refs.pop(0)
    if own:
        full_lat, full_rope = refs.pop(0), refs.pop(0)
    shipped = count - own
    parts = [[refs.pop(0) for _ in range(heads)] for _ in range(shipped)]
    earlier = [refs.pop(0) for _ in carried]
    w_hbm, out_ref, lat, rope, mixed, w_ref, sem = refs[:7]
    i = pl.program_id(0)
    total_rows = q_ref.shape[1]
    w_copy = pltpu.make_async_copy(w_hbm, w_ref, sem)

    @pl.when(i == 0)
    def _():
        w_copy.start()

    rows = lat.shape[0] // heads
    dims = rope.shape[0] // heads

    for j in range(count):

        @pl.when(i == j)
        def _():
            if own and j == 0:
                lat[...] = full_lat[0]
                rope[...] = full_rope[0]
                return
            for m in range(heads):
                part = parts[j - own][m]
                to = jnp.bitwise_xor(table[PLACE, 1], m)
                lat[pl.ds(pl.multiple_of(to * rows, rows), rows), :] = part[0, :rows, :]
                rope[pl.ds(pl.multiple_of(to * dims, dims), dims), :] = part[0, rows:, :]

    column = jnp.int32(plan[0]) + i
    length = info[table[OWNER, column], 0, bundles + table[SLOT, column]]
    live = lax.broadcasted_iota(jnp.int32, (block, lat.shape[0]), 1) < length
    for r in range(total_rows // block):
        at = slice(r * block, (r + 1) * block)
        s = lax.dot_general(
            q_ref[0, at, :], lat[...], (((1,), (1,)), ((), ())), preferred_element_type=jnp.float32
        )
        s = s + jnp.dot(qr_ref[0, at, :], rope[...], preferred_element_type=jnp.float32)
        s = jnp.where(live, s * scale, -1e30)
        w = jnp.exp(s - jnp.max(s, axis=1, keepdims=True))
        w = w * (1.0 / jnp.sum(w, axis=1, keepdims=True))
        o = jnp.dot(w.astype(jnp.bfloat16), lat[...], preferred_element_type=jnp.float32)
        for c in range(mixed.shape[0]):
            mixed[c, pl.ds(i * total_rows + r * block, block), :] = o[:, c * 128 : (c + 1) * 128]

    @pl.when(i == count - 1)
    def _():
        w_copy.wait()
        local_heads, _, value_width = w_ref.shape
        n = mixed.shape[1] // local_heads
        into, at = out_ref, 0
        if final:
            into = refs[7]
            for piece in earlier:
                into[pl.ds(at, piece.shape[0]), :] = piece[...]
                at += piece.shape[0]
        for h in range(local_heads):
            x = jnp.concatenate(
                [mixed[c, pl.ds(h, n, stride=local_heads), :] for c in range(mixed.shape[0])], axis=1
            ).astype(jnp.bfloat16)
            v = jnp.dot(x, w_ref[h], preferred_element_type=jnp.float32)
            into[pl.ds(at, n), h * value_width : (h + 1) * value_width] = v
        if final:
            out_ref[...] = into[...].astype(out_ref.dtype)


def attend_slots(plan, table, info, q, qr, full, parts, heads, bundles, w_uv, earlier=None):
    own = 1 if full is not None else 0
    final = earlier is not None
    earlier = list(earlier or ())
    count = len(plan)
    _, q_rows, wide = q.shape
    part_rows = parts[0][0][0].shape[1]
    dims = qr.shape[2] // heads
    rows = part_rows - dims
    block = math.gcd(q_rows, 128)
    local_heads, _, value_width = w_uv.shape
    carried = [e.shape[0] for e in earlier]

    def bundle(i, table, info):
        return table[BUNDLE, plan[0] + i], 0, 0

    in_specs = [
        pl.BlockSpec((1, q_rows, wide), bundle),
        pl.BlockSpec((1, q_rows, qr.shape[2]), bundle),
    ]
    args = [in_hbm(q), in_hbm(qr)]
    if own:
        here = lambda i, table, info: (table[SLOT, plan[0]], 0, 0)
        in_specs += [
            pl.BlockSpec((1, rows * heads, wide), here),
            pl.BlockSpec((1, dims * heads, wide), here),
        ]
        args += [in_hbm(x) for x in full]
    for slot in parts:
        for array, index in slot:
            in_specs.append(
                pl.BlockSpec((1, part_rows, wide), lambda i, *_, index=index: (index, 0, 0))
            )
            args.append(array)
    for piece in earlier:
        in_specs.append(pl.BlockSpec(piece.shape, lambda i, *_: (0, 0)))
        args.append(piece)
    in_specs.append(pl.BlockSpec(memory_space=pl.ANY))
    args.append(in_hbm(w_uv))
    done = sum(carried) + count * q_rows // local_heads
    out_shape = (done, local_heads * value_width)
    scratch = [
        pltpu.VMEM((rows * heads, wide), jnp.bfloat16),
        pltpu.VMEM((dims * heads, wide), jnp.bfloat16),
        pltpu.VMEM((wide // 128, count * q_rows, 128), jnp.float32),
        pltpu.VMEM(w_uv.shape, w_uv.dtype),
        pltpu.SemaphoreType.DMA,
    ]
    if final:
        scratch.append(pltpu.VMEM(out_shape, jnp.float32))
    return pl.pallas_call(
        functools.partial(
            slots_kernel, plan, own, heads, bundles, carried, final,
            1.0 / math.sqrt(VD + ROPE), block,
        ),
        out_shape=jax.ShapeDtypeStruct(out_shape, jnp.bfloat16 if final else jnp.float32),
        grid_spec=pltpu.PrefetchScalarGridSpec(
            num_scalar_prefetch=2,
            grid=(count,),
            in_specs=in_specs,
            out_specs=pl.BlockSpec(out_shape, lambda i, *_: (0, 0)),
            scratch_shapes=scratch,
        ),
        compiler_params=pltpu.CompilerParams(vmem_limit_bytes=24 * 2**20),
        name="attend_slots",
    )(table, info, *args)


def add_in(table, per_head, columns, own, got, before, after):
    part = own[...]
    for g in got:
        part = part + g[...].astype(jnp.float32)
    for y in range(per_head):
        rank = table[PLACE, 1] * per_head + y
        hit = table[OWNER, columns[0]] == rank
        for c in columns[1:]:
            hit = hit | (table[OWNER, c] == rank)
        now = jnp.where(hit, part, 0.0)
        after[y] = now if before is None else before[y] + now


def settle_kernel(heads, per_head, columns, prev_columns, has_total, table, both, *refs):
    refs = list(refs)
    if prev_columns:
        prev_own, prev_got = refs.pop(0), [refs.pop(0) for _ in range(heads - 1)]
        before = refs.pop(0) if has_total else None
    block = both.shape[0] // len(columns)
    sends = len(refs) - 1 - bool(prev_columns)
    own = refs[sends]
    head = table[PLACE, 1]
    if len(columns) == 1:
        own[...] = both[...]
        refs[0][...] = both[...].astype(jnp.bfloat16)
    else:
        for m in range(heads):
            first = table[TARGET, columns[0]] == jnp.bitwise_xor(head, m)
            piece = jnp.where(first, both[:block], both[block:])
            if m == 0:
                own[...] = piece
            else:
                refs[m - 1][...] = piece.astype(jnp.bfloat16)
    if prev_columns:
        add_in(table, per_head, prev_columns, prev_own, prev_got, before, refs[sends + 1])


def settle_step(table, heads, per_head, columns, both, previous):
    n = both.shape[0] // len(columns)
    wide = both.shape[1]
    vmem = pl.BlockSpec(memory_space=pltpu.MemorySpace.VMEM)
    args, prev_columns, has_total = [both], None, False
    if previous is not None:
        prev_columns, prev_own, prev_got, total = previous
        has_total = total is not None
        args += [prev_own, *prev_got] + ([total] if has_total else [])
    sends = 1 if len(columns) == 1 else heads - 1
    out = [jax.ShapeDtypeStruct((n, wide), jnp.bfloat16)] * sends
    out.append(jax.ShapeDtypeStruct((n, wide), jnp.float32))
    if previous is not None:
        out.append(jax.ShapeDtypeStruct((per_head, n, wide), jnp.float32))
    outs = pl.pallas_call(
        functools.partial(settle_kernel, heads, per_head, columns, prev_columns, has_total),
        out_shape=out,
        in_specs=[pl.BlockSpec(memory_space=pltpu.MemorySpace.SMEM)] + [vmem] * len(args),
        out_specs=[vmem] * len(out),
        compiler_params=pltpu.CompilerParams(vmem_limit_bytes=4 * 2**20),
        name="settle",
    )(table, *args)
    to_send = list(outs[:sends]) * (1 if sends > 1 else heads - 1)
    return to_send, outs[sends], outs[sends + 1] if previous is not None else None


def finish_kernel(heads, per_head, steps, roll, table, info, seen, before, *refs):
    out, total = refs[heads * len(steps) :]
    for i, columns in enumerate(steps):
        own, *got = refs[heads * i : heads * (i + 1)]
        add_in(table, per_head, columns, own, got, total if i else before, total)
    n = total.shape[1]
    slots = n // roll
    to = lax.broadcasted_iota(jnp.int32, (n, n), 0)
    source = lax.broadcasted_iota(jnp.int32, (n, n), 1)
    for y in range(per_head):
        rank = table[PLACE, 1] * per_head + y
        wanted = to
        for b in range(slots):
            place = jnp.int32(0)
            for c in range(slots):
                place = jnp.where(seen[rank, c] == info[rank, 0, b], c, place)
            inside = (to >= b * roll) & (to < (b + 1) * roll)
            wanted = jnp.where(inside, to + (place - b) * roll, wanted)
        pick = jnp.where(wanted == source, 1.0, 0.0).astype(jnp.bfloat16)
        moved = jnp.dot(pick, total[y].astype(jnp.bfloat16), preferred_element_type=jnp.float32)
        out[pl.ds(y * n, n), :] = moved.astype(out.dtype)


def finish(table, info, seen, heads, per_head, roll, total, states):
    _, n, wide = total.shape
    steps = [state[0] for state in states]
    args = [x for _, own, got in states for x in (own, *got)]
    vmem = pl.BlockSpec(memory_space=pltpu.MemorySpace.VMEM)
    smem = pl.BlockSpec(memory_space=pltpu.MemorySpace.SMEM)
    return pl.pallas_call(
        functools.partial(finish_kernel, heads, per_head, steps, roll),
        out_shape=jax.ShapeDtypeStruct((per_head * n, wide), jnp.bfloat16),
        in_specs=[smem] * 3 + [vmem] * (1 + len(args)),
        out_specs=vmem,
        scratch_shapes=[pltpu.VMEM((per_head, n, wide), jnp.float32)],
        compiler_params=pltpu.CompilerParams(vmem_limit_bytes=6 * 2**20),
        name="finish",
    )(table, info, seen, total, *args)


def local_ring(
    q_latent, q_rope, cache_latent, cache_rope, lengths, loads, owner_rank, owner_pick, w_uv, w_out
):
    ranks = lax.axis_size("dp")
    heads = lax.axis_size("head")
    bundles = owner_rank.shape[0]
    local_heads = w_uv.shape[0]
    roll_count = q_latent.shape[0] // bundles
    per_head = ranks // heads
    last = ranks // 2
    order, where, offsets, seen = ring_tables(ranks)
    seen = jnp.asarray(seen, jnp.int32)
    ahead = [(order[i], order[(i + 1) % ranks]) for i in range(ranks)]
    behind = [(b, a) for a, b in ahead]

    def move(x, pairs, axis="dp"):
        return lax.ppermute(x, axis, pairs)

    payload = payload_of(cache_latent, cache_rope, heads)
    slots = payload.shape[0]
    fore, back = move(payload, ahead), move(payload, behind)
    facts = jnp.concatenate([owner_rank, lengths])
    width = 32
    facts = jnp.pad(facts, (0, width - facts.shape[0]))
    info = lax.all_to_all(
        jnp.broadcast_to(facts[None], (ranks, width)), "dp", split_axis=0, concat_axis=0, tiled=True
    )
    info = jnp.maximum(info, 0)[:, None]
    table = plan_of(seen, owner_rank, owner_pick, loads, per_head)
    q = q_latent.reshape(bundles, roll_count * local_heads, -1)
    qr = q_rope.reshape(bundles, roll_count * local_heads, -1)

    def share(chosen):
        found = {0: chosen}
        bit = heads // 2
        while bit:
            pairs = [(i, i ^ bit) for i in range(heads)]
            for m in list(found):
                found[m ^ bit] = move(found[m], pairs, "head")
            bit //= 2
        return [found[m] for m in range(heads)]

    groups = {}
    for k in range(1, last):
        if k > 1:
            fore = move(fore, ahead)
            back = move(back, behind)
        chosen = choose(table, fore, back, [2 * k - 1, 2 * k])
        parts = share(chosen)
        groups[2 * k - 1] = [(p, 0) for p in parts]
        groups[2 * k] = [(p, 1) for p in parts]
    cut = slots // 2
    left = move(fore[:cut], ahead)
    right = move(back[cut:], behind)
    chosen = choose(table, left, right, [2 * last - 1], cut)
    parts = share(chosen)
    groups[2 * last - 1] = [(p, 0) for p in parts]

    def attend(plan, full=None, earlier=None):
        return attend_slots(
            plan, table, info, q, qr, full, [groups[c] for c in plan[(full is not None) :]],
            heads, bundles, w_uv, earlier,
        )

    chunks = []
    for tag, plans in chunk_plans(ranks).items():
        earlier = []
        for n, plan in enumerate(plans):
            full = (cache_latent, cache_rope) if plan[0] == 0 else None
            carried = earlier if n == len(plans) - 1 else None
            earlier.append(attend(plan, full, carried))
        chunks.append((tag, earlier[-1]))
    half = chunks[0][1].shape[1] // 2

    def project(pieces):
        return jnp.dot(jnp.concatenate(pieces), w_out, preferred_element_type=jnp.float32)

    def target(p, column):
        return order[(where[p] + offsets[column]) % ranks] // per_head

    def settle(columns, both, previous):
        to_send, own, total = settle_step(table, heads, per_head, columns, both, previous)
        got = []
        for m in range(1, heads):
            pairs = []
            for p in range(ranks):
                for t in sorted({target(p, c) for c in columns}):
                    pairs.append((p * heads + (t ^ m), p * heads + t))
            got.append(move(to_send[m - 1], pairs, ("dp", "head")))
        return columns, own, got, total

    arrived = {}
    for tag, values in chunks:
        fore = back = values
        for k in range(1, last):
            fore = move(fore, ahead)
            back = move(back, behind)
            arrived[tag, k] = fore, back
        fore, back = fore[:, :half], back[:, half:]
        left = move(fore, ahead)
        right = move(back, behind)
        arrived[tag, last] = (jnp.concatenate([left, right], axis=1),)
    state = settle([0], project([values for _, values in chunks]), None)
    for k in range(1, last):
        pieces = [arrived[tag, k][side] for side in (0, 1) for tag, _ in chunks]
        state = settle([2 * k - 1, 2 * k], project(pieces), state)
    ends = project([arrived[tag, last][0] for tag, _ in chunks])
    *before, total = state
    *final, _ = settle([2 * last - 1], ends, None)
    return finish(table, info, seen, heads, per_head, roll_count, total, [before, final])


def local(*args):
    ranks, heads = lax.axis_size("dp"), lax.axis_size("head")
    bundles = args[6].shape[0]
    if ranks == bundles and ring_fits(ranks, heads):
        return local_ring(*args)
    return local_general(*args)


def solution(mesh):
    in_specs = (
        P("dp", "head"),
        P("dp", "head"),
        P("dp", None, None),
        P("dp", None, None),
        P("dp"),
        P(),
        P("dp"),
        P("dp"),
        P("head", None, None),
        P("head", "dp"),
    )
    out_specs = P("head", "dp")
    return jax.shard_map(local, mesh=mesh, in_specs=in_specs, out_specs=out_specs, check_vma=False)
```

```python
import functools
import math

import jax
import jax.numpy as jnp
from jax import lax
from jax.experimental import pallas as pl
from jax.experimental.pallas import tpu as pltpu
from jax.sharding import PartitionSpec as P


ROPE = 64
VD = 128


def ring_order(size):
    fast = 1 << (max(size.bit_length() - 1, 0) // 2)
    slow = size // fast
    if fast == 1 or slow % 2:
        return list(range(size))
    cells = [(z, 0) for z in range(slow)]
    for step, z in enumerate(range(slow - 1, -1, -1)):
        ys = range(1, fast) if step % 2 == 0 else range(fast - 1, 0, -1)
        cells += [(z, y) for y in ys]
    return [z * fast + y for z, y in cells]


def ring_fits(ranks, heads):
    if ranks % 2 or ranks < 4 or ranks % heads or heads & (heads - 1):
        return False
    order, per_head = ring_order(ranks), ranks // heads
    return all(
        order[p - k] // per_head != order[(p + k) % ranks] // per_head
        for p in range(ranks)
        for k in range(1, ranks // 2)
    )


def slot_for(info, loads, width, bundles, requester, owner):
    pick = jnp.int32(0)
    for j in range(bundles):
        hit = info[requester * width + j] == owner
        pick = jnp.where(hit, info[requester * width + bundles + j], pick)
    return lax.rem(pick, loads[owner])


def pack_kernel(info, loads, place, lat_ref, rope_ref, out_ref):
    rows = lat_ref.shape[1]
    out_ref[0, :rows, :] = lat_ref[0]
    out_ref[0, rows:, :] = rope_ref[0]


def pack(info, loads, place, cache_latent, cache_rope, ranks, heads, width, bundles):
    rows = cache_latent.shape[1] // heads
    dims = cache_rope.shape[1] // heads
    wide = cache_latent.shape[2]

    def source(i, info, loads, place):
        return slot_for(info, loads, width, bundles, i, place[0]), place[1], 0

    return pl.pallas_call(
        pack_kernel,
        out_shape=jax.ShapeDtypeStruct((ranks, rows + dims, wide), cache_latent.dtype),
        grid_spec=pltpu.PrefetchScalarGridSpec(
            num_scalar_prefetch=3,
            grid=(ranks,),
            in_specs=[pl.BlockSpec((1, rows, wide), source), pl.BlockSpec((1, dims, wide), source)],
            out_specs=pl.BlockSpec((1, rows + dims, wide), lambda i, *_: (i, 0, 0)),
        ),
        name="pack",
    )(info, loads, place, cache_latent, cache_rope)


def attend_kernel(
    heads, width, bundles, scale, block, info, loads, place, q_ref, qr_ref, *refs
):
    parts = refs[:heads]
    w_ref, out_ref, lat, rope, mixed = refs[heads:]
    b = pl.program_id(0)
    rows = lat.shape[0] // heads
    dims = rope.shape[0] // heads
    for m in range(heads):
        at = jnp.bitwise_xor(place[1], m)
        lat[pl.ds(pl.multiple_of(at * rows, rows), rows), :] = parts[m][0, :rows, :]
        rope[pl.ds(pl.multiple_of(at * dims, dims), dims), :] = parts[m][0, rows:, :]
    base = place[0] * width
    owner = info[base + b]
    slot = lax.rem(info[base + bundles + b], loads[owner])
    length = info[owner * width + 2 * bundles + slot]
    total_rows = q_ref.shape[1]
    live = lax.broadcasted_iota(jnp.int32, (block, lat.shape[0]), 1) < length
    for i in range(total_rows // block):
        at = slice(i * block, (i + 1) * block)
        s = lax.dot_general(
            q_ref[0, at, :], lat[...], (((1,), (1,)), ((), ())), preferred_element_type=jnp.float32
        )
        s = s + jnp.dot(qr_ref[0, at, :], rope[...], preferred_element_type=jnp.float32)
        s = jnp.where(live, s * scale, -1e30)
        w = jnp.exp(s - jnp.max(s, axis=1, keepdims=True))
        w = w * (1.0 / jnp.sum(w, axis=1, keepdims=True))
        o = jnp.dot(w.astype(jnp.bfloat16), lat[...], preferred_element_type=jnp.float32)
        for c in range(mixed.shape[0]):
            piece = o[:, c * 128 : (c + 1) * 128]
            mixed[c, pl.ds(b * total_rows + i * block, block), :] = piece

    @pl.when(b == pl.num_programs(0) - 1)
    def _():
        local_heads, _, value_width = w_ref.shape
        n = mixed.shape[1] // local_heads
        for h in range(local_heads):
            x = jnp.concatenate(
                [mixed[c, pl.ds(h, n, stride=local_heads), :] for c in range(mixed.shape[0])], axis=1
            ).astype(jnp.bfloat16)
            v = jnp.dot(x, w_ref[h], preferred_element_type=jnp.float32)
            out_ref[:, h * value_width : (h + 1) * value_width] = v.astype(jnp.bfloat16)


def attend(info, loads, place, q, qr, parts, w_uv, width, bundles):
    heads = len(parts)
    _, q_rows, wide = q.shape
    _, part_rows, _ = parts[0].shape
    local_heads, _, value_width = w_uv.shape
    dims = qr.shape[2] // heads
    rows = part_rows - dims
    row_count = bundles * q_rows // local_heads

    def theirs(b, info, loads, place):
        return info[place[0] * width + b], 0, 0

    block = math.gcd(q_rows, 128)
    return pl.pallas_call(
        functools.partial(
            attend_kernel, heads, width, bundles, 1.0 / math.sqrt(VD + ROPE), block
        ),
        out_shape=jax.ShapeDtypeStruct((row_count, local_heads * value_width), jnp.bfloat16),
        grid_spec=pltpu.PrefetchScalarGridSpec(
            num_scalar_prefetch=3,
            grid=(bundles,),
            in_specs=[
                pl.BlockSpec((1, q_rows, wide), lambda b, *_: (b, 0, 0)),
                pl.BlockSpec((1, q_rows, qr.shape[2]), lambda b, *_: (b, 0, 0)),
            ]
            + [pl.BlockSpec((1, part_rows, wide), theirs)] * heads
            + [pl.BlockSpec(w_uv.shape, lambda b, *_: (0, 0, 0))],
            out_specs=pl.BlockSpec((row_count, local_heads * value_width), lambda b, *_: (0, 0)),
            scratch_shapes=[
                pltpu.VMEM((rows * heads, wide), jnp.bfloat16),
                pltpu.VMEM((dims * heads, wide), jnp.bfloat16),
                pltpu.VMEM((wide // 128, bundles * q_rows, 128), jnp.float32),
            ],
        ),
        name="attend",
    )(info, loads, place, q, qr, *parts, w_uv)


def local_general(
    q_latent, q_rope, cache_latent, cache_rope, lengths, loads, owner_rank, owner_pick, w_uv, w_out
):
    ranks = lax.axis_size("dp")
    heads = lax.axis_size("head")
    me = lax.axis_index("dp")
    head = lax.axis_index("head")
    bundles = owner_rank.shape[0]
    roll_count = q_latent.shape[0] // bundles
    local_heads = w_uv.shape[0]
    place = jnp.stack([me, head]).astype(jnp.int32)

    facts = jnp.concatenate([owner_rank, owner_pick, lengths])
    width = 32
    facts = jnp.pad(facts, (0, width - facts.shape[0]))
    info = lax.all_to_all(
        jnp.broadcast_to(facts[None], (ranks, width)), "dp", split_axis=0, concat_axis=0, tiled=True
    ).reshape(-1)
    q = q_latent.reshape(bundles, roll_count * local_heads, -1)
    qr = q_rope.reshape(bundles, roll_count * local_heads, -1)

    packed = pack(info, loads, place, cache_latent, cache_rope, ranks, heads, width, bundles)
    mine = lax.all_to_all(packed, "dp", split_axis=0, concat_axis=0, tiled=True)
    parts = [mine]
    bit = heads // 2
    found = {0: mine}
    while bit:
        pairs = [(i, i ^ bit) for i in range(heads)]
        for m in list(found):
            found[m ^ bit] = lax.ppermute(found[m], "head", pairs)
        bit //= 2
    parts = [found[m] for m in range(heads)]
    values = attend(info, loads, place, q, qr, parts, w_uv, width, bundles)

    order = ring_order(ranks)
    ahead = [(order[i], order[(i + 1) % ranks]) for i in range(ranks)]
    behind = [(b, a) for a, b in ahead]
    half = values.shape[1] // 2

    def project(x):
        return jnp.dot(x, w_out, preferred_element_type=jnp.float32).astype(jnp.bfloat16)

    partial = {0: project(values)}
    fore = back = values
    for step in range(1, (ranks + 1) // 2):
        fore = lax.ppermute(fore, "dp", ahead)
        back = lax.ppermute(back, "dp", behind)
        both = project(jnp.concatenate([fore, back], axis=0))
        partial[-step] = both[: values.shape[0]]
        partial[step] = both[values.shape[0] :]
    if ranks % 2 == 0:
        left = lax.ppermute(fore[:, :half], "dp", ahead)
        right = lax.ppermute(back[:, half:], "dp", behind)
        partial[ranks // 2] = project(jnp.concatenate([left, right], axis=1))
    stacked = jnp.stack([partial[k if 2 * k <= ranks else k - ranks] for k in range(ranks)])
    position = [0] * ranks
    for i, r in enumerate(order):
        position[r] = i
    position = jnp.asarray(position, jnp.int32)
    by_rank = stacked[(position - position[me]) % ranks]
    shares = by_rank.reshape(heads, -1, w_out.shape[1])
    got = lax.all_to_all(shares, "head", split_axis=0, concat_axis=0, tiled=True)
    return jnp.sum(got.astype(jnp.float32), axis=0).astype(jnp.bfloat16)


def in_hbm(x):
    return pltpu.with_memory_space_constraint(x, pltpu.MemorySpace.HBM)


def ring_tables(ranks):
    order = ring_order(ranks)
    where = [order.index(r) for r in range(ranks)]
    offsets = [0]
    for k in range(1, ranks // 2):
        offsets += [-k, k]
    offsets.append(ranks // 2)
    seen = [[order[(where[r] + o) % ranks] for o in offsets] for r in range(ranks)]
    return order, where, offsets, seen


BUNDLE, SLOT, TARGET, OWNER, PLACE, PLAN_ROWS = 0, 1, 2, 3, 4, 8


def chunk_plans(ranks):
    middle = ranks // 2
    return {
        "p": [list(range(middle - 1)), [middle - 1]],
        "s": [list(range(middle, ranks - 1)), [ranks - 1]],
    }


def plan_kernel(per_head, seen, owner_rank, owner_pick, loads, table):
    ranks = seen.shape[1]
    me, head = lax.axis_index("dp"), lax.axis_index("head")
    table[PLACE, 0] = me
    table[PLACE, 1] = head
    for c in range(ranks):
        owner = seen[me, c]
        bundle, pick = jnp.int32(0), jnp.int32(0)
        for b in range(owner_rank.shape[0]):
            hit = owner_rank[b] == owner
            bundle = jnp.where(hit, b, bundle)
            pick = jnp.where(hit, owner_pick[b], pick)
        table[BUNDLE, c] = bundle
        table[SLOT, c] = lax.rem(pick, loads[owner])
        table[TARGET, c] = lax.div(owner, per_head)
        table[OWNER, c] = owner


def plan_of(seen, owner_rank, owner_pick, loads, per_head):
    smem = pl.BlockSpec(memory_space=pltpu.MemorySpace.SMEM)
    return pl.pallas_call(
        functools.partial(plan_kernel, per_head),
        out_shape=jax.ShapeDtypeStruct((PLAN_ROWS, seen.shape[1]), jnp.int32),
        in_specs=[smem] * 4,
        out_specs=smem,
        name="plan",
    )(seen, owner_rank, owner_pick, loads)


def payload_kernel(lat, rope, out, sems):
    head = lax.axis_index("head")
    dims = rope.shape[1] * (out.shape[1]) // (rope.shape[1] + lat.shape[1])
    rows = out.shape[1] - dims
    copies = [
        pltpu.make_async_copy(
            lat.at[:, pl.ds(pl.multiple_of(head * rows, rows), rows), :],
            out.at[:, pl.ds(0, rows), :],
            sems.at[0],
        ),
        pltpu.make_async_copy(
            rope.at[:, pl.ds(pl.multiple_of(head * dims, dims), dims), :],
            out.at[:, pl.ds(rows, dims), :],
            sems.at[1],
        ),
    ]
    for copy in copies:
        copy.start()
    for copy in copies:
        copy.wait()


def payload_of(cache_latent, cache_rope, heads):
    slots, positions, wide = cache_latent.shape
    rows = (positions + cache_rope.shape[1]) // heads
    return pl.pallas_call(
        payload_kernel,
        out_shape=jax.ShapeDtypeStruct((slots, rows, wide), cache_latent.dtype),
        in_specs=[pl.BlockSpec(memory_space=pl.ANY)] * 2,
        out_specs=pl.BlockSpec(memory_space=pltpu.MemorySpace.VMEM),
        scratch_shapes=[pltpu.SemaphoreType.DMA((2,))],
        compiler_params=pltpu.CompilerParams(vmem_limit_bytes=4 * 2**20),
        name="payload",
    )(in_hbm(cache_latent), in_hbm(cache_rope))


def choose_kernel(cut, column, table, a_ref, b_ref, out_ref):
    if cut is None:
        out_ref[0] = a_ref[0]
        out_ref[1] = b_ref[0]
    else:
        first = table[SLOT, column] < cut

        @pl.when(first)
        def _():
            out_ref[0] = a_ref[0]

        @pl.when(jnp.logical_not(first))
        def _():
            out_ref[0] = b_ref[0]


def choose(table, a, b, columns, cut=None):
    _, rows, wide = a.shape
    if cut is None:
        index_a = lambda i, table: (table[SLOT, columns[0]], 0, 0)
        index_b = lambda i, table: (table[SLOT, columns[1]], 0, 0)
    else:
        index_a = lambda i, table: (jnp.minimum(table[SLOT, columns[0]], cut - 1), 0, 0)
        index_b = lambda i, table: (jnp.maximum(table[SLOT, columns[0]] - cut, 0), 0, 0)
    return pl.pallas_call(
        functools.partial(choose_kernel, cut, columns[0]),
        out_shape=jax.ShapeDtypeStruct((len(columns), rows, wide), a.dtype),
        grid_spec=pltpu.PrefetchScalarGridSpec(
            num_scalar_prefetch=1,
            grid=(1,),
            in_specs=[pl.BlockSpec((1, rows, wide), index_a), pl.BlockSpec((1, rows, wide), index_b)],
            out_specs=pl.BlockSpec((len(columns), rows, wide), lambda i, *_: (0, 0, 0)),
        ),
        compiler_params=pltpu.CompilerParams(vmem_limit_bytes=4 * 2**20),
        name="choose",
    )(table, a, b)


def slots_kernel(plan, own, indices, bundles, final, scale, table, info, *refs):
    count, heads = len(plan), len(indices[0])
    refs = list(refs)
    q_ref, qr_ref, w_ref = refs.pop(0), refs.pop(0), refs.pop(0)
    if own:
        full_lat, full_rope = refs.pop(0), refs.pop(0)
    parts = [[(refs.pop(0), index) for index in slot] for slot in indices]
    lat, rope, mixed = refs.pop(-3), refs.pop(-2), refs.pop(-1)
    if own:
        own_lat, own_rope, sems = refs.pop(-3), refs.pop(-2), refs.pop(-1)
        slot = table[SLOT, plan[0]]
        copies = [
            pltpu.make_async_copy(full_lat.at[slot], own_lat, sems.at[0]),
            pltpu.make_async_copy(full_rope.at[slot], own_rope, sems.at[1]),
        ]
        for copy in copies:
            copy.start()
    into = refs.pop(-1) if final else None
    out_ref = refs.pop(-1)
    earlier = refs
    total_rows = q_ref.shape[1]
    rows = lat.shape[0] // heads
    dims = rope.shape[0] // heads

    def bundle(i, _):
        j = lax.rem(i + own, count)
        for at in range(count):

            @pl.when(j == at)
            def _():
                if own and at == 0:
                    for copy in copies:
                        copy.wait()
                    lat[...] = own_lat[...]
                    rope[...] = own_rope[...]
                    return
                for m, (part, index) in enumerate(parts[at - own]):
                    to = jnp.bitwise_xor(table[PLACE, 1], m)
                    lat[pl.ds(pl.multiple_of(to * rows, rows), rows), :] = part[index, :rows, :]
                    rope[pl.ds(pl.multiple_of(to * dims, dims), dims), :] = part[index, rows:, :]

        column = plan[0] + j
        length = info[table[OWNER, column], 0, bundles + table[SLOT, column]]
        b = table[BUNDLE, column]
        past = lax.broadcasted_iota(jnp.int32, (1, lat.shape[0]), 1) >= length
        s = lax.dot_general(
            q_ref[b], lat[...], (((1,), (1,)), ((), ())), preferred_element_type=jnp.float32
        )
        s = s + jnp.dot(qr_ref[b], rope[...], preferred_element_type=jnp.float32)
        s = s + jnp.where(past, -1e30, 0.0)
        w = jnp.exp((s - jnp.max(s, axis=1, keepdims=True)) * scale)
        w = w * (1.0 / jnp.sum(w, axis=1, keepdims=True))
        o = jnp.dot(w.astype(jnp.bfloat16), lat[...], preferred_element_type=jnp.float32)
        start = pl.multiple_of(j * total_rows, total_rows)
        for c in range(mixed.shape[0]):
            mixed[c, pl.ds(start, total_rows), :] = o[:, c * 128 : (c + 1) * 128]
        return 0

    lax.fori_loop(0, count, bundle, 0)
    local_heads, _, value_width = w_ref.shape
    n = mixed.shape[1] // local_heads
    at = 0
    if final:
        for piece in earlier:
            into[pl.ds(at, piece.shape[0]), :] = piece[...]
            at += piece.shape[0]
    else:
        into = out_ref
    for h in range(local_heads):
        x = jnp.concatenate(
            [mixed[c, pl.ds(h, n, stride=local_heads), :] for c in range(mixed.shape[0])], axis=1
        ).astype(jnp.bfloat16)
        v = jnp.dot(x, w_ref[h], preferred_element_type=jnp.float32)
        into[pl.ds(at, n), h * value_width : (h + 1) * value_width] = v
    if final:
        out_ref[...] = into[...].astype(out_ref.dtype)


def attend_slots(plan, table, info, q, qr, full, parts, bundles, w_uv, earlier=None):
    own = 1 if full is not None else 0
    final = earlier is not None
    earlier = list(earlier or ())
    count, heads = len(plan), len(parts[0])
    _, q_rows, wide = q.shape
    dims = qr.shape[2]
    positions = (parts[0][0][0].shape[1] - dims // heads) * heads
    local_heads, _, value_width = w_uv.shape
    vmem = pl.BlockSpec(memory_space=pltpu.MemorySpace.VMEM)
    smem = pl.BlockSpec(memory_space=pltpu.MemorySpace.SMEM)
    args, in_specs = [q, qr, w_uv], [vmem] * 3
    if own:
        args += [in_hbm(x) for x in full]
        in_specs += [pl.BlockSpec(memory_space=pl.ANY)] * 2
    args += [array for slot in parts for array, _ in slot] + earlier
    in_specs += [vmem] * (len(args) - len(in_specs))
    done = sum(e.shape[0] for e in earlier) + count * q_rows // local_heads
    out_shape = (done, local_heads * value_width)
    caches = [pltpu.VMEM((positions, wide), jnp.bfloat16), pltpu.VMEM((dims, wide), jnp.bfloat16)]
    scratch = [pltpu.VMEM(out_shape, jnp.float32)] if final else []
    if own:
        scratch += caches + [pltpu.SemaphoreType.DMA((2,))]
    scratch += caches + [pltpu.VMEM((wide // 128, count * q_rows, 128), jnp.float32)]
    return pl.pallas_call(
        functools.partial(
            slots_kernel, plan, own, [[index for _, index in slot] for slot in parts], bundles,
            final, 1.0 / math.sqrt(VD + ROPE),
        ),
        out_shape=jax.ShapeDtypeStruct(out_shape, jnp.bfloat16 if final else jnp.float32),
        in_specs=[smem] * 2 + in_specs,
        out_specs=vmem,
        scratch_shapes=scratch,
        compiler_params=pltpu.CompilerParams(vmem_limit_bytes=14 * 2**20),
        name="attend_slots",
    )(table, info, *args)


def add_in(table, per_head, columns, own, got, before, after):
    part = own[...]
    for g in got:
        part = part + g[...].astype(jnp.float32)
    for y in range(per_head):
        rank = table[PLACE, 1] * per_head + y
        hit = table[OWNER, columns[0]] == rank
        for c in columns[1:]:
            hit = hit | (table[OWNER, c] == rank)
        now = jnp.where(hit, part, 0.0)
        after[y] = now if before is None else before[y] + now


def settle_kernel(heads, per_head, columns, prev_columns, has_total, table, both, *refs):
    refs = list(refs)
    if prev_columns:
        prev_own, prev_got = refs.pop(0), [refs.pop(0) for _ in range(heads - 1)]
        before = refs.pop(0) if has_total else None
    block = both.shape[0] // len(columns)
    sends = len(refs) - 1 - bool(prev_columns)
    own = refs[sends]
    head = table[PLACE, 1]
    if len(columns) == 1:
        own[...] = both[...]
        refs[0][...] = both[...].astype(jnp.bfloat16)
    else:
        for m in range(heads):
            first = table[TARGET, columns[0]] == jnp.bitwise_xor(head, m)
            piece = jnp.where(first, both[:block], both[block:])
            if m == 0:
                own[...] = piece
            else:
                refs[m - 1][...] = piece.astype(jnp.bfloat16)
    if prev_columns:
        add_in(table, per_head, prev_columns, prev_own, prev_got, before, refs[sends + 1])


def settle_step(table, heads, per_head, columns, both, previous):
    n = both.shape[0] // len(columns)
    wide = both.shape[1]
    vmem = pl.BlockSpec(memory_space=pltpu.MemorySpace.VMEM)
    args, prev_columns, has_total = [both], None, False
    if previous is not None:
        prev_columns, prev_own, prev_got, total = previous
        has_total = total is not None
        args += [prev_own, *prev_got] + ([total] if has_total else [])
    sends = 1 if len(columns) == 1 else heads - 1
    out = [jax.ShapeDtypeStruct((n, wide), jnp.bfloat16)] * sends
    out.append(jax.ShapeDtypeStruct((n, wide), jnp.float32))
    if previous is not None:
        out.append(jax.ShapeDtypeStruct((per_head, n, wide), jnp.float32))
    outs = pl.pallas_call(
        functools.partial(settle_kernel, heads, per_head, columns, prev_columns, has_total),
        out_shape=out,
        in_specs=[pl.BlockSpec(memory_space=pltpu.MemorySpace.SMEM)] + [vmem] * len(args),
        out_specs=[vmem] * len(out),
        compiler_params=pltpu.CompilerParams(vmem_limit_bytes=4 * 2**20),
        name="settle",
    )(table, *args)
    to_send = list(outs[:sends]) * (1 if sends > 1 else heads - 1)
    return to_send, outs[sends], outs[sends + 1] if previous is not None else None


def finish_kernel(heads, per_head, steps, roll, table, info, seen, before, *refs):
    out, total = refs[heads * len(steps) :]
    for i, columns in enumerate(steps):
        own, *got = refs[heads * i : heads * (i + 1)]
        add_in(table, per_head, columns, own, got, total if i else before, total)
    n = total.shape[1]
    slots = n // roll
    to = lax.broadcasted_iota(jnp.int32, (n, n), 0)
    source = lax.broadcasted_iota(jnp.int32, (n, n), 1)
    for y in range(per_head):
        rank = table[PLACE, 1] * per_head + y
        wanted = to
        for b in range(slots):
            place = jnp.int32(0)
            for c in range(slots):
                place = jnp.where(seen[rank, c] == info[rank, 0, b], c, place)
            inside = (to >= b * roll) & (to < (b + 1) * roll)
            wanted = jnp.where(inside, to + (place - b) * roll, wanted)
        pick = jnp.where(wanted == source, 1.0, 0.0).astype(jnp.bfloat16)
        moved = jnp.dot(pick, total[y].astype(jnp.bfloat16), preferred_element_type=jnp.float32)
        out[pl.ds(y * n, n), :] = moved.astype(out.dtype)


def finish(table, info, seen, heads, per_head, roll, total, states):
    _, n, wide = total.shape
    steps = [state[0] for state in states]
    args = [x for _, own, got in states for x in (own, *got)]
    vmem = pl.BlockSpec(memory_space=pltpu.MemorySpace.VMEM)
    smem = pl.BlockSpec(memory_space=pltpu.MemorySpace.SMEM)
    return pl.pallas_call(
        functools.partial(finish_kernel, heads, per_head, steps, roll),
        out_shape=jax.ShapeDtypeStruct((per_head * n, wide), jnp.bfloat16),
        in_specs=[smem] * 3 + [vmem] * (1 + len(args)),
        out_specs=vmem,
        scratch_shapes=[pltpu.VMEM((per_head, n, wide), jnp.float32)],
        compiler_params=pltpu.CompilerParams(vmem_limit_bytes=6 * 2**20),
        name="finish",
    )(table, info, seen, total, *args)


def local_ring(
    q_latent, q_rope, cache_latent, cache_rope, lengths, loads, owner_rank, owner_pick, w_uv, w_out
):
    ranks = lax.axis_size("dp")
    heads = lax.axis_size("head")
    bundles = owner_rank.shape[0]
    local_heads = w_uv.shape[0]
    roll_count = q_latent.shape[0] // bundles
    per_head = ranks // heads
    last = ranks // 2
    order, where, offsets, seen = ring_tables(ranks)
    seen = jnp.asarray(seen, jnp.int32)
    ahead = [(order[i], order[(i + 1) % ranks]) for i in range(ranks)]
    behind = [(b, a) for a, b in ahead]

    def move(x, pairs, axis="dp"):
        return lax.ppermute(x, axis, pairs)

    payload = payload_of(cache_latent, cache_rope, heads)
    slots = payload.shape[0]
    fore, back = move(payload, ahead), move(payload, behind)
    facts = jnp.concatenate([owner_rank, lengths])
    width = 32
    facts = jnp.pad(facts, (0, width - facts.shape[0]))
    info = lax.all_to_all(
        jnp.broadcast_to(facts[None], (ranks, width)), "dp", split_axis=0, concat_axis=0, tiled=True
    )
    info = jnp.maximum(info, 0)[:, None]
    table = plan_of(seen, owner_rank, owner_pick, loads, per_head)
    q = q_latent.reshape(bundles, roll_count * local_heads, -1)
    qr = q_rope.reshape(bundles, roll_count * local_heads, -1)

    def share(chosen):
        found = {0: chosen}
        bit = heads // 2
        while bit:
            pairs = [(i, i ^ bit) for i in range(heads)]
            for m in list(found):
                found[m ^ bit] = move(found[m], pairs, "head")
            bit //= 2
        return [found[m] for m in range(heads)]

    groups = {}
    for k in range(1, last):
        if k > 1:
            fore = move(fore, ahead)
            back = move(back, behind)
        chosen = choose(table, fore, back, [2 * k - 1, 2 * k])
        parts = share(chosen)
        groups[2 * k - 1] = [(p, 0) for p in parts]
        groups[2 * k] = [(p, 1) for p in parts]
    cut = slots // 2
    left = move(fore[:cut], ahead)
    right = move(back[cut:], behind)
    chosen = choose(table, left, right, [2 * last - 1], cut)
    parts = share(chosen)
    groups[2 * last - 1] = [(p, 0) for p in parts]

    def attend(plan, full=None, earlier=None):
        return attend_slots(
            plan, table, info, q, qr, full, [groups[c] for c in plan[(full is not None) :]],
            bundles, w_uv, earlier,
        )

    chunks = []
    for tag, plans in chunk_plans(ranks).items():
        earlier = []
        for n, plan in enumerate(plans):
            full = (cache_latent, cache_rope) if plan[0] == 0 else None
            carried = earlier if n == len(plans) - 1 else None
            earlier.append(attend(plan, full, carried))
        chunks.append((tag, earlier[-1]))
    half = chunks[0][1].shape[1] // 2

    def project(pieces):
        return jnp.dot(jnp.concatenate(pieces), w_out, preferred_element_type=jnp.float32)

    def target(p, column):
        return order[(where[p] + offsets[column]) % ranks] // per_head

    def settle(columns, both, previous):
        to_send, own, total = settle_step(table, heads, per_head, columns, both, previous)
        got = []
        for m in range(1, heads):
            pairs = []
            for p in range(ranks):
                for t in sorted({target(p, c) for c in columns}):
                    pairs.append((p * heads + (t ^ m), p * heads + t))
            got.append(move(to_send[m - 1], pairs, ("dp", "head")))
        return columns, own, got, total

    arrived = {}
    for tag, values in chunks:
        fore = back = values
        for k in range(1, last):
            fore = move(fore, ahead)
            back = move(back, behind)
            arrived[tag, k] = fore, back
        fore, back = fore[:, :half], back[:, half:]
        left = move(fore, ahead)
        right = move(back, behind)
        arrived[tag, last] = (jnp.concatenate([left, right], axis=1),)
    state = settle([0], project([values for _, values in chunks]), None)
    for k in range(1, last):
        pieces = [arrived[tag, k][side] for side in (0, 1) for tag, _ in chunks]
        state = settle([2 * k - 1, 2 * k], project(pieces), state)
    ends = project([arrived[tag, last][0] for tag, _ in chunks])
    *before, total = state
    *final, _ = settle([2 * last - 1], ends, None)
    return finish(table, info, seen, heads, per_head, roll_count, total, [before, final])


def local(*args):
    ranks, heads = lax.axis_size("dp"), lax.axis_size("head")
    bundles = args[6].shape[0]
    if ranks == bundles and ring_fits(ranks, heads):
        return local_ring(*args)
    return local_general(*args)


def solution(mesh):
    in_specs = (
        P("dp", "head"),
        P("dp", "head"),
        P("dp", None, None),
        P("dp", None, None),
        P("dp"),
        P(),
        P("dp"),
        P("dp"),
        P("head", None, None),
        P("head", "dp"),
    )
    out_specs = P("head", "dp")
    return jax.shard_map(local, mesh=mesh, in_specs=in_specs, out_specs=out_specs, check_vma=False)
```

```python
import functools
import math

import jax
import jax.numpy as jnp
from jax import lax
from jax.experimental import pallas as pl
from jax.experimental.pallas import tpu as pltpu
from jax.sharding import PartitionSpec as P


ROPE = 64
VD = 128


def ring_order(size):
    fast = 1 << (max(size.bit_length() - 1, 0) // 2)
    slow = size // fast
    if fast == 1 or slow % 2:
        return list(range(size))
    cells = [(z, 0) for z in range(slow)]
    for step, z in enumerate(range(slow - 1, -1, -1)):
        ys = range(1, fast) if step % 2 == 0 else range(fast - 1, 0, -1)
        cells += [(z, y) for y in ys]
    return [z * fast + y for z, y in cells]


def ring_fits(ranks, heads):
    if ranks % 2 or ranks < 4 or ranks % heads or heads & (heads - 1):
        return False
    order, per_head = ring_order(ranks), ranks // heads
    return all(
        order[p - k] // per_head != order[(p + k) % ranks] // per_head
        for p in range(ranks)
        for k in range(1, ranks // 2)
    )


def slot_for(info, loads, width, bundles, requester, owner):
    pick = jnp.int32(0)
    for j in range(bundles):
        hit = info[requester * width + j] == owner
        pick = jnp.where(hit, info[requester * width + bundles + j], pick)
    return lax.rem(pick, loads[owner])


def pack_kernel(info, loads, place, lat_ref, rope_ref, out_ref):
    rows = lat_ref.shape[1]
    out_ref[0, :rows, :] = lat_ref[0]
    out_ref[0, rows:, :] = rope_ref[0]


def pack(info, loads, place, cache_latent, cache_rope, ranks, heads, width, bundles):
    rows = cache_latent.shape[1] // heads
    dims = cache_rope.shape[1] // heads
    wide = cache_latent.shape[2]

    def source(i, info, loads, place):
        return slot_for(info, loads, width, bundles, i, place[0]), place[1], 0

    return pl.pallas_call(
        pack_kernel,
        out_shape=jax.ShapeDtypeStruct((ranks, rows + dims, wide), cache_latent.dtype),
        grid_spec=pltpu.PrefetchScalarGridSpec(
            num_scalar_prefetch=3,
            grid=(ranks,),
            in_specs=[pl.BlockSpec((1, rows, wide), source), pl.BlockSpec((1, dims, wide), source)],
            out_specs=pl.BlockSpec((1, rows + dims, wide), lambda i, *_: (i, 0, 0)),
        ),
        name="pack",
    )(info, loads, place, cache_latent, cache_rope)


def attend_kernel(
    heads, width, bundles, scale, block, info, loads, place, q_ref, qr_ref, *refs
):
    parts = refs[:heads]
    w_ref, out_ref, lat, rope, mixed = refs[heads:]
    b = pl.program_id(0)
    rows = lat.shape[0] // heads
    dims = rope.shape[0] // heads
    for m in range(heads):
        at = jnp.bitwise_xor(place[1], m)
        lat[pl.ds(pl.multiple_of(at * rows, rows), rows), :] = parts[m][0, :rows, :]
        rope[pl.ds(pl.multiple_of(at * dims, dims), dims), :] = parts[m][0, rows:, :]
    base = place[0] * width
    owner = info[base + b]
    slot = lax.rem(info[base + bundles + b], loads[owner])
    length = info[owner * width + 2 * bundles + slot]
    total_rows = q_ref.shape[1]
    live = lax.broadcasted_iota(jnp.int32, (block, lat.shape[0]), 1) < length
    for i in range(total_rows // block):
        at = slice(i * block, (i + 1) * block)
        s = lax.dot_general(
            q_ref[0, at, :], lat[...], (((1,), (1,)), ((), ())), preferred_element_type=jnp.float32
        )
        s = s + jnp.dot(qr_ref[0, at, :], rope[...], preferred_element_type=jnp.float32)
        s = jnp.where(live, s * scale, -1e30)
        w = jnp.exp(s - jnp.max(s, axis=1, keepdims=True))
        w = w * (1.0 / jnp.sum(w, axis=1, keepdims=True))
        o = jnp.dot(w.astype(jnp.bfloat16), lat[...], preferred_element_type=jnp.float32)
        for c in range(mixed.shape[0]):
            piece = o[:, c * 128 : (c + 1) * 128]
            mixed[c, pl.ds(b * total_rows + i * block, block), :] = piece

    @pl.when(b == pl.num_programs(0) - 1)
    def _():
        local_heads, _, value_width = w_ref.shape
        n = mixed.shape[1] // local_heads
        for h in range(local_heads):
            x = jnp.concatenate(
                [mixed[c, pl.ds(h, n, stride=local_heads), :] for c in range(mixed.shape[0])], axis=1
            ).astype(jnp.bfloat16)
            v = jnp.dot(x, w_ref[h], preferred_element_type=jnp.float32)
            out_ref[:, h * value_width : (h + 1) * value_width] = v.astype(jnp.bfloat16)


def attend(info, loads, place, q, qr, parts, w_uv, width, bundles):
    heads = len(parts)
    _, q_rows, wide = q.shape
    _, part_rows, _ = parts[0].shape
    local_heads, _, value_width = w_uv.shape
    dims = qr.shape[2] // heads
    rows = part_rows - dims
    row_count = bundles * q_rows // local_heads

    def theirs(b, info, loads, place):
        return info[place[0] * width + b], 0, 0

    block = math.gcd(q_rows, 128)
    return pl.pallas_call(
        functools.partial(
            attend_kernel, heads, width, bundles, 1.0 / math.sqrt(VD + ROPE), block
        ),
        out_shape=jax.ShapeDtypeStruct((row_count, local_heads * value_width), jnp.bfloat16),
        grid_spec=pltpu.PrefetchScalarGridSpec(
            num_scalar_prefetch=3,
            grid=(bundles,),
            in_specs=[
                pl.BlockSpec((1, q_rows, wide), lambda b, *_: (b, 0, 0)),
                pl.BlockSpec((1, q_rows, qr.shape[2]), lambda b, *_: (b, 0, 0)),
            ]
            + [pl.BlockSpec((1, part_rows, wide), theirs)] * heads
            + [pl.BlockSpec(w_uv.shape, lambda b, *_: (0, 0, 0))],
            out_specs=pl.BlockSpec((row_count, local_heads * value_width), lambda b, *_: (0, 0)),
            scratch_shapes=[
                pltpu.VMEM((rows * heads, wide), jnp.bfloat16),
                pltpu.VMEM((dims * heads, wide), jnp.bfloat16),
                pltpu.VMEM((wide // 128, bundles * q_rows, 128), jnp.float32),
            ],
        ),
        name="attend",
    )(info, loads, place, q, qr, *parts, w_uv)


def local_general(
    q_latent, q_rope, cache_latent, cache_rope, lengths, loads, owner_rank, owner_pick, w_uv, w_out
):
    ranks = lax.axis_size("dp")
    heads = lax.axis_size("head")
    me = lax.axis_index("dp")
    head = lax.axis_index("head")
    bundles = owner_rank.shape[0]
    roll_count = q_latent.shape[0] // bundles
    local_heads = w_uv.shape[0]
    place = jnp.stack([me, head]).astype(jnp.int32)

    facts = jnp.concatenate([owner_rank, owner_pick, lengths])
    width = 32
    facts = jnp.pad(facts, (0, width - facts.shape[0]))
    info = lax.all_to_all(
        jnp.broadcast_to(facts[None], (ranks, width)), "dp", split_axis=0, concat_axis=0, tiled=True
    ).reshape(-1)
    q = q_latent.reshape(bundles, roll_count * local_heads, -1)
    qr = q_rope.reshape(bundles, roll_count * local_heads, -1)

    packed = pack(info, loads, place, cache_latent, cache_rope, ranks, heads, width, bundles)
    mine = lax.all_to_all(packed, "dp", split_axis=0, concat_axis=0, tiled=True)
    parts = [mine]
    bit = heads // 2
    found = {0: mine}
    while bit:
        pairs = [(i, i ^ bit) for i in range(heads)]
        for m in list(found):
            found[m ^ bit] = lax.ppermute(found[m], "head", pairs)
        bit //= 2
    parts = [found[m] for m in range(heads)]
    values = attend(info, loads, place, q, qr, parts, w_uv, width, bundles)

    order = ring_order(ranks)
    ahead = [(order[i], order[(i + 1) % ranks]) for i in range(ranks)]
    behind = [(b, a) for a, b in ahead]
    half = values.shape[1] // 2

    def project(x):
        return jnp.dot(x, w_out, preferred_element_type=jnp.float32).astype(jnp.bfloat16)

    partial = {0: project(values)}
    fore = back = values
    for step in range(1, (ranks + 1) // 2):
        fore = lax.ppermute(fore, "dp", ahead)
        back = lax.ppermute(back, "dp", behind)
        both = project(jnp.concatenate([fore, back], axis=0))
        partial[-step] = both[: values.shape[0]]
        partial[step] = both[values.shape[0] :]
    if ranks % 2 == 0:
        left = lax.ppermute(fore[:, :half], "dp", ahead)
        right = lax.ppermute(back[:, half:], "dp", behind)
        partial[ranks // 2] = project(jnp.concatenate([left, right], axis=1))
    stacked = jnp.stack([partial[k if 2 * k <= ranks else k - ranks] for k in range(ranks)])
    position = [0] * ranks
    for i, r in enumerate(order):
        position[r] = i
    position = jnp.asarray(position, jnp.int32)
    by_rank = stacked[(position - position[me]) % ranks]
    shares = by_rank.reshape(heads, -1, w_out.shape[1])
    got = lax.all_to_all(shares, "head", split_axis=0, concat_axis=0, tiled=True)
    return jnp.sum(got.astype(jnp.float32), axis=0).astype(jnp.bfloat16)


def in_hbm(x):
    return pltpu.with_memory_space_constraint(x, pltpu.MemorySpace.HBM)


def ring_tables(ranks):
    order = ring_order(ranks)
    where = [order.index(r) for r in range(ranks)]
    offsets = [0]
    for k in range(1, ranks // 2):
        offsets += [-k, k]
    offsets.append(ranks // 2)
    seen = [[order[(where[r] + o) % ranks] for o in offsets] for r in range(ranks)]
    return order, where, offsets, seen


BUNDLE, SLOT, TARGET, OWNER, PLACE, PLAN_ROWS = 0, 1, 2, 3, 4, 8


def chunk_plans(ranks):
    middle = ranks // 2
    return {
        "p": [list(range(middle - 1)), [middle - 1]],
        "s": [list(range(middle, ranks - 1)), [ranks - 1]],
    }


def plan_kernel(per_head, seen, owner_rank, owner_pick, loads, table):
    ranks = seen.shape[1]
    me, head = lax.axis_index("dp"), lax.axis_index("head")
    table[PLACE, 0] = me
    table[PLACE, 1] = head
    for c in range(ranks):
        owner = seen[me, c]
        bundle, pick = jnp.int32(0), jnp.int32(0)
        for b in range(owner_rank.shape[0]):
            hit = owner_rank[b] == owner
            bundle = jnp.where(hit, b, bundle)
            pick = jnp.where(hit, owner_pick[b], pick)
        table[BUNDLE, c] = bundle
        table[SLOT, c] = lax.rem(pick, loads[owner])
        table[TARGET, c] = lax.div(owner, per_head)
        table[OWNER, c] = owner


def plan_of(seen, owner_rank, owner_pick, loads, per_head):
    smem = pl.BlockSpec(memory_space=pltpu.MemorySpace.SMEM)
    return pl.pallas_call(
        functools.partial(plan_kernel, per_head),
        out_shape=jax.ShapeDtypeStruct((PLAN_ROWS, seen.shape[1]), jnp.int32),
        in_specs=[smem] * 4,
        out_specs=smem,
        name="plan",
    )(seen, owner_rank, owner_pick, loads)


def payload_kernel(lat, rope, out, sems):
    head = lax.axis_index("head")
    dims = rope.shape[1] * (out.shape[1]) // (rope.shape[1] + lat.shape[1])
    rows = out.shape[1] - dims
    copies = [
        pltpu.make_async_copy(
            lat.at[:, pl.ds(pl.multiple_of(head * rows, rows), rows), :],
            out.at[:, pl.ds(0, rows), :],
            sems.at[0],
        ),
        pltpu.make_async_copy(
            rope.at[:, pl.ds(pl.multiple_of(head * dims, dims), dims), :],
            out.at[:, pl.ds(rows, dims), :],
            sems.at[1],
        ),
    ]
    for copy in copies:
        copy.start()
    for copy in copies:
        copy.wait()


def payload_of(cache_latent, cache_rope, heads):
    slots, positions, wide = cache_latent.shape
    rows = (positions + cache_rope.shape[1]) // heads
    return pl.pallas_call(
        payload_kernel,
        out_shape=jax.ShapeDtypeStruct((slots, rows, wide), cache_latent.dtype),
        in_specs=[pl.BlockSpec(memory_space=pl.ANY)] * 2,
        out_specs=pl.BlockSpec(memory_space=pltpu.MemorySpace.VMEM),
        scratch_shapes=[pltpu.SemaphoreType.DMA((2,))],
        compiler_params=pltpu.CompilerParams(vmem_limit_bytes=4 * 2**20),
        name="payload",
    )(in_hbm(cache_latent), in_hbm(cache_rope))


def upper(rows):
    return (rows // 2 + 15) // 16 * 16


def relay_kernel(bundles, offsets, table, info, loads, seen, fore, back, *outs):
    chosen, sends = outs[0], outs[1:]
    me = table[PLACE, 0]
    last = len(offsets) // 2
    rows = fore.shape[1]
    for side, (way, arrived, out) in enumerate(((1, fore, sends[0]), (-1, back, sends[1]))):
        chosen[side] = arrived[table[SLOT, offsets.index(-way)]]
        owner = seen[me, offsets.index(-way)]
        for d in range(2, last + 1):
            asker = seen[me, offsets.index(way * (d - 1))]
            pick = jnp.int32(0)
            for b in range(bundles):
                hit = info[asker, 0, b] == owner
                pick = jnp.where(hit, info[asker, 0, bundles + b], pick)
            slot = lax.rem(pick, loads[owner])
            start = (d - 2) * rows
            if d < last:
                out[pl.ds(start, rows), :] = arrived[slot]
            elif way == 1:
                out[pl.ds(start, upper(rows)), :] = arrived[slot, : upper(rows), :]
            else:
                out[pl.ds(start, rows - upper(rows)), :] = arrived[slot, upper(rows) :, :]


def relay(table, info, loads, seen, bundles, offsets, fore, back):
    _, rows, wide = fore.shape
    full = (len(offsets) // 2 - 2) * rows
    vmem = pl.BlockSpec(memory_space=pltpu.MemorySpace.VMEM)
    smem = pl.BlockSpec(memory_space=pltpu.MemorySpace.SMEM)
    return pl.pallas_call(
        functools.partial(relay_kernel, bundles, offsets),
        out_shape=[
            jax.ShapeDtypeStruct((2, rows, wide), fore.dtype),
            jax.ShapeDtypeStruct((full + upper(rows), wide), fore.dtype),
            jax.ShapeDtypeStruct((full + rows - upper(rows), wide), fore.dtype),
        ],
        in_specs=[smem] * 4 + [vmem] * 2,
        out_specs=[vmem] * 3,
        compiler_params=pltpu.CompilerParams(vmem_limit_bytes=6 * 2**20),
        name="relay",
    )(table, info, loads, seen, fore, back)


def join_kernel(rows, fore, back, out):
    if out.shape[0] == 2:
        out[0] = fore[:rows, :]
        out[1] = back[:rows, :]
    else:
        out[0, : fore.shape[0], :] = fore[...]
        out[0, fore.shape[0] :, :] = back[...]


def join(count, rows, fore, back):
    vmem = pl.BlockSpec(memory_space=pltpu.MemorySpace.VMEM)
    return pl.pallas_call(
        functools.partial(join_kernel, rows),
        out_shape=jax.ShapeDtypeStruct((count, rows, fore.shape[1]), fore.dtype),
        in_specs=[vmem] * 2,
        out_specs=vmem,
        compiler_params=pltpu.CompilerParams(vmem_limit_bytes=4 * 2**20),
        name="join",
    )(fore, back)


def slots_kernel(plan, own, indices, bundles, final, scale, table, info, *refs):
    count, heads = len(plan), len(indices[0])
    refs = list(refs)
    q_ref, qr_ref, w_hbm = refs.pop(0), refs.pop(0), refs.pop(0)
    w_ref, w_sem = refs.pop(-2), refs.pop(-1)
    w_copy = pltpu.make_async_copy(w_hbm, w_ref, w_sem)
    w_copy.start()
    if own:
        full_lat, full_rope = refs.pop(0), refs.pop(0)
    parts = [[(refs.pop(0), index) for index in slot] for slot in indices]
    lat, rope, mixed = refs.pop(-3), refs.pop(-2), refs.pop(-1)
    if own:
        own_lat, own_rope, sems = refs.pop(-3), refs.pop(-2), refs.pop(-1)
        slot = table[SLOT, plan[0]]
        copies = [
            pltpu.make_async_copy(full_lat.at[slot], own_lat, sems.at[0]),
            pltpu.make_async_copy(full_rope.at[slot], own_rope, sems.at[1]),
        ]
        for copy in copies:
            copy.start()
    into = refs.pop(-1) if final else None
    out_ref = refs.pop(-1)
    earlier = refs
    total_rows = q_ref.shape[1]
    rows = lat.shape[0] // heads
    dims = rope.shape[0] // heads

    def bundle(i, _):
        j = lax.rem(i + own, count)
        for at in range(count):

            @pl.when(j == at)
            def _():
                if own and at == 0:
                    for copy in copies:
                        copy.wait()
                    lat[...] = own_lat[...]
                    rope[...] = own_rope[...]
                    return
                for m, (part, index) in enumerate(parts[at - own]):
                    to = jnp.bitwise_xor(table[PLACE, 1], m)
                    lat[pl.ds(pl.multiple_of(to * rows, rows), rows), :] = part[index, :rows, :]
                    rope[pl.ds(pl.multiple_of(to * dims, dims), dims), :] = part[index, rows:, :]

        column = plan[0] + j
        length = info[table[OWNER, column], 0, 2 * bundles + table[SLOT, column]]
        b = table[BUNDLE, column]
        past = lax.broadcasted_iota(jnp.int32, (1, lat.shape[0]), 1) >= length
        s = lax.dot_general(
            q_ref[b], lat[...], (((1,), (1,)), ((), ())), preferred_element_type=jnp.float32
        )
        s = s + jnp.dot(qr_ref[b], rope[...], preferred_element_type=jnp.float32)
        s = s + jnp.where(past, -1e30, 0.0)
        w = jnp.exp((s - jnp.max(s, axis=1, keepdims=True)) * scale)
        w = w * (1.0 / jnp.sum(w, axis=1, keepdims=True))
        o = jnp.dot(w.astype(jnp.bfloat16), lat[...], preferred_element_type=jnp.float32)
        start = pl.multiple_of(j * total_rows, total_rows)
        for c in range(mixed.shape[0]):
            mixed[c, pl.ds(start, total_rows), :] = o[:, c * 128 : (c + 1) * 128]
        return 0

    lax.fori_loop(0, count, bundle, 0)
    w_copy.wait()
    local_heads, _, value_width = w_ref.shape
    n = mixed.shape[1] // local_heads
    at = 0
    if final:
        for piece in earlier:
            into[pl.ds(at, piece.shape[0]), :] = piece[...]
            at += piece.shape[0]
    else:
        into = out_ref
    for h in range(local_heads):
        x = jnp.concatenate(
            [mixed[c, pl.ds(h, n, stride=local_heads), :] for c in range(mixed.shape[0])], axis=1
        ).astype(jnp.bfloat16)
        v = jnp.dot(x, w_ref[h], preferred_element_type=jnp.float32)
        into[pl.ds(at, n), h * value_width : (h + 1) * value_width] = v
    if final:
        out_ref[...] = into[...].astype(out_ref.dtype)


def attend_slots(plan, table, info, q, qr, full, parts, bundles, w_uv, earlier=None):
    own = 1 if full is not None else 0
    final = earlier is not None
    earlier = list(earlier or ())
    count, heads = len(plan), len(parts[0])
    _, q_rows, wide = q.shape
    dims = qr.shape[2]
    positions = (parts[0][0][0].shape[1] - dims // heads) * heads
    local_heads, _, value_width = w_uv.shape
    vmem = pl.BlockSpec(memory_space=pltpu.MemorySpace.VMEM)
    smem = pl.BlockSpec(memory_space=pltpu.MemorySpace.SMEM)
    args, in_specs = [q, qr, in_hbm(w_uv)], [vmem, vmem, pl.BlockSpec(memory_space=pl.ANY)]
    if own:
        args += [in_hbm(x) for x in full]
        in_specs += [pl.BlockSpec(memory_space=pl.ANY)] * 2
    args += [array for slot in parts for array, _ in slot] + earlier
    in_specs += [vmem] * (len(args) - len(in_specs))
    done = sum(e.shape[0] for e in earlier) + count * q_rows // local_heads
    out_shape = (done, local_heads * value_width)
    caches = [pltpu.VMEM((positions, wide), jnp.bfloat16), pltpu.VMEM((dims, wide), jnp.bfloat16)]
    scratch = [pltpu.VMEM(out_shape, jnp.float32)] if final else []
    if own:
        scratch += caches + [pltpu.SemaphoreType.DMA((2,))]
    scratch += caches + [pltpu.VMEM((wide // 128, count * q_rows, 128), jnp.float32)]
    scratch += [pltpu.VMEM(w_uv.shape, w_uv.dtype), pltpu.SemaphoreType.DMA]
    return pl.pallas_call(
        functools.partial(
            slots_kernel, plan, own, [[index for _, index in slot] for slot in parts], bundles,
            final, 1.0 / math.sqrt(VD + ROPE),
        ),
        out_shape=jax.ShapeDtypeStruct(out_shape, jnp.bfloat16 if final else jnp.float32),
        in_specs=[smem] * 2 + in_specs,
        out_specs=vmem,
        scratch_shapes=scratch,
        compiler_params=pltpu.CompilerParams(vmem_limit_bytes=18 * 2**20),
        name="attend_slots",
    )(table, info, *args)


def add_in(table, per_head, columns, own, got, before, after):
    part = own[...]
    for g in got:
        part = part + g[...].astype(jnp.float32)
    for y in range(per_head):
        rank = table[PLACE, 1] * per_head + y
        hit = table[OWNER, columns[0]] == rank
        for c in columns[1:]:
            hit = hit | (table[OWNER, c] == rank)
        now = jnp.where(hit, part, 0.0)
        after[y] = now if before is None else before[y] + now


def settle_kernel(heads, per_head, columns, prev_columns, has_total, table, both, *refs):
    refs = list(refs)
    if prev_columns:
        prev_own, prev_got = refs.pop(0), [refs.pop(0) for _ in range(heads - 1)]
        before = refs.pop(0) if has_total else None
    block = both.shape[0] // len(columns)
    sends = len(refs) - 1 - bool(prev_columns)
    own = refs[sends]
    head = table[PLACE, 1]
    if len(columns) == 1:
        own[...] = both[...]
        refs[0][...] = both[...].astype(jnp.bfloat16)
    else:
        for m in range(heads):
            first = table[TARGET, columns[0]] == jnp.bitwise_xor(head, m)
            piece = jnp.where(first, both[:block], both[block:])
            if m == 0:
                own[...] = piece
            else:
                refs[m - 1][...] = piece.astype(jnp.bfloat16)
    if prev_columns:
        add_in(table, per_head, prev_columns, prev_own, prev_got, before, refs[sends + 1])


def settle_step(table, heads, per_head, columns, both, previous):
    n = both.shape[0] // len(columns)
    wide = both.shape[1]
    vmem = pl.BlockSpec(memory_space=pltpu.MemorySpace.VMEM)
    args, prev_columns, has_total = [both], None, False
    if previous is not None:
        prev_columns, prev_own, prev_got, total = previous
        has_total = total is not None
        args += [prev_own, *prev_got] + ([total] if has_total else [])
    sends = 1 if len(columns) == 1 else heads - 1
    out = [jax.ShapeDtypeStruct((n, wide), jnp.bfloat16)] * sends
    out.append(jax.ShapeDtypeStruct((n, wide), jnp.float32))
    if previous is not None:
        out.append(jax.ShapeDtypeStruct((per_head, n, wide), jnp.float32))
    outs = pl.pallas_call(
        functools.partial(settle_kernel, heads, per_head, columns, prev_columns, has_total),
        out_shape=out,
        in_specs=[pl.BlockSpec(memory_space=pltpu.MemorySpace.SMEM)] + [vmem] * len(args),
        out_specs=[vmem] * len(out),
        compiler_params=pltpu.CompilerParams(vmem_limit_bytes=4 * 2**20),
        name="settle",
    )(table, *args)
    to_send = list(outs[:sends]) * (1 if sends > 1 else heads - 1)
    return to_send, outs[sends], outs[sends + 1] if previous is not None else None


def finish_kernel(heads, per_head, steps, roll, table, info, seen, before, *refs):
    out, total = refs[heads * len(steps) :]
    for i, columns in enumerate(steps):
        own, *got = refs[heads * i : heads * (i + 1)]
        add_in(table, per_head, columns, own, got, total if i else before, total)
    n = total.shape[1]
    slots = n // roll
    to = lax.broadcasted_iota(jnp.int32, (n, n), 0)
    source = lax.broadcasted_iota(jnp.int32, (n, n), 1)
    for y in range(per_head):
        rank = table[PLACE, 1] * per_head + y
        wanted = to
        for b in range(slots):
            place = jnp.int32(0)
            for c in range(slots):
                place = jnp.where(seen[rank, c] == info[rank, 0, b], c, place)
            inside = (to >= b * roll) & (to < (b + 1) * roll)
            wanted = jnp.where(inside, to + (place - b) * roll, wanted)
        pick = jnp.where(wanted == source, 1.0, 0.0).astype(jnp.bfloat16)
        moved = jnp.dot(pick, total[y].astype(jnp.bfloat16), preferred_element_type=jnp.float32)
        out[pl.ds(y * n, n), :] = moved.astype(out.dtype)


def finish(table, info, seen, heads, per_head, roll, total, states):
    _, n, wide = total.shape
    steps = [state[0] for state in states]
    args = [x for _, own, got in states for x in (own, *got)]
    vmem = pl.BlockSpec(memory_space=pltpu.MemorySpace.VMEM)
    smem = pl.BlockSpec(memory_space=pltpu.MemorySpace.SMEM)
    return pl.pallas_call(
        functools.partial(finish_kernel, heads, per_head, steps, roll),
        out_shape=jax.ShapeDtypeStruct((per_head * n, wide), jnp.bfloat16),
        in_specs=[smem] * 3 + [vmem] * (1 + len(args)),
        out_specs=vmem,
        scratch_shapes=[pltpu.VMEM((per_head, n, wide), jnp.float32)],
        compiler_params=pltpu.CompilerParams(vmem_limit_bytes=6 * 2**20),
        name="finish",
    )(table, info, seen, total, *args)


def local_ring(
    q_latent, q_rope, cache_latent, cache_rope, lengths, loads, owner_rank, owner_pick, w_uv, w_out
):
    ranks = lax.axis_size("dp")
    heads = lax.axis_size("head")
    bundles = owner_rank.shape[0]
    local_heads = w_uv.shape[0]
    roll_count = q_latent.shape[0] // bundles
    per_head = ranks // heads
    last = ranks // 2
    order, where, offsets, seen = ring_tables(ranks)
    seen = jnp.asarray(seen, jnp.int32)
    ahead = [(order[i], order[(i + 1) % ranks]) for i in range(ranks)]
    behind = [(b, a) for a, b in ahead]

    def move(x, pairs, axis="dp"):
        return lax.ppermute(x, axis, pairs)

    payload = payload_of(cache_latent, cache_rope, heads)
    fore, back = move(payload, ahead), move(payload, behind)
    facts = jnp.concatenate([owner_rank, owner_pick, lengths])
    width = 32
    facts = jnp.pad(facts, (0, width - facts.shape[0]))
    info = lax.all_to_all(
        jnp.broadcast_to(facts[None], (ranks, width)), "dp", split_axis=0, concat_axis=0, tiled=True
    )
    info = jnp.maximum(info, 0)[:, None]
    table = plan_of(seen, owner_rank, owner_pick, loads, per_head)
    q = q_latent.reshape(bundles, roll_count * local_heads, -1)
    qr = q_rope.reshape(bundles, roll_count * local_heads, -1)

    def share(chosen):
        found = {0: chosen}
        bit = heads // 2
        while bit:
            pairs = [(i, i ^ bit) for i in range(heads)]
            for m in list(found):
                found[m ^ bit] = move(found[m], pairs, "head")
            bit //= 2
        return [found[m] for m in range(heads)]

    rows = payload.shape[1]
    chosen, fore, back = relay(table, info, loads, seen, bundles, offsets, fore, back)
    groups = {}
    for k in range(1, last + 1):
        if k > 1:
            if k > 2:
                fore, back = fore[rows:], back[rows:]
            fore = move(fore, ahead)
            back = move(back, behind)
            chosen = join(2 if k < last else 1, rows, fore, back)
        parts = share(chosen)
        groups[2 * k - 1] = [(p, 0) for p in parts]
        if k < last:
            groups[2 * k] = [(p, 1) for p in parts]

    def attend(plan, full=None, earlier=None):
        return attend_slots(
            plan, table, info, q, qr, full, [groups[c] for c in plan[(full is not None) :]],
            bundles, w_uv, earlier,
        )

    chunks = []
    for tag, plans in chunk_plans(ranks).items():
        earlier = []
        for n, plan in enumerate(plans):
            full = (cache_latent, cache_rope) if plan[0] == 0 else None
            carried = earlier if n == len(plans) - 1 else None
            earlier.append(attend(plan, full, carried))
        chunks.append((tag, earlier[-1]))
    half = chunks[0][1].shape[1] // 2

    def project(pieces):
        return jnp.dot(jnp.concatenate(pieces), w_out, preferred_element_type=jnp.float32)

    def target(p, column):
        return order[(where[p] + offsets[column]) % ranks] // per_head

    def settle(columns, both, previous):
        to_send, own, total = settle_step(table, heads, per_head, columns, both, previous)
        got = []
        for m in range(1, heads):
            pairs = []
            for p in range(ranks):
                for t in sorted({target(p, c) for c in columns}):
                    pairs.append((p * heads + (t ^ m), p * heads + t))
            got.append(move(to_send[m - 1], pairs, ("dp", "head")))
        return columns, own, got, total

    arrived = {}
    for tag, values in chunks:
        fore = back = values
        for k in range(1, last):
            fore = move(fore, ahead)
            back = move(back, behind)
            arrived[tag, k] = fore, back
        fore, back = fore[:, :half], back[:, half:]
        left = move(fore, ahead)
        right = move(back, behind)
        arrived[tag, last] = (jnp.concatenate([left, right], axis=1),)
    state = settle([0], project([values for _, values in chunks]), None)
    for k in range(1, last):
        pieces = [arrived[tag, k][side] for side in (0, 1) for tag, _ in chunks]
        state = settle([2 * k - 1, 2 * k], project(pieces), state)
    ends = project([arrived[tag, last][0] for tag, _ in chunks])
    *before, total = state
    *final, _ = settle([2 * last - 1], ends, None)
    return finish(table, info, seen, heads, per_head, roll_count, total, [before, final])


def local(*args):
    ranks, heads = lax.axis_size("dp"), lax.axis_size("head")
    bundles = args[6].shape[0]
    if ranks == bundles and ring_fits(ranks, heads):
        return local_ring(*args)
    return local_general(*args)


def solution(mesh):
    in_specs = (
        P("dp", "head"),
        P("dp", "head"),
        P("dp", None, None),
        P("dp", None, None),
        P("dp"),
        P(),
        P("dp"),
        P("dp"),
        P("head", None, None),
        P("head", "dp"),
    )
    out_specs = P("head", "dp")
    return jax.shard_map(local, mesh=mesh, in_specs=in_specs, out_specs=out_specs, check_vma=False)
```

```python
import functools
import math

import jax
import jax.numpy as jnp
from jax import lax
from jax.experimental import pallas as pl
from jax.experimental.pallas import tpu as pltpu
from jax.sharding import PartitionSpec as P


ROPE = 64
VD = 128


def ring_order(size):
    fast = 1 << (max(size.bit_length() - 1, 0) // 2)
    slow = size // fast
    if fast == 1 or slow % 2:
        return list(range(size))
    cells = [(z, 0) for z in range(slow)]
    for step, z in enumerate(range(slow - 1, -1, -1)):
        ys = range(1, fast) if step % 2 == 0 else range(fast - 1, 0, -1)
        cells += [(z, y) for y in ys]
    return [z * fast + y for z, y in cells]


def ring_fits(ranks, heads):
    if ranks % 2 or ranks < 4 or ranks % heads or heads & (heads - 1):
        return False
    order, per_head = ring_order(ranks), ranks // heads
    return all(
        order[p - k] // per_head != order[(p + k) % ranks] // per_head
        for p in range(ranks)
        for k in range(1, ranks // 2)
    )


def slot_for(info, loads, width, bundles, requester, owner):
    pick = jnp.int32(0)
    for j in range(bundles):
        hit = info[requester * width + j] == owner
        pick = jnp.where(hit, info[requester * width + bundles + j], pick)
    return lax.rem(pick, loads[owner])


def pack_kernel(info, loads, place, lat_ref, rope_ref, out_ref):
    rows = lat_ref.shape[1]
    out_ref[0, :rows, :] = lat_ref[0]
    out_ref[0, rows:, :] = rope_ref[0]


def pack(info, loads, place, cache_latent, cache_rope, ranks, heads, width, bundles):
    rows = cache_latent.shape[1] // heads
    dims = cache_rope.shape[1] // heads
    wide = cache_latent.shape[2]

    def source(i, info, loads, place):
        return slot_for(info, loads, width, bundles, i, place[0]), place[1], 0

    return pl.pallas_call(
        pack_kernel,
        out_shape=jax.ShapeDtypeStruct((ranks, rows + dims, wide), cache_latent.dtype),
        grid_spec=pltpu.PrefetchScalarGridSpec(
            num_scalar_prefetch=3,
            grid=(ranks,),
            in_specs=[pl.BlockSpec((1, rows, wide), source), pl.BlockSpec((1, dims, wide), source)],
            out_specs=pl.BlockSpec((1, rows + dims, wide), lambda i, *_: (i, 0, 0)),
        ),
        name="pack",
    )(info, loads, place, cache_latent, cache_rope)


def attend_kernel(
    heads, width, bundles, scale, block, info, loads, place, q_ref, qr_ref, *refs
):
    parts = refs[:heads]
    w_ref, out_ref, lat, rope, mixed = refs[heads:]
    b = pl.program_id(0)
    rows = lat.shape[0] // heads
    dims = rope.shape[0] // heads
    for m in range(heads):
        at = jnp.bitwise_xor(place[1], m)
        lat[pl.ds(pl.multiple_of(at * rows, rows), rows), :] = parts[m][0, :rows, :]
        rope[pl.ds(pl.multiple_of(at * dims, dims), dims), :] = parts[m][0, rows:, :]
    base = place[0] * width
    owner = info[base + b]
    slot = lax.rem(info[base + bundles + b], loads[owner])
    length = info[owner * width + 2 * bundles + slot]
    total_rows = q_ref.shape[1]
    live = lax.broadcasted_iota(jnp.int32, (block, lat.shape[0]), 1) < length
    for i in range(total_rows // block):
        at = slice(i * block, (i + 1) * block)
        s = lax.dot_general(
            q_ref[0, at, :], lat[...], (((1,), (1,)), ((), ())), preferred_element_type=jnp.float32
        )
        s = s + jnp.dot(qr_ref[0, at, :], rope[...], preferred_element_type=jnp.float32)
        s = jnp.where(live, s * scale, -1e30)
        w = jnp.exp(s - jnp.max(s, axis=1, keepdims=True))
        w = w * (1.0 / jnp.sum(w, axis=1, keepdims=True))
        o = jnp.dot(w.astype(jnp.bfloat16), lat[...], preferred_element_type=jnp.float32)
        for c in range(mixed.shape[0]):
            piece = o[:, c * 128 : (c + 1) * 128]
            mixed[c, pl.ds(b * total_rows + i * block, block), :] = piece

    @pl.when(b == pl.num_programs(0) - 1)
    def _():
        local_heads, _, value_width = w_ref.shape
        n = mixed.shape[1] // local_heads
        for h in range(local_heads):
            x = jnp.concatenate(
                [mixed[c, pl.ds(h, n, stride=local_heads), :] for c in range(mixed.shape[0])], axis=1
            ).astype(jnp.bfloat16)
            v = jnp.dot(x, w_ref[h], preferred_element_type=jnp.float32)
            out_ref[:, h * value_width : (h + 1) * value_width] = v.astype(jnp.bfloat16)


def attend(info, loads, place, q, qr, parts, w_uv, width, bundles):
    heads = len(parts)
    _, q_rows, wide = q.shape
    _, part_rows, _ = parts[0].shape
    local_heads, _, value_width = w_uv.shape
    dims = qr.shape[2] // heads
    rows = part_rows - dims
    row_count = bundles * q_rows // local_heads

    def theirs(b, info, loads, place):
        return info[place[0] * width + b], 0, 0

    block = math.gcd(q_rows, 128)
    return pl.pallas_call(
        functools.partial(
            attend_kernel, heads, width, bundles, 1.0 / math.sqrt(VD + ROPE), block
        ),
        out_shape=jax.ShapeDtypeStruct((row_count, local_heads * value_width), jnp.bfloat16),
        grid_spec=pltpu.PrefetchScalarGridSpec(
            num_scalar_prefetch=3,
            grid=(bundles,),
            in_specs=[
                pl.BlockSpec((1, q_rows, wide), lambda b, *_: (b, 0, 0)),
                pl.BlockSpec((1, q_rows, qr.shape[2]), lambda b, *_: (b, 0, 0)),
            ]
            + [pl.BlockSpec((1, part_rows, wide), theirs)] * heads
            + [pl.BlockSpec(w_uv.shape, lambda b, *_: (0, 0, 0))],
            out_specs=pl.BlockSpec((row_count, local_heads * value_width), lambda b, *_: (0, 0)),
            scratch_shapes=[
                pltpu.VMEM((rows * heads, wide), jnp.bfloat16),
                pltpu.VMEM((dims * heads, wide), jnp.bfloat16),
                pltpu.VMEM((wide // 128, bundles * q_rows, 128), jnp.float32),
            ],
        ),
        name="attend",
    )(info, loads, place, q, qr, *parts, w_uv)


def local_general(
    q_latent, q_rope, cache_latent, cache_rope, lengths, loads, owner_rank, owner_pick, w_uv, w_out
):
    ranks = lax.axis_size("dp")
    heads = lax.axis_size("head")
    me = lax.axis_index("dp")
    head = lax.axis_index("head")
    bundles = owner_rank.shape[0]
    roll_count = q_latent.shape[0] // bundles
    local_heads = w_uv.shape[0]
    place = jnp.stack([me, head]).astype(jnp.int32)

    facts = jnp.concatenate([owner_rank, owner_pick, lengths])
    width = 32
    facts = jnp.pad(facts, (0, width - facts.shape[0]))
    info = lax.all_to_all(
        jnp.broadcast_to(facts[None], (ranks, width)), "dp", split_axis=0, concat_axis=0, tiled=True
    ).reshape(-1)
    q = q_latent.reshape(bundles, roll_count * local_heads, -1)
    qr = q_rope.reshape(bundles, roll_count * local_heads, -1)

    packed = pack(info, loads, place, cache_latent, cache_rope, ranks, heads, width, bundles)
    mine = lax.all_to_all(packed, "dp", split_axis=0, concat_axis=0, tiled=True)
    parts = [mine]
    bit = heads // 2
    found = {0: mine}
    while bit:
        pairs = [(i, i ^ bit) for i in range(heads)]
        for m in list(found):
            found[m ^ bit] = lax.ppermute(found[m], "head", pairs)
        bit //= 2
    parts = [found[m] for m in range(heads)]
    values = attend(info, loads, place, q, qr, parts, w_uv, width, bundles)

    order = ring_order(ranks)
    ahead = [(order[i], order[(i + 1) % ranks]) for i in range(ranks)]
    behind = [(b, a) for a, b in ahead]
    half = values.shape[1] // 2

    def project(x):
        return jnp.dot(x, w_out, preferred_element_type=jnp.float32).astype(jnp.bfloat16)

    partial = {0: project(values)}
    fore = back = values
    for step in range(1, (ranks + 1) // 2):
        fore = lax.ppermute(fore, "dp", ahead)
        back = lax.ppermute(back, "dp", behind)
        both = project(jnp.concatenate([fore, back], axis=0))
        partial[-step] = both[: values.shape[0]]
        partial[step] = both[values.shape[0] :]
    if ranks % 2 == 0:
        left = lax.ppermute(fore[:, :half], "dp", ahead)
        right = lax.ppermute(back[:, half:], "dp", behind)
        partial[ranks // 2] = project(jnp.concatenate([left, right], axis=1))
    stacked = jnp.stack([partial[k if 2 * k <= ranks else k - ranks] for k in range(ranks)])
    position = [0] * ranks
    for i, r in enumerate(order):
        position[r] = i
    position = jnp.asarray(position, jnp.int32)
    by_rank = stacked[(position - position[me]) % ranks]
    shares = by_rank.reshape(heads, -1, w_out.shape[1])
    got = lax.all_to_all(shares, "head", split_axis=0, concat_axis=0, tiled=True)
    return jnp.sum(got.astype(jnp.float32), axis=0).astype(jnp.bfloat16)


def in_hbm(x):
    return pltpu.with_memory_space_constraint(x, pltpu.MemorySpace.HBM)


def ring_tables(ranks):
    order = ring_order(ranks)
    where = [order.index(r) for r in range(ranks)]
    offsets = [0]
    for k in range(1, ranks // 2):
        offsets += [-k, k]
    offsets.append(ranks // 2)
    seen = [[order[(where[r] + o) % ranks] for o in offsets] for r in range(ranks)]
    return order, where, offsets, seen


BUNDLE, SLOT, TARGET, OWNER, PLACE, PLAN_ROWS = 0, 1, 2, 3, 4, 8


def chunk_plans(ranks):
    middle = ranks // 2
    return {
        "p": [list(range(middle - 1)), [middle - 1]],
        "s": [list(range(middle, ranks - 1)), [ranks - 1]],
    }


def plan_kernel(per_head, seen, owner_rank, owner_pick, loads, table):
    ranks = seen.shape[1]
    me, head = lax.axis_index("dp"), lax.axis_index("head")
    table[PLACE, 0] = me
    table[PLACE, 1] = head
    for c in range(ranks):
        owner = seen[me, c]
        bundle, pick = jnp.int32(0), jnp.int32(0)
        for b in range(owner_rank.shape[0]):
            hit = owner_rank[b] == owner
            bundle = jnp.where(hit, b, bundle)
            pick = jnp.where(hit, owner_pick[b], pick)
        table[BUNDLE, c] = bundle
        table[SLOT, c] = lax.rem(pick, loads[owner])
        table[TARGET, c] = lax.div(owner, per_head)
        table[OWNER, c] = owner


def plan_of(seen, owner_rank, owner_pick, loads, per_head):
    smem = pl.BlockSpec(memory_space=pltpu.MemorySpace.SMEM)
    return pl.pallas_call(
        functools.partial(plan_kernel, per_head),
        out_shape=jax.ShapeDtypeStruct((PLAN_ROWS, seen.shape[1]), jnp.int32),
        in_specs=[smem] * 4,
        out_specs=smem,
        name="plan",
    )(seen, owner_rank, owner_pick, loads)


def payload_kernel(lat, rope, out, sems):
    head = lax.axis_index("head")
    dims = rope.shape[1] * (out.shape[1]) // (rope.shape[1] + lat.shape[1])
    rows = out.shape[1] - dims
    copies = [
        pltpu.make_async_copy(
            lat.at[:, pl.ds(pl.multiple_of(head * rows, rows), rows), :],
            out.at[:, pl.ds(0, rows), :],
            sems.at[0],
        ),
        pltpu.make_async_copy(
            rope.at[:, pl.ds(pl.multiple_of(head * dims, dims), dims), :],
            out.at[:, pl.ds(rows, dims), :],
            sems.at[1],
        ),
    ]
    for copy in copies:
        copy.start()
    for copy in copies:
        copy.wait()


def payload_of(cache_latent, cache_rope, heads):
    slots, positions, wide = cache_latent.shape
    rows = (positions + cache_rope.shape[1]) // heads
    return pl.pallas_call(
        payload_kernel,
        out_shape=jax.ShapeDtypeStruct((slots, rows, wide), cache_latent.dtype),
        in_specs=[pl.BlockSpec(memory_space=pl.ANY)] * 2,
        out_specs=pl.BlockSpec(memory_space=pltpu.MemorySpace.VMEM),
        scratch_shapes=[pltpu.SemaphoreType.DMA((2,))],
        compiler_params=pltpu.CompilerParams(vmem_limit_bytes=4 * 2**20),
        name="payload",
    )(in_hbm(cache_latent), in_hbm(cache_rope))


def upper(rows):
    return (rows // 2 + 15) // 16 * 16


def relay_kernel(bundles, offsets, table, info, loads, seen, fore, back, *outs):
    chosen, sends = outs[0], outs[1:]
    me = table[PLACE, 0]
    last = len(offsets) // 2
    rows = fore.shape[1]
    for side, (way, arrived, out) in enumerate(((1, fore, sends[0]), (-1, back, sends[1]))):
        chosen[side] = arrived[table[SLOT, offsets.index(-way)]]
        owner = seen[me, offsets.index(-way)]
        for d in range(2, last + 1):
            asker = seen[me, offsets.index(way * (d - 1))]
            pick = jnp.int32(0)
            for b in range(bundles):
                hit = info[asker, 0, b] == owner
                pick = jnp.where(hit, info[asker, 0, bundles + b], pick)
            slot = lax.rem(pick, loads[owner])
            start = (d - 2) * rows
            if d < last:
                out[pl.ds(start, rows), :] = arrived[slot]
            elif way == 1:
                out[pl.ds(start, upper(rows)), :] = arrived[slot, : upper(rows), :]
            else:
                out[pl.ds(start, rows - upper(rows)), :] = arrived[slot, upper(rows) :, :]


def relay(table, info, loads, seen, bundles, offsets, fore, back):
    _, rows, wide = fore.shape
    full = (len(offsets) // 2 - 2) * rows
    vmem = pl.BlockSpec(memory_space=pltpu.MemorySpace.VMEM)
    smem = pl.BlockSpec(memory_space=pltpu.MemorySpace.SMEM)
    return pl.pallas_call(
        functools.partial(relay_kernel, bundles, offsets),
        out_shape=[
            jax.ShapeDtypeStruct((2, rows, wide), fore.dtype),
            jax.ShapeDtypeStruct((full + upper(rows), wide), fore.dtype),
            jax.ShapeDtypeStruct((full + rows - upper(rows), wide), fore.dtype),
        ],
        in_specs=[smem] * 4 + [vmem] * 2,
        out_specs=[vmem] * 3,
        compiler_params=pltpu.CompilerParams(vmem_limit_bytes=6 * 2**20),
        name="relay",
    )(table, info, loads, seen, fore, back)


def join_kernel(rows, fore, back, out):
    if out.shape[0] == 2:
        out[0] = fore[:rows, :]
        out[1] = back[:rows, :]
    else:
        out[0, : fore.shape[0], :] = fore[...]
        out[0, fore.shape[0] :, :] = back[...]


def join(count, rows, fore, back):
    vmem = pl.BlockSpec(memory_space=pltpu.MemorySpace.VMEM)
    return pl.pallas_call(
        functools.partial(join_kernel, rows),
        out_shape=jax.ShapeDtypeStruct((count, rows, fore.shape[1]), fore.dtype),
        in_specs=[vmem] * 2,
        out_specs=vmem,
        compiler_params=pltpu.CompilerParams(vmem_limit_bytes=4 * 2**20),
        name="join",
    )(fore, back)


def slots_kernel(plan, own, indices, bundles, final, scale, table, info, *refs):
    count, heads = len(plan), len(indices[0])
    refs = list(refs)
    q_ref, qr_ref, w_hbm = refs.pop(0), refs.pop(0), refs.pop(0)
    w_ref = w_hbm
    if count > 1:
        w_ref, w_sem = refs.pop(-2), refs.pop(-1)
        w_copy = pltpu.make_async_copy(w_hbm, w_ref, w_sem)
        w_copy.start()
    if own:
        full_lat, full_rope = refs.pop(0), refs.pop(0)
    parts = [[(refs.pop(0), index) for index in slot] for slot in indices]
    lat, rope, mixed = refs.pop(-3), refs.pop(-2), refs.pop(-1)
    if own:
        own_lat, own_rope, sems = refs.pop(-3), refs.pop(-2), refs.pop(-1)
        slot = table[SLOT, plan[0]]
        copies = [
            pltpu.make_async_copy(full_lat.at[slot], own_lat, sems.at[0]),
            pltpu.make_async_copy(full_rope.at[slot], own_rope, sems.at[1]),
        ]
        for copy in copies:
            copy.start()
    into = refs.pop(-1) if final else None
    out_ref = refs.pop(-1)
    earlier = refs
    total_rows = q_ref.shape[1]
    rows = lat.shape[0] // heads
    dims = rope.shape[0] // heads

    def bundle(i, _):
        j = lax.rem(i + own, count)
        for at in range(count):

            @pl.when(j == at)
            def _():
                if own and at == 0:
                    for copy in copies:
                        copy.wait()
                    lat[...] = own_lat[...]
                    rope[...] = own_rope[...]
                    return
                for m, (part, index) in enumerate(parts[at - own]):
                    to = jnp.bitwise_xor(table[PLACE, 1], m)
                    lat[pl.ds(pl.multiple_of(to * rows, rows), rows), :] = part[index, :rows, :]
                    rope[pl.ds(pl.multiple_of(to * dims, dims), dims), :] = part[index, rows:, :]

        column = plan[0] + j
        length = info[table[OWNER, column], 0, 2 * bundles + table[SLOT, column]]
        b = table[BUNDLE, column]
        past = lax.broadcasted_iota(jnp.int32, (1, lat.shape[0]), 1) >= length
        s = lax.dot_general(
            q_ref[b], lat[...], (((1,), (1,)), ((), ())), preferred_element_type=jnp.float32
        )
        s = s + jnp.dot(qr_ref[b], rope[...], preferred_element_type=jnp.float32)
        s = s + jnp.where(past, -1e30, 0.0)
        w = jnp.exp((s - jnp.max(s, axis=1, keepdims=True)) * scale)
        w = w * (1.0 / jnp.sum(w, axis=1, keepdims=True))
        o = jnp.dot(w.astype(jnp.bfloat16), lat[...], preferred_element_type=jnp.float32)
        start = pl.multiple_of(j * total_rows, total_rows)
        for c in range(mixed.shape[0]):
            mixed[c, pl.ds(start, total_rows), :] = o[:, c * 128 : (c + 1) * 128]
        return 0

    lax.fori_loop(0, count, bundle, 0)
    if count > 1:
        w_copy.wait()
    local_heads, _, value_width = w_ref.shape
    n = mixed.shape[1] // local_heads
    at = 0
    if final:
        for piece in earlier:
            into[pl.ds(at, piece.shape[0]), :] = piece[...]
            at += piece.shape[0]
    else:
        into = out_ref
    for h in range(local_heads):
        x = jnp.concatenate(
            [mixed[c, pl.ds(h, n, stride=local_heads), :] for c in range(mixed.shape[0])], axis=1
        ).astype(jnp.bfloat16)
        v = jnp.dot(x, w_ref[h], preferred_element_type=jnp.float32)
        into[pl.ds(at, n), h * value_width : (h + 1) * value_width] = v
    if final:
        out_ref[...] = into[...].astype(out_ref.dtype)


def attend_slots(plan, table, info, q, qr, full, parts, bundles, w_uv, earlier=None):
    own = 1 if full is not None else 0
    final = earlier is not None
    earlier = list(earlier or ())
    count, heads = len(plan), len(parts[0])
    _, q_rows, wide = q.shape
    dims = qr.shape[2]
    positions = (parts[0][0][0].shape[1] - dims // heads) * heads
    local_heads, _, value_width = w_uv.shape
    vmem = pl.BlockSpec(memory_space=pltpu.MemorySpace.VMEM)
    smem = pl.BlockSpec(memory_space=pltpu.MemorySpace.SMEM)
    fetch = count > 1
    args = [q, qr, in_hbm(w_uv) if fetch else w_uv]
    in_specs = [vmem, vmem, pl.BlockSpec(memory_space=pl.ANY) if fetch else vmem]
    if own:
        args += [in_hbm(x) for x in full]
        in_specs += [pl.BlockSpec(memory_space=pl.ANY)] * 2
    args += [array for slot in parts for array, _ in slot] + earlier
    in_specs += [vmem] * (len(args) - len(in_specs))
    done = sum(e.shape[0] for e in earlier) + count * q_rows // local_heads
    out_shape = (done, local_heads * value_width)
    caches = [pltpu.VMEM((positions, wide), jnp.bfloat16), pltpu.VMEM((dims, wide), jnp.bfloat16)]
    scratch = [pltpu.VMEM(out_shape, jnp.float32)] if final else []
    if own:
        scratch += caches + [pltpu.SemaphoreType.DMA((2,))]
    scratch += caches + [pltpu.VMEM((wide // 128, count * q_rows, 128), jnp.float32)]
    if fetch:
        scratch += [pltpu.VMEM(w_uv.shape, w_uv.dtype), pltpu.SemaphoreType.DMA]
    return pl.pallas_call(
        functools.partial(
            slots_kernel, plan, own, [[index for _, index in slot] for slot in parts], bundles,
            final, 1.0 / math.sqrt(VD + ROPE),
        ),
        out_shape=jax.ShapeDtypeStruct(out_shape, jnp.bfloat16 if final else jnp.float32),
        in_specs=[smem] * 2 + in_specs,
        out_specs=vmem,
        scratch_shapes=scratch,
        compiler_params=pltpu.CompilerParams(vmem_limit_bytes=(18 if fetch else 12) * 2**20),
        name="attend_slots",
    )(table, info, *args)


def add_in(table, per_head, columns, own, got, before, after):
    part = own[...]
    for g in got:
        part = part + g[...].astype(jnp.float32)
    for y in range(per_head):
        rank = table[PLACE, 1] * per_head + y
        hit = table[OWNER, columns[0]] == rank
        for c in columns[1:]:
            hit = hit | (table[OWNER, c] == rank)
        now = jnp.where(hit, part, 0.0)
        after[y] = now if before is None else before[y] + now


def settle_kernel(heads, per_head, columns, prev_columns, has_total, table, both, *refs):
    refs = list(refs)
    if prev_columns:
        prev_own, prev_got = refs.pop(0), [refs.pop(0) for _ in range(heads - 1)]
        before = refs.pop(0) if has_total else None
    block = both.shape[0] // len(columns)
    sends = len(refs) - 1 - bool(prev_columns)
    own = refs[sends]
    head = table[PLACE, 1]
    if len(columns) == 1:
        own[...] = both[...]
        refs[0][...] = both[...].astype(jnp.bfloat16)
    else:
        for m in range(heads):
            first = table[TARGET, columns[0]] == jnp.bitwise_xor(head, m)
            piece = jnp.where(first, both[:block], both[block:])
            if m == 0:
                own[...] = piece
            else:
                refs[m - 1][...] = piece.astype(jnp.bfloat16)
    if prev_columns:
        add_in(table, per_head, prev_columns, prev_own, prev_got, before, refs[sends + 1])


def settle_step(table, heads, per_head, columns, both, previous):
    n = both.shape[0] // len(columns)
    wide = both.shape[1]
    vmem = pl.BlockSpec(memory_space=pltpu.MemorySpace.VMEM)
    args, prev_columns, has_total = [both], None, False
    if previous is not None:
        prev_columns, prev_own, prev_got, total = previous
        has_total = total is not None
        args += [prev_own, *prev_got] + ([total] if has_total else [])
    sends = 1 if len(columns) == 1 else heads - 1
    out = [jax.ShapeDtypeStruct((n, wide), jnp.bfloat16)] * sends
    out.append(jax.ShapeDtypeStruct((n, wide), jnp.float32))
    if previous is not None:
        out.append(jax.ShapeDtypeStruct((per_head, n, wide), jnp.float32))
    outs = pl.pallas_call(
        functools.partial(settle_kernel, heads, per_head, columns, prev_columns, has_total),
        out_shape=out,
        in_specs=[pl.BlockSpec(memory_space=pltpu.MemorySpace.SMEM)] + [vmem] * len(args),
        out_specs=[vmem] * len(out),
        compiler_params=pltpu.CompilerParams(vmem_limit_bytes=4 * 2**20),
        name="settle",
    )(table, *args)
    to_send = list(outs[:sends]) * (1 if sends > 1 else heads - 1)
    return to_send, outs[sends], outs[sends + 1] if previous is not None else None


def finish_kernel(heads, per_head, steps, roll, table, info, seen, before, *refs):
    out, total = refs[heads * len(steps) :]
    for i, columns in enumerate(steps):
        own, *got = refs[heads * i : heads * (i + 1)]
        add_in(table, per_head, columns, own, got, total if i else before, total)
    n = total.shape[1]
    slots = n // roll
    to = lax.broadcasted_iota(jnp.int32, (n, n), 0)
    source = lax.broadcasted_iota(jnp.int32, (n, n), 1)
    for y in range(per_head):
        rank = table[PLACE, 1] * per_head + y
        wanted = to
        for b in range(slots):
            place = jnp.int32(0)
            for c in range(slots):
                place = jnp.where(seen[rank, c] == info[rank, 0, b], c, place)
            inside = (to >= b * roll) & (to < (b + 1) * roll)
            wanted = jnp.where(inside, to + (place - b) * roll, wanted)
        pick = jnp.where(wanted == source, 1.0, 0.0).astype(jnp.bfloat16)
        moved = jnp.dot(pick, total[y].astype(jnp.bfloat16), preferred_element_type=jnp.float32)
        out[pl.ds(y * n, n), :] = moved.astype(out.dtype)


def finish(table, info, seen, heads, per_head, roll, total, states):
    _, n, wide = total.shape
    steps = [state[0] for state in states]
    args = [x for _, own, got in states for x in (own, *got)]
    vmem = pl.BlockSpec(memory_space=pltpu.MemorySpace.VMEM)
    smem = pl.BlockSpec(memory_space=pltpu.MemorySpace.SMEM)
    return pl.pallas_call(
        functools.partial(finish_kernel, heads, per_head, steps, roll),
        out_shape=jax.ShapeDtypeStruct((per_head * n, wide), jnp.bfloat16),
        in_specs=[smem] * 3 + [vmem] * (1 + len(args)),
        out_specs=vmem,
        scratch_shapes=[pltpu.VMEM((per_head, n, wide), jnp.float32)],
        compiler_params=pltpu.CompilerParams(vmem_limit_bytes=6 * 2**20),
        name="finish",
    )(table, info, seen, total, *args)


def local_ring(
    q_latent, q_rope, cache_latent, cache_rope, lengths, loads, owner_rank, owner_pick, w_uv, w_out
):
    ranks = lax.axis_size("dp")
    heads = lax.axis_size("head")
    bundles = owner_rank.shape[0]
    local_heads = w_uv.shape[0]
    roll_count = q_latent.shape[0] // bundles
    per_head = ranks // heads
    last = ranks // 2
    order, where, offsets, seen = ring_tables(ranks)
    seen = jnp.asarray(seen, jnp.int32)
    ahead = [(order[i], order[(i + 1) % ranks]) for i in range(ranks)]
    behind = [(b, a) for a, b in ahead]

    def move(x, pairs, axis="dp"):
        return lax.ppermute(x, axis, pairs)

    payload = payload_of(cache_latent, cache_rope, heads)
    fore, back = move(payload, ahead), move(payload, behind)
    facts = jnp.concatenate([owner_rank, owner_pick, lengths])
    width = 32
    facts = jnp.pad(facts, (0, width - facts.shape[0]))
    info = lax.all_to_all(
        jnp.broadcast_to(facts[None], (ranks, width)), "dp", split_axis=0, concat_axis=0, tiled=True
    )
    info = jnp.maximum(info, 0)[:, None]
    table = plan_of(seen, owner_rank, owner_pick, loads, per_head)
    q = q_latent.reshape(bundles, roll_count * local_heads, -1)
    qr = q_rope.reshape(bundles, roll_count * local_heads, -1)

    def share(chosen):
        found = {0: chosen}
        bit = heads // 2
        while bit:
            pairs = [(i, i ^ bit) for i in range(heads)]
            for m in list(found):
                found[m ^ bit] = move(found[m], pairs, "head")
            bit //= 2
        return [found[m] for m in range(heads)]

    rows = payload.shape[1]
    chosen, fore, back = relay(table, info, loads, seen, bundles, offsets, fore, back)
    groups = {}
    for k in range(1, last + 1):
        if k > 1:
            if k > 2:
                fore, back = fore[rows:], back[rows:]
            fore = move(fore, ahead)
            back = move(back, behind)
            chosen = join(2 if k < last else 1, rows, fore, back)
        parts = share(chosen)
        groups[2 * k - 1] = [(p, 0) for p in parts]
        if k < last:
            groups[2 * k] = [(p, 1) for p in parts]

    def attend(plan, full=None, earlier=None):
        return attend_slots(
            plan, table, info, q, qr, full, [groups[c] for c in plan[(full is not None) :]],
            bundles, w_uv, earlier,
        )

    chunks = []
    for tag, plans in chunk_plans(ranks).items():
        earlier = []
        for n, plan in enumerate(plans):
            full = (cache_latent, cache_rope) if plan[0] == 0 else None
            carried = earlier if n == len(plans) - 1 else None
            earlier.append(attend(plan, full, carried))
        chunks.append((tag, earlier[-1]))
    half = chunks[0][1].shape[1] // 2

    def project(pieces):
        return jnp.dot(jnp.concatenate(pieces), w_out, preferred_element_type=jnp.float32)

    def target(p, column):
        return order[(where[p] + offsets[column]) % ranks] // per_head

    def settle(columns, both, previous):
        if previous is None and len(columns) == 1:
            to_send, own, total = [both.astype(jnp.bfloat16)] * (heads - 1), both, None
        else:
            to_send, own, total = settle_step(table, heads, per_head, columns, both, previous)
        got = []
        for m in range(1, heads):
            pairs = []
            for p in range(ranks):
                for t in sorted({target(p, c) for c in columns}):
                    pairs.append((p * heads + (t ^ m), p * heads + t))
            got.append(move(to_send[m - 1], pairs, ("dp", "head")))
        return columns, own, got, total

    arrived = {}
    for tag, values in chunks:
        fore = back = values
        for k in range(1, last - 1):
            fore = move(fore, ahead)
            back = move(back, behind)
            arrived[tag, k] = fore, back
        fore_on, fore_end = fore[:, :half], fore[:, half:]
        back_on, back_end = back[:, half:], back[:, :half]
        fore_on = move(fore_on, ahead)
        back_on = move(back_on, behind)
        fore_end = move(fore_end, ahead)
        back_end = move(back_end, behind)
        arrived[tag, last - 1] = (
            jnp.concatenate([fore_on, fore_end], axis=1),
            jnp.concatenate([back_end, back_on], axis=1),
        )
        left = move(fore_on, ahead)
        right = move(back_on, behind)
        arrived[tag, last] = (jnp.concatenate([left, right], axis=1),)
    state = settle([0], project([values for _, values in chunks]), None)
    for k in range(1, last):
        pieces = [arrived[tag, k][side] for side in (0, 1) for tag, _ in chunks]
        state = settle([2 * k - 1, 2 * k], project(pieces), state)
    ends = project([arrived[tag, last][0] for tag, _ in chunks])
    *before, total = state
    *final, _ = settle([2 * last - 1], ends, None)
    return finish(table, info, seen, heads, per_head, roll_count, total, [before, final])


def local(*args):
    ranks, heads = lax.axis_size("dp"), lax.axis_size("head")
    bundles = args[6].shape[0]
    if ranks == bundles and ring_fits(ranks, heads):
        return local_ring(*args)
    return local_general(*args)


def solution(mesh):
    in_specs = (
        P("dp", "head"),
        P("dp", "head"),
        P("dp", None, None),
        P("dp", None, None),
        P("dp"),
        P(),
        P("dp"),
        P("dp"),
        P("head", None, None),
        P("head", "dp"),
    )
    out_specs = P("head", "dp")
    return jax.shard_map(local, mesh=mesh, in_specs=in_specs, out_specs=out_specs, check_vma=False)
```

```python
import functools
import math

import jax
import jax.numpy as jnp
from jax import lax
from jax.experimental import pallas as pl
from jax.experimental.pallas import tpu as pltpu
from jax.sharding import PartitionSpec as P


ROPE = 64
VD = 128


def ring_order(size):
    fast = 1 << (max(size.bit_length() - 1, 0) // 2)
    slow = size // fast
    if fast == 1 or slow % 2:
        return list(range(size))
    cells = [(z, 0) for z in range(slow)]
    for step, z in enumerate(range(slow - 1, -1, -1)):
        ys = range(1, fast) if step % 2 == 0 else range(fast - 1, 0, -1)
        cells += [(z, y) for y in ys]
    return [z * fast + y for z, y in cells]


def ring_fits(ranks, heads):
    if ranks % 2 or ranks < 4 or ranks % heads or heads & (heads - 1):
        return False
    order, per_head = ring_order(ranks), ranks // heads
    return all(
        order[p - k] // per_head != order[(p + k) % ranks] // per_head
        for p in range(ranks)
        for k in range(1, ranks // 2)
    )


def slot_for(info, loads, width, bundles, requester, owner):
    pick = jnp.int32(0)
    for j in range(bundles):
        hit = info[requester * width + j] == owner
        pick = jnp.where(hit, info[requester * width + bundles + j], pick)
    return lax.rem(pick, loads[owner])


def pack_kernel(info, loads, place, lat_ref, rope_ref, out_ref):
    rows = lat_ref.shape[1]
    out_ref[0, :rows, :] = lat_ref[0]
    out_ref[0, rows:, :] = rope_ref[0]


def pack(info, loads, place, cache_latent, cache_rope, ranks, heads, width, bundles):
    rows = cache_latent.shape[1] // heads
    dims = cache_rope.shape[1] // heads
    wide = cache_latent.shape[2]

    def source(i, info, loads, place):
        return slot_for(info, loads, width, bundles, i, place[0]), place[1], 0

    return pl.pallas_call(
        pack_kernel,
        out_shape=jax.ShapeDtypeStruct((ranks, rows + dims, wide), cache_latent.dtype),
        grid_spec=pltpu.PrefetchScalarGridSpec(
            num_scalar_prefetch=3,
            grid=(ranks,),
            in_specs=[pl.BlockSpec((1, rows, wide), source), pl.BlockSpec((1, dims, wide), source)],
            out_specs=pl.BlockSpec((1, rows + dims, wide), lambda i, *_: (i, 0, 0)),
        ),
        name="pack",
    )(info, loads, place, cache_latent, cache_rope)


def attend_kernel(
    heads, width, bundles, scale, block, info, loads, place, q_ref, qr_ref, *refs
):
    parts = refs[:heads]
    w_ref, out_ref, lat, rope, mixed = refs[heads:]
    b = pl.program_id(0)
    rows = lat.shape[0] // heads
    dims = rope.shape[0] // heads
    for m in range(heads):
        at = jnp.bitwise_xor(place[1], m)
        lat[pl.ds(pl.multiple_of(at * rows, rows), rows), :] = parts[m][0, :rows, :]
        rope[pl.ds(pl.multiple_of(at * dims, dims), dims), :] = parts[m][0, rows:, :]
    base = place[0] * width
    owner = info[base + b]
    slot = lax.rem(info[base + bundles + b], loads[owner])
    length = info[owner * width + 2 * bundles + slot]
    total_rows = q_ref.shape[1]
    live = lax.broadcasted_iota(jnp.int32, (block, lat.shape[0]), 1) < length
    for i in range(total_rows // block):
        at = slice(i * block, (i + 1) * block)
        s = lax.dot_general(
            q_ref[0, at, :], lat[...], (((1,), (1,)), ((), ())), preferred_element_type=jnp.float32
        )
        s = s + jnp.dot(qr_ref[0, at, :], rope[...], preferred_element_type=jnp.float32)
        s = jnp.where(live, s * scale, -1e30)
        w = jnp.exp(s - jnp.max(s, axis=1, keepdims=True))
        w = w * (1.0 / jnp.sum(w, axis=1, keepdims=True))
        o = jnp.dot(w.astype(jnp.bfloat16), lat[...], preferred_element_type=jnp.float32)
        for c in range(mixed.shape[0]):
            piece = o[:, c * 128 : (c + 1) * 128]
            mixed[c, pl.ds(b * total_rows + i * block, block), :] = piece

    @pl.when(b == pl.num_programs(0) - 1)
    def _():
        local_heads, _, value_width = w_ref.shape
        n = mixed.shape[1] // local_heads
        for h in range(local_heads):
            x = jnp.concatenate(
                [mixed[c, pl.ds(h, n, stride=local_heads), :] for c in range(mixed.shape[0])], axis=1
            ).astype(jnp.bfloat16)
            v = jnp.dot(x, w_ref[h], preferred_element_type=jnp.float32)
            out_ref[:, h * value_width : (h + 1) * value_width] = v.astype(jnp.bfloat16)


def attend(info, loads, place, q, qr, parts, w_uv, width, bundles):
    heads = len(parts)
    _, q_rows, wide = q.shape
    _, part_rows, _ = parts[0].shape
    local_heads, _, value_width = w_uv.shape
    dims = qr.shape[2] // heads
    rows = part_rows - dims
    row_count = bundles * q_rows // local_heads

    def theirs(b, info, loads, place):
        return info[place[0] * width + b], 0, 0

    block = math.gcd(q_rows, 128)
    return pl.pallas_call(
        functools.partial(
            attend_kernel, heads, width, bundles, 1.0 / math.sqrt(VD + ROPE), block
        ),
        out_shape=jax.ShapeDtypeStruct((row_count, local_heads * value_width), jnp.bfloat16),
        grid_spec=pltpu.PrefetchScalarGridSpec(
            num_scalar_prefetch=3,
            grid=(bundles,),
            in_specs=[
                pl.BlockSpec((1, q_rows, wide), lambda b, *_: (b, 0, 0)),
                pl.BlockSpec((1, q_rows, qr.shape[2]), lambda b, *_: (b, 0, 0)),
            ]
            + [pl.BlockSpec((1, part_rows, wide), theirs)] * heads
            + [pl.BlockSpec(w_uv.shape, lambda b, *_: (0, 0, 0))],
            out_specs=pl.BlockSpec((row_count, local_heads * value_width), lambda b, *_: (0, 0)),
            scratch_shapes=[
                pltpu.VMEM((rows * heads, wide), jnp.bfloat16),
                pltpu.VMEM((dims * heads, wide), jnp.bfloat16),
                pltpu.VMEM((wide // 128, bundles * q_rows, 128), jnp.float32),
            ],
        ),
        name="attend",
    )(info, loads, place, q, qr, *parts, w_uv)


def local_general(
    q_latent, q_rope, cache_latent, cache_rope, lengths, loads, owner_rank, owner_pick, w_uv, w_out
):
    ranks = lax.axis_size("dp")
    heads = lax.axis_size("head")
    me = lax.axis_index("dp")
    head = lax.axis_index("head")
    bundles = owner_rank.shape[0]
    roll_count = q_latent.shape[0] // bundles
    local_heads = w_uv.shape[0]
    place = jnp.stack([me, head]).astype(jnp.int32)

    facts = jnp.concatenate([owner_rank, owner_pick, lengths])
    width = 32
    facts = jnp.pad(facts, (0, width - facts.shape[0]))
    info = lax.all_to_all(
        jnp.broadcast_to(facts[None], (ranks, width)), "dp", split_axis=0, concat_axis=0, tiled=True
    ).reshape(-1)
    q = q_latent.reshape(bundles, roll_count * local_heads, -1)
    qr = q_rope.reshape(bundles, roll_count * local_heads, -1)

    packed = pack(info, loads, place, cache_latent, cache_rope, ranks, heads, width, bundles)
    mine = lax.all_to_all(packed, "dp", split_axis=0, concat_axis=0, tiled=True)
    parts = [mine]
    bit = heads // 2
    found = {0: mine}
    while bit:
        pairs = [(i, i ^ bit) for i in range(heads)]
        for m in list(found):
            found[m ^ bit] = lax.ppermute(found[m], "head", pairs)
        bit //= 2
    parts = [found[m] for m in range(heads)]
    values = attend(info, loads, place, q, qr, parts, w_uv, width, bundles)

    order = ring_order(ranks)
    ahead = [(order[i], order[(i + 1) % ranks]) for i in range(ranks)]
    behind = [(b, a) for a, b in ahead]
    half = values.shape[1] // 2

    def project(x):
        return jnp.dot(x, w_out, preferred_element_type=jnp.float32).astype(jnp.bfloat16)

    partial = {0: project(values)}
    fore = back = values
    for step in range(1, (ranks + 1) // 2):
        fore = lax.ppermute(fore, "dp", ahead)
        back = lax.ppermute(back, "dp", behind)
        both = project(jnp.concatenate([fore, back], axis=0))
        partial[-step] = both[: values.shape[0]]
        partial[step] = both[values.shape[0] :]
    if ranks % 2 == 0:
        left = lax.ppermute(fore[:, :half], "dp", ahead)
        right = lax.ppermute(back[:, half:], "dp", behind)
        partial[ranks // 2] = project(jnp.concatenate([left, right], axis=1))
    stacked = jnp.stack([partial[k if 2 * k <= ranks else k - ranks] for k in range(ranks)])
    position = [0] * ranks
    for i, r in enumerate(order):
        position[r] = i
    position = jnp.asarray(position, jnp.int32)
    by_rank = stacked[(position - position[me]) % ranks]
    shares = by_rank.reshape(heads, -1, w_out.shape[1])
    got = lax.all_to_all(shares, "head", split_axis=0, concat_axis=0, tiled=True)
    return jnp.sum(got.astype(jnp.float32), axis=0).astype(jnp.bfloat16)


def in_hbm(x):
    return pltpu.with_memory_space_constraint(x, pltpu.MemorySpace.HBM)


def ring_tables(ranks):
    order = ring_order(ranks)
    where = [order.index(r) for r in range(ranks)]
    offsets = [0]
    for k in range(1, ranks // 2):
        offsets += [-k, k]
    offsets.append(ranks // 2)
    seen = [[order[(where[r] + o) % ranks] for o in offsets] for r in range(ranks)]
    return order, where, offsets, seen


BUNDLE, SLOT, TARGET, OWNER, PLACE, PLAN_ROWS = 0, 1, 2, 3, 4, 8


def chunk_plans(ranks):
    middle = ranks // 2
    return {
        "p": [list(range(middle - 1)), [middle - 1]],
        "s": [list(range(middle, ranks - 1)), [ranks - 1]],
    }


def plan_kernel(per_head, seen, owner_rank, owner_pick, loads, table):
    ranks = seen.shape[1]
    me, head = lax.axis_index("dp"), lax.axis_index("head")
    table[PLACE, 0] = me
    table[PLACE, 1] = head
    for c in range(ranks):
        owner = seen[me, c]
        bundle, pick = jnp.int32(0), jnp.int32(0)
        for b in range(owner_rank.shape[0]):
            hit = owner_rank[b] == owner
            bundle = jnp.where(hit, b, bundle)
            pick = jnp.where(hit, owner_pick[b], pick)
        table[BUNDLE, c] = bundle
        table[SLOT, c] = lax.rem(pick, loads[owner])
        table[TARGET, c] = lax.div(owner, per_head)
        table[OWNER, c] = owner


def plan_of(seen, owner_rank, owner_pick, loads, per_head):
    smem = pl.BlockSpec(memory_space=pltpu.MemorySpace.SMEM)
    return pl.pallas_call(
        functools.partial(plan_kernel, per_head),
        out_shape=jax.ShapeDtypeStruct((PLAN_ROWS, seen.shape[1]), jnp.int32),
        in_specs=[smem] * 4,
        out_specs=smem,
        name="plan",
    )(seen, owner_rank, owner_pick, loads)


def payload_kernel(lat, rope, out, sems):
    head = lax.axis_index("head")
    dims = rope.shape[1] * (out.shape[1]) // (rope.shape[1] + lat.shape[1])
    rows = out.shape[1] - dims
    copies = [
        pltpu.make_async_copy(
            lat.at[:, pl.ds(pl.multiple_of(head * rows, rows), rows), :],
            out.at[:, pl.ds(0, rows), :],
            sems.at[0],
        ),
        pltpu.make_async_copy(
            rope.at[:, pl.ds(pl.multiple_of(head * dims, dims), dims), :],
            out.at[:, pl.ds(rows, dims), :],
            sems.at[1],
        ),
    ]
    for copy in copies:
        copy.start()
    for copy in copies:
        copy.wait()


def payload_of(cache_latent, cache_rope, heads):
    slots, positions, wide = cache_latent.shape
    rows = (positions + cache_rope.shape[1]) // heads
    return pl.pallas_call(
        payload_kernel,
        out_shape=jax.ShapeDtypeStruct((slots, rows, wide), cache_latent.dtype),
        in_specs=[pl.BlockSpec(memory_space=pl.ANY)] * 2,
        out_specs=pl.BlockSpec(memory_space=pltpu.MemorySpace.VMEM),
        scratch_shapes=[pltpu.SemaphoreType.DMA((2,))],
        compiler_params=pltpu.CompilerParams(vmem_limit_bytes=4 * 2**20),
        name="payload",
    )(in_hbm(cache_latent), in_hbm(cache_rope))


def upper(rows):
    return (rows // 2 + 15) // 16 * 16


def relay_kernel(bundles, offsets, table, info, loads, seen, fore, back, *outs):
    chosen, sends = outs[0], outs[1:]
    me = table[PLACE, 0]
    last = len(offsets) // 2
    rows = fore.shape[1]
    for side, (way, arrived, out) in enumerate(((1, fore, sends[0]), (-1, back, sends[1]))):
        chosen[side] = arrived[table[SLOT, offsets.index(-way)]]
        owner = seen[me, offsets.index(-way)]
        for d in range(2, last + 1):
            asker = seen[me, offsets.index(way * (d - 1))]
            pick = jnp.int32(0)
            for b in range(bundles):
                hit = info[asker, 0, b] == owner
                pick = jnp.where(hit, info[asker, 0, bundles + b], pick)
            slot = lax.rem(pick, loads[owner])
            start = (d - 2) * rows
            if d < last:
                out[pl.ds(start, rows), :] = arrived[slot]
            elif way == 1:
                out[pl.ds(start, upper(rows)), :] = arrived[slot, : upper(rows), :]
            else:
                out[pl.ds(start, rows - upper(rows)), :] = arrived[slot, upper(rows) :, :]


def relay(table, info, loads, seen, bundles, offsets, fore, back):
    _, rows, wide = fore.shape
    full = (len(offsets) // 2 - 2) * rows
    vmem = pl.BlockSpec(memory_space=pltpu.MemorySpace.VMEM)
    smem = pl.BlockSpec(memory_space=pltpu.MemorySpace.SMEM)
    return pl.pallas_call(
        functools.partial(relay_kernel, bundles, offsets),
        out_shape=[
            jax.ShapeDtypeStruct((2, rows, wide), fore.dtype),
            jax.ShapeDtypeStruct((full + upper(rows), wide), fore.dtype),
            jax.ShapeDtypeStruct((full + rows - upper(rows), wide), fore.dtype),
        ],
        in_specs=[smem] * 4 + [vmem] * 2,
        out_specs=[vmem] * 3,
        compiler_params=pltpu.CompilerParams(vmem_limit_bytes=6 * 2**20),
        name="relay",
    )(table, info, loads, seen, fore, back)


def join_kernel(rows, fore, back, out):
    if out.shape[0] == 2:
        out[0] = fore[:rows, :]
        out[1] = back[:rows, :]
    else:
        out[0, : fore.shape[0], :] = fore[...]
        out[0, fore.shape[0] :, :] = back[...]


def join(count, rows, fore, back):
    vmem = pl.BlockSpec(memory_space=pltpu.MemorySpace.VMEM)
    return pl.pallas_call(
        functools.partial(join_kernel, rows),
        out_shape=jax.ShapeDtypeStruct((count, rows, fore.shape[1]), fore.dtype),
        in_specs=[vmem] * 2,
        out_specs=vmem,
        compiler_params=pltpu.CompilerParams(vmem_limit_bytes=4 * 2**20),
        name="join",
    )(fore, back)


def slots_kernel(plan, own, indices, bundles, final, scale, table, info, *refs):
    count, heads = len(plan), len(indices[0])
    refs = list(refs)
    q_ref, qr_ref, w_hbm = refs.pop(0), refs.pop(0), refs.pop(0)
    w_ref = w_hbm
    if count > 1:
        w_ref, w_sem = refs.pop(-2), refs.pop(-1)
        w_copy = pltpu.make_async_copy(w_hbm, w_ref, w_sem)
        w_copy.start()
    if own:
        full_lat, full_rope = refs.pop(0), refs.pop(0)
    parts = [[(refs.pop(0), index) for index in slot] for slot in indices]
    lat, rope, mixed = refs.pop(-3), refs.pop(-2), refs.pop(-1)
    if own:
        own_lat, own_rope, sems = refs.pop(-3), refs.pop(-2), refs.pop(-1)
        slot = table[SLOT, plan[0]]
        copies = [
            pltpu.make_async_copy(full_lat.at[slot], own_lat, sems.at[0]),
            pltpu.make_async_copy(full_rope.at[slot], own_rope, sems.at[1]),
        ]
        for copy in copies:
            copy.start()
    into = refs.pop(-1) if final else None
    out_ref = refs.pop(-1)
    earlier = refs
    total_rows = q_ref.shape[1]
    rows = lat.shape[0] // heads
    dims = rope.shape[0] // heads

    def bundle(i, _):
        j = lax.rem(i + own, count)
        for at in range(count):

            @pl.when(j == at)
            def _():
                if own and at == 0:
                    for copy in copies:
                        copy.wait()
                    lat[...] = own_lat[...]
                    rope[...] = own_rope[...]
                    return
                for m, (part, index) in enumerate(parts[at - own]):
                    to = jnp.bitwise_xor(table[PLACE, 1], m)
                    lat[pl.ds(pl.multiple_of(to * rows, rows), rows), :] = part[index, :rows, :]
                    rope[pl.ds(pl.multiple_of(to * dims, dims), dims), :] = part[index, rows:, :]

        column = plan[0] + j
        length = info[table[OWNER, column], 0, 2 * bundles + table[SLOT, column]]
        b = table[BUNDLE, column]
        past = lax.broadcasted_iota(jnp.int32, (1, lat.shape[0]), 1) >= length
        s = lax.dot_general(
            q_ref[b], lat[...], (((1,), (1,)), ((), ())), preferred_element_type=jnp.float32
        )
        s = s + jnp.dot(qr_ref[b], rope[...], preferred_element_type=jnp.float32)
        s = s + jnp.where(past, -1e30, 0.0)
        w = jnp.exp((s - jnp.max(s, axis=1, keepdims=True)) * scale)
        w = w * (1.0 / jnp.sum(w, axis=1, keepdims=True))
        o = jnp.dot(w.astype(jnp.bfloat16), lat[...], preferred_element_type=jnp.float32)
        start = pl.multiple_of(j * total_rows, total_rows)
        for c in range(mixed.shape[0]):
            mixed[c, pl.ds(start, total_rows), :] = o[:, c * 128 : (c + 1) * 128]
        return 0

    lax.fori_loop(0, count, bundle, 0)
    if count > 1:
        w_copy.wait()
    local_heads, _, value_width = w_ref.shape
    n = mixed.shape[1] // local_heads
    at = 0
    if final:
        for piece in earlier:
            into[pl.ds(at, piece.shape[0]), :] = piece[...]
            at += piece.shape[0]
    else:
        into = out_ref
    for h in range(local_heads):
        x = jnp.concatenate(
            [mixed[c, pl.ds(h, n, stride=local_heads), :] for c in range(mixed.shape[0])], axis=1
        ).astype(jnp.bfloat16)
        v = jnp.dot(x, w_ref[h], preferred_element_type=jnp.float32)
        into[pl.ds(at, n), h * value_width : (h + 1) * value_width] = v
    if final:
        out_ref[...] = into[...].astype(out_ref.dtype)


def attend_slots(plan, table, info, q, qr, full, parts, bundles, w_uv, earlier=None):
    own = 1 if full is not None else 0
    final = earlier is not None
    earlier = list(earlier or ())
    count, heads = len(plan), len(parts[0])
    _, q_rows, wide = q.shape
    dims = qr.shape[2]
    positions = (parts[0][0][0].shape[1] - dims // heads) * heads
    local_heads, _, value_width = w_uv.shape
    vmem = pl.BlockSpec(memory_space=pltpu.MemorySpace.VMEM)
    smem = pl.BlockSpec(memory_space=pltpu.MemorySpace.SMEM)
    fetch = count > 1
    args = [q, qr, in_hbm(w_uv) if fetch else w_uv]
    in_specs = [vmem, vmem, pl.BlockSpec(memory_space=pl.ANY) if fetch else vmem]
    if own:
        args += [in_hbm(x) for x in full]
        in_specs += [pl.BlockSpec(memory_space=pl.ANY)] * 2
    args += [array for slot in parts for array, _ in slot] + earlier
    in_specs += [vmem] * (len(args) - len(in_specs))
    done = sum(e.shape[0] for e in earlier) + count * q_rows // local_heads
    out_shape = (done, local_heads * value_width)
    caches = [pltpu.VMEM((positions, wide), jnp.bfloat16), pltpu.VMEM((dims, wide), jnp.bfloat16)]
    scratch = [pltpu.VMEM(out_shape, jnp.float32)] if final else []
    if own:
        scratch += caches + [pltpu.SemaphoreType.DMA((2,))]
    scratch += caches + [pltpu.VMEM((wide // 128, count * q_rows, 128), jnp.float32)]
    if fetch:
        scratch += [pltpu.VMEM(w_uv.shape, w_uv.dtype), pltpu.SemaphoreType.DMA]
    return pl.pallas_call(
        functools.partial(
            slots_kernel, plan, own, [[index for _, index in slot] for slot in parts], bundles,
            final, 1.0 / math.sqrt(VD + ROPE),
        ),
        out_shape=jax.ShapeDtypeStruct(out_shape, jnp.bfloat16 if final else jnp.float32),
        in_specs=[smem] * 2 + in_specs,
        out_specs=vmem,
        scratch_shapes=scratch,
        compiler_params=pltpu.CompilerParams(vmem_limit_bytes=(18 if fetch else 12) * 2**20),
        name="attend_slots",
    )(table, info, *args)


def add_in(table, per_head, columns, own, got, before, after):
    part = own[...]
    for g in got:
        part = part + g[...].astype(jnp.float32)
    for y in range(per_head):
        rank = table[PLACE, 1] * per_head + y
        hit = table[OWNER, columns[0]] == rank
        for c in columns[1:]:
            hit = hit | (table[OWNER, c] == rank)
        now = jnp.where(hit, part, 0.0)
        after[y] = now if before is None else before[y] + now


def settle_kernel(masks, per_head, columns, prev_columns, has_total, table, both, near, *refs):
    refs = list(refs)
    if prev_columns:
        prev_own, prev_got = refs.pop(0), [refs.pop(0) for _ in masks]
        before = refs.pop(0) if has_total else None
    block = both.shape[0] // len(columns)
    sends = 1 if len(columns) == 1 else len(masks)
    own = refs[sends]
    head = table[PLACE, 1]
    chip = both[...].astype(jnp.float32) + near[...].astype(jnp.float32)
    if len(columns) == 1:
        own[...] = chip
        refs[0][...] = chip.astype(jnp.bfloat16)
    else:
        for k, m in enumerate((0, *masks)):
            first = table[TARGET, columns[0]] == jnp.bitwise_xor(head, m)
            piece = jnp.where(first, chip[:block], chip[block:])
            if m == 0:
                own[...] = piece
            else:
                refs[k - 1][...] = piece.astype(jnp.bfloat16)
    if prev_columns:
        add_in(table, per_head, prev_columns, prev_own, prev_got, before, refs[sends + 1])


def settle_step(table, masks, per_head, columns, both, near, previous):
    n = both.shape[0] // len(columns)
    wide = both.shape[1]
    vmem = pl.BlockSpec(memory_space=pltpu.MemorySpace.VMEM)
    args, prev_columns, has_total = [both, near], None, False
    if previous is not None:
        prev_columns, prev_own, prev_got, total = previous
        has_total = total is not None
        args += [prev_own, *prev_got] + ([total] if has_total else [])
    sends = 1 if len(columns) == 1 else len(masks)
    out = [jax.ShapeDtypeStruct((n, wide), jnp.bfloat16)] * sends
    out.append(jax.ShapeDtypeStruct((n, wide), jnp.float32))
    if previous is not None:
        out.append(jax.ShapeDtypeStruct((per_head, n, wide), jnp.float32))
    outs = pl.pallas_call(
        functools.partial(settle_kernel, masks, per_head, columns, prev_columns, has_total),
        out_shape=out,
        in_specs=[pl.BlockSpec(memory_space=pltpu.MemorySpace.SMEM)] + [vmem] * len(args),
        out_specs=[vmem] * len(out),
        compiler_params=pltpu.CompilerParams(vmem_limit_bytes=4 * 2**20),
        name="settle",
    )(table, *args)
    to_send = list(outs[:sends]) * (1 if len(columns) > 1 else len(masks))
    return to_send, outs[sends], outs[sends + 1] if previous is not None else None


def finish_kernel(per_head, steps, roll, table, info, seen, before, *refs):
    *refs, out, total = refs
    each = len(refs) // len(steps)
    for i, columns in enumerate(steps):
        own, *got = refs[each * i : each * (i + 1)]
        add_in(table, per_head, columns, own, got, total if i else before, total)
    n = total.shape[1]
    slots = n // roll
    to = lax.broadcasted_iota(jnp.int32, (n, n), 0)
    source = lax.broadcasted_iota(jnp.int32, (n, n), 1)
    for y in range(per_head):
        rank = table[PLACE, 1] * per_head + y
        wanted = to
        for b in range(slots):
            place = jnp.int32(0)
            for c in range(slots):
                place = jnp.where(seen[rank, c] == info[rank, 0, b], c, place)
            inside = (to >= b * roll) & (to < (b + 1) * roll)
            wanted = jnp.where(inside, to + (place - b) * roll, wanted)
        pick = jnp.where(wanted == source, 1.0, 0.0).astype(jnp.bfloat16)
        moved = jnp.dot(pick, total[y].astype(jnp.bfloat16), preferred_element_type=jnp.float32)
        out[pl.ds(y * n, n), :] = moved.astype(out.dtype)


def finish(table, info, seen, per_head, roll, total, states):
    _, n, wide = total.shape
    steps = [state[0] for state in states]
    args = [x for _, own, got in states for x in (own, *got)]
    vmem = pl.BlockSpec(memory_space=pltpu.MemorySpace.VMEM)
    smem = pl.BlockSpec(memory_space=pltpu.MemorySpace.SMEM)
    return pl.pallas_call(
        functools.partial(finish_kernel, per_head, steps, roll),
        out_shape=jax.ShapeDtypeStruct((per_head * n, wide), jnp.bfloat16),
        in_specs=[smem] * 3 + [vmem] * (1 + len(args)),
        out_specs=vmem,
        scratch_shapes=[pltpu.VMEM((per_head, n, wide), jnp.float32)],
        compiler_params=pltpu.CompilerParams(vmem_limit_bytes=6 * 2**20),
        name="finish",
    )(table, info, seen, total, *args)


def local_ring(
    q_latent, q_rope, cache_latent, cache_rope, lengths, loads, owner_rank, owner_pick, w_uv, w_out
):
    ranks = lax.axis_size("dp")
    heads = lax.axis_size("head")
    bundles = owner_rank.shape[0]
    local_heads = w_uv.shape[0]
    roll_count = q_latent.shape[0] // bundles
    per_head = ranks // heads
    last = ranks // 2
    order, where, offsets, seen = ring_tables(ranks)
    seen = jnp.asarray(seen, jnp.int32)
    ahead = [(order[i], order[(i + 1) % ranks]) for i in range(ranks)]
    behind = [(b, a) for a, b in ahead]

    def move(x, pairs, axis="dp"):
        return lax.ppermute(x, axis, pairs)

    payload = payload_of(cache_latent, cache_rope, heads)
    fore, back = move(payload, ahead), move(payload, behind)
    facts = jnp.concatenate([owner_rank, owner_pick, lengths])
    width = 32
    facts = jnp.pad(facts, (0, width - facts.shape[0]))
    info = lax.all_to_all(
        jnp.broadcast_to(facts[None], (ranks, width)), "dp", split_axis=0, concat_axis=0, tiled=True
    )
    info = jnp.maximum(info, 0)[:, None]
    table = plan_of(seen, owner_rank, owner_pick, loads, per_head)
    q = q_latent.reshape(bundles, roll_count * local_heads, -1)
    qr = q_rope.reshape(bundles, roll_count * local_heads, -1)

    def share(chosen):
        found = {0: chosen}
        bit = heads // 2
        while bit:
            pairs = [(i, i ^ bit) for i in range(heads)]
            for m in list(found):
                found[m ^ bit] = move(found[m], pairs, "head")
            bit //= 2
        return [found[m] for m in range(heads)]

    rows = payload.shape[1]
    chosen, fore, back = relay(table, info, loads, seen, bundles, offsets, fore, back)
    groups = {}
    for k in range(1, last + 1):
        if k > 1:
            if k > 2:
                fore, back = fore[rows:], back[rows:]
            fore = move(fore, ahead)
            back = move(back, behind)
            chosen = join(2 if k < last else 1, rows, fore, back)
        parts = share(chosen)
        groups[2 * k - 1] = [(p, 0) for p in parts]
        if k < last:
            groups[2 * k] = [(p, 1) for p in parts]

    def attend(plan, full=None, earlier=None):
        return attend_slots(
            plan, table, info, q, qr, full, [groups[c] for c in plan[(full is not None) :]],
            bundles, w_uv, earlier,
        )

    chunks = []
    for tag, plans in chunk_plans(ranks).items():
        earlier = []
        for n, plan in enumerate(plans):
            full = (cache_latent, cache_rope) if plan[0] == 0 else None
            carried = earlier if n == len(plans) - 1 else None
            earlier.append(attend(plan, full, carried))
        chunks.append((tag, earlier[-1]))
    half = chunks[0][1].shape[1] // 2

    def project(pieces):
        product = jnp.dot(jnp.concatenate(pieces), w_out, preferred_element_type=jnp.float32)
        return product.astype(jnp.bfloat16)

    def target(p, column):
        return order[(where[p] + offsets[column]) % ranks] // per_head

    masks = list(range(2, heads, 2))

    def settle(columns, both, previous):
        near = move(both, [(i, i ^ 1) for i in range(heads)], "head")
        to_send, own, total = settle_step(table, masks, per_head, columns, both, near, previous)
        got = []
        for k, m in enumerate(masks):
            pairs = []
            for p in range(ranks):
                for t in sorted({target(p, c) for c in columns}):
                    pairs.append((p * heads + (t ^ m), p * heads + t))
            got.append(move(to_send[k], pairs, ("dp", "head")))
        return columns, own, got, total

    arrived = {}
    for tag, values in chunks:
        fore = back = values
        for k in range(1, last):
            if k == last - 1 and tag == chunks[-1][0]:
                break
            fore = move(fore, ahead)
            back = move(back, behind)
            arrived[tag, k] = fore, back
        fore_on, fore_end = fore[:, :half], fore[:, half:]
        back_on, back_end = back[:, half:], back[:, :half]
        if k == last - 1 and (tag, k) not in arrived:
            fore_on = move(fore_on, ahead)
            back_on = move(back_on, behind)
            fore_end = move(fore_end, ahead)
            back_end = move(back_end, behind)
            arrived[tag, k] = (
                jnp.concatenate([fore_on, fore_end], axis=1),
                jnp.concatenate([back_end, back_on], axis=1),
            )
        left = move(fore_on, ahead)
        right = move(back_on, behind)
        arrived[tag, last] = (jnp.concatenate([left, right], axis=1),)
    state = settle([0], project([values for _, values in chunks]), None)
    for k in range(1, last):
        pieces = [arrived[tag, k][side] for side in (0, 1) for tag, _ in chunks]
        state = settle([2 * k - 1, 2 * k], project(pieces), state)
    ends = project([arrived[tag, last][0] for tag, _ in chunks])
    *before, total = state
    *final, _ = settle([2 * last - 1], ends, None)
    return finish(table, info, seen, per_head, roll_count, total, [before, final])


def local(*args):
    ranks, heads = lax.axis_size("dp"), lax.axis_size("head")
    bundles = args[6].shape[0]
    if ranks == bundles and ring_fits(ranks, heads):
        return local_ring(*args)
    return local_general(*args)


def solution(mesh):
    in_specs = (
        P("dp", "head"),
        P("dp", "head"),
        P("dp", None, None),
        P("dp", None, None),
        P("dp"),
        P(),
        P("dp"),
        P("dp"),
        P("head", None, None),
        P("head", "dp"),
    )
    out_specs = P("head", "dp")
    return jax.shard_map(local, mesh=mesh, in_specs=in_specs, out_specs=out_specs, check_vma=False)
```

```python
import functools
import math

import jax
import jax.numpy as jnp
from jax import lax
from jax.experimental import pallas as pl
from jax.experimental.pallas import tpu as pltpu
from jax.sharding import PartitionSpec as P


ROPE = 64
VD = 128


def ring_order(size):
    fast = 1 << (max(size.bit_length() - 1, 0) // 2)
    slow = size // fast
    if fast == 1 or slow % 2:
        return list(range(size))
    cells = [(z, 0) for z in range(slow)]
    for step, z in enumerate(range(slow - 1, -1, -1)):
        ys = range(1, fast) if step % 2 == 0 else range(fast - 1, 0, -1)
        cells += [(z, y) for y in ys]
    return [z * fast + y for z, y in cells]


def ring_fits(ranks, heads):
    if ranks % 2 or ranks < 4 or ranks % heads or heads & (heads - 1):
        return False
    order, per_head = ring_order(ranks), ranks // heads
    return all(
        order[p - k] // per_head != order[(p + k) % ranks] // per_head
        for p in range(ranks)
        for k in range(1, ranks // 2)
    )


def slot_for(info, loads, width, bundles, requester, owner):
    pick = jnp.int32(0)
    for j in range(bundles):
        hit = info[requester * width + j] == owner
        pick = jnp.where(hit, info[requester * width + bundles + j], pick)
    return lax.rem(pick, loads[owner])


def pack_kernel(info, loads, place, lat_ref, rope_ref, out_ref):
    rows = lat_ref.shape[1]
    out_ref[0, :rows, :] = lat_ref[0]
    out_ref[0, rows:, :] = rope_ref[0]


def pack(info, loads, place, cache_latent, cache_rope, ranks, heads, width, bundles):
    rows = cache_latent.shape[1] // heads
    dims = cache_rope.shape[1] // heads
    wide = cache_latent.shape[2]

    def source(i, info, loads, place):
        return slot_for(info, loads, width, bundles, i, place[0]), place[1], 0

    return pl.pallas_call(
        pack_kernel,
        out_shape=jax.ShapeDtypeStruct((ranks, rows + dims, wide), cache_latent.dtype),
        grid_spec=pltpu.PrefetchScalarGridSpec(
            num_scalar_prefetch=3,
            grid=(ranks,),
            in_specs=[pl.BlockSpec((1, rows, wide), source), pl.BlockSpec((1, dims, wide), source)],
            out_specs=pl.BlockSpec((1, rows + dims, wide), lambda i, *_: (i, 0, 0)),
        ),
        name="pack",
    )(info, loads, place, cache_latent, cache_rope)


def attend_kernel(
    heads, width, bundles, scale, block, info, loads, place, q_ref, qr_ref, *refs
):
    parts = refs[:heads]
    w_ref, out_ref, lat, rope, mixed = refs[heads:]
    b = pl.program_id(0)
    rows = lat.shape[0] // heads
    dims = rope.shape[0] // heads
    for m in range(heads):
        at = jnp.bitwise_xor(place[1], m)
        lat[pl.ds(pl.multiple_of(at * rows, rows), rows), :] = parts[m][0, :rows, :]
        rope[pl.ds(pl.multiple_of(at * dims, dims), dims), :] = parts[m][0, rows:, :]
    base = place[0] * width
    owner = info[base + b]
    slot = lax.rem(info[base + bundles + b], loads[owner])
    length = info[owner * width + 2 * bundles + slot]
    total_rows = q_ref.shape[1]
    live = lax.broadcasted_iota(jnp.int32, (block, lat.shape[0]), 1) < length
    for i in range(total_rows // block):
        at = slice(i * block, (i + 1) * block)
        s = lax.dot_general(
            q_ref[0, at, :], lat[...], (((1,), (1,)), ((), ())), preferred_element_type=jnp.float32
        )
        s = s + jnp.dot(qr_ref[0, at, :], rope[...], preferred_element_type=jnp.float32)
        s = jnp.where(live, s * scale, -1e30)
        w = jnp.exp(s - jnp.max(s, axis=1, keepdims=True))
        w = w * (1.0 / jnp.sum(w, axis=1, keepdims=True))
        o = jnp.dot(w.astype(jnp.bfloat16), lat[...], preferred_element_type=jnp.float32)
        for c in range(mixed.shape[0]):
            piece = o[:, c * 128 : (c + 1) * 128]
            mixed[c, pl.ds(b * total_rows + i * block, block), :] = piece

    @pl.when(b == pl.num_programs(0) - 1)
    def _():
        local_heads, _, value_width = w_ref.shape
        n = mixed.shape[1] // local_heads
        for h in range(local_heads):
            x = jnp.concatenate(
                [mixed[c, pl.ds(h, n, stride=local_heads), :] for c in range(mixed.shape[0])], axis=1
            ).astype(jnp.bfloat16)
            v = jnp.dot(x, w_ref[h], preferred_element_type=jnp.float32)
            out_ref[:, h * value_width : (h + 1) * value_width] = v.astype(jnp.bfloat16)


def attend(info, loads, place, q, qr, parts, w_uv, width, bundles):
    heads = len(parts)
    _, q_rows, wide = q.shape
    _, part_rows, _ = parts[0].shape
    local_heads, _, value_width = w_uv.shape
    dims = qr.shape[2] // heads
    rows = part_rows - dims
    row_count = bundles * q_rows // local_heads

    def theirs(b, info, loads, place):
        return info[place[0] * width + b], 0, 0

    block = math.gcd(q_rows, 128)
    return pl.pallas_call(
        functools.partial(
            attend_kernel, heads, width, bundles, 1.0 / math.sqrt(VD + ROPE), block
        ),
        out_shape=jax.ShapeDtypeStruct((row_count, local_heads * value_width), jnp.bfloat16),
        grid_spec=pltpu.PrefetchScalarGridSpec(
            num_scalar_prefetch=3,
            grid=(bundles,),
            in_specs=[
                pl.BlockSpec((1, q_rows, wide), lambda b, *_: (b, 0, 0)),
                pl.BlockSpec((1, q_rows, qr.shape[2]), lambda b, *_: (b, 0, 0)),
            ]
            + [pl.BlockSpec((1, part_rows, wide), theirs)] * heads
            + [pl.BlockSpec(w_uv.shape, lambda b, *_: (0, 0, 0))],
            out_specs=pl.BlockSpec((row_count, local_heads * value_width), lambda b, *_: (0, 0)),
            scratch_shapes=[
                pltpu.VMEM((rows * heads, wide), jnp.bfloat16),
                pltpu.VMEM((dims * heads, wide), jnp.bfloat16),
                pltpu.VMEM((wide // 128, bundles * q_rows, 128), jnp.float32),
            ],
        ),
        name="attend",
    )(info, loads, place, q, qr, *parts, w_uv)


def local_general(
    q_latent, q_rope, cache_latent, cache_rope, lengths, loads, owner_rank, owner_pick, w_uv, w_out
):
    ranks = lax.axis_size("dp")
    heads = lax.axis_size("head")
    me = lax.axis_index("dp")
    head = lax.axis_index("head")
    bundles = owner_rank.shape[0]
    roll_count = q_latent.shape[0] // bundles
    local_heads = w_uv.shape[0]
    place = jnp.stack([me, head]).astype(jnp.int32)

    facts = jnp.concatenate([owner_rank, owner_pick, lengths])
    width = 32
    facts = jnp.pad(facts, (0, width - facts.shape[0]))
    info = lax.all_to_all(
        jnp.broadcast_to(facts[None], (ranks, width)), "dp", split_axis=0, concat_axis=0, tiled=True
    ).reshape(-1)
    q = q_latent.reshape(bundles, roll_count * local_heads, -1)
    qr = q_rope.reshape(bundles, roll_count * local_heads, -1)

    packed = pack(info, loads, place, cache_latent, cache_rope, ranks, heads, width, bundles)
    mine = lax.all_to_all(packed, "dp", split_axis=0, concat_axis=0, tiled=True)
    parts = [mine]
    bit = heads // 2
    found = {0: mine}
    while bit:
        pairs = [(i, i ^ bit) for i in range(heads)]
        for m in list(found):
            found[m ^ bit] = lax.ppermute(found[m], "head", pairs)
        bit //= 2
    parts = [found[m] for m in range(heads)]
    values = attend(info, loads, place, q, qr, parts, w_uv, width, bundles)

    order = ring_order(ranks)
    ahead = [(order[i], order[(i + 1) % ranks]) for i in range(ranks)]
    behind = [(b, a) for a, b in ahead]
    half = values.shape[1] // 2

    def project(x):
        return jnp.dot(x, w_out, preferred_element_type=jnp.float32).astype(jnp.bfloat16)

    partial = {0: project(values)}
    fore = back = values
    for step in range(1, (ranks + 1) // 2):
        fore = lax.ppermute(fore, "dp", ahead)
        back = lax.ppermute(back, "dp", behind)
        both = project(jnp.concatenate([fore, back], axis=0))
        partial[-step] = both[: values.shape[0]]
        partial[step] = both[values.shape[0] :]
    if ranks % 2 == 0:
        left = lax.ppermute(fore[:, :half], "dp", ahead)
        right = lax.ppermute(back[:, half:], "dp", behind)
        partial[ranks // 2] = project(jnp.concatenate([left, right], axis=1))
    stacked = jnp.stack([partial[k if 2 * k <= ranks else k - ranks] for k in range(ranks)])
    position = [0] * ranks
    for i, r in enumerate(order):
        position[r] = i
    position = jnp.asarray(position, jnp.int32)
    by_rank = stacked[(position - position[me]) % ranks]
    shares = by_rank.reshape(heads, -1, w_out.shape[1])
    got = lax.all_to_all(shares, "head", split_axis=0, concat_axis=0, tiled=True)
    return jnp.sum(got.astype(jnp.float32), axis=0).astype(jnp.bfloat16)


def in_hbm(x):
    return pltpu.with_memory_space_constraint(x, pltpu.MemorySpace.HBM)


def ring_tables(ranks):
    order = ring_order(ranks)
    where = [order.index(r) for r in range(ranks)]
    offsets = [0]
    for k in range(1, ranks // 2):
        offsets += [-k, k]
    offsets.append(ranks // 2)
    seen = [[order[(where[r] + o) % ranks] for o in offsets] for r in range(ranks)]
    return order, where, offsets, seen


BUNDLE, SLOT, TARGET, OWNER, PLACE, PLAN_ROWS = 0, 1, 2, 3, 4, 8


def chunk_plans(ranks):
    middle = ranks // 2
    return {
        "p": [list(range(middle - 1)), [middle - 1]],
        "s": [[c] for c in range(middle, ranks - 2)] + [[ranks - 2, ranks - 1]],
    }


def plan_kernel(per_head, seen, owner_rank, owner_pick, loads, table):
    ranks = seen.shape[1]
    me, head = lax.axis_index("dp"), lax.axis_index("head")
    table[PLACE, 0] = me
    table[PLACE, 1] = head
    for c in range(ranks):
        owner = seen[me, c]
        bundle, pick = jnp.int32(0), jnp.int32(0)
        for b in range(owner_rank.shape[0]):
            hit = owner_rank[b] == owner
            bundle = jnp.where(hit, b, bundle)
            pick = jnp.where(hit, owner_pick[b], pick)
        table[BUNDLE, c] = bundle
        table[SLOT, c] = lax.rem(pick, loads[owner])
        table[TARGET, c] = lax.div(owner, per_head)
        table[OWNER, c] = owner


def plan_of(seen, owner_rank, owner_pick, loads, per_head):
    smem = pl.BlockSpec(memory_space=pltpu.MemorySpace.SMEM)
    return pl.pallas_call(
        functools.partial(plan_kernel, per_head),
        out_shape=jax.ShapeDtypeStruct((PLAN_ROWS, seen.shape[1]), jnp.int32),
        in_specs=[smem] * 4,
        out_specs=smem,
        name="plan",
    )(seen, owner_rank, owner_pick, loads)


def payload_kernel(lat, rope, out, sems):
    head = lax.axis_index("head")
    dims = rope.shape[1] * (out.shape[1]) // (rope.shape[1] + lat.shape[1])
    rows = out.shape[1] - dims
    copies = [
        pltpu.make_async_copy(
            lat.at[:, pl.ds(pl.multiple_of(head * rows, rows), rows), :],
            out.at[:, pl.ds(0, rows), :],
            sems.at[0],
        ),
        pltpu.make_async_copy(
            rope.at[:, pl.ds(pl.multiple_of(head * dims, dims), dims), :],
            out.at[:, pl.ds(rows, dims), :],
            sems.at[1],
        ),
    ]
    for copy in copies:
        copy.start()
    for copy in copies:
        copy.wait()


def payload_of(cache_latent, cache_rope, heads):
    slots, positions, wide = cache_latent.shape
    rows = (positions + cache_rope.shape[1]) // heads
    return pl.pallas_call(
        payload_kernel,
        out_shape=jax.ShapeDtypeStruct((slots, rows, wide), cache_latent.dtype),
        in_specs=[pl.BlockSpec(memory_space=pl.ANY)] * 2,
        out_specs=pl.BlockSpec(memory_space=pltpu.MemorySpace.VMEM),
        scratch_shapes=[pltpu.SemaphoreType.DMA((2,))],
        compiler_params=pltpu.CompilerParams(vmem_limit_bytes=4 * 2**20),
        name="payload",
    )(in_hbm(cache_latent), in_hbm(cache_rope))


def upper(rows):
    return (rows // 2 + 15) // 16 * 16


def relay_kernel(bundles, offsets, table, info, loads, seen, fore, back, *outs):
    chosen, sends = outs[0], outs[1:]
    me = table[PLACE, 0]
    last = len(offsets) // 2
    rows = fore.shape[1]
    for side, (way, arrived, out) in enumerate(((1, fore, sends[0]), (-1, back, sends[1]))):
        chosen[side] = arrived[table[SLOT, offsets.index(-way)]]
        owner = seen[me, offsets.index(-way)]
        for d in range(2, last + 1):
            asker = seen[me, offsets.index(way * (d - 1))]
            pick = jnp.int32(0)
            for b in range(bundles):
                hit = info[asker, 0, b] == owner
                pick = jnp.where(hit, info[asker, 0, bundles + b], pick)
            slot = lax.rem(pick, loads[owner])
            start = (d - 2) * rows
            if d < last:
                out[pl.ds(start, rows), :] = arrived[slot]
            elif way == 1:
                out[pl.ds(start, upper(rows)), :] = arrived[slot, : upper(rows), :]
            else:
                out[pl.ds(start, rows - upper(rows)), :] = arrived[slot, upper(rows) :, :]


def relay(table, info, loads, seen, bundles, offsets, fore, back):
    _, rows, wide = fore.shape
    full = (len(offsets) // 2 - 2) * rows
    vmem = pl.BlockSpec(memory_space=pltpu.MemorySpace.VMEM)
    smem = pl.BlockSpec(memory_space=pltpu.MemorySpace.SMEM)
    return pl.pallas_call(
        functools.partial(relay_kernel, bundles, offsets),
        out_shape=[
            jax.ShapeDtypeStruct((2, rows, wide), fore.dtype),
            jax.ShapeDtypeStruct((full + upper(rows), wide), fore.dtype),
            jax.ShapeDtypeStruct((full + rows - upper(rows), wide), fore.dtype),
        ],
        in_specs=[smem] * 4 + [vmem] * 2,
        out_specs=[vmem] * 3,
        compiler_params=pltpu.CompilerParams(vmem_limit_bytes=6 * 2**20),
        name="relay",
    )(table, info, loads, seen, fore, back)


def join_kernel(rows, fore, back, out):
    if out.shape[0] == 2:
        out[0] = fore[:rows, :]
        out[1] = back[:rows, :]
    else:
        out[0, : fore.shape[0], :] = fore[...]
        out[0, fore.shape[0] :, :] = back[...]


def join(count, rows, fore, back):
    vmem = pl.BlockSpec(memory_space=pltpu.MemorySpace.VMEM)
    return pl.pallas_call(
        functools.partial(join_kernel, rows),
        out_shape=jax.ShapeDtypeStruct((count, rows, fore.shape[1]), fore.dtype),
        in_specs=[vmem] * 2,
        out_specs=vmem,
        compiler_params=pltpu.CompilerParams(vmem_limit_bytes=4 * 2**20),
        name="join",
    )(fore, back)


def slots_kernel(plan, own, indices, bundles, final, scale, table, info, *refs):
    count, heads = len(plan), len(indices[0])
    refs = list(refs)
    q_ref, qr_ref, w_hbm = refs.pop(0), refs.pop(0), refs.pop(0)
    w_ref = w_hbm
    if count > 1:
        w_ref, w_sem = refs.pop(-2), refs.pop(-1)
        w_copy = pltpu.make_async_copy(w_hbm, w_ref, w_sem)
        w_copy.start()
    if own:
        full_lat, full_rope = refs.pop(0), refs.pop(0)
    parts = [[(refs.pop(0), index) for index in slot] for slot in indices]
    lat, rope, mixed = refs.pop(-3), refs.pop(-2), refs.pop(-1)
    if own:
        own_lat, own_rope, sems = refs.pop(-3), refs.pop(-2), refs.pop(-1)
        slot = table[SLOT, plan[0]]
        copies = [
            pltpu.make_async_copy(full_lat.at[slot], own_lat, sems.at[0]),
            pltpu.make_async_copy(full_rope.at[slot], own_rope, sems.at[1]),
        ]
        for copy in copies:
            copy.start()
    into = refs.pop(-1) if final else None
    out_ref = refs.pop(-1)
    earlier = refs
    total_rows = q_ref.shape[1]
    rows = lat.shape[0] // heads
    dims = rope.shape[0] // heads

    def bundle(i, _):
        j = lax.rem(i + own, count)
        for at in range(count):

            @pl.when(j == at)
            def _():
                if own and at == 0:
                    for copy in copies:
                        copy.wait()
                    lat[...] = own_lat[...]
                    rope[...] = own_rope[...]
                    return
                for m, (part, index) in enumerate(parts[at - own]):
                    to = jnp.bitwise_xor(table[PLACE, 1], m)
                    lat[pl.ds(pl.multiple_of(to * rows, rows), rows), :] = part[index, :rows, :]
                    rope[pl.ds(pl.multiple_of(to * dims, dims), dims), :] = part[index, rows:, :]

        column = plan[0] + j
        length = info[table[OWNER, column], 0, 2 * bundles + table[SLOT, column]]
        b = table[BUNDLE, column]
        past = lax.broadcasted_iota(jnp.int32, (1, lat.shape[0]), 1) >= length
        s = lax.dot_general(
            q_ref[b], lat[...], (((1,), (1,)), ((), ())), preferred_element_type=jnp.float32
        )
        s = s + jnp.dot(qr_ref[b], rope[...], preferred_element_type=jnp.float32)
        s = s + jnp.where(past, -1e30, 0.0)
        w = jnp.exp((s - jnp.max(s, axis=1, keepdims=True)) * scale)
        w = w * (1.0 / jnp.sum(w, axis=1, keepdims=True))
        o = jnp.dot(w.astype(jnp.bfloat16), lat[...], preferred_element_type=jnp.float32)
        start = pl.multiple_of(j * total_rows, total_rows)
        for c in range(mixed.shape[0]):
            mixed[c, pl.ds(start, total_rows), :] = o[:, c * 128 : (c + 1) * 128]
        return 0

    lax.fori_loop(0, count, bundle, 0)
    if count > 1:
        w_copy.wait()
    local_heads, _, value_width = w_ref.shape
    n = mixed.shape[1] // local_heads
    at = 0
    if final:
        for piece in earlier:
            into[pl.ds(at, piece.shape[0]), :] = piece[...]
            at += piece.shape[0]
    else:
        into = out_ref
    for h in range(local_heads):
        x = jnp.concatenate(
            [mixed[c, pl.ds(h, n, stride=local_heads), :] for c in range(mixed.shape[0])], axis=1
        ).astype(jnp.bfloat16)
        v = jnp.dot(x, w_ref[h], preferred_element_type=jnp.float32)
        into[pl.ds(at, n), h * value_width : (h + 1) * value_width] = v
    if final:
        out_ref[...] = into[...].astype(out_ref.dtype)


def attend_slots(plan, table, info, q, qr, full, parts, bundles, w_uv, earlier=None):
    own = 1 if full is not None else 0
    final = earlier is not None
    earlier = list(earlier or ())
    count, heads = len(plan), len(parts[0])
    _, q_rows, wide = q.shape
    dims = qr.shape[2]
    positions = (parts[0][0][0].shape[1] - dims // heads) * heads
    local_heads, _, value_width = w_uv.shape
    vmem = pl.BlockSpec(memory_space=pltpu.MemorySpace.VMEM)
    smem = pl.BlockSpec(memory_space=pltpu.MemorySpace.SMEM)
    fetch = count > 1
    args = [q, qr, in_hbm(w_uv) if fetch else w_uv]
    in_specs = [vmem, vmem, pl.BlockSpec(memory_space=pl.ANY) if fetch else vmem]
    if own:
        args += [in_hbm(x) for x in full]
        in_specs += [pl.BlockSpec(memory_space=pl.ANY)] * 2
    args += [array for slot in parts for array, _ in slot] + earlier
    in_specs += [vmem] * (len(args) - len(in_specs))
    done = sum(e.shape[0] for e in earlier) + count * q_rows // local_heads
    out_shape = (done, local_heads * value_width)
    caches = [pltpu.VMEM((positions, wide), jnp.bfloat16), pltpu.VMEM((dims, wide), jnp.bfloat16)]
    scratch = [pltpu.VMEM(out_shape, jnp.float32)] if final else []
    if own:
        scratch += caches + [pltpu.SemaphoreType.DMA((2,))]
    scratch += caches + [pltpu.VMEM((wide // 128, count * q_rows, 128), jnp.float32)]
    if fetch:
        scratch += [pltpu.VMEM(w_uv.shape, w_uv.dtype), pltpu.SemaphoreType.DMA]
    return pl.pallas_call(
        functools.partial(
            slots_kernel, plan, own, [[index for _, index in slot] for slot in parts], bundles,
            final, 1.0 / math.sqrt(VD + ROPE),
        ),
        out_shape=jax.ShapeDtypeStruct(out_shape, jnp.bfloat16 if final else jnp.float32),
        in_specs=[smem] * 2 + in_specs,
        out_specs=vmem,
        scratch_shapes=scratch,
        compiler_params=pltpu.CompilerParams(vmem_limit_bytes=(18 if fetch else 12) * 2**20),
        name="attend_slots",
    )(table, info, *args)


def add_in(table, per_head, columns, own, got, before, after):
    part = own[...]
    for g in got:
        part = part + g[...].astype(jnp.float32)
    for y in range(per_head):
        rank = table[PLACE, 1] * per_head + y
        hit = table[OWNER, columns[0]] == rank
        for c in columns[1:]:
            hit = hit | (table[OWNER, c] == rank)
        now = jnp.where(hit, part, 0.0)
        after[y] = now if before is None else before[y] + now


def settle_kernel(masks, per_head, groups, prev_columns, has_total, table, *refs):
    refs = list(refs)
    sources = [(refs.pop(0), refs.pop(0)) for _ in groups]
    if prev_columns:
        prev_own, prev_got = refs.pop(0), [refs.pop(0) for _ in masks]
        before = refs.pop(0) if has_total else None
    head = table[PLACE, 1]
    for columns, (both, near) in zip(groups, sources):
        chip = both[...].astype(jnp.float32) + near[...].astype(jnp.float32)
        block = chip.shape[0] // len(columns)
        one = chip[:block]
        other = chip[block:] if len(columns) > 1 else None
        for m in masks if other is not None else masks[:1]:
            piece = one
            if other is not None:
                piece = jnp.where(table[TARGET, columns[0]] == jnp.bitwise_xor(head, m), one, other)
            refs.pop(0)[...] = piece.astype(jnp.bfloat16)
        if other is not None:
            one = jnp.where(table[TARGET, columns[0]] == head, one, other)
        refs.pop(0)[...] = one
    if prev_columns:
        add_in(table, per_head, prev_columns, prev_own, prev_got, before, refs.pop(0))


def settle_step(table, masks, per_head, groups, sources, previous):
    n = sources[0][0].shape[0] // len(groups[0])
    wide = sources[0][0].shape[1]
    vmem = pl.BlockSpec(memory_space=pltpu.MemorySpace.VMEM)
    args, prev_columns, has_total = [x for source in sources for x in source], None, False
    if previous is not None:
        prev_columns, prev_own, prev_got, total = previous
        has_total = total is not None
        args += [prev_own, *prev_got] + ([total] if has_total else [])
    out = []
    for columns in groups:
        sends = len(masks) if len(columns) > 1 else 1
        out += [jax.ShapeDtypeStruct((n, wide), jnp.bfloat16)] * sends
        out.append(jax.ShapeDtypeStruct((n, wide), jnp.float32))
    if previous is not None:
        out.append(jax.ShapeDtypeStruct((per_head, n, wide), jnp.float32))
    outs = pl.pallas_call(
        functools.partial(settle_kernel, masks, per_head, groups, prev_columns, has_total),
        out_shape=out,
        in_specs=[pl.BlockSpec(memory_space=pltpu.MemorySpace.SMEM)] + [vmem] * len(args),
        out_specs=[vmem] * len(out),
        compiler_params=pltpu.CompilerParams(vmem_limit_bytes=4 * 2**20),
        name="settle",
    )(table, *args)
    outs = list(outs)
    states = []
    for columns in groups:
        sends = [outs.pop(0) for _ in (masks if len(columns) > 1 else masks[:1])]
        states.append((sends * (1 if len(columns) > 1 else len(masks)), outs.pop(0)))
    return states, outs.pop(0) if previous is not None else None


def finish_kernel(per_head, steps, roll, table, info, seen, before, *refs):
    *refs, out, total = refs
    each = len(refs) // len(steps)
    for i, columns in enumerate(steps):
        own, *got = refs[each * i : each * (i + 1)]
        add_in(table, per_head, columns, own, got, total if i else before, total)
    n = total.shape[1]
    slots = n // roll
    to = lax.broadcasted_iota(jnp.int32, (n, n), 0)
    source = lax.broadcasted_iota(jnp.int32, (n, n), 1)
    for y in range(per_head):
        rank = table[PLACE, 1] * per_head + y
        wanted = to
        for b in range(slots):
            place = jnp.int32(0)
            for c in range(slots):
                place = jnp.where(seen[rank, c] == info[rank, 0, b], c, place)
            inside = (to >= b * roll) & (to < (b + 1) * roll)
            wanted = jnp.where(inside, to + (place - b) * roll, wanted)
        pick = jnp.where(wanted == source, 1.0, 0.0).astype(jnp.bfloat16)
        moved = jnp.dot(pick, total[y].astype(jnp.bfloat16), preferred_element_type=jnp.float32)
        out[pl.ds(y * n, n), :] = moved.astype(out.dtype)


def finish(table, info, seen, per_head, roll, total, states):
    _, n, wide = total.shape
    steps = [state[0] for state in states]
    args = [x for _, own, got in states for x in (own, *got)]
    vmem = pl.BlockSpec(memory_space=pltpu.MemorySpace.VMEM)
    smem = pl.BlockSpec(memory_space=pltpu.MemorySpace.SMEM)
    return pl.pallas_call(
        functools.partial(finish_kernel, per_head, steps, roll),
        out_shape=jax.ShapeDtypeStruct((per_head * n, wide), jnp.bfloat16),
        in_specs=[smem] * 3 + [vmem] * (1 + len(args)),
        out_specs=vmem,
        scratch_shapes=[pltpu.VMEM((per_head, n, wide), jnp.float32)],
        compiler_params=pltpu.CompilerParams(vmem_limit_bytes=6 * 2**20),
        name="finish",
    )(table, info, seen, total, *args)


def local_ring(
    q_latent, q_rope, cache_latent, cache_rope, lengths, loads, owner_rank, owner_pick, w_uv, w_out
):
    ranks = lax.axis_size("dp")
    heads = lax.axis_size("head")
    bundles = owner_rank.shape[0]
    local_heads = w_uv.shape[0]
    roll_count = q_latent.shape[0] // bundles
    per_head = ranks // heads
    last = ranks // 2
    order, where, offsets, seen = ring_tables(ranks)
    seen = jnp.asarray(seen, jnp.int32)
    ahead = [(order[i], order[(i + 1) % ranks]) for i in range(ranks)]
    behind = [(b, a) for a, b in ahead]

    def move(x, pairs, axis="dp"):
        return lax.ppermute(x, axis, pairs)

    payload = payload_of(cache_latent, cache_rope, heads)
    fore, back = move(payload, ahead), move(payload, behind)
    facts = jnp.concatenate([owner_rank, owner_pick, lengths])
    width = 32
    facts = jnp.pad(facts, (0, width - facts.shape[0]))
    info = lax.all_to_all(
        jnp.broadcast_to(facts[None], (ranks, width)), "dp", split_axis=0, concat_axis=0, tiled=True
    )
    info = jnp.maximum(info, 0)[:, None]
    table = in_hbm(plan_of(seen, owner_rank, owner_pick, loads, per_head))
    q = q_latent.reshape(bundles, roll_count * local_heads, -1)
    qr = q_rope.reshape(bundles, roll_count * local_heads, -1)

    def share(chosen):
        found = {0: chosen}
        bit = heads // 2
        while bit:
            pairs = [(i, i ^ bit) for i in range(heads)]
            for m in list(found):
                found[m ^ bit] = move(found[m], pairs, "head")
            bit //= 2
        return [found[m] for m in range(heads)]

    rows = payload.shape[1]
    chosen, fore, back = relay(table, info, loads, seen, bundles, offsets, fore, back)
    groups = {}
    for k in range(1, last + 1):
        if k > 1:
            if k > 2:
                fore, back = fore[rows:], back[rows:]
            fore = move(fore, ahead)
            back = move(back, behind)
            chosen = join(2 if k < last else 1, rows, fore, back)
        parts = share(chosen)
        groups[2 * k - 1] = [(p, 0) for p in parts]
        if k < last:
            groups[2 * k] = [(p, 1) for p in parts]

    def attend(plan, full=None, earlier=None):
        return attend_slots(
            plan, table, info, q, qr, full, [groups[c] for c in plan[(full is not None) :]],
            bundles, w_uv, earlier,
        )

    chunks = []
    for tag, plans in chunk_plans(ranks).items():
        earlier = []
        for n, plan in enumerate(plans):
            full = (cache_latent, cache_rope) if plan[0] == 0 else None
            carried = earlier if n == len(plans) - 1 else None
            earlier.append(attend(plan, full, carried))
        chunks.append((tag, earlier[-1]))
    half = chunks[0][1].shape[1] // 2

    def project(pieces):
        product = jnp.dot(jnp.concatenate(pieces), w_out, preferred_element_type=jnp.float32)
        return product.astype(jnp.bfloat16)

    def target(p, column):
        return order[(where[p] + offsets[column]) % ranks] // per_head

    masks = list(range(2, heads, 2))

    def settle(groups, products, previous):
        cores = [(i, i ^ 1) for i in range(heads)]
        sources = [(both, move(both, cores, "head")) for both in products]
        made, total = settle_step(table, masks, per_head, groups, sources, previous)
        states = []
        for columns, (to_send, own) in zip(groups, made):
            got = []
            for k, m in enumerate(masks):
                pairs = []
                for p in range(ranks):
                    for t in sorted({target(p, c) for c in columns}):
                        pairs.append((p * heads + (t ^ m), p * heads + t))
                got.append(move(to_send[k], pairs, ("dp", "head")))
            states.append((columns, own, got))
        return states, total

    arrived = {}
    for tag, values in chunks:
        fore = back = values
        for k in range(1, last):
            if k == last - 1 and tag == chunks[-1][0]:
                break
            fore = move(fore, ahead)
            back = move(back, behind)
            arrived[tag, k] = fore, back
        fore_on, fore_end = fore[:, :half], fore[:, half:]
        back_on, back_end = back[:, half:], back[:, :half]
        if k == last - 1 and (tag, k) not in arrived:
            fore_on = move(fore_on, ahead)
            back_on = move(back_on, behind)
            fore_end = move(fore_end, ahead)
            back_end = move(back_end, behind)
            arrived[tag, k] = (
                jnp.concatenate([fore_on, fore_end], axis=1),
                jnp.concatenate([back_end, back_on], axis=1),
            )
        left = move(fore_on, ahead)
        right = move(back_on, behind)
        arrived[tag, last] = (jnp.concatenate([left, right], axis=1),)

    def pieces(k):
        return [arrived[tag, k][side] for side in range(2 if k < last else 1) for tag, _ in chunks]

    products = [project([values for _, values in chunks])]
    products += [project(pieces(k)) for k in range(1, last + 1)]
    (state,), total = settle([[0]], products[:1], None)
    for k in range(1, last - 1):
        columns = [2 * k - 1, 2 * k]
        (state,), total = settle([columns], products[k : k + 1], (*state, total))
    groups = [[2 * last - 3, 2 * last - 2], [2 * last - 1]]
    states, total = settle(groups, products[last - 1 :], (*state, total))
    return finish(table, info, seen, per_head, roll_count, total, states)


def local(*args):
    ranks, heads = lax.axis_size("dp"), lax.axis_size("head")
    bundles = args[6].shape[0]
    if ranks == bundles and ring_fits(ranks, heads):
        return local_ring(*args)
    return local_general(*args)


def solution(mesh):
    in_specs = (
        P("dp", "head"),
        P("dp", "head"),
        P("dp", None, None),
        P("dp", None, None),
        P("dp"),
        P(),
        P("dp"),
        P("dp"),
        P("head", None, None),
        P("head", "dp"),
    )
    out_specs = P("head", "dp")
    return jax.shard_map(local, mesh=mesh, in_specs=in_specs, out_specs=out_specs, check_vma=False)
```

```python
import functools
import math

import jax
import jax.numpy as jnp
from jax import lax
from jax.experimental import pallas as pl
from jax.experimental.pallas import tpu as pltpu
from jax.sharding import PartitionSpec as P


ROPE = 64
VD = 128


def ring_order(size):
    fast = 1 << (max(size.bit_length() - 1, 0) // 2)
    slow = size // fast
    if fast == 1 or slow % 2:
        return list(range(size))
    cells = [(z, 0) for z in range(slow)]
    for step, z in enumerate(range(slow - 1, -1, -1)):
        ys = range(1, fast) if step % 2 == 0 else range(fast - 1, 0, -1)
        cells += [(z, y) for y in ys]
    return [z * fast + y for z, y in cells]


def ring_fits(ranks, heads):
    if ranks % 2 or ranks < 4 or ranks % heads or heads & (heads - 1):
        return False
    order, per_head = ring_order(ranks), ranks // heads
    return all(
        order[p - k] // per_head != order[(p + k) % ranks] // per_head
        for p in range(ranks)
        for k in range(1, ranks // 2)
    )


def slot_for(info, loads, width, bundles, requester, owner):
    pick = jnp.int32(0)
    for j in range(bundles):
        hit = info[requester * width + j] == owner
        pick = jnp.where(hit, info[requester * width + bundles + j], pick)
    return lax.rem(pick, loads[owner])


def pack_kernel(info, loads, place, lat_ref, rope_ref, out_ref):
    rows = lat_ref.shape[1]
    out_ref[0, :rows, :] = lat_ref[0]
    out_ref[0, rows:, :] = rope_ref[0]


def pack(info, loads, place, cache_latent, cache_rope, ranks, heads, width, bundles):
    rows = cache_latent.shape[1] // heads
    dims = cache_rope.shape[1] // heads
    wide = cache_latent.shape[2]

    def source(i, info, loads, place):
        return slot_for(info, loads, width, bundles, i, place[0]), place[1], 0

    return pl.pallas_call(
        pack_kernel,
        out_shape=jax.ShapeDtypeStruct((ranks, rows + dims, wide), cache_latent.dtype),
        grid_spec=pltpu.PrefetchScalarGridSpec(
            num_scalar_prefetch=3,
            grid=(ranks,),
            in_specs=[pl.BlockSpec((1, rows, wide), source), pl.BlockSpec((1, dims, wide), source)],
            out_specs=pl.BlockSpec((1, rows + dims, wide), lambda i, *_: (i, 0, 0)),
        ),
        name="pack",
    )(info, loads, place, cache_latent, cache_rope)


def attend_kernel(
    heads, width, bundles, scale, block, info, loads, place, q_ref, qr_ref, *refs
):
    parts = refs[:heads]
    w_ref, out_ref, lat, rope, mixed = refs[heads:]
    b = pl.program_id(0)
    rows = lat.shape[0] // heads
    dims = rope.shape[0] // heads
    for m in range(heads):
        at = jnp.bitwise_xor(place[1], m)
        lat[pl.ds(pl.multiple_of(at * rows, rows), rows), :] = parts[m][0, :rows, :]
        rope[pl.ds(pl.multiple_of(at * dims, dims), dims), :] = parts[m][0, rows:, :]
    base = place[0] * width
    owner = info[base + b]
    slot = lax.rem(info[base + bundles + b], loads[owner])
    length = info[owner * width + 2 * bundles + slot]
    total_rows = q_ref.shape[1]
    live = lax.broadcasted_iota(jnp.int32, (block, lat.shape[0]), 1) < length
    for i in range(total_rows // block):
        at = slice(i * block, (i + 1) * block)
        s = lax.dot_general(
            q_ref[0, at, :], lat[...], (((1,), (1,)), ((), ())), preferred_element_type=jnp.float32
        )
        s = s + jnp.dot(qr_ref[0, at, :], rope[...], preferred_element_type=jnp.float32)
        s = jnp.where(live, s * scale, -1e30)
        w = jnp.exp(s - jnp.max(s, axis=1, keepdims=True))
        w = w * (1.0 / jnp.sum(w, axis=1, keepdims=True))
        o = jnp.dot(w.astype(jnp.bfloat16), lat[...], preferred_element_type=jnp.float32)
        for c in range(mixed.shape[0]):
            piece = o[:, c * 128 : (c + 1) * 128]
            mixed[c, pl.ds(b * total_rows + i * block, block), :] = piece

    @pl.when(b == pl.num_programs(0) - 1)
    def _():
        local_heads, _, value_width = w_ref.shape
        n = mixed.shape[1] // local_heads
        for h in range(local_heads):
            x = jnp.concatenate(
                [mixed[c, pl.ds(h, n, stride=local_heads), :] for c in range(mixed.shape[0])], axis=1
            ).astype(jnp.bfloat16)
            v = jnp.dot(x, w_ref[h], preferred_element_type=jnp.float32)
            out_ref[:, h * value_width : (h + 1) * value_width] = v.astype(jnp.bfloat16)


def attend(info, loads, place, q, qr, parts, w_uv, width, bundles):
    heads = len(parts)
    _, q_rows, wide = q.shape
    _, part_rows, _ = parts[0].shape
    local_heads, _, value_width = w_uv.shape
    dims = qr.shape[2] // heads
    rows = part_rows - dims
    row_count = bundles * q_rows // local_heads

    def theirs(b, info, loads, place):
        return info[place[0] * width + b], 0, 0

    block = math.gcd(q_rows, 128)
    return pl.pallas_call(
        functools.partial(
            attend_kernel, heads, width, bundles, 1.0 / math.sqrt(VD + ROPE), block
        ),
        out_shape=jax.ShapeDtypeStruct((row_count, local_heads * value_width), jnp.bfloat16),
        grid_spec=pltpu.PrefetchScalarGridSpec(
            num_scalar_prefetch=3,
            grid=(bundles,),
            in_specs=[
                pl.BlockSpec((1, q_rows, wide), lambda b, *_: (b, 0, 0)),
                pl.BlockSpec((1, q_rows, qr.shape[2]), lambda b, *_: (b, 0, 0)),
            ]
            + [pl.BlockSpec((1, part_rows, wide), theirs)] * heads
            + [pl.BlockSpec(w_uv.shape, lambda b, *_: (0, 0, 0))],
            out_specs=pl.BlockSpec((row_count, local_heads * value_width), lambda b, *_: (0, 0)),
            scratch_shapes=[
                pltpu.VMEM((rows * heads, wide), jnp.bfloat16),
                pltpu.VMEM((dims * heads, wide), jnp.bfloat16),
                pltpu.VMEM((wide // 128, bundles * q_rows, 128), jnp.float32),
            ],
        ),
        name="attend",
    )(info, loads, place, q, qr, *parts, w_uv)


def local_general(
    q_latent, q_rope, cache_latent, cache_rope, lengths, loads, owner_rank, owner_pick, w_uv, w_out
):
    ranks = lax.axis_size("dp")
    heads = lax.axis_size("head")
    me = lax.axis_index("dp")
    head = lax.axis_index("head")
    bundles = owner_rank.shape[0]
    roll_count = q_latent.shape[0] // bundles
    local_heads = w_uv.shape[0]
    place = jnp.stack([me, head]).astype(jnp.int32)

    facts = jnp.concatenate([owner_rank, owner_pick, lengths])
    width = 32
    facts = jnp.pad(facts, (0, width - facts.shape[0]))
    info = lax.all_to_all(
        jnp.broadcast_to(facts[None], (ranks, width)), "dp", split_axis=0, concat_axis=0, tiled=True
    ).reshape(-1)
    q = q_latent.reshape(bundles, roll_count * local_heads, -1)
    qr = q_rope.reshape(bundles, roll_count * local_heads, -1)

    packed = pack(info, loads, place, cache_latent, cache_rope, ranks, heads, width, bundles)
    mine = lax.all_to_all(packed, "dp", split_axis=0, concat_axis=0, tiled=True)
    parts = [mine]
    bit = heads // 2
    found = {0: mine}
    while bit:
        pairs = [(i, i ^ bit) for i in range(heads)]
        for m in list(found):
            found[m ^ bit] = lax.ppermute(found[m], "head", pairs)
        bit //= 2
    parts = [found[m] for m in range(heads)]
    values = attend(info, loads, place, q, qr, parts, w_uv, width, bundles)

    order = ring_order(ranks)
    ahead = [(order[i], order[(i + 1) % ranks]) for i in range(ranks)]
    behind = [(b, a) for a, b in ahead]
    half = values.shape[1] // 2

    def project(x):
        return jnp.dot(x, w_out, preferred_element_type=jnp.float32).astype(jnp.bfloat16)

    partial = {0: project(values)}
    fore = back = values
    for step in range(1, (ranks + 1) // 2):
        fore = lax.ppermute(fore, "dp", ahead)
        back = lax.ppermute(back, "dp", behind)
        both = project(jnp.concatenate([fore, back], axis=0))
        partial[-step] = both[: values.shape[0]]
        partial[step] = both[values.shape[0] :]
    if ranks % 2 == 0:
        left = lax.ppermute(fore[:, :half], "dp", ahead)
        right = lax.ppermute(back[:, half:], "dp", behind)
        partial[ranks // 2] = project(jnp.concatenate([left, right], axis=1))
    stacked = jnp.stack([partial[k if 2 * k <= ranks else k - ranks] for k in range(ranks)])
    position = [0] * ranks
    for i, r in enumerate(order):
        position[r] = i
    position = jnp.asarray(position, jnp.int32)
    by_rank = stacked[(position - position[me]) % ranks]
    shares = by_rank.reshape(heads, -1, w_out.shape[1])
    got = lax.all_to_all(shares, "head", split_axis=0, concat_axis=0, tiled=True)
    return jnp.sum(got.astype(jnp.float32), axis=0).astype(jnp.bfloat16)


def in_hbm(x):
    return pltpu.with_memory_space_constraint(x, pltpu.MemorySpace.HBM)


def ring_tables(ranks):
    order = ring_order(ranks)
    where = [order.index(r) for r in range(ranks)]
    offsets = [0]
    for k in range(1, ranks // 2):
        offsets += [-k, k]
    offsets.append(ranks // 2)
    seen = [[order[(where[r] + o) % ranks] for o in offsets] for r in range(ranks)]
    return order, where, offsets, seen


BUNDLE, SLOT, TARGET, OWNER, PLACE, PLAN_ROWS = 0, 1, 2, 3, 4, 8


def chunk_plans(ranks):
    middle = ranks // 2
    return {
        "p": [list(range(middle - 1)), [middle - 1]],
        "s": [[c] for c in range(middle, ranks - 2)] + [[ranks - 2, ranks - 1]],
    }


def plan_kernel(per_head, seen, owner_rank, owner_pick, loads, table):
    ranks = seen.shape[1]
    me, head = lax.axis_index("dp"), lax.axis_index("head")
    table[PLACE, 0] = me
    table[PLACE, 1] = head
    for c in range(ranks):
        owner = seen[me, c]
        bundle, pick = jnp.int32(0), jnp.int32(0)
        for b in range(owner_rank.shape[0]):
            hit = owner_rank[b] == owner
            bundle = jnp.where(hit, b, bundle)
            pick = jnp.where(hit, owner_pick[b], pick)
        table[BUNDLE, c] = bundle
        table[SLOT, c] = lax.rem(pick, loads[owner])
        table[TARGET, c] = lax.div(owner, per_head)
        table[OWNER, c] = owner


def plan_of(seen, owner_rank, owner_pick, loads, per_head):
    smem = pl.BlockSpec(memory_space=pltpu.MemorySpace.SMEM)
    return pl.pallas_call(
        functools.partial(plan_kernel, per_head),
        out_shape=jax.ShapeDtypeStruct((PLAN_ROWS, seen.shape[1]), jnp.int32),
        in_specs=[smem] * 4,
        out_specs=smem,
        name="plan",
    )(seen, owner_rank, owner_pick, loads)


def payload_kernel(lat, rope, out, sems):
    head = lax.axis_index("head")
    dims = rope.shape[1] * (out.shape[1]) // (rope.shape[1] + lat.shape[1])
    rows = out.shape[1] - dims
    copies = [
        pltpu.make_async_copy(
            lat.at[:, pl.ds(pl.multiple_of(head * rows, rows), rows), :],
            out.at[:, pl.ds(0, rows), :],
            sems.at[0],
        ),
        pltpu.make_async_copy(
            rope.at[:, pl.ds(pl.multiple_of(head * dims, dims), dims), :],
            out.at[:, pl.ds(rows, dims), :],
            sems.at[1],
        ),
    ]
    for copy in copies:
        copy.start()
    for copy in copies:
        copy.wait()


def payload_of(cache_latent, cache_rope, heads):
    slots, positions, wide = cache_latent.shape
    rows = (positions + cache_rope.shape[1]) // heads
    return pl.pallas_call(
        payload_kernel,
        out_shape=jax.ShapeDtypeStruct((slots, rows, wide), cache_latent.dtype),
        in_specs=[pl.BlockSpec(memory_space=pl.ANY)] * 2,
        out_specs=pl.BlockSpec(memory_space=pltpu.MemorySpace.VMEM),
        scratch_shapes=[pltpu.SemaphoreType.DMA((2,))],
        compiler_params=pltpu.CompilerParams(vmem_limit_bytes=4 * 2**20),
        name="payload",
    )(in_hbm(cache_latent), in_hbm(cache_rope))


def upper(rows):
    return (rows // 2 + 15) // 16 * 16


def relay_kernel(bundles, offsets, table, info, loads, seen, fore, back, *outs):
    chosen, sends = outs[0], outs[1:]
    me = table[PLACE, 0]
    last = len(offsets) // 2
    rows = fore.shape[1]
    for side, (way, arrived, out) in enumerate(((1, fore, sends[0]), (-1, back, sends[1]))):
        chosen[side] = arrived[table[SLOT, offsets.index(-way)]]
        owner = seen[me, offsets.index(-way)]
        for d in range(2, last + 1):
            asker = seen[me, offsets.index(way * (d - 1))]
            pick = jnp.int32(0)
            for b in range(bundles):
                hit = info[asker, 0, b] == owner
                pick = jnp.where(hit, info[asker, 0, bundles + b], pick)
            slot = lax.rem(pick, loads[owner])
            start = (d - 2) * rows
            if d < last:
                out[pl.ds(start, rows), :] = arrived[slot]
            elif way == 1:
                out[pl.ds(start, upper(rows)), :] = arrived[slot, : upper(rows), :]
            else:
                out[pl.ds(start, rows - upper(rows)), :] = arrived[slot, upper(rows) :, :]


def relay(table, info, loads, seen, bundles, offsets, fore, back):
    _, rows, wide = fore.shape
    full = (len(offsets) // 2 - 2) * rows
    vmem = pl.BlockSpec(memory_space=pltpu.MemorySpace.VMEM)
    smem = pl.BlockSpec(memory_space=pltpu.MemorySpace.SMEM)
    return pl.pallas_call(
        functools.partial(relay_kernel, bundles, offsets),
        out_shape=[
            jax.ShapeDtypeStruct((2, rows, wide), fore.dtype),
            jax.ShapeDtypeStruct((full + upper(rows), wide), fore.dtype),
            jax.ShapeDtypeStruct((full + rows - upper(rows), wide), fore.dtype),
        ],
        in_specs=[smem] * 4 + [vmem] * 2,
        out_specs=[vmem] * 3,
        compiler_params=pltpu.CompilerParams(vmem_limit_bytes=6 * 2**20),
        name="relay",
    )(table, info, loads, seen, fore, back)


def join_kernel(rows, fore, back, out):
    if out.shape[0] == 2:
        out[0] = fore[:rows, :]
        out[1] = back[:rows, :]
    else:
        out[0, : fore.shape[0], :] = fore[...]
        out[0, fore.shape[0] :, :] = back[...]


def join(count, rows, fore, back):
    vmem = pl.BlockSpec(memory_space=pltpu.MemorySpace.VMEM)
    return pl.pallas_call(
        functools.partial(join_kernel, rows),
        out_shape=jax.ShapeDtypeStruct((count, rows, fore.shape[1]), fore.dtype),
        in_specs=[vmem] * 2,
        out_specs=vmem,
        compiler_params=pltpu.CompilerParams(vmem_limit_bytes=4 * 2**20),
        name="join",
    )(fore, back)


def slots_kernel(plan, own, indices, bundles, final, scale, table, info, *refs):
    count, heads = len(plan), len(indices[0])
    refs = list(refs)
    q_ref, qr_ref, w_hbm = refs.pop(0), refs.pop(0), refs.pop(0)
    w_ref = w_hbm
    if count > 1:
        w_ref, w_sem = refs.pop(-2), refs.pop(-1)
        w_copy = pltpu.make_async_copy(w_hbm, w_ref, w_sem)
        w_copy.start()
    if own:
        full_lat, full_rope = refs.pop(0), refs.pop(0)
    parts = [[(refs.pop(0), index) for index in slot] for slot in indices]
    lat, rope, mixed = refs.pop(-3), refs.pop(-2), refs.pop(-1)
    if own:
        own_lat, own_rope, sems = refs.pop(-3), refs.pop(-2), refs.pop(-1)
        slot = table[SLOT, plan[0]]
        copies = [
            pltpu.make_async_copy(full_lat.at[slot], own_lat, sems.at[0]),
            pltpu.make_async_copy(full_rope.at[slot], own_rope, sems.at[1]),
        ]
        for copy in copies:
            copy.start()
    into = refs.pop(-1) if final else None
    out_ref = refs.pop(-1)
    earlier = refs
    total_rows = q_ref.shape[1]
    rows = lat.shape[0] // heads
    dims = rope.shape[0] // heads

    def bundle(i, _):
        j = lax.rem(i + own, count)
        for at in range(count):

            @pl.when(j == at)
            def _():
                if own and at == 0:
                    for copy in copies:
                        copy.wait()
                    lat[...] = own_lat[...]
                    rope[...] = own_rope[...]
                    return
                for m, (part, index) in enumerate(parts[at - own]):
                    to = jnp.bitwise_xor(table[PLACE, 1], m)
                    lat[pl.ds(pl.multiple_of(to * rows, rows), rows), :] = part[index, :rows, :]
                    rope[pl.ds(pl.multiple_of(to * dims, dims), dims), :] = part[index, rows:, :]

        column = plan[0] + j
        length = info[table[OWNER, column], 0, 2 * bundles + table[SLOT, column]]
        b = table[BUNDLE, column]
        past = lax.broadcasted_iota(jnp.int32, (1, lat.shape[0]), 1) >= length
        s = lax.dot_general(
            q_ref[b], lat[...], (((1,), (1,)), ((), ())), preferred_element_type=jnp.float32
        )
        s = s + jnp.dot(qr_ref[b], rope[...], preferred_element_type=jnp.float32)
        s = s + jnp.where(past, -1e30, 0.0)
        w = jnp.exp((s - jnp.max(s, axis=1, keepdims=True)) * scale)
        w = w * (1.0 / jnp.sum(w, axis=1, keepdims=True))
        o = jnp.dot(w.astype(jnp.bfloat16), lat[...], preferred_element_type=jnp.float32)
        start = pl.multiple_of(j * total_rows, total_rows)
        for c in range(mixed.shape[0]):
            mixed[c, pl.ds(start, total_rows), :] = o[:, c * 128 : (c + 1) * 128]
        return 0

    lax.fori_loop(0, count, bundle, 0)
    if count > 1:
        w_copy.wait()
    local_heads, _, value_width = w_ref.shape
    n = mixed.shape[1] // local_heads
    at = 0
    if final:
        for piece in earlier:
            into[pl.ds(at, piece.shape[0]), :] = piece[...]
            at += piece.shape[0]
    else:
        into = out_ref
    for h in range(local_heads):
        x = jnp.concatenate(
            [mixed[c, pl.ds(h, n, stride=local_heads), :] for c in range(mixed.shape[0])], axis=1
        ).astype(jnp.bfloat16)
        v = jnp.dot(x, w_ref[h], preferred_element_type=jnp.float32)
        into[pl.ds(at, n), h * value_width : (h + 1) * value_width] = v
    if final:
        out_ref[...] = into[...].astype(out_ref.dtype)


def attend_slots(plan, table, info, q, qr, full, parts, bundles, w_uv, earlier=None):
    own = 1 if full is not None else 0
    final = earlier is not None
    earlier = list(earlier or ())
    count, heads = len(plan), len(parts[0])
    _, q_rows, wide = q.shape
    dims = qr.shape[2]
    positions = (parts[0][0][0].shape[1] - dims // heads) * heads
    local_heads, _, value_width = w_uv.shape
    vmem = pl.BlockSpec(memory_space=pltpu.MemorySpace.VMEM)
    smem = pl.BlockSpec(memory_space=pltpu.MemorySpace.SMEM)
    fetch = count > 1
    args = [q, qr, in_hbm(w_uv) if fetch else w_uv]
    in_specs = [vmem, vmem, pl.BlockSpec(memory_space=pl.ANY) if fetch else vmem]
    if own:
        args += [in_hbm(x) for x in full]
        in_specs += [pl.BlockSpec(memory_space=pl.ANY)] * 2
    args += [array for slot in parts for array, _ in slot] + earlier
    in_specs += [vmem] * (len(args) - len(in_specs))
    done = sum(e.shape[0] for e in earlier) + count * q_rows // local_heads
    out_shape = (done, local_heads * value_width)
    caches = [pltpu.VMEM((positions, wide), jnp.bfloat16), pltpu.VMEM((dims, wide), jnp.bfloat16)]
    scratch = [pltpu.VMEM(out_shape, jnp.float32)] if final else []
    if own:
        scratch += caches + [pltpu.SemaphoreType.DMA((2,))]
    scratch += caches + [pltpu.VMEM((wide // 128, count * q_rows, 128), jnp.float32)]
    if fetch:
        scratch += [pltpu.VMEM(w_uv.shape, w_uv.dtype), pltpu.SemaphoreType.DMA]
    return pl.pallas_call(
        functools.partial(
            slots_kernel, plan, own, [[index for _, index in slot] for slot in parts], bundles,
            final, 1.0 / math.sqrt(VD + ROPE),
        ),
        out_shape=jax.ShapeDtypeStruct(out_shape, jnp.bfloat16 if final else jnp.float32),
        in_specs=[smem] * 2 + in_specs,
        out_specs=vmem,
        scratch_shapes=scratch,
        compiler_params=pltpu.CompilerParams(vmem_limit_bytes=(18 if fetch else 12) * 2**20),
        name="attend_slots",
    )(table, info, *args)


def add_in(table, per_head, columns, own, got, before, after):
    part = own[...]
    for g in got:
        part = part + g[...].astype(jnp.float32)
    for y in range(per_head):
        rank = table[PLACE, 1] * per_head + y
        hit = table[OWNER, columns[0]] == rank
        for c in columns[1:]:
            hit = hit | (table[OWNER, c] == rank)
        now = jnp.where(hit, part, 0.0)
        after[y] = now if before is None else before[y] + now


def settle_kernel(masks, per_head, groups, prev_columns, has_total, table, *refs):
    refs = list(refs)
    sources = [(refs.pop(0), refs.pop(0)) for _ in groups]
    if prev_columns:
        prev_own, prev_got = refs.pop(0), [refs.pop(0) for _ in masks]
        before = refs.pop(0) if has_total else None
    head = table[PLACE, 1]
    for columns, (both, near) in zip(groups, sources):
        chip = both[...].astype(jnp.float32) + near[...].astype(jnp.float32)
        block = chip.shape[0] // len(columns)
        one = chip[:block]
        other = chip[block:] if len(columns) > 1 else None
        for m in masks if other is not None else masks[:1]:
            piece = one
            if other is not None:
                piece = jnp.where(table[TARGET, columns[0]] == jnp.bitwise_xor(head, m), one, other)
            refs.pop(0)[...] = piece.astype(jnp.bfloat16)
        if other is not None:
            one = jnp.where(table[TARGET, columns[0]] == head, one, other)
        refs.pop(0)[...] = one
    if prev_columns:
        add_in(table, per_head, prev_columns, prev_own, prev_got, before, refs.pop(0))


def settle_step(table, masks, per_head, groups, sources, previous):
    n = sources[0][0].shape[0] // len(groups[0])
    wide = sources[0][0].shape[1]
    vmem = pl.BlockSpec(memory_space=pltpu.MemorySpace.VMEM)
    args, prev_columns, has_total = [x for source in sources for x in source], None, False
    if previous is not None:
        prev_columns, prev_own, prev_got, total = previous
        has_total = total is not None
        args += [prev_own, *prev_got] + ([total] if has_total else [])
    out = []
    for columns in groups:
        sends = len(masks) if len(columns) > 1 else 1
        out += [jax.ShapeDtypeStruct((n, wide), jnp.bfloat16)] * sends
        out.append(jax.ShapeDtypeStruct((n, wide), jnp.float32))
    if previous is not None:
        out.append(jax.ShapeDtypeStruct((per_head, n, wide), jnp.float32))
    outs = pl.pallas_call(
        functools.partial(settle_kernel, masks, per_head, groups, prev_columns, has_total),
        out_shape=out,
        in_specs=[pl.BlockSpec(memory_space=pltpu.MemorySpace.SMEM)] + [vmem] * len(args),
        out_specs=[vmem] * len(out),
        compiler_params=pltpu.CompilerParams(vmem_limit_bytes=4 * 2**20),
        name="settle",
    )(table, *args)
    outs = list(outs)
    states = []
    for columns in groups:
        sends = [outs.pop(0) for _ in (masks if len(columns) > 1 else masks[:1])]
        states.append((sends * (1 if len(columns) > 1 else len(masks)), outs.pop(0)))
    return states, outs.pop(0) if previous is not None else None


def finish_kernel(per_head, steps, roll, table, info, seen, before, *refs):
    *refs, out, total = refs
    each = len(refs) // len(steps)
    for i, columns in enumerate(steps):
        own, *got = refs[each * i : each * (i + 1)]
        add_in(table, per_head, columns, own, got, total if i else before, total)
    n = total.shape[1]
    slots = n // roll
    to = lax.broadcasted_iota(jnp.int32, (n, n), 0)
    source = lax.broadcasted_iota(jnp.int32, (n, n), 1)
    for y in range(per_head):
        rank = table[PLACE, 1] * per_head + y
        wanted = to
        for b in range(slots):
            place = jnp.int32(0)
            for c in range(slots):
                place = jnp.where(seen[rank, c] == info[rank, 0, b], c, place)
            inside = (to >= b * roll) & (to < (b + 1) * roll)
            wanted = jnp.where(inside, to + (place - b) * roll, wanted)
        pick = jnp.where(wanted == source, 1.0, 0.0).astype(jnp.bfloat16)
        moved = jnp.dot(pick, total[y].astype(jnp.bfloat16), preferred_element_type=jnp.float32)
        out[pl.ds(y * n, n), :] = moved.astype(out.dtype)


def finish(table, info, seen, per_head, roll, total, states):
    _, n, wide = total.shape
    steps = [state[0] for state in states]
    args = [x for _, own, got in states for x in (own, *got)]
    vmem = pl.BlockSpec(memory_space=pltpu.MemorySpace.VMEM)
    smem = pl.BlockSpec(memory_space=pltpu.MemorySpace.SMEM)
    return pl.pallas_call(
        functools.partial(finish_kernel, per_head, steps, roll),
        out_shape=jax.ShapeDtypeStruct((per_head * n, wide), jnp.bfloat16),
        in_specs=[smem] * 3 + [vmem] * (1 + len(args)),
        out_specs=vmem,
        scratch_shapes=[pltpu.VMEM((per_head, n, wide), jnp.float32)],
        compiler_params=pltpu.CompilerParams(vmem_limit_bytes=6 * 2**20),
        name="finish",
    )(table, info, seen, total, *args)


def local_ring(
    q_latent, q_rope, cache_latent, cache_rope, lengths, loads, owner_rank, owner_pick, w_uv, w_out
):
    ranks = lax.axis_size("dp")
    heads = lax.axis_size("head")
    bundles = owner_rank.shape[0]
    local_heads = w_uv.shape[0]
    roll_count = q_latent.shape[0] // bundles
    per_head = ranks // heads
    last = ranks // 2
    order, where, offsets, seen = ring_tables(ranks)
    seen = jnp.asarray(seen, jnp.int32)
    ahead = [(order[i], order[(i + 1) % ranks]) for i in range(ranks)]
    behind = [(b, a) for a, b in ahead]

    def move(x, pairs, axis="dp"):
        return lax.ppermute(x, axis, pairs)

    payload = payload_of(cache_latent, cache_rope, heads)
    fore, back = move(payload, ahead), move(payload, behind)
    facts = jnp.concatenate([owner_rank, owner_pick, lengths])
    width = 32
    facts = jnp.pad(facts, (0, width - facts.shape[0]))
    info = lax.all_to_all(
        jnp.broadcast_to(facts[None], (ranks, width)), "dp", split_axis=0, concat_axis=0, tiled=True
    )
    info = jnp.maximum(info, 0)[:, None]
    table = in_hbm(plan_of(seen, owner_rank, owner_pick, loads, per_head))
    q = q_latent.reshape(bundles, roll_count * local_heads, -1)
    qr = q_rope.reshape(bundles, roll_count * local_heads, -1)

    def share(chosen):
        found = {0: chosen}
        bit = heads // 2
        while bit:
            pairs = [(i, i ^ bit) for i in range(heads)]
            for m in list(found):
                found[m ^ bit] = move(found[m], pairs, "head")
            bit //= 2
        return [found[m] for m in range(heads)]

    rows = payload.shape[1]
    chosen, fore, back = relay(table, info, loads, seen, bundles, offsets, fore, back)
    groups = {}
    for k in range(1, last + 1):
        if k > 1:
            if k > 2:
                fore, back = fore[rows:], back[rows:]
            fore = move(fore, ahead)
            back = move(back, behind)
            chosen = join(2 if k < last else 1, rows, fore, back)
        parts = share(chosen)
        groups[2 * k - 1] = [(p, 0) for p in parts]
        if k < last:
            groups[2 * k] = [(p, 1) for p in parts]

    def attend(plan, full=None, earlier=None):
        return attend_slots(
            plan, table, info, q, qr, full, [groups[c] for c in plan[(full is not None) :]],
            bundles, w_uv, earlier,
        )

    chunks = []
    for tag, plans in chunk_plans(ranks).items():
        earlier = []
        for n, plan in enumerate(plans):
            full = (cache_latent, cache_rope) if plan[0] == 0 else None
            carried = earlier if n == len(plans) - 1 else None
            earlier.append(attend(plan, full, carried))
        chunks.append((tag, earlier[-1]))
    half = chunks[0][1].shape[1] // 2

    def project(pieces):
        product = jnp.dot(jnp.concatenate(pieces), w_out, preferred_element_type=jnp.float32)
        return product.astype(jnp.bfloat16)

    def target(p, column):
        return order[(where[p] + offsets[column]) % ranks] // per_head

    masks = list(range(2, heads, 2))

    def settle(groups, products, previous):
        cores = [(i, i ^ 1) for i in range(heads)]
        sources = [(both, move(both, cores, "head")) for both in products]
        made, total = settle_step(table, masks, per_head, groups, sources, previous)
        states = []
        for columns, (to_send, own) in zip(groups, made):
            got = []
            for k, m in enumerate(masks):
                pairs = []
                for p in range(ranks):
                    for t in sorted({target(p, c) for c in columns}):
                        pairs.append((p * heads + (t ^ m), p * heads + t))
                got.append(move(to_send[k], pairs, ("dp", "head")))
            states.append((columns, own, got))
        return states, total

    arrived = {}
    for tag, values in chunks:
        fore = back = values
        for k in range(1, last):
            if k == last - 1 and tag == chunks[-1][0]:
                break
            fore = move(fore, ahead)
            back = move(back, behind)
            arrived[tag, k] = fore, back
        fore_on, fore_end = fore[:, :half], fore[:, half:]
        back_on, back_end = back[:, half:], back[:, :half]
        if k == last - 1 and (tag, k) not in arrived:
            fore_on = move(fore_on, ahead)
            back_on = move(back_on, behind)
            fore_end = move(fore_end, ahead)
            back_end = move(back_end, behind)
            arrived[tag, k] = (
                jnp.concatenate([fore_on, fore_end], axis=1),
                jnp.concatenate([back_end, back_on], axis=1),
            )
        left = move(fore_on, ahead)
        right = move(back_on, behind)
        arrived[tag, last] = (jnp.concatenate([left, right], axis=1),)

    def pieces(k):
        return [arrived[tag, k][side] for side in range(2 if k < last else 1) for tag, _ in chunks]

    products = [project([values for _, values in chunks])]
    products += [project(pieces(k)) for k in range(1, last + 1)]
    (state,), total = settle([[0]], products[:1], None)
    for k in range(1, last - 1):
        columns = [2 * k - 1, 2 * k]
        (state,), total = settle([columns], products[k : k + 1], (*state, total))
    columns = [2 * last - 3, 2 * last - 2]
    before, total = settle([columns], products[last - 1 : last], (*state, total))
    final, _ = settle([[2 * last - 1]], products[last:], None)
    states = before + final
    return finish(table, info, seen, per_head, roll_count, total, states)


def local(*args):
    ranks, heads = lax.axis_size("dp"), lax.axis_size("head")
    bundles = args[6].shape[0]
    if ranks == bundles and ring_fits(ranks, heads):
        return local_ring(*args)
    return local_general(*args)


def solution(mesh):
    in_specs = (
        P("dp", "head"),
        P("dp", "head"),
        P("dp", None, None),
        P("dp", None, None),
        P("dp"),
        P(),
        P("dp"),
        P("dp"),
        P("head", None, None),
        P("head", "dp"),
    )
    out_specs = P("head", "dp")
    return jax.shard_map(local, mesh=mesh, in_specs=in_specs, out_specs=out_specs, check_vma=False)
```

```python
import functools
import math

import jax
import jax.numpy as jnp
from jax import lax
from jax.experimental import pallas as pl
from jax.experimental.pallas import tpu as pltpu
from jax.sharding import PartitionSpec as P


ROPE = 64
VD = 128


def ring_order(size):
    fast = 1 << (max(size.bit_length() - 1, 0) // 2)
    slow = size // fast
    if fast == 1 or slow % 2:
        return list(range(size))
    cells = [(z, 0) for z in range(slow)]
    for step, z in enumerate(range(slow - 1, -1, -1)):
        ys = range(1, fast) if step % 2 == 0 else range(fast - 1, 0, -1)
        cells += [(z, y) for y in ys]
    return [z * fast + y for z, y in cells]


def ring_fits(ranks, heads):
    if ranks % 2 or ranks < 4 or ranks % heads or heads & (heads - 1):
        return False
    order, per_head = ring_order(ranks), ranks // heads
    return all(
        order[p - k] // per_head != order[(p + k) % ranks] // per_head
        for p in range(ranks)
        for k in range(1, ranks // 2)
    )


def slot_for(info, loads, width, bundles, requester, owner):
    pick = jnp.int32(0)
    for j in range(bundles):
        hit = info[requester * width + j] == owner
        pick = jnp.where(hit, info[requester * width + bundles + j], pick)
    return lax.rem(pick, loads[owner])


def pack_kernel(info, loads, place, lat_ref, rope_ref, out_ref):
    rows = lat_ref.shape[1]
    out_ref[0, :rows, :] = lat_ref[0]
    out_ref[0, rows:, :] = rope_ref[0]


def pack(info, loads, place, cache_latent, cache_rope, ranks, heads, width, bundles):
    rows = cache_latent.shape[1] // heads
    dims = cache_rope.shape[1] // heads
    wide = cache_latent.shape[2]

    def source(i, info, loads, place):
        return slot_for(info, loads, width, bundles, i, place[0]), place[1], 0

    return pl.pallas_call(
        pack_kernel,
        out_shape=jax.ShapeDtypeStruct((ranks, rows + dims, wide), cache_latent.dtype),
        grid_spec=pltpu.PrefetchScalarGridSpec(
            num_scalar_prefetch=3,
            grid=(ranks,),
            in_specs=[pl.BlockSpec((1, rows, wide), source), pl.BlockSpec((1, dims, wide), source)],
            out_specs=pl.BlockSpec((1, rows + dims, wide), lambda i, *_: (i, 0, 0)),
        ),
        name="pack",
    )(info, loads, place, cache_latent, cache_rope)


def attend_kernel(
    heads, width, bundles, scale, block, info, loads, place, q_ref, qr_ref, *refs
):
    parts = refs[:heads]
    w_ref, out_ref, lat, rope, mixed = refs[heads:]
    b = pl.program_id(0)
    rows = lat.shape[0] // heads
    dims = rope.shape[0] // heads
    for m in range(heads):
        at = jnp.bitwise_xor(place[1], m)
        lat[pl.ds(pl.multiple_of(at * rows, rows), rows), :] = parts[m][0, :rows, :]
        rope[pl.ds(pl.multiple_of(at * dims, dims), dims), :] = parts[m][0, rows:, :]
    base = place[0] * width
    owner = info[base + b]
    slot = lax.rem(info[base + bundles + b], loads[owner])
    length = info[owner * width + 2 * bundles + slot]
    total_rows = q_ref.shape[1]
    live = lax.broadcasted_iota(jnp.int32, (block, lat.shape[0]), 1) < length
    for i in range(total_rows // block):
        at = slice(i * block, (i + 1) * block)
        s = lax.dot_general(
            q_ref[0, at, :], lat[...], (((1,), (1,)), ((), ())), preferred_element_type=jnp.float32
        )
        s = s + jnp.dot(qr_ref[0, at, :], rope[...], preferred_element_type=jnp.float32)
        s = jnp.where(live, s * scale, -1e30)
        w = jnp.exp(s - jnp.max(s, axis=1, keepdims=True))
        w = w * (1.0 / jnp.sum(w, axis=1, keepdims=True))
        o = jnp.dot(w.astype(jnp.bfloat16), lat[...], preferred_element_type=jnp.float32)
        for c in range(mixed.shape[0]):
            piece = o[:, c * 128 : (c + 1) * 128]
            mixed[c, pl.ds(b * total_rows + i * block, block), :] = piece

    @pl.when(b == pl.num_programs(0) - 1)
    def _():
        local_heads, _, value_width = w_ref.shape
        n = mixed.shape[1] // local_heads
        for h in range(local_heads):
            x = jnp.concatenate(
                [mixed[c, pl.ds(h, n, stride=local_heads), :] for c in range(mixed.shape[0])], axis=1
            ).astype(jnp.bfloat16)
            v = jnp.dot(x, w_ref[h], preferred_element_type=jnp.float32)
            out_ref[:, h * value_width : (h + 1) * value_width] = v.astype(jnp.bfloat16)


def attend(info, loads, place, q, qr, parts, w_uv, width, bundles):
    heads = len(parts)
    _, q_rows, wide = q.shape
    _, part_rows, _ = parts[0].shape
    local_heads, _, value_width = w_uv.shape
    dims = qr.shape[2] // heads
    rows = part_rows - dims
    row_count = bundles * q_rows // local_heads

    def theirs(b, info, loads, place):
        return info[place[0] * width + b], 0, 0

    block = math.gcd(q_rows, 128)
    return pl.pallas_call(
        functools.partial(
            attend_kernel, heads, width, bundles, 1.0 / math.sqrt(VD + ROPE), block
        ),
        out_shape=jax.ShapeDtypeStruct((row_count, local_heads * value_width), jnp.bfloat16),
        grid_spec=pltpu.PrefetchScalarGridSpec(
            num_scalar_prefetch=3,
            grid=(bundles,),
            in_specs=[
                pl.BlockSpec((1, q_rows, wide), lambda b, *_: (b, 0, 0)),
                pl.BlockSpec((1, q_rows, qr.shape[2]), lambda b, *_: (b, 0, 0)),
            ]
            + [pl.BlockSpec((1, part_rows, wide), theirs)] * heads
            + [pl.BlockSpec(w_uv.shape, lambda b, *_: (0, 0, 0))],
            out_specs=pl.BlockSpec((row_count, local_heads * value_width), lambda b, *_: (0, 0)),
            scratch_shapes=[
                pltpu.VMEM((rows * heads, wide), jnp.bfloat16),
                pltpu.VMEM((dims * heads, wide), jnp.bfloat16),
                pltpu.VMEM((wide // 128, bundles * q_rows, 128), jnp.float32),
            ],
        ),
        name="attend",
    )(info, loads, place, q, qr, *parts, w_uv)


def local_general(
    q_latent, q_rope, cache_latent, cache_rope, lengths, loads, owner_rank, owner_pick, w_uv, w_out
):
    ranks = lax.axis_size("dp")
    heads = lax.axis_size("head")
    me = lax.axis_index("dp")
    head = lax.axis_index("head")
    bundles = owner_rank.shape[0]
    roll_count = q_latent.shape[0] // bundles
    local_heads = w_uv.shape[0]
    place = jnp.stack([me, head]).astype(jnp.int32)

    facts = jnp.concatenate([owner_rank, owner_pick, lengths])
    width = 32
    facts = jnp.pad(facts, (0, width - facts.shape[0]))
    info = lax.all_to_all(
        jnp.broadcast_to(facts[None], (ranks, width)), "dp", split_axis=0, concat_axis=0, tiled=True
    ).reshape(-1)
    q = q_latent.reshape(bundles, roll_count * local_heads, -1)
    qr = q_rope.reshape(bundles, roll_count * local_heads, -1)

    packed = pack(info, loads, place, cache_latent, cache_rope, ranks, heads, width, bundles)
    mine = lax.all_to_all(packed, "dp", split_axis=0, concat_axis=0, tiled=True)
    parts = [mine]
    bit = heads // 2
    found = {0: mine}
    while bit:
        pairs = [(i, i ^ bit) for i in range(heads)]
        for m in list(found):
            found[m ^ bit] = lax.ppermute(found[m], "head", pairs)
        bit //= 2
    parts = [found[m] for m in range(heads)]
    values = attend(info, loads, place, q, qr, parts, w_uv, width, bundles)

    order = ring_order(ranks)
    ahead = [(order[i], order[(i + 1) % ranks]) for i in range(ranks)]
    behind = [(b, a) for a, b in ahead]
    half = values.shape[1] // 2

    def project(x):
        return jnp.dot(x, w_out, preferred_element_type=jnp.float32).astype(jnp.bfloat16)

    partial = {0: project(values)}
    fore = back = values
    for step in range(1, (ranks + 1) // 2):
        fore = lax.ppermute(fore, "dp", ahead)
        back = lax.ppermute(back, "dp", behind)
        both = project(jnp.concatenate([fore, back], axis=0))
        partial[-step] = both[: values.shape[0]]
        partial[step] = both[values.shape[0] :]
    if ranks % 2 == 0:
        left = lax.ppermute(fore[:, :half], "dp", ahead)
        right = lax.ppermute(back[:, half:], "dp", behind)
        partial[ranks // 2] = project(jnp.concatenate([left, right], axis=1))
    stacked = jnp.stack([partial[k if 2 * k <= ranks else k - ranks] for k in range(ranks)])
    position = [0] * ranks
    for i, r in enumerate(order):
        position[r] = i
    position = jnp.asarray(position, jnp.int32)
    by_rank = stacked[(position - position[me]) % ranks]
    shares = by_rank.reshape(heads, -1, w_out.shape[1])
    got = lax.all_to_all(shares, "head", split_axis=0, concat_axis=0, tiled=True)
    return jnp.sum(got.astype(jnp.float32), axis=0).astype(jnp.bfloat16)


def in_hbm(x):
    return pltpu.with_memory_space_constraint(x, pltpu.MemorySpace.HBM)


def ring_tables(ranks):
    order = ring_order(ranks)
    where = [order.index(r) for r in range(ranks)]
    offsets = [0]
    for k in range(1, ranks // 2):
        offsets += [-k, k]
    offsets.append(ranks // 2)
    seen = [[order[(where[r] + o) % ranks] for o in offsets] for r in range(ranks)]
    return order, where, offsets, seen


BUNDLE, SLOT, TARGET, OWNER, PLACE, PLAN_ROWS = 0, 1, 2, 3, 4, 8


def chunk_plans(ranks):
    middle = ranks // 2
    return {
        "p": [[0], list(range(1, middle - 1)), [middle - 1]],
        "s": [[c] for c in range(middle, ranks - 2)] + [[ranks - 2, ranks - 1]],
    }


def plan_kernel(per_head, seen, owner_rank, owner_pick, loads, table):
    ranks = seen.shape[1]
    me, head = lax.axis_index("dp"), lax.axis_index("head")
    table[PLACE, 0] = me
    table[PLACE, 1] = head
    for c in range(ranks):
        owner = seen[me, c]
        bundle, pick = jnp.int32(0), jnp.int32(0)
        for b in range(owner_rank.shape[0]):
            hit = owner_rank[b] == owner
            bundle = jnp.where(hit, b, bundle)
            pick = jnp.where(hit, owner_pick[b], pick)
        table[BUNDLE, c] = bundle
        table[SLOT, c] = lax.rem(pick, loads[owner])
        table[TARGET, c] = lax.div(owner, per_head)
        table[OWNER, c] = owner


def plan_of(seen, owner_rank, owner_pick, loads, per_head):
    smem = pl.BlockSpec(memory_space=pltpu.MemorySpace.SMEM)
    return pl.pallas_call(
        functools.partial(plan_kernel, per_head),
        out_shape=jax.ShapeDtypeStruct((PLAN_ROWS, seen.shape[1]), jnp.int32),
        in_specs=[smem] * 4,
        out_specs=smem,
        name="plan",
    )(seen, owner_rank, owner_pick, loads)


def payload_kernel(lat, rope, out, sems):
    head = lax.axis_index("head")
    dims = rope.shape[1] * (out.shape[1]) // (rope.shape[1] + lat.shape[1])
    rows = out.shape[1] - dims
    copies = [
        pltpu.make_async_copy(
            lat.at[:, pl.ds(pl.multiple_of(head * rows, rows), rows), :],
            out.at[:, pl.ds(0, rows), :],
            sems.at[0],
        ),
        pltpu.make_async_copy(
            rope.at[:, pl.ds(pl.multiple_of(head * dims, dims), dims), :],
            out.at[:, pl.ds(rows, dims), :],
            sems.at[1],
        ),
    ]
    for copy in copies:
        copy.start()
    for copy in copies:
        copy.wait()


def payload_of(cache_latent, cache_rope, heads):
    slots, positions, wide = cache_latent.shape
    rows = (positions + cache_rope.shape[1]) // heads
    return pl.pallas_call(
        payload_kernel,
        out_shape=jax.ShapeDtypeStruct((slots, rows, wide), cache_latent.dtype),
        in_specs=[pl.BlockSpec(memory_space=pl.ANY)] * 2,
        out_specs=pl.BlockSpec(memory_space=pltpu.MemorySpace.VMEM),
        scratch_shapes=[pltpu.SemaphoreType.DMA((2,))],
        compiler_params=pltpu.CompilerParams(vmem_limit_bytes=4 * 2**20),
        name="payload",
    )(in_hbm(cache_latent), in_hbm(cache_rope))


def upper(rows):
    return (rows // 2 + 15) // 16 * 16


def relay_kernel(bundles, offsets, table, info, loads, seen, fore, back, *outs):
    chosen, sends = outs[0], outs[1:]
    me = table[PLACE, 0]
    last = len(offsets) // 2
    rows = fore.shape[1]
    for side, (way, arrived, out) in enumerate(((1, fore, sends[0]), (-1, back, sends[1]))):
        chosen[side] = arrived[table[SLOT, offsets.index(-way)]]
        owner = seen[me, offsets.index(-way)]
        for d in range(2, last + 1):
            asker = seen[me, offsets.index(way * (d - 1))]
            pick = jnp.int32(0)
            for b in range(bundles):
                hit = info[asker, 0, b] == owner
                pick = jnp.where(hit, info[asker, 0, bundles + b], pick)
            slot = lax.rem(pick, loads[owner])
            start = (d - 2) * rows
            if d < last:
                out[pl.ds(start, rows), :] = arrived[slot]
            elif way == 1:
                out[pl.ds(start, upper(rows)), :] = arrived[slot, : upper(rows), :]
            else:
                out[pl.ds(start, rows - upper(rows)), :] = arrived[slot, upper(rows) :, :]


def relay(table, info, loads, seen, bundles, offsets, fore, back):
    _, rows, wide = fore.shape
    full = (len(offsets) // 2 - 2) * rows
    vmem = pl.BlockSpec(memory_space=pltpu.MemorySpace.VMEM)
    smem = pl.BlockSpec(memory_space=pltpu.MemorySpace.SMEM)
    return pl.pallas_call(
        functools.partial(relay_kernel, bundles, offsets),
        out_shape=[
            jax.ShapeDtypeStruct((2, rows, wide), fore.dtype),
            jax.ShapeDtypeStruct((full + upper(rows), wide), fore.dtype),
            jax.ShapeDtypeStruct((full + rows - upper(rows), wide), fore.dtype),
        ],
        in_specs=[smem] * 4 + [vmem] * 2,
        out_specs=[vmem] * 3,
        compiler_params=pltpu.CompilerParams(vmem_limit_bytes=6 * 2**20),
        name="relay",
    )(table, info, loads, seen, fore, back)


def join_kernel(rows, fore, back, out):
    if out.shape[0] == 2:
        out[0] = fore[:rows, :]
        out[1] = back[:rows, :]
    else:
        out[0, : fore.shape[0], :] = fore[...]
        out[0, fore.shape[0] :, :] = back[...]


def join(count, rows, fore, back):
    vmem = pl.BlockSpec(memory_space=pltpu.MemorySpace.VMEM)
    return pl.pallas_call(
        functools.partial(join_kernel, rows),
        out_shape=jax.ShapeDtypeStruct((count, rows, fore.shape[1]), fore.dtype),
        in_specs=[vmem] * 2,
        out_specs=vmem,
        compiler_params=pltpu.CompilerParams(vmem_limit_bytes=4 * 2**20),
        name="join",
    )(fore, back)


def slots_kernel(plan, own, heads, indices, bundles, final, scale, table, info, *refs):
    count = len(plan)
    refs = list(refs)
    q_ref, qr_ref, w_hbm = refs.pop(0), refs.pop(0), refs.pop(0)
    w_ref, fetch = w_hbm, own or count > 1
    if fetch:
        w_ref, w_sem = refs.pop(-2), refs.pop(-1)
        w_copy = pltpu.make_async_copy(w_hbm, w_ref, w_sem)
        w_copy.start()
    if own:
        full_lat, full_rope = refs.pop(0), refs.pop(0)
    parts = [[(refs.pop(0), index) for index in slot] for slot in indices]
    lat, rope, mixed = refs.pop(-3), refs.pop(-2), refs.pop(-1)
    if own:
        own_lat, own_rope, sems = refs.pop(-3), refs.pop(-2), refs.pop(-1)
        slot = table[SLOT, plan[0]]
        copies = [
            pltpu.make_async_copy(full_lat.at[slot], own_lat, sems.at[0]),
            pltpu.make_async_copy(full_rope.at[slot], own_rope, sems.at[1]),
        ]
        for copy in copies:
            copy.start()
    into = refs.pop(-1) if final else None
    out_ref = refs.pop(-1)
    earlier = refs
    total_rows = q_ref.shape[1]
    rows = lat.shape[0] // heads
    dims = rope.shape[0] // heads

    def bundle(i, _):
        j = lax.rem(i + own, count)
        for at in range(count):

            @pl.when(j == at)
            def _():
                if own and at == 0:
                    for copy in copies:
                        copy.wait()
                    lat[...] = own_lat[...]
                    rope[...] = own_rope[...]
                    return
                for m, (part, index) in enumerate(parts[at - own]):
                    to = jnp.bitwise_xor(table[PLACE, 1], m)
                    lat[pl.ds(pl.multiple_of(to * rows, rows), rows), :] = part[index, :rows, :]
                    rope[pl.ds(pl.multiple_of(to * dims, dims), dims), :] = part[index, rows:, :]

        column = plan[0] + j
        length = info[table[OWNER, column], 0, 2 * bundles + table[SLOT, column]]
        b = table[BUNDLE, column]
        past = lax.broadcasted_iota(jnp.int32, (1, lat.shape[0]), 1) >= length
        s = lax.dot_general(
            q_ref[b], lat[...], (((1,), (1,)), ((), ())), preferred_element_type=jnp.float32
        )
        s = s + jnp.dot(qr_ref[b], rope[...], preferred_element_type=jnp.float32)
        s = s + jnp.where(past, -1e30, 0.0)
        w = jnp.exp((s - jnp.max(s, axis=1, keepdims=True)) * scale)
        w = w * (1.0 / jnp.sum(w, axis=1, keepdims=True))
        o = jnp.dot(w.astype(jnp.bfloat16), lat[...], preferred_element_type=jnp.float32)
        start = pl.multiple_of(j * total_rows, total_rows)
        for c in range(mixed.shape[0]):
            mixed[c, pl.ds(start, total_rows), :] = o[:, c * 128 : (c + 1) * 128]
        return 0

    lax.fori_loop(0, count, bundle, 0)
    if fetch:
        w_copy.wait()
    local_heads, _, value_width = w_ref.shape
    n = mixed.shape[1] // local_heads
    at = 0
    if final:
        for piece in earlier:
            into[pl.ds(at, piece.shape[0]), :] = piece[...]
            at += piece.shape[0]
    else:
        into = out_ref
    for h in range(local_heads):
        x = jnp.concatenate(
            [mixed[c, pl.ds(h, n, stride=local_heads), :] for c in range(mixed.shape[0])], axis=1
        ).astype(jnp.bfloat16)
        v = jnp.dot(x, w_ref[h], preferred_element_type=jnp.float32)
        into[pl.ds(at, n), h * value_width : (h + 1) * value_width] = v
    if final:
        out_ref[...] = into[...].astype(out_ref.dtype)


def attend_slots(plan, table, info, q, qr, full, parts, heads, positions, bundles, w_uv, earlier=None):
    own = 1 if full is not None else 0
    final = earlier is not None
    earlier = list(earlier or ())
    count = len(plan)
    _, q_rows, wide = q.shape
    dims = qr.shape[2]
    local_heads, _, value_width = w_uv.shape
    vmem = pl.BlockSpec(memory_space=pltpu.MemorySpace.VMEM)
    smem = pl.BlockSpec(memory_space=pltpu.MemorySpace.SMEM)
    fetch = own or count > 1
    args = [q, qr, in_hbm(w_uv) if fetch else w_uv]
    in_specs = [vmem, vmem, pl.BlockSpec(memory_space=pl.ANY) if fetch else vmem]
    if own:
        args += [in_hbm(x) for x in full]
        in_specs += [pl.BlockSpec(memory_space=pl.ANY)] * 2
    args += [array for slot in parts for array, _ in slot] + earlier
    in_specs += [vmem] * (len(args) - len(in_specs))
    done = sum(e.shape[0] for e in earlier) + count * q_rows // local_heads
    out_shape = (done, local_heads * value_width)
    caches = [pltpu.VMEM((positions, wide), jnp.bfloat16), pltpu.VMEM((dims, wide), jnp.bfloat16)]
    scratch = [pltpu.VMEM(out_shape, jnp.float32)] if final else []
    if own:
        scratch += caches + [pltpu.SemaphoreType.DMA((2,))]
    scratch += caches + [pltpu.VMEM((wide // 128, count * q_rows, 128), jnp.float32)]
    if fetch:
        scratch += [pltpu.VMEM(w_uv.shape, w_uv.dtype), pltpu.SemaphoreType.DMA]
    return pl.pallas_call(
        functools.partial(
            slots_kernel, plan, own, heads, [[index for _, index in slot] for slot in parts],
            bundles, final, 1.0 / math.sqrt(VD + ROPE),
        ),
        out_shape=jax.ShapeDtypeStruct(out_shape, jnp.bfloat16 if final else jnp.float32),
        in_specs=[smem] * 2 + in_specs,
        out_specs=vmem,
        scratch_shapes=scratch,
        compiler_params=pltpu.CompilerParams(vmem_limit_bytes=(18 if fetch else 12) * 2**20),
        name="attend_slots",
    )(table, info, *args)


def add_in(table, per_head, columns, own, got, before, after):
    part = own[...]
    for g in got:
        part = part + g[...].astype(jnp.float32)
    for y in range(per_head):
        rank = table[PLACE, 1] * per_head + y
        hit = table[OWNER, columns[0]] == rank
        for c in columns[1:]:
            hit = hit | (table[OWNER, c] == rank)
        now = jnp.where(hit, part, 0.0)
        after[y] = now if before is None else before[y] + now


def settle_kernel(masks, per_head, groups, prev_columns, has_total, table, *refs):
    refs = list(refs)
    sources = [(refs.pop(0), refs.pop(0)) for _ in groups]
    if prev_columns:
        prev_own, prev_got = refs.pop(0), [refs.pop(0) for _ in masks]
        before = refs.pop(0) if has_total else None
    head = table[PLACE, 1]
    for columns, (both, near) in zip(groups, sources):
        chip = both[...].astype(jnp.float32) + near[...].astype(jnp.float32)
        block = chip.shape[0] // len(columns)
        one = chip[:block]
        other = chip[block:] if len(columns) > 1 else None
        for m in masks if other is not None else masks[:1]:
            piece = one
            if other is not None:
                piece = jnp.where(table[TARGET, columns[0]] == jnp.bitwise_xor(head, m), one, other)
            refs.pop(0)[...] = piece.astype(jnp.bfloat16)
        if other is not None:
            one = jnp.where(table[TARGET, columns[0]] == head, one, other)
        refs.pop(0)[...] = one
    if prev_columns:
        add_in(table, per_head, prev_columns, prev_own, prev_got, before, refs.pop(0))


def settle_step(table, masks, per_head, groups, sources, previous):
    n = sources[0][0].shape[0] // len(groups[0])
    wide = sources[0][0].shape[1]
    vmem = pl.BlockSpec(memory_space=pltpu.MemorySpace.VMEM)
    args, prev_columns, has_total = [x for source in sources for x in source], None, False
    if previous is not None:
        prev_columns, prev_own, prev_got, total = previous
        has_total = total is not None
        args += [prev_own, *prev_got] + ([total] if has_total else [])
    out = []
    for columns in groups:
        sends = len(masks) if len(columns) > 1 else 1
        out += [jax.ShapeDtypeStruct((n, wide), jnp.bfloat16)] * sends
        out.append(jax.ShapeDtypeStruct((n, wide), jnp.float32))
    if previous is not None:
        out.append(jax.ShapeDtypeStruct((per_head, n, wide), jnp.float32))
    outs = pl.pallas_call(
        functools.partial(settle_kernel, masks, per_head, groups, prev_columns, has_total),
        out_shape=out,
        in_specs=[pl.BlockSpec(memory_space=pltpu.MemorySpace.SMEM)] + [vmem] * len(args),
        out_specs=[vmem] * len(out),
        compiler_params=pltpu.CompilerParams(vmem_limit_bytes=4 * 2**20),
        name="settle",
    )(table, *args)
    outs = list(outs)
    states = []
    for columns in groups:
        sends = [outs.pop(0) for _ in (masks if len(columns) > 1 else masks[:1])]
        states.append((sends * (1 if len(columns) > 1 else len(masks)), outs.pop(0)))
    return states, outs.pop(0) if previous is not None else None


def finish_kernel(per_head, steps, roll, table, info, seen, before, *refs):
    *refs, out = refs
    each = len(refs) // len(steps)
    parts = []
    for i in range(len(steps)):
        own, *got = refs[each * i : each * (i + 1)]
        part = own[...]
        for g in got:
            part = part + g[...].astype(jnp.float32)
        parts.append(part)
    n = before.shape[1]
    slots = n // roll
    to = lax.broadcasted_iota(jnp.int32, (n, n), 0)
    source = lax.broadcasted_iota(jnp.int32, (n, n), 1)
    for y in range(per_head):
        rank = table[PLACE, 1] * per_head + y
        wanted = to
        for b in range(slots):
            place = jnp.int32(0)
            for c in range(slots):
                place = jnp.where(seen[rank, c] == info[rank, 0, b], c, place)
            inside = (to >= b * roll) & (to < (b + 1) * roll)
            wanted = jnp.where(inside, to + (place - b) * roll, wanted)
        pick = jnp.where(wanted == source, 1.0, 0.0).astype(jnp.bfloat16)
        total = before[y]
        for columns, part in zip(steps, parts):
            hit = table[OWNER, columns[0]] == rank
            for c in columns[1:]:
                hit = hit | (table[OWNER, c] == rank)
            total = total + jnp.where(hit, part, 0.0)
        moved = jnp.dot(pick, total.astype(jnp.bfloat16), preferred_element_type=jnp.float32)
        out[pl.ds(y * n, n), :] = moved.astype(out.dtype)


def finish(table, info, seen, per_head, roll, total, states):
    _, n, wide = total.shape
    steps = [state[0] for state in states]
    args = [x for _, own, got in states for x in (own, *got)]
    vmem = pl.BlockSpec(memory_space=pltpu.MemorySpace.VMEM)
    smem = pl.BlockSpec(memory_space=pltpu.MemorySpace.SMEM)
    return pl.pallas_call(
        functools.partial(finish_kernel, per_head, steps, roll),
        out_shape=jax.ShapeDtypeStruct((per_head * n, wide), jnp.bfloat16),
        in_specs=[smem] * 3 + [vmem] * (1 + len(args)),
        out_specs=vmem,
        compiler_params=pltpu.CompilerParams(vmem_limit_bytes=6 * 2**20),
        name="finish",
    )(table, info, seen, total, *args)


def local_ring(
    q_latent, q_rope, cache_latent, cache_rope, lengths, loads, owner_rank, owner_pick, w_uv, w_out
):
    ranks = lax.axis_size("dp")
    heads = lax.axis_size("head")
    bundles = owner_rank.shape[0]
    local_heads = w_uv.shape[0]
    roll_count = q_latent.shape[0] // bundles
    per_head = ranks // heads
    last = ranks // 2
    order, where, offsets, seen = ring_tables(ranks)
    seen = jnp.asarray(seen, jnp.int32)
    ahead = [(order[i], order[(i + 1) % ranks]) for i in range(ranks)]
    behind = [(b, a) for a, b in ahead]

    def move(x, pairs, axis="dp"):
        return lax.ppermute(x, axis, pairs)

    payload = payload_of(cache_latent, cache_rope, heads)
    fore, back = move(payload, ahead), move(payload, behind)
    facts = [jnp.broadcast_to(x[None], (ranks, x.shape[0])) for x in (owner_rank, owner_pick, lengths)]
    info = lax.all_to_all(
        jnp.concatenate(facts, axis=1), "dp", split_axis=0, concat_axis=0, tiled=True
    )
    info = jnp.maximum(info, 0)[:, None]
    table = in_hbm(plan_of(seen, owner_rank, owner_pick, loads, per_head))
    q = q_latent.reshape(bundles, roll_count * local_heads, -1)
    qr = q_rope.reshape(bundles, roll_count * local_heads, -1)

    def share(chosen):
        found = {0: chosen}
        bit = heads // 2
        while bit:
            pairs = [(i, i ^ bit) for i in range(heads)]
            for m in list(found):
                found[m ^ bit] = move(found[m], pairs, "head")
            bit //= 2
        return [found[m] for m in range(heads)]

    rows = payload.shape[1]
    chosen, fore, back = relay(table, info, loads, seen, bundles, offsets, fore, back)
    groups = {}
    for k in range(1, last + 1):
        if k > 1:
            if k > 2:
                fore, back = fore[rows:], back[rows:]
            fore = move(fore, ahead)
            back = move(back, behind)
            chosen = join(2 if k < last else 1, rows, fore, back)
        parts = share(chosen)
        groups[2 * k - 1] = [(p, 0) for p in parts]
        if k < last:
            groups[2 * k] = [(p, 1) for p in parts]

    def attend(plan, full=None, earlier=None):
        return attend_slots(
            plan, table, info, q, qr, full, [groups[c] for c in plan[(full is not None) :]],
            heads, cache_latent.shape[1], bundles, w_uv, earlier,
        )

    chunks = []
    for tag, plans in chunk_plans(ranks).items():
        earlier = []
        for n, plan in enumerate(plans):
            full = (cache_latent, cache_rope) if plan[0] == 0 else None
            carried = earlier if n == len(plans) - 1 else None
            earlier.append(attend(plan, full, carried))
        chunks.append((tag, earlier[-1]))
    half = chunks[0][1].shape[1] // 2

    def project(pieces):
        product = jnp.dot(jnp.concatenate(pieces), w_out, preferred_element_type=jnp.float32)
        return product.astype(jnp.bfloat16)

    def target(p, column):
        return order[(where[p] + offsets[column]) % ranks] // per_head

    masks = list(range(2, heads, 2))

    def settle(groups, products, previous):
        cores = [(i, i ^ 1) for i in range(heads)]
        sources = [(both, move(both, cores, "head")) for both in products]
        made, total = settle_step(table, masks, per_head, groups, sources, previous)
        states = []
        for columns, (to_send, own) in zip(groups, made):
            got = []
            for k, m in enumerate(masks):
                pairs = []
                for p in range(ranks):
                    for t in sorted({target(p, c) for c in columns}):
                        pairs.append((p * heads + (t ^ m), p * heads + t))
                got.append(move(to_send[k], pairs, ("dp", "head")))
            states.append((columns, own, got))
        return states, total

    arrived = {}
    for tag, values in chunks:
        fore = back = values
        for k in range(1, last):
            if k == last - 1 and tag == chunks[-1][0]:
                break
            fore = move(fore, ahead)
            back = move(back, behind)
            arrived[tag, k] = fore, back
        fore_on, fore_end = fore[:, :half], fore[:, half:]
        back_on, back_end = back[:, half:], back[:, :half]
        if k == last - 1 and (tag, k) not in arrived:
            fore_on = move(fore_on, ahead)
            back_on = move(back_on, behind)
            fore_end = move(fore_end, ahead)
            back_end = move(back_end, behind)
            arrived[tag, k] = (
                jnp.concatenate([fore_on, fore_end], axis=1),
                jnp.concatenate([back_end, back_on], axis=1),
            )
        left = move(fore_on, ahead)
        right = move(back_on, behind)
        arrived[tag, last] = (jnp.concatenate([left, right], axis=1),)

    def pieces(k):
        return [arrived[tag, k][side] for side in range(2 if k < last else 1) for tag, _ in chunks]

    products = [project([values for _, values in chunks])]
    products += [project(pieces(k)) for k in range(1, last + 1)]
    (state,), total = settle([[0]], products[:1], None)
    for k in range(1, last - 1):
        columns = [2 * k - 1, 2 * k]
        (state,), total = settle([columns], products[k : k + 1], (*state, total))
    columns = [2 * last - 3, 2 * last - 2]
    before, total = settle([columns], products[last - 1 : last], (*state, total))
    final, _ = settle([[2 * last - 1]], products[last:], None)
    states = before + final
    return finish(table, info, seen, per_head, roll_count, total, states)


def local(*args):
    ranks, heads = lax.axis_size("dp"), lax.axis_size("head")
    bundles = args[6].shape[0]
    if ranks == bundles and ring_fits(ranks, heads):
        return local_ring(*args)
    return local_general(*args)


def solution(mesh):
    in_specs = (
        P("dp", "head"),
        P("dp", "head"),
        P("dp", None, None),
        P("dp", None, None),
        P("dp"),
        P(),
        P("dp"),
        P("dp"),
        P("head", None, None),
        P("head", "dp"),
    )
    out_specs = P("head", "dp")
    return jax.shard_map(local, mesh=mesh, in_specs=in_specs, out_specs=out_specs, check_vma=False)
```

```python
import functools
import math

import jax
import jax.numpy as jnp
from jax import lax
from jax.experimental import pallas as pl
from jax.experimental.pallas import tpu as pltpu
from jax.sharding import PartitionSpec as P


ROPE = 64
VD = 128


def ring_order(size):
    fast = 1 << (max(size.bit_length() - 1, 0) // 2)
    slow = size // fast
    if fast == 1 or slow % 2:
        return list(range(size))
    cells = [(z, 0) for z in range(slow)]
    for step, z in enumerate(range(slow - 1, -1, -1)):
        ys = range(1, fast) if step % 2 == 0 else range(fast - 1, 0, -1)
        cells += [(z, y) for y in ys]
    return [z * fast + y for z, y in cells]


def ring_fits(ranks, heads):
    if ranks % 2 or ranks < 4 or ranks % heads or heads & (heads - 1):
        return False
    order, per_head = ring_order(ranks), ranks // heads
    return all(
        order[p - k] // per_head != order[(p + k) % ranks] // per_head
        for p in range(ranks)
        for k in range(1, ranks // 2)
    )


def slot_for(info, loads, width, bundles, requester, owner):
    pick = jnp.int32(0)
    for j in range(bundles):
        hit = info[requester * width + j] == owner
        pick = jnp.where(hit, info[requester * width + bundles + j], pick)
    return lax.rem(pick, loads[owner])


def pack_kernel(info, loads, place, lat_ref, rope_ref, out_ref):
    rows = lat_ref.shape[1]
    out_ref[0, :rows, :] = lat_ref[0]
    out_ref[0, rows:, :] = rope_ref[0]


def pack(info, loads, place, cache_latent, cache_rope, ranks, heads, width, bundles):
    rows = cache_latent.shape[1] // heads
    dims = cache_rope.shape[1] // heads
    wide = cache_latent.shape[2]

    def source(i, info, loads, place):
        return slot_for(info, loads, width, bundles, i, place[0]), place[1], 0

    return pl.pallas_call(
        pack_kernel,
        out_shape=jax.ShapeDtypeStruct((ranks, rows + dims, wide), cache_latent.dtype),
        grid_spec=pltpu.PrefetchScalarGridSpec(
            num_scalar_prefetch=3,
            grid=(ranks,),
            in_specs=[pl.BlockSpec((1, rows, wide), source), pl.BlockSpec((1, dims, wide), source)],
            out_specs=pl.BlockSpec((1, rows + dims, wide), lambda i, *_: (i, 0, 0)),
        ),
        name="pack",
    )(info, loads, place, cache_latent, cache_rope)


def attend_kernel(
    heads, width, bundles, scale, block, info, loads, place, q_ref, qr_ref, *refs
):
    parts = refs[:heads]
    w_ref, out_ref, lat, rope, mixed = refs[heads:]
    b = pl.program_id(0)
    rows = lat.shape[0] // heads
    dims = rope.shape[0] // heads
    for m in range(heads):
        at = jnp.bitwise_xor(place[1], m)
        lat[pl.ds(pl.multiple_of(at * rows, rows), rows), :] = parts[m][0, :rows, :]
        rope[pl.ds(pl.multiple_of(at * dims, dims), dims), :] = parts[m][0, rows:, :]
    base = place[0] * width
    owner = info[base + b]
    slot = lax.rem(info[base + bundles + b], loads[owner])
    length = info[owner * width + 2 * bundles + slot]
    total_rows = q_ref.shape[1]
    live = lax.broadcasted_iota(jnp.int32, (block, lat.shape[0]), 1) < length
    for i in range(total_rows // block):
        at = slice(i * block, (i + 1) * block)
        s = lax.dot_general(
            q_ref[0, at, :], lat[...], (((1,), (1,)), ((), ())), preferred_element_type=jnp.float32
        )
        s = s + jnp.dot(qr_ref[0, at, :], rope[...], preferred_element_type=jnp.float32)
        s = jnp.where(live, s * scale, -1e30)
        w = jnp.exp(s - jnp.max(s, axis=1, keepdims=True))
        w = w * (1.0 / jnp.sum(w, axis=1, keepdims=True))
        o = jnp.dot(w.astype(jnp.bfloat16), lat[...], preferred_element_type=jnp.float32)
        for c in range(mixed.shape[0]):
            piece = o[:, c * 128 : (c + 1) * 128]
            mixed[c, pl.ds(b * total_rows + i * block, block), :] = piece

    @pl.when(b == pl.num_programs(0) - 1)
    def _():
        local_heads, _, value_width = w_ref.shape
        n = mixed.shape[1] // local_heads
        for h in range(local_heads):
            x = jnp.concatenate(
                [mixed[c, pl.ds(h, n, stride=local_heads), :] for c in range(mixed.shape[0])], axis=1
            ).astype(jnp.bfloat16)
            v = jnp.dot(x, w_ref[h], preferred_element_type=jnp.float32)
            out_ref[:, h * value_width : (h + 1) * value_width] = v.astype(jnp.bfloat16)


def attend(info, loads, place, q, qr, parts, w_uv, width, bundles):
    heads = len(parts)
    _, q_rows, wide = q.shape
    _, part_rows, _ = parts[0].shape
    local_heads, _, value_width = w_uv.shape
    dims = qr.shape[2] // heads
    rows = part_rows - dims
    row_count = bundles * q_rows // local_heads

    def theirs(b, info, loads, place):
        return info[place[0] * width + b], 0, 0

    block = math.gcd(q_rows, 128)
    return pl.pallas_call(
        functools.partial(
            attend_kernel, heads, width, bundles, 1.0 / math.sqrt(VD + ROPE), block
        ),
        out_shape=jax.ShapeDtypeStruct((row_count, local_heads * value_width), jnp.bfloat16),
        grid_spec=pltpu.PrefetchScalarGridSpec(
            num_scalar_prefetch=3,
            grid=(bundles,),
            in_specs=[
                pl.BlockSpec((1, q_rows, wide), lambda b, *_: (b, 0, 0)),
                pl.BlockSpec((1, q_rows, qr.shape[2]), lambda b, *_: (b, 0, 0)),
            ]
            + [pl.BlockSpec((1, part_rows, wide), theirs)] * heads
            + [pl.BlockSpec(w_uv.shape, lambda b, *_: (0, 0, 0))],
            out_specs=pl.BlockSpec((row_count, local_heads * value_width), lambda b, *_: (0, 0)),
            scratch_shapes=[
                pltpu.VMEM((rows * heads, wide), jnp.bfloat16),
                pltpu.VMEM((dims * heads, wide), jnp.bfloat16),
                pltpu.VMEM((wide // 128, bundles * q_rows, 128), jnp.float32),
            ],
        ),
        name="attend",
    )(info, loads, place, q, qr, *parts, w_uv)


def local_general(
    q_latent, q_rope, cache_latent, cache_rope, lengths, loads, owner_rank, owner_pick, w_uv, w_out
):
    ranks = lax.axis_size("dp")
    heads = lax.axis_size("head")
    me = lax.axis_index("dp")
    head = lax.axis_index("head")
    bundles = owner_rank.shape[0]
    roll_count = q_latent.shape[0] // bundles
    local_heads = w_uv.shape[0]
    place = jnp.stack([me, head]).astype(jnp.int32)

    facts = jnp.concatenate([owner_rank, owner_pick, lengths])
    width = 32
    facts = jnp.pad(facts, (0, width - facts.shape[0]))
    info = lax.all_to_all(
        jnp.broadcast_to(facts[None], (ranks, width)), "dp", split_axis=0, concat_axis=0, tiled=True
    ).reshape(-1)
    q = q_latent.reshape(bundles, roll_count * local_heads, -1)
    qr = q_rope.reshape(bundles, roll_count * local_heads, -1)

    packed = pack(info, loads, place, cache_latent, cache_rope, ranks, heads, width, bundles)
    mine = lax.all_to_all(packed, "dp", split_axis=0, concat_axis=0, tiled=True)
    parts = [mine]
    bit = heads // 2
    found = {0: mine}
    while bit:
        pairs = [(i, i ^ bit) for i in range(heads)]
        for m in list(found):
            found[m ^ bit] = lax.ppermute(found[m], "head", pairs)
        bit //= 2
    parts = [found[m] for m in range(heads)]
    values = attend(info, loads, place, q, qr, parts, w_uv, width, bundles)

    order = ring_order(ranks)
    ahead = [(order[i], order[(i + 1) % ranks]) for i in range(ranks)]
    behind = [(b, a) for a, b in ahead]
    half = values.shape[1] // 2

    def project(x):
        return jnp.dot(x, w_out, preferred_element_type=jnp.float32).astype(jnp.bfloat16)

    partial = {0: project(values)}
    fore = back = values
    for step in range(1, (ranks + 1) // 2):
        fore = lax.ppermute(fore, "dp", ahead)
        back = lax.ppermute(back, "dp", behind)
        both = project(jnp.concatenate([fore, back], axis=0))
        partial[-step] = both[: values.shape[0]]
        partial[step] = both[values.shape[0] :]
    if ranks % 2 == 0:
        left = lax.ppermute(fore[:, :half], "dp", ahead)
        right = lax.ppermute(back[:, half:], "dp", behind)
        partial[ranks // 2] = project(jnp.concatenate([left, right], axis=1))
    stacked = jnp.stack([partial[k if 2 * k <= ranks else k - ranks] for k in range(ranks)])
    position = [0] * ranks
    for i, r in enumerate(order):
        position[r] = i
    position = jnp.asarray(position, jnp.int32)
    by_rank = stacked[(position - position[me]) % ranks]
    shares = by_rank.reshape(heads, -1, w_out.shape[1])
    got = lax.all_to_all(shares, "head", split_axis=0, concat_axis=0, tiled=True)
    return jnp.sum(got.astype(jnp.float32), axis=0).astype(jnp.bfloat16)


def in_hbm(x):
    return pltpu.with_memory_space_constraint(x, pltpu.MemorySpace.HBM)


def ring_tables(ranks):
    order = ring_order(ranks)
    where = [order.index(r) for r in range(ranks)]
    offsets = [0]
    for k in range(1, ranks // 2):
        offsets += [-k, k]
    offsets.append(ranks // 2)
    seen = [[order[(where[r] + o) % ranks] for o in offsets] for r in range(ranks)]
    return order, where, offsets, seen


BUNDLE, SLOT, TARGET, OWNER, PLACE, PLAN_ROWS = 0, 1, 2, 3, 4, 8


def chunk_plans(ranks):
    middle = ranks // 2
    return {
        "p": [list(range(middle - 1)), [middle - 1]],
        "s": [[c] for c in range(middle, ranks - 2)] + [[ranks - 2, ranks - 1]],
    }


def plan_kernel(per_head, seen, owner_rank, owner_pick, loads, table):
    ranks = seen.shape[1]
    me, head = lax.axis_index("dp"), lax.axis_index("head")
    table[PLACE, 0] = me
    table[PLACE, 1] = head
    for c in range(ranks):
        owner = seen[me, c]
        bundle, pick = jnp.int32(0), jnp.int32(0)
        for b in range(owner_rank.shape[0]):
            hit = owner_rank[b] == owner
            bundle = jnp.where(hit, b, bundle)
            pick = jnp.where(hit, owner_pick[b], pick)
        table[BUNDLE, c] = bundle
        table[SLOT, c] = lax.rem(pick, loads[owner])
        table[TARGET, c] = lax.div(owner, per_head)
        table[OWNER, c] = owner


def plan_of(seen, owner_rank, owner_pick, loads, per_head):
    smem = pl.BlockSpec(memory_space=pltpu.MemorySpace.SMEM)
    return pl.pallas_call(
        functools.partial(plan_kernel, per_head),
        out_shape=jax.ShapeDtypeStruct((PLAN_ROWS, seen.shape[1]), jnp.int32),
        in_specs=[smem] * 4,
        out_specs=smem,
        name="plan",
    )(seen, owner_rank, owner_pick, loads)


def payload_kernel(lat, rope, out, sems):
    head = lax.axis_index("head")
    dims = rope.shape[1] * (out.shape[1]) // (rope.shape[1] + lat.shape[1])
    rows = out.shape[1] - dims
    copies = [
        pltpu.make_async_copy(
            lat.at[:, pl.ds(pl.multiple_of(head * rows, rows), rows), :],
            out.at[:, pl.ds(0, rows), :],
            sems.at[0],
        ),
        pltpu.make_async_copy(
            rope.at[:, pl.ds(pl.multiple_of(head * dims, dims), dims), :],
            out.at[:, pl.ds(rows, dims), :],
            sems.at[1],
        ),
    ]
    for copy in copies:
        copy.start()
    for copy in copies:
        copy.wait()


def payload_of(cache_latent, cache_rope, heads):
    slots, positions, wide = cache_latent.shape
    rows = (positions + cache_rope.shape[1]) // heads
    return pl.pallas_call(
        payload_kernel,
        out_shape=jax.ShapeDtypeStruct((slots, rows, wide), cache_latent.dtype),
        in_specs=[pl.BlockSpec(memory_space=pl.ANY)] * 2,
        out_specs=pl.BlockSpec(memory_space=pltpu.MemorySpace.VMEM),
        scratch_shapes=[pltpu.SemaphoreType.DMA((2,))],
        compiler_params=pltpu.CompilerParams(vmem_limit_bytes=4 * 2**20),
        name="payload",
    )(in_hbm(cache_latent), in_hbm(cache_rope))


def upper(rows):
    return (rows // 2 + 15) // 16 * 16


def relay_kernel(bundles, offsets, table, info, loads, seen, fore, back, *outs):
    chosen, sends = outs[0], outs[1:]
    me = table[PLACE, 0]
    last = len(offsets) // 2
    rows = fore.shape[1]
    for side, (way, arrived, out) in enumerate(((1, fore, sends[0]), (-1, back, sends[1]))):
        chosen[side] = arrived[table[SLOT, offsets.index(-way)]]
        owner = seen[me, offsets.index(-way)]
        for d in range(2, last + 1):
            asker = seen[me, offsets.index(way * (d - 1))]
            pick = jnp.int32(0)
            for b in range(bundles):
                hit = info[asker, 0, b] == owner
                pick = jnp.where(hit, info[asker, 0, bundles + b], pick)
            slot = lax.rem(pick, loads[owner])
            start = (d - 2) * rows
            if d < last:
                out[pl.ds(start, rows), :] = arrived[slot]
            elif way == 1:
                out[pl.ds(start, upper(rows)), :] = arrived[slot, : upper(rows), :]
            else:
                out[pl.ds(start, rows - upper(rows)), :] = arrived[slot, upper(rows) :, :]


def relay(table, info, loads, seen, bundles, offsets, fore, back):
    _, rows, wide = fore.shape
    full = (len(offsets) // 2 - 2) * rows
    vmem = pl.BlockSpec(memory_space=pltpu.MemorySpace.VMEM)
    smem = pl.BlockSpec(memory_space=pltpu.MemorySpace.SMEM)
    return pl.pallas_call(
        functools.partial(relay_kernel, bundles, offsets),
        out_shape=[
            jax.ShapeDtypeStruct((2, rows, wide), fore.dtype),
            jax.ShapeDtypeStruct((full + upper(rows), wide), fore.dtype),
            jax.ShapeDtypeStruct((full + rows - upper(rows), wide), fore.dtype),
        ],
        in_specs=[smem] * 4 + [vmem] * 2,
        out_specs=[vmem] * 3,
        compiler_params=pltpu.CompilerParams(vmem_limit_bytes=6 * 2**20),
        name="relay",
    )(table, info, loads, seen, fore, back)


def join_kernel(rows, fore, back, out):
    if out.shape[0] == 2:
        out[0] = fore[:rows, :]
        out[1] = back[:rows, :]
    else:
        out[0, : fore.shape[0], :] = fore[...]
        out[0, fore.shape[0] :, :] = back[...]


def join(count, rows, fore, back):
    vmem = pl.BlockSpec(memory_space=pltpu.MemorySpace.VMEM)
    return pl.pallas_call(
        functools.partial(join_kernel, rows),
        out_shape=jax.ShapeDtypeStruct((count, rows, fore.shape[1]), fore.dtype),
        in_specs=[vmem] * 2,
        out_specs=vmem,
        compiler_params=pltpu.CompilerParams(vmem_limit_bytes=4 * 2**20),
        name="join",
    )(fore, back)


def slots_kernel(plan, own, indices, bundles, final, scale, table, info, *refs):
    count, heads = len(plan), len(indices[0])
    refs = list(refs)
    q_ref, qr_ref, w_hbm = refs.pop(0), refs.pop(0), refs.pop(0)
    w_ref = w_hbm
    if count > 1:
        w_ref, w_sem = refs.pop(-2), refs.pop(-1)
        w_copy = pltpu.make_async_copy(w_hbm, w_ref, w_sem)
        w_copy.start()
    if own:
        full_lat, full_rope = refs.pop(0), refs.pop(0)
    parts = [[(refs.pop(0), index) for index in slot] for slot in indices]
    lat, rope, mixed = refs.pop(-3), refs.pop(-2), refs.pop(-1)
    if own:
        own_lat, own_rope, sems = refs.pop(-3), refs.pop(-2), refs.pop(-1)
        slot = table[SLOT, plan[0]]
        copies = [
            pltpu.make_async_copy(full_lat.at[slot], own_lat, sems.at[0]),
            pltpu.make_async_copy(full_rope.at[slot], own_rope, sems.at[1]),
        ]
        for copy in copies:
            copy.start()
    into = refs.pop(-1) if final else None
    out_ref = refs.pop(-1)
    earlier = refs
    total_rows = q_ref.shape[1]
    rows = lat.shape[0] // heads
    dims = rope.shape[0] // heads

    def bundle(i, _):
        j = lax.rem(i + own, count)
        for at in range(count):

            @pl.when(j == at)
            def _():
                if own and at == 0:
                    for copy in copies:
                        copy.wait()
                    lat[...] = own_lat[...]
                    rope[...] = own_rope[...]
                    return
                for m, (part, index) in enumerate(parts[at - own]):
                    to = jnp.bitwise_xor(table[PLACE, 1], m)
                    lat[pl.ds(pl.multiple_of(to * rows, rows), rows), :] = part[index, :rows, :]
                    rope[pl.ds(pl.multiple_of(to * dims, dims), dims), :] = part[index, rows:, :]

        column = plan[0] + j
        length = info[table[OWNER, column], 0, 2 * bundles + table[SLOT, column]]
        b = table[BUNDLE, column]
        past = lax.broadcasted_iota(jnp.int32, (1, lat.shape[0]), 1) >= length
        s = lax.dot_general(
            q_ref[b], lat[...], (((1,), (1,)), ((), ())), preferred_element_type=jnp.float32
        )
        s = s + jnp.dot(qr_ref[b], rope[...], preferred_element_type=jnp.float32)
        s = s + jnp.where(past, -1e30, 0.0)
        w = jnp.exp((s - jnp.max(s, axis=1, keepdims=True)) * scale)
        w = w * (1.0 / jnp.sum(w, axis=1, keepdims=True))
        o = jnp.dot(w.astype(jnp.bfloat16), lat[...], preferred_element_type=jnp.float32)
        start = pl.multiple_of(j * total_rows, total_rows)
        for c in range(mixed.shape[0]):
            mixed[c, pl.ds(start, total_rows), :] = o[:, c * 128 : (c + 1) * 128]
        return 0

    lax.fori_loop(0, count, bundle, 0)
    if count > 1:
        w_copy.wait()
    local_heads, _, value_width = w_ref.shape
    n = mixed.shape[1] // local_heads
    at = 0
    if final:
        for piece in earlier:
            into[pl.ds(at, piece.shape[0]), :] = piece[...]
            at += piece.shape[0]
    else:
        into = out_ref
    for h in range(local_heads):
        x = jnp.concatenate(
            [mixed[c, pl.ds(h, n, stride=local_heads), :] for c in range(mixed.shape[0])], axis=1
        ).astype(jnp.bfloat16)
        v = jnp.dot(x, w_ref[h], preferred_element_type=jnp.float32)
        into[pl.ds(at, n), h * value_width : (h + 1) * value_width] = v
    if final:
        out_ref[...] = into[...].astype(out_ref.dtype)


def attend_slots(plan, table, info, q, qr, full, parts, bundles, w_uv, earlier=None):
    own = 1 if full is not None else 0
    final = earlier is not None
    earlier = list(earlier or ())
    count, heads = len(plan), len(parts[0])
    _, q_rows, wide = q.shape
    dims = qr.shape[2]
    positions = (parts[0][0][0].shape[1] - dims // heads) * heads
    local_heads, _, value_width = w_uv.shape
    vmem = pl.BlockSpec(memory_space=pltpu.MemorySpace.VMEM)
    smem = pl.BlockSpec(memory_space=pltpu.MemorySpace.SMEM)
    fetch = count > 1
    args = [q, qr, in_hbm(w_uv) if fetch else w_uv]
    in_specs = [vmem, vmem, pl.BlockSpec(memory_space=pl.ANY) if fetch else vmem]
    if own:
        args += [in_hbm(x) for x in full]
        in_specs += [pl.BlockSpec(memory_space=pl.ANY)] * 2
    args += [array for slot in parts for array, _ in slot] + earlier
    in_specs += [vmem] * (len(args) - len(in_specs))
    done = sum(e.shape[0] for e in earlier) + count * q_rows // local_heads
    out_shape = (done, local_heads * value_width)
    caches = [pltpu.VMEM((positions, wide), jnp.bfloat16), pltpu.VMEM((dims, wide), jnp.bfloat16)]
    scratch = [pltpu.VMEM(out_shape, jnp.float32)] if final else []
    if own:
        scratch += caches + [pltpu.SemaphoreType.DMA((2,))]
    scratch += caches + [pltpu.VMEM((wide // 128, count * q_rows, 128), jnp.float32)]
    if fetch:
        scratch += [pltpu.VMEM(w_uv.shape, w_uv.dtype), pltpu.SemaphoreType.DMA]
    return pl.pallas_call(
        functools.partial(
            slots_kernel, plan, own, [[index for _, index in slot] for slot in parts], bundles,
            final, 1.0 / math.sqrt(VD + ROPE),
        ),
        out_shape=jax.ShapeDtypeStruct(out_shape, jnp.bfloat16 if final else jnp.float32),
        in_specs=[smem] * 2 + in_specs,
        out_specs=vmem,
        scratch_shapes=scratch,
        compiler_params=pltpu.CompilerParams(vmem_limit_bytes=(18 if fetch else 12) * 2**20),
        name="attend_slots",
    )(table, info, *args)


def add_in(table, per_head, columns, own, got, before, after):
    part = own[...]
    for g in got:
        part = part + g[...].astype(jnp.float32)
    for y in range(per_head):
        rank = table[PLACE, 1] * per_head + y
        hit = table[OWNER, columns[0]] == rank
        for c in columns[1:]:
            hit = hit | (table[OWNER, c] == rank)
        now = jnp.where(hit, part, 0.0)
        after[y] = now if before is None else before[y] + now


def settle_kernel(masks, per_head, groups, prev_columns, has_total, table, *refs):
    refs = list(refs)
    sources = [(refs.pop(0), refs.pop(0)) for _ in groups]
    if prev_columns:
        prev_own, prev_got = refs.pop(0), [refs.pop(0) for _ in masks]
        before = refs.pop(0) if has_total else None
    head = table[PLACE, 1]
    for columns, (both, near) in zip(groups, sources):
        chip = both[...].astype(jnp.float32) + near[...].astype(jnp.float32)
        block = chip.shape[0] // len(columns)
        one = chip[:block]
        other = chip[block:] if len(columns) > 1 else None
        for m in masks if other is not None else masks[:1]:
            piece = one
            if other is not None:
                piece = jnp.where(table[TARGET, columns[0]] == jnp.bitwise_xor(head, m), one, other)
            refs.pop(0)[...] = piece.astype(jnp.bfloat16)
        if other is not None:
            one = jnp.where(table[TARGET, columns[0]] == head, one, other)
        refs.pop(0)[...] = one
    if prev_columns:
        add_in(table, per_head, prev_columns, prev_own, prev_got, before, refs.pop(0))


def settle_step(table, masks, per_head, groups, sources, previous):
    n = sources[0][0].shape[0] // len(groups[0])
    wide = sources[0][0].shape[1]
    vmem = pl.BlockSpec(memory_space=pltpu.MemorySpace.VMEM)
    args, prev_columns, has_total = [x for source in sources for x in source], None, False
    if previous is not None:
        prev_columns, prev_own, prev_got, total = previous
        has_total = total is not None
        args += [prev_own, *prev_got] + ([total] if has_total else [])
    out = []
    for columns in groups:
        sends = len(masks) if len(columns) > 1 else 1
        out += [jax.ShapeDtypeStruct((n, wide), jnp.bfloat16)] * sends
        out.append(jax.ShapeDtypeStruct((n, wide), jnp.float32))
    if previous is not None:
        out.append(jax.ShapeDtypeStruct((per_head, n, wide), jnp.float32))
    outs = pl.pallas_call(
        functools.partial(settle_kernel, masks, per_head, groups, prev_columns, has_total),
        out_shape=out,
        in_specs=[pl.BlockSpec(memory_space=pltpu.MemorySpace.SMEM)] + [vmem] * len(args),
        out_specs=[vmem] * len(out),
        compiler_params=pltpu.CompilerParams(vmem_limit_bytes=4 * 2**20),
        name="settle",
    )(table, *args)
    outs = list(outs)
    states = []
    for columns in groups:
        sends = [outs.pop(0) for _ in (masks if len(columns) > 1 else masks[:1])]
        states.append((sends * (1 if len(columns) > 1 else len(masks)), outs.pop(0)))
    return states, outs.pop(0) if previous is not None else None


def finish_kernel(per_head, steps, roll, table, info, seen, before, *refs):
    *refs, out = refs
    each = len(refs) // len(steps)
    parts = []
    for i in range(len(steps)):
        own, *got = refs[each * i : each * (i + 1)]
        part = own[...]
        for g in got:
            part = part + g[...].astype(jnp.float32)
        parts.append(part)
    n = before.shape[1]
    slots = n // roll
    to = lax.broadcasted_iota(jnp.int32, (n, n), 0)
    source = lax.broadcasted_iota(jnp.int32, (n, n), 1)
    for y in range(per_head):
        rank = table[PLACE, 1] * per_head + y
        wanted = to
        for b in range(slots):
            place = jnp.int32(0)
            for c in range(slots):
                place = jnp.where(seen[rank, c] == info[rank, 0, b], c, place)
            inside = (to >= b * roll) & (to < (b + 1) * roll)
            wanted = jnp.where(inside, to + (place - b) * roll, wanted)
        pick = jnp.where(wanted == source, 1.0, 0.0).astype(jnp.bfloat16)
        total = before[y]
        for columns, part in zip(steps, parts):
            hit = table[OWNER, columns[0]] == rank
            for c in columns[1:]:
                hit = hit | (table[OWNER, c] == rank)
            total = total + jnp.where(hit, part, 0.0)
        moved = jnp.dot(pick, total.astype(jnp.bfloat16), preferred_element_type=jnp.float32)
        out[pl.ds(y * n, n), :] = moved.astype(out.dtype)


def finish(table, info, seen, per_head, roll, total, states):
    _, n, wide = total.shape
    steps = [state[0] for state in states]
    args = [x for _, own, got in states for x in (own, *got)]
    vmem = pl.BlockSpec(memory_space=pltpu.MemorySpace.VMEM)
    smem = pl.BlockSpec(memory_space=pltpu.MemorySpace.SMEM)
    return pl.pallas_call(
        functools.partial(finish_kernel, per_head, steps, roll),
        out_shape=jax.ShapeDtypeStruct((per_head * n, wide), jnp.bfloat16),
        in_specs=[smem] * 3 + [vmem] * (1 + len(args)),
        out_specs=vmem,
        compiler_params=pltpu.CompilerParams(vmem_limit_bytes=6 * 2**20),
        name="finish",
    )(table, info, seen, total, *args)


def local_ring(
    q_latent, q_rope, cache_latent, cache_rope, lengths, loads, owner_rank, owner_pick, w_uv, w_out
):
    ranks = lax.axis_size("dp")
    heads = lax.axis_size("head")
    bundles = owner_rank.shape[0]
    local_heads = w_uv.shape[0]
    roll_count = q_latent.shape[0] // bundles
    per_head = ranks // heads
    last = ranks // 2
    order, where, offsets, seen = ring_tables(ranks)
    seen = jnp.asarray(seen, jnp.int32)
    ahead = [(order[i], order[(i + 1) % ranks]) for i in range(ranks)]
    behind = [(b, a) for a, b in ahead]

    def move(x, pairs, axis="dp"):
        return lax.ppermute(x, axis, pairs)

    payload = payload_of(cache_latent, cache_rope, heads)
    fore, back = move(payload, ahead), move(payload, behind)
    facts = [jnp.broadcast_to(x[None], (ranks, x.shape[0])) for x in (owner_rank, owner_pick, lengths)]
    info = lax.all_to_all(
        jnp.concatenate(facts, axis=1), "dp", split_axis=0, concat_axis=0, tiled=True
    )
    info = jnp.maximum(info, 0)[:, None]
    table = in_hbm(plan_of(seen, owner_rank, owner_pick, loads, per_head))
    q = q_latent.reshape(bundles, roll_count * local_heads, -1)
    qr = q_rope.reshape(bundles, roll_count * local_heads, -1)

    def share(chosen):
        found = {0: chosen}
        bit = heads // 2
        while bit:
            pairs = [(i, i ^ bit) for i in range(heads)]
            for m in list(found):
                found[m ^ bit] = move(found[m], pairs, "head")
            bit //= 2
        return [found[m] for m in range(heads)]

    rows = payload.shape[1]
    chosen, fore, back = relay(table, info, loads, seen, bundles, offsets, fore, back)
    groups = {}
    for k in range(1, last + 1):
        if k > 1:
            if k > 2:
                fore, back = fore[rows:], back[rows:]
            fore = move(fore, ahead)
            back = move(back, behind)
            chosen = join(2 if k < last else 1, rows, fore, back)
        parts = share(chosen)
        groups[2 * k - 1] = [(p, 0) for p in parts]
        if k < last:
            groups[2 * k] = [(p, 1) for p in parts]

    def attend(plan, full=None, earlier=None):
        return attend_slots(
            plan, table, info, q, qr, full, [groups[c] for c in plan[(full is not None) :]],
            bundles, w_uv, earlier,
        )

    chunks = []
    for tag, plans in chunk_plans(ranks).items():
        earlier = []
        for n, plan in enumerate(plans):
            full = (cache_latent, cache_rope) if plan[0] == 0 else None
            carried = earlier if n == len(plans) - 1 else None
            earlier.append(attend(plan, full, carried))
        chunks.append((tag, earlier[-1]))
    half = chunks[0][1].shape[1] // 2

    def project(pieces):
        product = jnp.dot(jnp.concatenate(pieces), w_out, preferred_element_type=jnp.float32)
        return product.astype(jnp.bfloat16)

    def target(p, column):
        return order[(where[p] + offsets[column]) % ranks] // per_head

    masks = list(range(2, heads, 2))

    def settle(groups, products, previous):
        cores = [(i, i ^ 1) for i in range(heads)]
        sources = [(both, move(both, cores, "head")) for both in products]
        made, total = settle_step(table, masks, per_head, groups, sources, previous)
        states = []
        for columns, (to_send, own) in zip(groups, made):
            got = []
            for k, m in enumerate(masks):
                pairs = []
                for p in range(ranks):
                    for t in sorted({target(p, c) for c in columns}):
                        pairs.append((p * heads + (t ^ m), p * heads + t))
                got.append(move(to_send[k], pairs, ("dp", "head")))
            states.append((columns, own, got))
        return states, total

    arrived = {}
    for tag, values in chunks:
        fore = back = values
        for k in range(1, last):
            if k == last - 1 and tag == chunks[-1][0]:
                break
            fore = move(fore, ahead)
            back = move(back, behind)
            arrived[tag, k] = fore, back
        fore_on, fore_end = fore[:, :half], fore[:, half:]
        back_on, back_end = back[:, half:], back[:, :half]
        if k == last - 1 and (tag, k) not in arrived:
            fore_on = move(fore_on, ahead)
            back_on = move(back_on, behind)
            fore_end = move(fore_end, ahead)
            back_end = move(back_end, behind)
            arrived[tag, k] = (
                jnp.concatenate([fore_on, fore_end], axis=1),
                jnp.concatenate([back_end, back_on], axis=1),
            )
        left = move(fore_on, ahead)
        right = move(back_on, behind)
        arrived[tag, last] = (jnp.concatenate([left, right], axis=1),)

    def pieces(k):
        return [arrived[tag, k][side] for side in range(2 if k < last else 1) for tag, _ in chunks]

    products = [project([values for _, values in chunks])]
    products += [project(pieces(k)) for k in range(1, last + 1)]
    (state,), total = settle([[0]], products[:1], None)
    for k in range(1, last - 1):
        columns = [2 * k - 1, 2 * k]
        (state,), total = settle([columns], products[k : k + 1], (*state, total))
    columns = [2 * last - 3, 2 * last - 2]
    before, total = settle([columns], products[last - 1 : last], (*state, total))
    final, _ = settle([[2 * last - 1]], products[last:], None)
    states = before + final
    return finish(table, info, seen, per_head, roll_count, total, states)


def local(*args):
    ranks, heads = lax.axis_size("dp"), lax.axis_size("head")
    bundles = args[6].shape[0]
    if ranks == bundles and ring_fits(ranks, heads):
        return local_ring(*args)
    return local_general(*args)


def solution(mesh):
    in_specs = (
        P("dp", "head"),
        P("dp", "head"),
        P("dp", None, None),
        P("dp", None, None),
        P("dp"),
        P(),
        P("dp"),
        P("dp"),
        P("head", None, None),
        P("head", "dp"),
    )
    out_specs = P("head", "dp")
    return jax.shard_map(local, mesh=mesh, in_specs=in_specs, out_specs=out_specs, check_vma=False)
```
